128 devices in a mesh: wide: 16 (over z_hi, x, core), narrow: 8 (over z_lo, y).
Axes of the slice: x: 4, y: 4, z: 4 (z_hi: 2, z_lo: 2; z = z_hi * 2 + z_lo), core: 2. Of those that a mesh axis runs over, the one named last changes fastest.
Arguments:
- tokens: bfloat16 [12288, 1024], P(('wide', 'narrow')), may hold values from -6 to 6
- cotangent: bfloat16 [12288, 1024], P(('wide', 'narrow')), may hold values from -6 to 6
- segments: int32 [16, 768], P('wide'), may hold values from 0 to 3, never falling along the last dimension, each value on 1 to 384 neighbouring positions
- w_query: bfloat16 [1024, 1024], P(None, 'narrow'), may hold values from -0.1875 to 0.1875
- w_key: bfloat16 [1024, 1024], P(None, 'narrow'), may hold values from -0.1875 to 0.1875
- w_value: bfloat16 [1024, 1024], P(None, 'narrow'), may hold values from -0.1875 to 0.1875
- w_out: bfloat16 [1024, 1024], P('narrow'), may hold values from -1.5 to 1.5
- w_gate: bfloat16 [1024, 4096], P(None, 'narrow'), may hold values from -0.1875 to 0.1875
- w_up: bfloat16 [1024, 4096], P(None, 'narrow'), may hold values from -0.1875 to 0.1875
- w_down: bfloat16 [4096, 1024], P('narrow'), may hold values from -0.09375 to 0.09375
- gain_one: float32 [1024], replicated, may hold values from 0.25 to 1.75
- bias_one: float32 [1024], replicated, may hold values from -2.5 to 2.5
- gain_two: float32 [1024], replicated, may hold values from 0.25 to 1.75
- bias_two: float32 [1024], replicated, may hold values from -2.5 to 2.5
Outputs:
- layer_out: float32 [12288, 1024], P(('wide', 'narrow'))
- input_grad: float32 [12288, 1024], P(('wide', 'narrow'))
- grad_query: float32 [1024, 1024], P(None, 'narrow')
- grad_key: float32 [1024, 1024], P(None, 'narrow')
- grad_value: float32 [1024, 1024], P(None, 'narrow')
- grad_out: float32 [1024, 1024], P('narrow')
- grad_gate: float32 [1024, 4096], P(None, 'narrow')
- grad_up: float32 [1024, 4096], P(None, 'narrow')
- grad_down: float32 [4096, 1024], P('narrow')
- grad_gain_one: float32 [1024], replicated
- grad_bias_one: float32 [1024], replicated
- grad_gain_two: float32 [1024], replicated
- grad_bias_two: float32 [1024], replicated
The draws below stay inside these ranges and needn't reach their ends.
Inputs may be any that keep to these rules, and one draw needn't show every extreme that they name: `segments`: within each row of 768 tokens segment numbers never fall; each segment holds 1 to 384 tokens and one holds exactly 384.
All inputs are finite; a program needn't handle non-finite values.
Results may differ from the reference program's by a relative error of at most 0.03.
Values may be sent and summed in bfloat16 or wider, within the bound.
No kernel may reach another device: no remote copies, remote signals or barrier semaphores. Data moves between devices by JAX's collectives and lax.ppermute only.
A program may use at most 128 MiB of HBM per device.

```python
import math
import jax
import jax.numpy as jnp
import numpy as np
from jax import lax

D = 1024
HEADS = 16
HD = 64
FF = 4096
LEN = 768
SEGS = 4
SPAN = 384
NROWS = 16
TOKENS = 12288


def block_levels(rng, extent, split, smallest, top_value):
    loudness, own = 1.0, jax.random.fold_in(rng, 6)
    for dim, parts in split:
        heights = jnp.exp(jax.random.uniform(jax.random.fold_in(own, dim), (parts,), jnp.float32, smallest / len(split), top_value / len(split)))
        loudness = loudness * jnp.repeat(heights, extent[dim] // parts).reshape([-1 if axis == dim else 1 for axis in range(len(extent))])
    return loudness


def split_up(count, total, bound, slope):
    portions = [(1 << 20) // math.isqrt(rank ** slope) + 1 for rank in range(2, count + 1)]
    surplus, given = total - bound - (count - 1), [1] * (count - 1)
    while surplus > 0:
        movable = [i for i in range(count - 1) if given[i] < bound]
        pool, left = sum([portions[i] for i in movable]), surplus
        for i in movable:
            addition = min(bound - given[i], max(1, left * portions[i] // pool), surplus)
            given[i] = given[i] + addition
            surplus = surplus - addition
    return np.array([bound] + given)


def uneven_parts(own_key, number_of, total, reach, lean):
    if number_of == 2:
        one = jax.random.randint(own_key, (), max(1, total - reach), min(reach, total - 1) + 1)
        return jnp.stack([one, total - one])
    sizes = jnp.asarray(split_up(number_of, total, reach, lean), jnp.int32)
    twos = (number_of - 1) // 2
    giver, taker = sizes[1:1 + 2 * twos:2], sizes[2:2 + 2 * twos:2]
    room = jnp.minimum(giver - 1, reach - taker)
    shifted = jax.random.randint(jax.random.fold_in(own_key, 1), (twos,), 0, 1 << 20) % (room + 1)
    sizes = sizes.at[1:1 + 2 * twos:2].set(giver - shifted).at[2:2 + 2 * twos:2].set(taker + shifted)
    return sizes[jax.random.permutation(jax.random.fold_in(own_key, 2), number_of)]


def scatter_about(key, shape, scale, most, cuts=(), kind=jnp.bfloat16):
    values = scale * jax.random.normal(key, shape, jnp.float32)
    if cuts:
        values = values * block_levels(key, shape, cuts, -0.22, 0.18)
    return jnp.clip(values, -most, most).astype(kind)


def setup_inputs(seed: int = 0) -> dict:
    key_list = jax.random.split(jax.random.key(seed), 15)
    tokens = scatter_about(key_list[0], (TOKENS, D), 1.0, 6.0, ((0, 128),))
    cotangent = scatter_about(key_list[1], (TOKENS, D), 1.0, 6.0, ((0, 128),))
    segments = jax.vmap(lambda own: jnp.searchsorted(jnp.cumsum(uneven_parts(own, SEGS, LEN, SPAN, 1)), jnp.arange(LEN), side="right"))(jax.random.split(key_list[2], NROWS)).reshape((NROWS, LEN)).astype(jnp.int32)
    w_query = scatter_about(key_list[3], (D, D), D ** -0.5, 0.1875, ((1, 8),))
    w_key = scatter_about(key_list[4], (D, D), D ** -0.5, 0.1875, ((1, 8),))
    w_value = scatter_about(key_list[5], (D, D), D ** -0.5, 0.1875, ((1, 8),))
    w_out = scatter_about(key_list[6], (D, D), (D // 64) ** -0.5, 1.5, ((0, 8),))
    w_gate = scatter_about(key_list[7], (D, FF), D ** -0.5, 0.1875, ((1, 8),))
    w_up = scatter_about(key_list[8], (D, FF), D ** -0.5, 0.1875, ((1, 8),))
    w_down = scatter_about(key_list[9], (FF, D), FF ** -0.5, 0.09375, ((0, 8),))
    gain_one = jnp.clip(1.0 + 0.15 * jax.random.normal(key_list[10], (D,), jnp.float32), 0.25, 1.75)
    bias_one = scatter_about(key_list[11], (D,), 0.3, 2.5, (), jnp.float32)
    gain_two = jnp.clip(1.0 + 0.15 * jax.random.normal(key_list[12], (D,), jnp.float32), 0.25, 1.75)
    bias_two = scatter_about(key_list[13], (D,), 0.3, 2.5, (), jnp.float32)
    return dict(tokens=tokens, cotangent=cotangent, segments=segments, w_query=w_query, w_key=w_key, w_value=w_value, w_out=w_out, w_gate=w_gate, w_up=w_up, w_down=w_down, gain_one=gain_one, bias_one=bias_one, gain_two=gain_two, bias_two=bias_two)


EPS = 1e-05
MASKED = -1e+30
HIGH = lax.Precision.HIGHEST

@jax.custom_vjp
def low(v):
    return lax.optimization_barrier(v.astype(jnp.bfloat16)).astype(jnp.float32)

@jax.custom_vjp
def low_back(v):
    return v

def low_keep(v):
    return (low(v), None)

def low_pass(kept, grad):
    return (grad,)

def back_keep(v):
    return (v, None)

def back_low(kept, grad):
    return (low(grad),)
low.defvjp(low_keep, low_pass)
low_back.defvjp(back_keep, back_low)

def layer_norm(values, gain_vec, bias_vec):
    centred = values - lax.optimization_barrier(jnp.mean(values, axis=-1, keepdims=True))
    spread = lax.optimization_barrier(jnp.mean(centred * centred, axis=-1, keepdims=True))
    return centred * lax.rsqrt(spread + EPS) * gain_vec + bias_vec

def rotary_tables(seg_rows):
    length = seg_rows.shape[-1]
    column = lax.broadcasted_iota(jnp.int32, (length, length), 1)
    row_index = lax.broadcasted_iota(jnp.int32, (length,), 0)
    same_segment = seg_rows[..., :, None] == seg_rows[..., None, :]
    first_index = lax.optimization_barrier(jnp.min(jnp.where(same_segment, column, length), axis=-1))
    position = (row_index - first_index).astype(jnp.float32)
    half_width = HD // 2
    inverse = 10000.0 ** (-(2.0 * jnp.arange(half_width).astype(jnp.float32) / HD))
    angles = position[..., None] * inverse
    return (jnp.cos(angles), jnp.sin(angles), same_segment)

def rotate(values, cosine_table, sine_table):
    half_width = values.shape[-1] // 2
    first_half = values[..., :half_width]
    second_half = values[..., half_width:]
    cosine = cosine_table[..., None, :]
    sine_part = sine_table[..., None, :]
    return jnp.concatenate([first_half * cosine - second_half * sine_part, second_half * cosine + first_half * sine_part], axis=-1)

def attend_row(row_items):
    query_row, key_row, value_row, seg_row = row_items
    cosine_table, sine_table, same_segment = rotary_tables(seg_row)
    queries = low(rotate(query_row, cosine_table, sine_table))
    key_rows = low(rotate(key_row, cosine_table, sine_table))
    score_scale = 1.0 / math.sqrt(HD)
    scores = low_back(jnp.einsum('qhd,khd->hqk', queries, key_rows, precision=HIGH) * score_scale)
    scores = jnp.where(same_segment[None], scores, MASKED)
    row_peak = lax.optimization_barrier(jnp.max(scores, axis=-1, keepdims=True))
    exponent = jnp.exp(scores - row_peak)
    probabilities = low(exponent / lax.optimization_barrier(jnp.sum(exponent, axis=-1, keepdims=True)))
    return jnp.einsum('hqk,khd->qhd', probabilities, value_row, precision=HIGH)

def forward(operands, segments):
    tokens, w_query, w_key, w_value, w_out, w_gate, w_up, w_down, gain_one, bias_one, gain_two, bias_two = operands
    normed_one = low(layer_norm(tokens, gain_one, bias_one))
    query_pre = low_back(jnp.dot(normed_one, w_query, precision=HIGH))
    key_pre = low_back(jnp.dot(normed_one, w_key, precision=HIGH))
    value_all = low_back(low(jnp.dot(normed_one, w_value, precision=HIGH)))
    head_shape = (NROWS, LEN, HEADS, HD)
    attended = lax.map(jax.checkpoint(attend_row), (query_pre.reshape(head_shape), key_pre.reshape(head_shape), value_all.reshape(head_shape), segments))
    attended = low_back(low(attended.reshape(TOKENS, D)))
    branch = low_back(jnp.dot(attended, w_out, precision=HIGH))
    middle = tokens + branch
    normed_two = low(layer_norm(middle, gain_two, bias_two))
    gate_pre = low_back(jnp.dot(normed_two, w_gate, precision=HIGH))
    up_pre = low_back(jnp.dot(normed_two, w_up, precision=HIGH))
    hidden = low(jax.nn.silu(gate_pre) * up_pre)
    return middle + low_back(jnp.dot(hidden, w_down, precision=HIGH))

def reference(tokens, cotangent, segments, w_query, w_key, w_value, w_out, w_gate, w_up, w_down, gain_one, bias_one, gain_two, bias_two):
    operands = tuple((member.astype(jnp.float32) for member in (tokens, w_query, w_key, w_value, w_out, w_gate, w_up, w_down, gain_one, bias_one, gain_two, bias_two)))

    def layer(layer_operands):
        return forward(layer_operands, segments)
    layer_out, pullback = jax.vjp(layer, operands)
    gradients, = pullback(cotangent.astype(jnp.float32))
    return (layer_out, gradients[0], gradients[1], gradients[2], gradients[3], gradients[4], gradients[5], gradients[6], gradients[7], gradients[8], gradients[9], gradients[10], gradients[11])
```

```python
import math

import jax
import jax.numpy as jnp
from jax import lax
from jax.sharding import PartitionSpec as P

HD = 64
EPS = 1e-05
MASKED = -1e30
F32 = jnp.float32
BF16 = jnp.bfloat16


def normalize(values, gain_vec, bias_vec):
    centred = values - jnp.mean(values, axis=-1, keepdims=True)
    inverse = lax.rsqrt(jnp.mean(centred * centred, axis=-1, keepdims=True) + EPS)
    scaled = centred * inverse
    return (scaled * gain_vec + bias_vec, scaled, inverse)


def normalize_back(grad_in, scaled, inverse, gain_vec):
    along = grad_in * gain_vec
    return inverse * (
        along
        - jnp.mean(along, axis=-1, keepdims=True)
        - scaled * jnp.mean(along * scaled, axis=-1, keepdims=True)
    )


def contract_last(left_side, right_side):
    return lax.dot_general(
        left_side, right_side, (((1,), (1,)), ((), ())), preferred_element_type=F32
    )


def contract_first(left_side, right_side):
    return lax.dot_general(
        left_side, right_side, (((0,), (0,)), ((), ())), preferred_element_type=F32
    )


def rotate(values, cosine_table, sine_table):
    half_width = values.shape[-1] // 2
    first_half = values[..., :half_width]
    second_half = values[..., half_width:]
    cosine = cosine_table[:, None, :]
    sine_part = sine_table[:, None, :]
    return jnp.concatenate(
        [
            first_half * cosine - second_half * sine_part,
            second_half * cosine + first_half * sine_part,
        ],
        axis=-1,
    )


def unrotate(values, cosine_table, sine_table):
    half_width = values.shape[-1] // 2
    first_half = values[..., :half_width]
    second_half = values[..., half_width:]
    cosine = cosine_table[:, None, :]
    sine_part = sine_table[:, None, :]
    return jnp.concatenate(
        [
            first_half * cosine + second_half * sine_part,
            second_half * cosine - first_half * sine_part,
        ],
        axis=-1,
    )


def roll_blocks(values, shift_rows):
    doubled = jnp.concatenate([values, values], axis=0)
    return lax.dynamic_slice_in_dim(doubled, shift_rows, values.shape[0], 0)


def narrow_gather(own, count):
    pieces = [own]
    for k in range(1, count):
        pieces.append(
            lax.ppermute(own, "narrow", [((i + k) % count, i) for i in range(count)])
        )
    return jnp.concatenate(pieces, axis=0)


def narrow_scatter(partial, count):
    blocks = partial.reshape(count, partial.shape[0] // count, partial.shape[1])
    total = blocks[0].astype(F32)
    for k in range(1, count):
        total = total + lax.ppermute(
            blocks[k], "narrow", [(i, (i + k) % count) for i in range(count)]
        ).astype(F32)
    return total


def wide_perm(mapping, wide):
    return [(w, mapping(w)) for w in range(wide)]


def wide_allreduce(grads, wide):
    chips_x = wide // 4
    w = lax.axis_index("wide")
    core = w % 2
    xpos = (w // 2) % chips_x
    zhi = w // (2 * chips_x)

    def to_core(v):
        return v ^ 1

    def to_x(k):
        def mapping(v):
            c, xx, zz = v % 2, (v // 2) % chips_x, v // (2 * chips_x)
            return zz * 2 * chips_x + ((xx + k) % chips_x) * 2 + c

        return mapping

    def to_z(v):
        c, xx, zz = v % 2, (v // 2) % chips_x, v // (2 * chips_x)
        return (1 - zz) * 2 * chips_x + xx * 2 + c

    results = []
    for g in grads:
        rows, cols = g.shape
        half = rows // 2
        parts = g.reshape(2, half, cols)
        keep = lax.dynamic_index_in_dim(parts, core, 0, keepdims=False)
        send = lax.dynamic_index_in_dim(parts, 1 - core, 0, keepdims=False)
        summed = keep.astype(F32) + lax.ppermute(send, "wide", wide_perm(to_core, wide)).astype(F32)
        quarter = half // chips_x
        quarters = summed.reshape(chips_x, quarter, cols)
        acc = lax.dynamic_index_in_dim(quarters, xpos, 0, keepdims=False)
        for k in range(1, chips_x):
            piece = lax.dynamic_index_in_dim(quarters, (xpos + k) % chips_x, 0, keepdims=False)
            acc = acc + lax.ppermute(
                piece.astype(BF16), "wide", wide_perm(to_x(k), wide)
            ).astype(F32)
        eighth = quarter // 2
        eighths = acc.reshape(2, eighth, cols)
        mine = lax.dynamic_index_in_dim(eighths, zhi, 0, keepdims=False)
        other = lax.dynamic_index_in_dim(eighths, 1 - zhi, 0, keepdims=False)
        final = (mine + lax.ppermute(other.astype(BF16), "wide", wide_perm(to_z, wide)).astype(F32)).astype(BF16)
        got = lax.ppermute(final, "wide", wide_perm(to_z, wide))
        pair = jnp.concatenate([final, got], axis=0)
        pair = roll_blocks(pair, zhi * eighth)
        pieces = [pair]
        for k in range(1, chips_x):
            pieces.append(
                lax.ppermute(pair, "wide", [(to_x(k)(v), v) for v in range(wide)])
            )
        ring = jnp.concatenate(pieces, axis=0)
        halfrow = roll_blocks(ring, ((chips_x - xpos) % chips_x) * quarter)
        partner = lax.ppermute(halfrow, "wide", wide_perm(to_core, wide))
        whole = jnp.concatenate([halfrow, partner], axis=0)
        whole = roll_blocks(whole, core * half)
        results.append(whole.astype(F32))
    return results


def per_device(
    tokens,
    cotangent,
    segments,
    w_query,
    w_key,
    w_value,
    w_out,
    w_gate,
    w_up,
    w_down,
    gain_one,
    bias_one,
    gain_two,
    bias_two,
):
    count = lax.axis_size("narrow")
    wide = lax.axis_size("wide")
    block = tokens.shape[0]
    narrow_index = lax.axis_index("narrow")
    shift = narrow_index * block

    seg = segments[0]
    length = seg.shape[0]
    column = lax.broadcasted_iota(jnp.int32, (length, length), 1)
    same_orig = seg[:, None] == seg[None, :]
    first_index = jnp.min(jnp.where(same_orig, column, length), axis=-1)
    position = jnp.arange(length, dtype=jnp.int32) - first_index
    seg_rot = roll_blocks(seg, shift)
    pos_rot = roll_blocks(position, shift).astype(F32)
    same_segment = seg_rot[:, None] == seg_rot[None, :]
    inverse = 10000.0 ** (-(2.0 * jnp.arange(HD // 2).astype(F32) / HD))
    angles = pos_rot[:, None] * inverse
    cosine_table, sine_table = jnp.cos(angles), jnp.sin(angles)

    tok_full = narrow_gather(tokens, count)
    cot_full = narrow_gather(cotangent, count)

    inputs = tok_full.astype(F32)
    normed_float, scaled_one, inverse_one = normalize(inputs, gain_one, bias_one)
    normed_one = normed_float.astype(BF16)
    own_scaled_one = scaled_one[:block]
    own_inverse_one = inverse_one[:block]

    heads = w_query.shape[1] // HD
    head_shape = (length, heads, HD)
    queries = rotate(
        jnp.dot(normed_one, w_query, preferred_element_type=F32).reshape(head_shape),
        cosine_table,
        sine_table,
    ).astype(BF16)
    key_rows = rotate(
        jnp.dot(normed_one, w_key, preferred_element_type=F32).reshape(head_shape),
        cosine_table,
        sine_table,
    ).astype(BF16)
    value_rows = (
        jnp.dot(normed_one, w_value, preferred_element_type=F32).astype(BF16).reshape(head_shape)
    )
    score_scale = 1.0 / math.sqrt(HD)
    scores = (
        jnp.einsum("qhd,khd->hqk", queries, key_rows, preferred_element_type=F32) * score_scale
    )
    scores = jnp.where(same_segment[None], scores, MASKED)
    row_peak = jnp.max(scores, axis=-1, keepdims=True)
    exponent = jnp.exp(scores - row_peak)
    row_total = jnp.sum(exponent, axis=-1, keepdims=True)
    probs = exponent / row_total
    probs_low = probs.astype(BF16)
    attended = (
        jnp.einsum("hqk,khd->qhd", probs_low, value_rows, preferred_element_type=F32)
        .astype(BF16)
        .reshape(length, -1)
    )

    branch_partial = jnp.dot(attended, w_out, preferred_element_type=F32).astype(BF16)
    branch_own = narrow_scatter(branch_partial, count)
    middle_own = tokens.astype(F32) + branch_own
    normed_two_float, scaled_two, inverse_two = normalize(middle_own, gain_two, bias_two)
    normed_two = narrow_gather(normed_two_float.astype(BF16), count)

    gate_pre = jnp.dot(normed_two, w_gate, preferred_element_type=F32)
    up_pre = jnp.dot(normed_two, w_up, preferred_element_type=F32)
    sigmoid_gate = jax.nn.sigmoid(gate_pre)
    active = gate_pre * sigmoid_gate
    hidden = (active * up_pre).astype(BF16)
    ffn_partial = jnp.dot(hidden, w_down, preferred_element_type=F32).astype(BF16)
    layer_out = middle_own + narrow_scatter(ffn_partial, count)

    hidden_grad = contract_last(cot_full, w_down)
    grad_down = contract_first(hidden, cot_full)
    gate_grad = (
        hidden_grad * up_pre * sigmoid_gate * (1.0 + gate_pre * (1.0 - sigmoid_gate))
    ).astype(BF16)
    up_grad = (hidden_grad * active).astype(BF16)
    grad_gate = contract_first(normed_two, gate_grad)
    grad_up = contract_first(normed_two, up_grad)
    two_partial = (contract_last(gate_grad, w_gate) + contract_last(up_grad, w_up)).astype(BF16)
    ffn_grads = wide_allreduce(
        [grad_gate.astype(BF16), grad_up.astype(BF16), grad_down.astype(BF16)], wide
    )

    own_two_grad = narrow_scatter(two_partial, count)
    middle_grad = cotangent.astype(F32) + normalize_back(
        own_two_grad, scaled_two, inverse_two, gain_two
    )
    branch_grad = narrow_gather(middle_grad.astype(BF16), count)

    grad_out = contract_first(attended, branch_grad)
    attended_grad = contract_last(branch_grad, w_out).astype(BF16).reshape(head_shape)
    prob_grad = jnp.einsum(
        "qhd,khd->hqk", attended_grad, value_rows, preferred_element_type=F32
    )
    score_grad = (
        probs * (prob_grad - jnp.sum(probs * prob_grad, axis=-1, keepdims=True))
    ).astype(BF16)
    query_grad = score_scale * jnp.einsum(
        "hqk,khd->qhd", score_grad, key_rows, preferred_element_type=F32
    )
    key_grad = score_scale * jnp.einsum(
        "hqk,qhd->khd", score_grad, queries, preferred_element_type=F32
    )
    value_grad = jnp.einsum(
        "hqk,qhd->khd", probs_low, attended_grad, preferred_element_type=F32
    ).astype(BF16).reshape(length, -1)
    query_grad = unrotate(query_grad, cosine_table, sine_table).astype(BF16).reshape(length, -1)
    key_grad = unrotate(key_grad, cosine_table, sine_table).astype(BF16).reshape(length, -1)
    grad_query = contract_first(normed_one, query_grad)
    grad_key = contract_first(normed_one, key_grad)
    grad_value = contract_first(normed_one, value_grad)
    one_partial = (
        contract_last(query_grad, w_query)
        + contract_last(key_grad, w_key)
        + contract_last(value_grad, w_value)
    ).astype(BF16)
    attn_grads = wide_allreduce(
        [
            grad_query.astype(BF16),
            grad_key.astype(BF16),
            grad_value.astype(BF16),
            grad_out.astype(BF16),
        ],
        wide,
    )
    own_one_grad = narrow_scatter(one_partial, count)
    input_grad = middle_grad + normalize_back(
        own_one_grad, own_scaled_one, own_inverse_one, gain_one
    )
    norm_grads = lax.psum(
        (
            jnp.sum(own_one_grad * own_scaled_one, axis=0),
            jnp.sum(own_one_grad, axis=0),
            jnp.sum(own_two_grad * scaled_two, axis=0),
            jnp.sum(own_two_grad, axis=0),
        ),
        ("wide", "narrow"),
    )
    return (
        layer_out,
        input_grad,
        attn_grads[0],
        attn_grads[1],
        attn_grads[2],
        attn_grads[3],
        ffn_grads[0],
        ffn_grads[1],
        ffn_grads[2],
        norm_grads[0],
        norm_grads[1],
        norm_grads[2],
        norm_grads[3],
    )


def solution(mesh):
    placed = (
        P(("wide", "narrow"), None),
        P(("wide", "narrow"), None),
        P("wide", None),
        P(None, "narrow"),
        P(None, "narrow"),
        P(None, "narrow"),
        P("narrow", None),
        P(None, "narrow"),
        P(None, "narrow"),
        P("narrow", None),
        P(),
        P(),
        P(),
        P(),
    )
    return jax.shard_map(
        per_device,
        mesh=mesh,
        in_specs=placed,
        out_specs=(
            P(("wide", "narrow"), None),
            P(("wide", "narrow"), None),
            P(None, "narrow"),
            P(None, "narrow"),
            P(None, "narrow"),
            P("narrow", None),
            P(None, "narrow"),
            P(None, "narrow"),
            P("narrow", None),
            P(),
            P(),
            P(),
            P(),
        ),
        check_vma=False,
    )
```

```python
import math

import jax
import jax.numpy as jnp
from jax import lax
from jax.sharding import PartitionSpec as P

HD = 64
EPS = 1e-05
MASKED = -1e30
F32 = jnp.float32
BF16 = jnp.bfloat16


def normalize(values, gain_vec, bias_vec):
    centred = values - jnp.mean(values, axis=-1, keepdims=True)
    inverse = lax.rsqrt(jnp.mean(centred * centred, axis=-1, keepdims=True) + EPS)
    scaled = centred * inverse
    return (scaled * gain_vec + bias_vec, scaled, inverse)


def normalize_back(grad_in, scaled, inverse, gain_vec):
    along = grad_in * gain_vec
    return inverse * (
        along
        - jnp.mean(along, axis=-1, keepdims=True)
        - scaled * jnp.mean(along * scaled, axis=-1, keepdims=True)
    )


def contract_last(left_side, right_side):
    return lax.dot_general(
        left_side, right_side, (((1,), (1,)), ((), ())), preferred_element_type=F32
    )


def contract_first(left_side, right_side):
    return lax.dot_general(
        left_side, right_side, (((0,), (0,)), ((), ())), preferred_element_type=F32
    )


def rotate(values, cosine_table, sine_table):
    half_width = values.shape[-1] // 2
    first_half = values[..., :half_width]
    second_half = values[..., half_width:]
    cosine = cosine_table[:, None, :]
    sine_part = sine_table[:, None, :]
    return jnp.concatenate(
        [
            first_half * cosine - second_half * sine_part,
            second_half * cosine + first_half * sine_part,
        ],
        axis=-1,
    )


def unrotate(values, cosine_table, sine_table):
    half_width = values.shape[-1] // 2
    first_half = values[..., :half_width]
    second_half = values[..., half_width:]
    cosine = cosine_table[:, None, :]
    sine_part = sine_table[:, None, :]
    return jnp.concatenate(
        [
            first_half * cosine + second_half * sine_part,
            second_half * cosine - first_half * sine_part,
        ],
        axis=-1,
    )


def narrow_gather(own, count):
    slots = jnp.broadcast_to(own[None], (count,) + own.shape)
    got = lax.all_to_all(slots, "narrow", 0, 0, tiled=False)
    return got.reshape(count * own.shape[0], own.shape[1])


def narrow_scatter(partial, count):
    blocks = partial.reshape(count, partial.shape[0] // count, partial.shape[1])
    got = lax.all_to_all(blocks, "narrow", 0, 0, tiled=False)
    return jnp.sum(got.astype(F32), axis=0)


def narrow_gather_async(own, count):
    index = lax.axis_index("narrow")
    rows = own.shape[0]
    whole = jnp.zeros((count * rows, own.shape[1]), own.dtype)
    whole = lax.dynamic_update_slice_in_dim(whole, own, index * rows, 0)
    for k in range(1, count):
        got = lax.ppermute(own, "narrow", [((i + k) % count, i) for i in range(count)])
        whole = lax.dynamic_update_slice_in_dim(whole, got, ((index + k) % count) * rows, 0)
    return whole


def split_hi_lo(values):
    high = values.astype(BF16)
    return high, (values - high.astype(F32)).astype(BF16)


def wide_layout(wide):
    chips_x = wide // 4
    w = lax.axis_index("wide")
    return chips_x, w % 2, (w // 2) % chips_x, w // (2 * chips_x)


def wide_map(wide, dcore=0, dx=0, dz=0, flip_core=False, xor_x=0):
    chips_x = wide // 4
    pairs = []
    for v in range(wide):
        c, xx, zz = v % 2, (v // 2) % chips_x, v // (2 * chips_x)
        c2 = (1 - c) if flip_core else c
        x2 = ((xx ^ xor_x) + dx) % chips_x
        z2 = (zz + dz) % 2
        pairs.append((v, z2 * 2 * chips_x + x2 * 2 + c2))
    return pairs


def wide_allreduce(grad, wide):
    chips_x, core, xpos, zhi = wide_layout(wide)
    rows, cols = grad.shape
    half = rows // 2
    quarter = half // chips_x
    eighth = quarter // 2
    keep = lax.dynamic_slice_in_dim(grad, core * half, half, 0)
    send = lax.dynamic_slice_in_dim(grad, (1 - core) * half, half, 0)
    summed = keep.astype(F32) + lax.ppermute(send, "wide", wide_map(wide, flip_core=True)).astype(F32)
    acc = lax.dynamic_slice_in_dim(summed, xpos * quarter, quarter, 0)
    for k in range(1, chips_x):
        piece = lax.dynamic_slice_in_dim(summed, ((xpos + k) % chips_x) * quarter, quarter, 0)
        acc = acc + lax.ppermute(piece.astype(BF16), "wide", wide_map(wide, dx=k)).astype(F32)
    mine = lax.dynamic_slice_in_dim(acc, zhi * eighth, eighth, 0)
    other = lax.dynamic_slice_in_dim(acc, (1 - zhi) * eighth, eighth, 0)
    final = (mine + lax.ppermute(other.astype(BF16), "wide", wide_map(wide, dz=1)).astype(F32)).astype(BF16)
    part = jnp.zeros((quarter, cols), BF16)
    part = lax.dynamic_update_slice_in_dim(part, final, zhi * eighth, 0)
    part = lax.dynamic_update_slice_in_dim(
        part, lax.ppermute(final, "wide", wide_map(wide, dz=1)), (1 - zhi) * eighth, 0
    )
    halfrows = jnp.zeros((half, cols), BF16)
    halfrows = lax.dynamic_update_slice_in_dim(halfrows, part, xpos * quarter, 0)
    for k in range(1, chips_x):
        got = lax.ppermute(part, "wide", wide_map(wide, dx=chips_x - k))
        halfrows = lax.dynamic_update_slice_in_dim(
            halfrows, got, ((xpos + k) % chips_x) * quarter, 0
        )
    whole = jnp.zeros((rows, cols), BF16)
    whole = lax.dynamic_update_slice_in_dim(whole, halfrows, core * half, 0)
    whole = lax.dynamic_update_slice_in_dim(
        whole, lax.ppermute(halfrows, "wide", wide_map(wide, flip_core=True)), (1 - core) * half, 0
    )
    return whole.astype(F32)


def wide_allreduce_small(values, wide):
    chips_x = wide // 4
    values = values + lax.ppermute(values, "wide", wide_map(wide, flip_core=True))
    values = values + lax.ppermute(values, "wide", wide_map(wide, xor_x=1))
    if chips_x > 2:
        values = values + lax.ppermute(values, "wide", wide_map(wide, xor_x=2))
    return values + lax.ppermute(values, "wide", wide_map(wide, dz=1))


def per_device(
    tokens,
    cotangent,
    segments,
    w_query,
    w_key,
    w_value,
    w_out,
    w_gate,
    w_up,
    w_down,
    gain_one,
    bias_one,
    gain_two,
    bias_two,
):
    count = lax.axis_size("narrow")
    wide = lax.axis_size("wide")
    block = tokens.shape[0]
    narrow_index = lax.axis_index("narrow")
    own_rows = narrow_index * block

    seg = segments[0]
    length = seg.shape[0]
    column = lax.broadcasted_iota(jnp.int32, (length, length), 1)
    same_segment = seg[:, None] == seg[None, :]
    first_index = jnp.min(jnp.where(same_segment, column, length), axis=-1)
    position = (jnp.arange(length, dtype=jnp.int32) - first_index).astype(F32)
    inverse = 10000.0 ** (-(2.0 * jnp.arange(HD // 2).astype(F32) / HD))
    angles = position[:, None] * inverse
    cosine_table, sine_table = jnp.cos(angles), jnp.sin(angles)

    tok_full = narrow_gather(tokens, count)
    cot_full = narrow_gather_async(cotangent, count)

    inputs = tok_full.astype(F32)
    normed_float, scaled_one, inverse_one = normalize(inputs, gain_one, bias_one)
    normed_one = normed_float.astype(BF16)
    own_scaled_one = lax.dynamic_slice_in_dim(scaled_one, own_rows, block, 0)
    own_inverse_one = lax.dynamic_slice_in_dim(inverse_one, own_rows, block, 0)

    heads = w_query.shape[1] // HD
    head_shape = (length, heads, HD)
    queries = rotate(
        jnp.dot(normed_one, w_query, preferred_element_type=F32).reshape(head_shape),
        cosine_table,
        sine_table,
    ).astype(BF16)
    key_rows = rotate(
        jnp.dot(normed_one, w_key, preferred_element_type=F32).reshape(head_shape),
        cosine_table,
        sine_table,
    ).astype(BF16)
    value_rows = (
        jnp.dot(normed_one, w_value, preferred_element_type=F32).astype(BF16).reshape(head_shape)
    )
    score_scale = 1.0 / math.sqrt(HD)
    scores = (
        jnp.einsum("qhd,khd->hqk", queries, key_rows, preferred_element_type=F32) * score_scale
    )
    scores = jnp.where(same_segment[None], scores, MASKED)
    row_peak = jnp.max(scores, axis=-1, keepdims=True)
    exponent = jnp.exp(scores - row_peak)
    row_total = jnp.sum(exponent, axis=-1, keepdims=True)
    probs = exponent / row_total
    probs_low = probs.astype(BF16)
    attended = (
        jnp.einsum("hqk,khd->qhd", probs_low, value_rows, preferred_element_type=F32)
        .astype(BF16)
        .reshape(length, -1)
    )

    branch_partial = jnp.dot(attended, w_out, preferred_element_type=F32).astype(BF16)
    branch_own = narrow_scatter(branch_partial, count)
    middle_own = tokens.astype(F32) + branch_own
    normed_two_float, scaled_two, inverse_two = normalize(middle_own, gain_two, bias_two)
    normed_two = narrow_gather(normed_two_float.astype(BF16), count)

    gate_pre = jnp.dot(normed_two, w_gate, preferred_element_type=F32)
    up_pre = jnp.dot(normed_two, w_up, preferred_element_type=F32)
    sigmoid_gate = jax.nn.sigmoid(gate_pre)
    active = gate_pre * sigmoid_gate
    hidden = (active * up_pre).astype(BF16)
    ffn_partial = jnp.dot(hidden, w_down, preferred_element_type=F32).astype(BF16)

    hidden_grad = contract_last(cot_full, w_down)
    gate_grad = (
        hidden_grad * up_pre * sigmoid_gate * (1.0 + gate_pre * (1.0 - sigmoid_gate))
    ).astype(BF16)
    up_grad = (hidden_grad * active).astype(BF16)
    ffn_grads = jnp.concatenate(
        [
            contract_first(normed_two, jnp.concatenate([gate_grad, up_grad], axis=1)),
            contract_first(cot_full, hidden),
        ],
        axis=1,
    ).astype(BF16)
    two_partial = (contract_last(gate_grad, w_gate) + contract_last(up_grad, w_up)).astype(BF16)
    both = narrow_scatter(jnp.concatenate([ffn_partial, two_partial], axis=1), count)
    d_model = tokens.shape[1]
    layer_out = middle_own + both[:, :d_model]
    own_two_grad = both[:, d_model:]
    ffn_total = wide_allreduce(ffn_grads, wide)

    middle_grad = cotangent.astype(F32) + normalize_back(
        own_two_grad, scaled_two, inverse_two, gain_two
    )
    branch_grad = narrow_gather(middle_grad.astype(BF16), count)

    attended_grad = contract_last(branch_grad, w_out).astype(BF16).reshape(head_shape)
    prob_grad = jnp.einsum(
        "qhd,khd->hqk", attended_grad, value_rows, preferred_element_type=F32
    )
    score_grad = (
        probs * (prob_grad - jnp.sum(probs * prob_grad, axis=-1, keepdims=True))
    ).astype(BF16)
    query_grad = score_scale * jnp.einsum(
        "hqk,khd->qhd", score_grad, key_rows, preferred_element_type=F32
    )
    key_grad = score_scale * jnp.einsum(
        "hqk,qhd->khd", score_grad, queries, preferred_element_type=F32
    )
    value_grad = jnp.einsum(
        "hqk,qhd->khd", probs_low, attended_grad, preferred_element_type=F32
    ).astype(BF16).reshape(length, -1)
    query_grad = unrotate(query_grad, cosine_table, sine_table).astype(BF16).reshape(length, -1)
    key_grad = unrotate(key_grad, cosine_table, sine_table).astype(BF16).reshape(length, -1)
    projection_grads = jnp.concatenate([query_grad, key_grad, value_grad], axis=1)
    attn_grads = jnp.concatenate(
        [
            contract_first(normed_one, projection_grads),
            contract_first(branch_grad, attended),
        ],
        axis=1,
    ).astype(BF16)
    one_float = contract_last(
        projection_grads, jnp.concatenate([w_query, w_key, w_value], axis=1)
    )
    norm_one = jnp.stack(
        [jnp.sum(one_float * scaled_one, axis=0), jnp.sum(one_float, axis=0)]
    )
    norm_two = jnp.stack(
        [jnp.sum(own_two_grad * scaled_two, axis=0), jnp.sum(own_two_grad, axis=0)]
    )
    norm_parts = jnp.concatenate([norm_one, norm_two], axis=0)
    high, low = split_hi_lo(norm_parts)
    extra = jnp.concatenate([high, low, jnp.zeros((8, d_model), BF16)], axis=0)
    one_blocks = one_float.astype(BF16).reshape(count, block, d_model)
    payload = jnp.concatenate(
        [one_blocks, jnp.broadcast_to(extra[None], (count,) + extra.shape)], axis=1
    )
    got = lax.all_to_all(payload, "narrow", 0, 0, tiled=False).astype(F32)
    summed = jnp.sum(got, axis=0)
    own_one_grad = summed[:block]
    norm_narrow = summed[block : block + 4] + summed[block + 4 : block + 8]
    attn_total = wide_allreduce(attn_grads, wide)
    norm_total = wide_allreduce_small(norm_narrow, wide)
    input_grad = middle_grad + normalize_back(
        own_one_grad, own_scaled_one, own_inverse_one, gain_one
    )
    projections = w_query.shape[1]
    ff_cols = w_gate.shape[1]
    return (
        layer_out,
        input_grad,
        attn_total[:, :projections],
        attn_total[:, projections : 2 * projections],
        attn_total[:, 2 * projections : 3 * projections],
        attn_total[:, 3 * projections :].T,
        ffn_total[:, :ff_cols],
        ffn_total[:, ff_cols : 2 * ff_cols],
        ffn_total[:, 2 * ff_cols :].T,
        norm_total[0],
        norm_total[1],
        norm_total[2],
        norm_total[3],
    )


def solution(mesh):
    placed = (
        P(("wide", "narrow"), None),
        P(("wide", "narrow"), None),
        P("wide", None),
        P(None, "narrow"),
        P(None, "narrow"),
        P(None, "narrow"),
        P("narrow", None),
        P(None, "narrow"),
        P(None, "narrow"),
        P("narrow", None),
        P(),
        P(),
        P(),
        P(),
    )
    return jax.shard_map(
        per_device,
        mesh=mesh,
        in_specs=placed,
        out_specs=(
            P(("wide", "narrow"), None),
            P(("wide", "narrow"), None),
            P(None, "narrow"),
            P(None, "narrow"),
            P(None, "narrow"),
            P("narrow", None),
            P(None, "narrow"),
            P(None, "narrow"),
            P("narrow", None),
            P(),
            P(),
            P(),
            P(),
        ),
        check_vma=False,
    )
```

```python
import math

import jax
import jax.numpy as jnp
from jax import lax
from jax.sharding import PartitionSpec as P

HD = 64
EPS = 1e-05
MASKED = -1e30
F32 = jnp.float32
BF16 = jnp.bfloat16


def normalize(values, gain_vec, bias_vec):
    centred = values - jnp.mean(values, axis=-1, keepdims=True)
    inverse = lax.rsqrt(jnp.mean(centred * centred, axis=-1, keepdims=True) + EPS)
    scaled = centred * inverse
    return (scaled * gain_vec + bias_vec, scaled, inverse)


def normalize_back(grad_in, scaled, inverse, gain_vec):
    along = grad_in * gain_vec
    return inverse * (
        along
        - jnp.mean(along, axis=-1, keepdims=True)
        - scaled * jnp.mean(along * scaled, axis=-1, keepdims=True)
    )


def contract_last(left_side, right_side):
    return lax.dot_general(
        left_side, right_side, (((1,), (1,)), ((), ())), preferred_element_type=F32
    )


def contract_first(left_side, right_side):
    return lax.dot_general(
        left_side, right_side, (((0,), (0,)), ((), ())), preferred_element_type=F32
    )


def rotate(values, cosine_table, sine_table):
    half_width = values.shape[-1] // 2
    first_half = values[..., :half_width]
    second_half = values[..., half_width:]
    cosine = cosine_table[:, None, :]
    sine_part = sine_table[:, None, :]
    return jnp.concatenate(
        [
            first_half * cosine - second_half * sine_part,
            second_half * cosine + first_half * sine_part,
        ],
        axis=-1,
    )


def unrotate(values, cosine_table, sine_table):
    half_width = values.shape[-1] // 2
    first_half = values[..., :half_width]
    second_half = values[..., half_width:]
    cosine = cosine_table[:, None, :]
    sine_part = sine_table[:, None, :]
    return jnp.concatenate(
        [
            first_half * cosine + second_half * sine_part,
            second_half * cosine - first_half * sine_part,
        ],
        axis=-1,
    )


def narrow_gather(own, count):
    slots = jnp.broadcast_to(own[None], (count,) + own.shape)
    got = lax.all_to_all(slots, "narrow", 0, 0, tiled=False)
    return got.reshape(count * own.shape[0], own.shape[1])


def narrow_scatter(partial, count):
    blocks = partial.reshape(count, partial.shape[0] // count, partial.shape[1])
    got = lax.all_to_all(blocks, "narrow", 0, 0, tiled=False)
    return jnp.sum(got.astype(F32), axis=0)


def narrow_gather_async(own, count):
    index = lax.axis_index("narrow")
    rows = own.shape[0]
    whole = jnp.zeros((count * rows, own.shape[1]), own.dtype)
    whole = lax.dynamic_update_slice_in_dim(whole, own, index * rows, 0)
    for k in range(1, count):
        got = lax.ppermute(own, "narrow", [((i + k) % count, i) for i in range(count)])
        whole = lax.dynamic_update_slice_in_dim(whole, got, ((index + k) % count) * rows, 0)
    return whole


def split_hi_lo(values):
    high = values.astype(BF16)
    return high, (values - high.astype(F32)).astype(BF16)


def wide_layout(wide):
    chips_x = wide // 4
    w = lax.axis_index("wide")
    return chips_x, w % 2, (w // 2) % chips_x, w // (2 * chips_x)


def wide_map(wide, dcore=0, dx=0, dz=0, flip_core=False, xor_x=0):
    chips_x = wide // 4
    pairs = []
    for v in range(wide):
        c, xx, zz = v % 2, (v // 2) % chips_x, v // (2 * chips_x)
        c2 = (1 - c) if flip_core else c
        x2 = ((xx ^ xor_x) + dx) % chips_x
        z2 = (zz + dz) % 2
        pairs.append((v, z2 * 2 * chips_x + x2 * 2 + c2))
    return pairs


def wide_allreduce(grad, wide):
    chips_x, core, xpos, zhi = wide_layout(wide)
    rows, cols = grad.shape
    half = rows // 2
    quarter = half // chips_x
    eighth = quarter // 2
    keep = lax.dynamic_slice_in_dim(grad, core * half, half, 0)
    send = lax.dynamic_slice_in_dim(grad, (1 - core) * half, half, 0)
    summed = keep.astype(F32) + lax.ppermute(send, "wide", wide_map(wide, flip_core=True)).astype(F32)
    acc = lax.dynamic_slice_in_dim(summed, xpos * quarter, quarter, 0)
    for k in range(1, chips_x):
        piece = lax.dynamic_slice_in_dim(summed, ((xpos + k) % chips_x) * quarter, quarter, 0)
        acc = acc + lax.ppermute(piece.astype(BF16), "wide", wide_map(wide, dx=k)).astype(F32)
    mine = lax.dynamic_slice_in_dim(acc, zhi * eighth, eighth, 0)
    other = lax.dynamic_slice_in_dim(acc, (1 - zhi) * eighth, eighth, 0)
    final = (mine + lax.ppermute(other.astype(BF16), "wide", wide_map(wide, dz=1)).astype(F32)).astype(BF16)
    part = jnp.zeros((quarter, cols), BF16)
    part = lax.dynamic_update_slice_in_dim(part, final, zhi * eighth, 0)
    part = lax.dynamic_update_slice_in_dim(
        part, lax.ppermute(final, "wide", wide_map(wide, dz=1)), (1 - zhi) * eighth, 0
    )
    halfrows = jnp.zeros((half, cols), BF16)
    halfrows = lax.dynamic_update_slice_in_dim(halfrows, part, xpos * quarter, 0)
    for k in range(1, chips_x):
        got = lax.ppermute(part, "wide", wide_map(wide, dx=chips_x - k))
        halfrows = lax.dynamic_update_slice_in_dim(
            halfrows, got, ((xpos + k) % chips_x) * quarter, 0
        )
    whole = jnp.zeros((rows, cols), BF16)
    whole = lax.dynamic_update_slice_in_dim(whole, halfrows, core * half, 0)
    whole = lax.dynamic_update_slice_in_dim(
        whole, lax.ppermute(halfrows, "wide", wide_map(wide, flip_core=True)), (1 - core) * half, 0
    )
    return whole.astype(F32)


def wide_allreduce_small(values, wide):
    chips_x = wide // 4
    values = values + lax.ppermute(values, "wide", wide_map(wide, flip_core=True))
    values = values + lax.ppermute(values, "wide", wide_map(wide, xor_x=1))
    if chips_x > 2:
        values = values + lax.ppermute(values, "wide", wide_map(wide, xor_x=2))
    return values + lax.ppermute(values, "wide", wide_map(wide, dz=1))


def per_device(
    tokens,
    cotangent,
    segments,
    w_query,
    w_key,
    w_value,
    w_out,
    w_gate,
    w_up,
    w_down,
    gain_one,
    bias_one,
    gain_two,
    bias_two,
):
    count = lax.axis_size("narrow")
    wide = lax.axis_size("wide")
    block, d_model = tokens.shape
    narrow_index = lax.axis_index("narrow")
    own_rows = narrow_index * block

    seg = segments[0]
    length = seg.shape[0]
    column = lax.broadcasted_iota(jnp.int32, (length, length), 1)
    same_segment = seg[:, None] == seg[None, :]
    first_index = jnp.min(jnp.where(same_segment, column, length), axis=-1)
    position = (jnp.arange(length, dtype=jnp.int32) - first_index).astype(F32)
    inverse = 10000.0 ** (-(2.0 * jnp.arange(HD // 2).astype(F32) / HD))
    angles = position[:, None] * inverse
    cosine_table, sine_table = jnp.cos(angles), jnp.sin(angles)

    tok_full = narrow_gather(tokens, count)
    head_rows = w_out.shape[0]
    side = narrow_gather(jnp.concatenate([cotangent, w_out], axis=0), count).reshape(
        count, block + head_rows, d_model
    )
    cot_full = side[:, :block].reshape(length, d_model)
    w_out_full = side[:, block:]

    inputs = tok_full.astype(F32)
    normed_float, scaled_one, inverse_one = normalize(inputs, gain_one, bias_one)
    normed_one = normed_float.astype(BF16)
    own_scaled_one = lax.dynamic_slice_in_dim(scaled_one, own_rows, block, 0)
    own_inverse_one = lax.dynamic_slice_in_dim(inverse_one, own_rows, block, 0)

    heads = w_query.shape[1] // HD
    head_shape = (length, heads, HD)
    queries = rotate(
        jnp.dot(normed_one, w_query, preferred_element_type=F32).reshape(head_shape),
        cosine_table,
        sine_table,
    ).astype(BF16)
    key_rows = rotate(
        jnp.dot(normed_one, w_key, preferred_element_type=F32).reshape(head_shape),
        cosine_table,
        sine_table,
    ).astype(BF16)
    value_rows = (
        jnp.dot(normed_one, w_value, preferred_element_type=F32).astype(BF16).reshape(head_shape)
    )
    score_scale = 1.0 / math.sqrt(HD)
    scores = (
        jnp.einsum("qhd,khd->hqk", queries, key_rows, preferred_element_type=F32) * score_scale
    )
    scores = jnp.where(same_segment[None], scores, MASKED)
    row_peak = jnp.max(scores, axis=-1, keepdims=True)
    exponent = jnp.exp(scores - row_peak)
    row_total = jnp.sum(exponent, axis=-1, keepdims=True)
    probs = exponent / row_total
    probs_low = probs.astype(BF16)
    attended = (
        jnp.einsum("hqk,khd->qhd", probs_low, value_rows, preferred_element_type=F32)
        .astype(BF16)
        .reshape(length, -1)
    )

    attended_all = lax.all_to_all(
        jnp.broadcast_to(attended[None], (count,) + attended.shape), "narrow", 0, 0, tiled=False
    )
    branch = jnp.einsum(
        "jtc,jcd->td", attended_all, w_out_full, preferred_element_type=F32
    )
    middle = inputs + branch
    normed_two_float, scaled_two, inverse_two = normalize(middle, gain_two, bias_two)
    normed_two = normed_two_float.astype(BF16)

    gate_pre = jnp.dot(normed_two, w_gate, preferred_element_type=F32)
    up_pre = jnp.dot(normed_two, w_up, preferred_element_type=F32)
    sigmoid_gate = jax.nn.sigmoid(gate_pre)
    active = gate_pre * sigmoid_gate
    hidden = (active * up_pre).astype(BF16)
    ffn_partial = jnp.dot(hidden, w_down, preferred_element_type=F32).astype(BF16)
    layer_out = lax.dynamic_slice_in_dim(middle, own_rows, block, 0) + narrow_scatter(
        ffn_partial, count
    )

    hidden_grad = contract_last(cot_full, w_down)
    gate_grad = (
        hidden_grad * up_pre * sigmoid_gate * (1.0 + gate_pre * (1.0 - sigmoid_gate))
    ).astype(BF16)
    up_grad = (hidden_grad * active).astype(BF16)
    ffn_grads = jnp.concatenate(
        [
            contract_first(normed_two, jnp.concatenate([gate_grad, up_grad], axis=1)),
            contract_first(hidden, cot_full),
        ],
        axis=0,
    ).astype(BF16)
    ffn_total = wide_allreduce(ffn_grads, wide)
    two_partial = (contract_last(gate_grad, w_gate) + contract_last(up_grad, w_up)).astype(BF16)
    own_two_grad = narrow_scatter(two_partial, count)
    own_scaled_two = lax.dynamic_slice_in_dim(scaled_two, own_rows, block, 0)
    own_inverse_two = lax.dynamic_slice_in_dim(inverse_two, own_rows, block, 0)

    middle_grad = cotangent.astype(F32) + normalize_back(
        own_two_grad, own_scaled_two, own_inverse_two, gain_two
    )
    branch_grad = narrow_gather(middle_grad.astype(BF16), count)

    attended_grad = contract_last(branch_grad, w_out).astype(BF16).reshape(head_shape)
    prob_grad = jnp.einsum(
        "qhd,khd->hqk", attended_grad, value_rows, preferred_element_type=F32
    )
    score_grad = (
        probs * (prob_grad - jnp.sum(probs * prob_grad, axis=-1, keepdims=True))
    ).astype(BF16)
    query_grad = score_scale * jnp.einsum(
        "hqk,khd->qhd", score_grad, key_rows, preferred_element_type=F32
    )
    key_grad = score_scale * jnp.einsum(
        "hqk,qhd->khd", score_grad, queries, preferred_element_type=F32
    )
    value_grad = jnp.einsum(
        "hqk,qhd->khd", probs_low, attended_grad, preferred_element_type=F32
    ).astype(BF16).reshape(length, -1)
    query_grad = unrotate(query_grad, cosine_table, sine_table).astype(BF16).reshape(length, -1)
    key_grad = unrotate(key_grad, cosine_table, sine_table).astype(BF16).reshape(length, -1)
    projection_grads = jnp.concatenate([query_grad, key_grad, value_grad], axis=1)
    projections = w_query.shape[1]
    qkv_grads = contract_first(normed_one, projection_grads).astype(BF16)
    attn_grads = jnp.concatenate(
        [
            qkv_grads.reshape(-1, d_model),
            contract_first(attended, branch_grad).astype(BF16),
        ],
        axis=0,
    )
    attn_total = wide_allreduce(attn_grads, wide)
    one_float = contract_last(
        projection_grads, jnp.concatenate([w_query, w_key, w_value], axis=1)
    )
    norm_one = jnp.stack(
        [jnp.sum(one_float * scaled_one, axis=0), jnp.sum(one_float, axis=0)]
    )
    norm_two = jnp.stack(
        [jnp.sum(own_two_grad * own_scaled_two, axis=0), jnp.sum(own_two_grad, axis=0)]
    )
    norm_parts = jnp.concatenate([norm_one, norm_two], axis=0)
    high, low = split_hi_lo(norm_parts)
    extra = jnp.concatenate([high, low, jnp.zeros((8, d_model), BF16)], axis=0)
    one_blocks = one_float.astype(BF16).reshape(count, block, d_model)
    payload = jnp.concatenate(
        [one_blocks, jnp.broadcast_to(extra[None], (count,) + extra.shape)], axis=1
    )
    got = lax.all_to_all(payload, "narrow", 0, 0, tiled=False).astype(F32)
    summed = jnp.sum(got, axis=0)
    own_one_grad = summed[:block]
    norm_narrow = summed[block : block + 4] + summed[block + 4 : block + 8]
    norm_total = wide_allreduce_small(norm_narrow, wide)
    input_grad = middle_grad + normalize_back(
        own_one_grad, own_scaled_one, own_inverse_one, gain_one
    )
    ff_cols = w_gate.shape[1]
    qkv_total = attn_total[: qkv_grads.shape[0] * qkv_grads.shape[1] // d_model].reshape(
        qkv_grads.shape
    )
    return (
        layer_out,
        input_grad,
        qkv_total[:, :projections],
        qkv_total[:, projections : 2 * projections],
        qkv_total[:, 2 * projections :],
        attn_total[qkv_grads.shape[0] * qkv_grads.shape[1] // d_model :],
        ffn_total[:d_model, :ff_cols],
        ffn_total[:d_model, ff_cols:],
        ffn_total[d_model:],
        norm_total[0],
        norm_total[1],
        norm_total[2],
        norm_total[3],
    )


def solution(mesh):
    placed = (
        P(("wide", "narrow"), None),
        P(("wide", "narrow"), None),
        P("wide", None),
        P(None, "narrow"),
        P(None, "narrow"),
        P(None, "narrow"),
        P("narrow", None),
        P(None, "narrow"),
        P(None, "narrow"),
        P("narrow", None),
        P(),
        P(),
        P(),
        P(),
    )
    return jax.shard_map(
        per_device,
        mesh=mesh,
        in_specs=placed,
        out_specs=(
            P(("wide", "narrow"), None),
            P(("wide", "narrow"), None),
            P(None, "narrow"),
            P(None, "narrow"),
            P(None, "narrow"),
            P("narrow", None),
            P(None, "narrow"),
            P(None, "narrow"),
            P("narrow", None),
            P(),
            P(),
            P(),
            P(),
        ),
        check_vma=False,
    )
```

```python
import math

import jax
import jax.numpy as jnp
from jax import lax
from jax.sharding import PartitionSpec as P

HD = 64
EPS = 1e-05
MASKED = -1e30
F32 = jnp.float32
BF16 = jnp.bfloat16


def normalize(values, gain_vec, bias_vec):
    centred = values - jnp.mean(values, axis=-1, keepdims=True)
    inverse = lax.rsqrt(jnp.mean(centred * centred, axis=-1, keepdims=True) + EPS)
    scaled = centred * inverse
    return (scaled * gain_vec + bias_vec, scaled, inverse)


def normalize_back(grad_in, scaled, inverse, gain_vec):
    along = grad_in * gain_vec
    return inverse * (
        along
        - jnp.mean(along, axis=-1, keepdims=True)
        - scaled * jnp.mean(along * scaled, axis=-1, keepdims=True)
    )


def contract_last(left_side, right_side):
    return lax.dot_general(
        left_side, right_side, (((1,), (1,)), ((), ())), preferred_element_type=F32
    )


def contract_first(left_side, right_side):
    return lax.dot_general(
        left_side, right_side, (((0,), (0,)), ((), ())), preferred_element_type=F32
    )


def rotate(values, cosine_table, sine_table):
    half_width = values.shape[-1] // 2
    first_half = values[..., :half_width]
    second_half = values[..., half_width:]
    cosine = cosine_table[:, None, :]
    sine_part = sine_table[:, None, :]
    return jnp.concatenate(
        [
            first_half * cosine - second_half * sine_part,
            second_half * cosine + first_half * sine_part,
        ],
        axis=-1,
    )


def unrotate(values, cosine_table, sine_table):
    half_width = values.shape[-1] // 2
    first_half = values[..., :half_width]
    second_half = values[..., half_width:]
    cosine = cosine_table[:, None, :]
    sine_part = sine_table[:, None, :]
    return jnp.concatenate(
        [
            first_half * cosine + second_half * sine_part,
            second_half * cosine - first_half * sine_part,
        ],
        axis=-1,
    )


def narrow_gather(own, count):
    slots = jnp.broadcast_to(own[None], (count,) + own.shape)
    got = lax.all_to_all(slots, "narrow", 0, 0, tiled=False)
    return got.reshape(count * own.shape[0], own.shape[1])


def narrow_scatter(partial, count):
    blocks = partial.reshape(count, partial.shape[0] // count, partial.shape[1])
    got = lax.all_to_all(blocks, "narrow", 0, 0, tiled=False)
    return jnp.sum(got.astype(F32), axis=0)


def narrow_gather_async(own, count):
    index = lax.axis_index("narrow")
    rows = own.shape[0]
    whole = jnp.zeros((count * rows, own.shape[1]), own.dtype)
    whole = lax.dynamic_update_slice_in_dim(whole, own, index * rows, 0)
    for k in range(1, count):
        got = lax.ppermute(own, "narrow", [((i + k) % count, i) for i in range(count)])
        whole = lax.dynamic_update_slice_in_dim(whole, got, ((index + k) % count) * rows, 0)
    return whole


def split_hi_lo(values):
    high = values.astype(BF16)
    return high, (values - high.astype(F32)).astype(BF16)


def wide_layout(wide):
    chips_x = wide // 4
    w = lax.axis_index("wide")
    return chips_x, w % 2, (w // 2) % chips_x, w // (2 * chips_x)


def wide_map(wide, dcore=0, dx=0, dz=0, flip_core=False, xor_x=0):
    chips_x = wide // 4
    pairs = []
    for v in range(wide):
        c, xx, zz = v % 2, (v // 2) % chips_x, v // (2 * chips_x)
        c2 = (1 - c) if flip_core else c
        x2 = ((xx ^ xor_x) + dx) % chips_x
        z2 = (zz + dz) % 2
        pairs.append((v, z2 * 2 * chips_x + x2 * 2 + c2))
    return pairs


def wide_allreduce(grad, wide):
    chips_x, core, xpos, zhi = wide_layout(wide)
    rows, cols = grad.shape
    half = rows // 2
    quarter = half // chips_x
    eighth = quarter // 2
    keep = lax.dynamic_slice_in_dim(grad, core * half, half, 0)
    send = lax.dynamic_slice_in_dim(grad, (1 - core) * half, half, 0)
    summed = keep.astype(F32) + lax.ppermute(send, "wide", wide_map(wide, flip_core=True)).astype(F32)
    acc = lax.dynamic_slice_in_dim(summed, xpos * quarter, quarter, 0)
    for k in range(1, chips_x):
        piece = lax.dynamic_slice_in_dim(summed, ((xpos + k) % chips_x) * quarter, quarter, 0)
        acc = acc + lax.ppermute(piece.astype(BF16), "wide", wide_map(wide, dx=k)).astype(F32)
    mine = lax.dynamic_slice_in_dim(acc, zhi * eighth, eighth, 0)
    other = lax.dynamic_slice_in_dim(acc, (1 - zhi) * eighth, eighth, 0)
    final = (mine + lax.ppermute(other.astype(BF16), "wide", wide_map(wide, dz=1)).astype(F32)).astype(BF16)
    part = jnp.zeros((quarter, cols), BF16)
    part = lax.dynamic_update_slice_in_dim(part, final, zhi * eighth, 0)
    part = lax.dynamic_update_slice_in_dim(
        part, lax.ppermute(final, "wide", wide_map(wide, dz=1)), (1 - zhi) * eighth, 0
    )
    halfrows = jnp.zeros((half, cols), BF16)
    halfrows = lax.dynamic_update_slice_in_dim(halfrows, part, xpos * quarter, 0)
    for k in range(1, chips_x):
        got = lax.ppermute(part, "wide", wide_map(wide, dx=chips_x - k))
        halfrows = lax.dynamic_update_slice_in_dim(
            halfrows, got, ((xpos + k) % chips_x) * quarter, 0
        )
    whole = jnp.zeros((rows, cols), BF16)
    whole = lax.dynamic_update_slice_in_dim(whole, halfrows, core * half, 0)
    whole = lax.dynamic_update_slice_in_dim(
        whole, lax.ppermute(halfrows, "wide", wide_map(wide, flip_core=True)), (1 - core) * half, 0
    )
    return whole.astype(F32)


def wide_allreduce_small(values, wide):
    chips_x = wide // 4
    values = values + lax.ppermute(values, "wide", wide_map(wide, flip_core=True))
    values = values + lax.ppermute(values, "wide", wide_map(wide, xor_x=1))
    if chips_x > 2:
        values = values + lax.ppermute(values, "wide", wide_map(wide, xor_x=2))
    return values + lax.ppermute(values, "wide", wide_map(wide, dz=1))


def per_device(
    tokens,
    cotangent,
    segments,
    w_query,
    w_key,
    w_value,
    w_out,
    w_gate,
    w_up,
    w_down,
    gain_one,
    bias_one,
    gain_two,
    bias_two,
):
    count = lax.axis_size("narrow")
    wide = lax.axis_size("wide")
    block, d_model = tokens.shape
    narrow_index = lax.axis_index("narrow")
    own_rows = narrow_index * block

    seg = segments[0]
    length = seg.shape[0]
    column = lax.broadcasted_iota(jnp.int32, (length, length), 1)
    same_segment = seg[:, None] == seg[None, :]
    first_index = jnp.min(jnp.where(same_segment, column, length), axis=-1)
    position = (jnp.arange(length, dtype=jnp.int32) - first_index).astype(F32)
    inverse = 10000.0 ** (-(2.0 * jnp.arange(HD // 2).astype(F32) / HD))
    angles = position[:, None] * inverse
    cosine_table, sine_table = jnp.cos(angles), jnp.sin(angles)

    head_rows = w_out.shape[0]
    first = narrow_gather(
        jnp.concatenate([tokens, cotangent, w_out], axis=0), count
    ).reshape(count, 2 * block + head_rows, d_model)
    tok_full = first[:, :block].reshape(length, d_model)
    cot_full = first[:, block : 2 * block].reshape(length, d_model)
    w_out_full = first[:, 2 * block :]

    inputs = tok_full.astype(F32)
    normed_float, scaled_one, inverse_one = normalize(inputs, gain_one, bias_one)
    normed_one = normed_float.astype(BF16)
    own_scaled_one = lax.dynamic_slice_in_dim(scaled_one, own_rows, block, 0)
    own_inverse_one = lax.dynamic_slice_in_dim(inverse_one, own_rows, block, 0)

    heads = w_query.shape[1] // HD
    head_shape = (length, heads, HD)
    queries = rotate(
        jnp.dot(normed_one, w_query, preferred_element_type=F32).reshape(head_shape),
        cosine_table,
        sine_table,
    ).astype(BF16)
    key_rows = rotate(
        jnp.dot(normed_one, w_key, preferred_element_type=F32).reshape(head_shape),
        cosine_table,
        sine_table,
    ).astype(BF16)
    value_rows = (
        jnp.dot(normed_one, w_value, preferred_element_type=F32).astype(BF16).reshape(head_shape)
    )
    score_scale = 1.0 / math.sqrt(HD)
    scores = (
        jnp.einsum("qhd,khd->hqk", queries, key_rows, preferred_element_type=F32) * score_scale
    )
    scores = jnp.where(same_segment[None], scores, MASKED)
    row_peak = jnp.max(scores, axis=-1, keepdims=True)
    exponent = jnp.exp(scores - row_peak)
    row_total = jnp.sum(exponent, axis=-1, keepdims=True)
    probs = exponent / row_total
    probs_low = probs.astype(BF16)
    attended = (
        jnp.einsum("hqk,khd->qhd", probs_low, value_rows, preferred_element_type=F32)
        .astype(BF16)
        .reshape(length, -1)
    )

    attended_all = lax.all_to_all(
        jnp.broadcast_to(attended[None], (count,) + attended.shape), "narrow", 0, 0, tiled=False
    )
    branch = jnp.einsum(
        "jtc,jcd->td", attended_all, w_out_full, preferred_element_type=F32
    )
    middle = inputs + branch
    normed_two_float, scaled_two, inverse_two = normalize(middle, gain_two, bias_two)
    normed_two = normed_two_float.astype(BF16)

    gate_pre = jnp.dot(normed_two, w_gate, preferred_element_type=F32)
    up_pre = jnp.dot(normed_two, w_up, preferred_element_type=F32)
    sigmoid_gate = jax.nn.sigmoid(gate_pre)
    active = gate_pre * sigmoid_gate
    hidden = (active * up_pre).astype(BF16)
    ffn_partial = jnp.dot(hidden, w_down, preferred_element_type=F32).astype(BF16)

    hidden_grad = contract_last(cot_full, w_down)
    gate_grad = (
        hidden_grad * up_pre * sigmoid_gate * (1.0 + gate_pre * (1.0 - sigmoid_gate))
    ).astype(BF16)
    up_grad = (hidden_grad * active).astype(BF16)
    ffn_grads = jnp.concatenate(
        [
            contract_first(normed_two, jnp.concatenate([gate_grad, up_grad], axis=1)),
            contract_first(hidden, cot_full),
        ],
        axis=0,
    ).astype(BF16)
    ffn_total = wide_allreduce(ffn_grads, wide)
    two_partial = (contract_last(gate_grad, w_gate) + contract_last(up_grad, w_up)).astype(BF16)
    both = narrow_scatter(jnp.concatenate([ffn_partial, two_partial], axis=1), count)
    layer_out = lax.dynamic_slice_in_dim(middle, own_rows, block, 0) + both[:, :d_model]
    own_two_grad = both[:, d_model:]
    own_scaled_two = lax.dynamic_slice_in_dim(scaled_two, own_rows, block, 0)
    own_inverse_two = lax.dynamic_slice_in_dim(inverse_two, own_rows, block, 0)

    middle_grad = cotangent.astype(F32) + normalize_back(
        own_two_grad, own_scaled_two, own_inverse_two, gain_two
    )
    branch_grad = narrow_gather(middle_grad.astype(BF16), count)

    attended_grad = contract_last(branch_grad, w_out).astype(BF16).reshape(head_shape)
    prob_grad = jnp.einsum(
        "qhd,khd->hqk", attended_grad, value_rows, preferred_element_type=F32
    )
    score_grad = (
        probs * (prob_grad - jnp.sum(probs * prob_grad, axis=-1, keepdims=True))
    ).astype(BF16)
    query_grad = score_scale * jnp.einsum(
        "hqk,khd->qhd", score_grad, key_rows, preferred_element_type=F32
    )
    key_grad = score_scale * jnp.einsum(
        "hqk,qhd->khd", score_grad, queries, preferred_element_type=F32
    )
    value_grad = jnp.einsum(
        "hqk,qhd->khd", probs_low, attended_grad, preferred_element_type=F32
    ).astype(BF16).reshape(length, -1)
    query_grad = unrotate(query_grad, cosine_table, sine_table).astype(BF16).reshape(length, -1)
    key_grad = unrotate(key_grad, cosine_table, sine_table).astype(BF16).reshape(length, -1)
    projection_grads = jnp.concatenate([query_grad, key_grad, value_grad], axis=1)
    projections = w_query.shape[1]
    qkv_grads = contract_first(normed_one, projection_grads).astype(BF16)
    attn_grads = jnp.concatenate(
        [qkv_grads, contract_first(branch_grad, attended).astype(BF16)], axis=1
    )
    attn_total = wide_allreduce(attn_grads, wide)
    one_float = contract_last(
        projection_grads, jnp.concatenate([w_query, w_key, w_value], axis=1)
    )
    norm_one = jnp.stack(
        [jnp.sum(one_float * scaled_one, axis=0), jnp.sum(one_float, axis=0)]
    )
    norm_two = jnp.stack(
        [jnp.sum(own_two_grad * own_scaled_two, axis=0), jnp.sum(own_two_grad, axis=0)]
    )
    norm_parts = jnp.concatenate([norm_one, norm_two], axis=0)
    high, low = split_hi_lo(norm_parts)
    extra = jnp.concatenate([high, low, jnp.zeros((8, d_model), BF16)], axis=0)
    one_blocks = one_float.astype(BF16).reshape(count, block, d_model)
    payload = jnp.concatenate(
        [one_blocks, jnp.broadcast_to(extra[None], (count,) + extra.shape)], axis=1
    )
    got = lax.all_to_all(payload, "narrow", 0, 0, tiled=False).astype(F32)
    summed = jnp.sum(got, axis=0)
    own_one_grad = summed[:block]
    norm_narrow = summed[block : block + 4] + summed[block + 4 : block + 8]
    norm_total = wide_allreduce_small(norm_narrow, wide)
    input_grad = middle_grad + normalize_back(
        own_one_grad, own_scaled_one, own_inverse_one, gain_one
    )
    ff_cols = w_gate.shape[1]
    return (
        layer_out,
        input_grad,
        attn_total[:, :projections],
        attn_total[:, projections : 2 * projections],
        attn_total[:, 2 * projections : 3 * projections],
        attn_total[:, 3 * projections :].T,
        ffn_total[:d_model, :ff_cols],
        ffn_total[:d_model, ff_cols:],
        ffn_total[d_model:],
        norm_total[0],
        norm_total[1],
        norm_total[2],
        norm_total[3],
    )


def solution(mesh):
    placed = (
        P(("wide", "narrow"), None),
        P(("wide", "narrow"), None),
        P("wide", None),
        P(None, "narrow"),
        P(None, "narrow"),
        P(None, "narrow"),
        P("narrow", None),
        P(None, "narrow"),
        P(None, "narrow"),
        P("narrow", None),
        P(),
        P(),
        P(),
        P(),
    )
    return jax.shard_map(
        per_device,
        mesh=mesh,
        in_specs=placed,
        out_specs=(
            P(("wide", "narrow"), None),
            P(("wide", "narrow"), None),
            P(None, "narrow"),
            P(None, "narrow"),
            P(None, "narrow"),
            P("narrow", None),
            P(None, "narrow"),
            P(None, "narrow"),
            P("narrow", None),
            P(),
            P(),
            P(),
            P(),
        ),
        check_vma=False,
    )
```

```python
import math

import jax
import jax.numpy as jnp
from jax import lax
from jax.sharding import PartitionSpec as P

HD = 64
EPS = 1e-05
MASKED = -1e30
F32 = jnp.float32
BF16 = jnp.bfloat16


def normalize(values, gain_vec, bias_vec):
    centred = values - jnp.mean(values, axis=-1, keepdims=True)
    inverse = lax.rsqrt(jnp.mean(centred * centred, axis=-1, keepdims=True) + EPS)
    scaled = centred * inverse
    return (scaled * gain_vec + bias_vec, scaled, inverse)


def normalize_back(grad_in, scaled, inverse, gain_vec):
    along = grad_in * gain_vec
    return inverse * (
        along
        - jnp.mean(along, axis=-1, keepdims=True)
        - scaled * jnp.mean(along * scaled, axis=-1, keepdims=True)
    )


def contract_last(left_side, right_side):
    return lax.dot_general(
        left_side, right_side, (((1,), (1,)), ((), ())), preferred_element_type=F32
    )


def contract_first(left_side, right_side):
    return lax.dot_general(
        left_side, right_side, (((0,), (0,)), ((), ())), preferred_element_type=F32
    )


def rotate(values, cosine_table, sine_table):
    half_width = values.shape[-1] // 2
    first_half = values[..., :half_width]
    second_half = values[..., half_width:]
    cosine = cosine_table[:, None, :]
    sine_part = sine_table[:, None, :]
    return jnp.concatenate(
        [
            first_half * cosine - second_half * sine_part,
            second_half * cosine + first_half * sine_part,
        ],
        axis=-1,
    )


def unrotate(values, cosine_table, sine_table):
    half_width = values.shape[-1] // 2
    first_half = values[..., :half_width]
    second_half = values[..., half_width:]
    cosine = cosine_table[:, None, :]
    sine_part = sine_table[:, None, :]
    return jnp.concatenate(
        [
            first_half * cosine + second_half * sine_part,
            second_half * cosine - first_half * sine_part,
        ],
        axis=-1,
    )


def narrow_gather(own, count):
    slots = jnp.broadcast_to(own[None], (count,) + own.shape)
    got = lax.all_to_all(slots, "narrow", 0, 0, tiled=False)
    return got.reshape(count * own.shape[0], own.shape[1])


def narrow_scatter(partial, count):
    blocks = partial.reshape(count, partial.shape[0] // count, partial.shape[1])
    got = lax.all_to_all(blocks, "narrow", 0, 0, tiled=False)
    return jnp.sum(got.astype(F32), axis=0)


def narrow_maps(count):
    plane = count // 2

    def build(mapping):
        return [(z * plane + y, mapping(z, y)) for z in range(2) for y in range(plane)]

    up = build(lambda z, y: z * plane + (y + 1) % plane)
    down = build(lambda z, y: z * plane + (y - 1) % plane)
    across = build(lambda z, y: (1 - z) * plane + y)
    return up, down, across


def tree_gather(own, count):
    up, down, across = narrow_maps(count)
    from_below = lax.ppermute(own, "narrow", up)
    from_above = lax.ppermute(own, "narrow", down)
    from_across = lax.ppermute(own, "narrow", across)
    two_above = lax.ppermute(from_below, "narrow", up)
    across_above = lax.ppermute(from_across, "narrow", down)
    across_below = lax.ppermute(from_below, "narrow", across)
    across_two = lax.ppermute(two_above, "narrow", across)
    return jnp.stack(
        [own, from_below, from_above, from_across, two_above, across_above, across_below, across_two]
    )


def slot_order(count):
    plane = count // 2
    index = lax.axis_index("narrow")
    z, y = index // plane, index % plane
    block = jnp.arange(count)
    dz = (block // plane - z) % 2
    dy = (block % plane - y) % plane
    same = jnp.array([0, 2, 4, 1], jnp.int32)
    other = jnp.array([3, 5, 7, 6], jnp.int32)
    return jnp.where(dz == 0, same[dy], other[dy])


def tree_gather_rows(own, count):
    slots = tree_gather(own, count)
    return jnp.take(slots, slot_order(count), axis=0)


def narrow_gather_async(own, count):
    index = lax.axis_index("narrow")
    rows = own.shape[0]
    whole = jnp.zeros((count * rows, own.shape[1]), own.dtype)
    whole = lax.dynamic_update_slice_in_dim(whole, own, index * rows, 0)
    for k in range(1, count):
        got = lax.ppermute(own, "narrow", [((i + k) % count, i) for i in range(count)])
        whole = lax.dynamic_update_slice_in_dim(whole, got, ((index + k) % count) * rows, 0)
    return whole


def split_hi_lo(values):
    high = values.astype(BF16)
    return high, (values - high.astype(F32)).astype(BF16)


def wide_layout(wide):
    chips_x = wide // 4
    w = lax.axis_index("wide")
    return chips_x, w % 2, (w // 2) % chips_x, w // (2 * chips_x)


def wide_map(wide, dcore=0, dx=0, dz=0, flip_core=False, xor_x=0):
    chips_x = wide // 4
    pairs = []
    for v in range(wide):
        c, xx, zz = v % 2, (v // 2) % chips_x, v // (2 * chips_x)
        c2 = (1 - c) if flip_core else c
        x2 = ((xx ^ xor_x) + dx) % chips_x
        z2 = (zz + dz) % 2
        pairs.append((v, z2 * 2 * chips_x + x2 * 2 + c2))
    return pairs


def wide_allreduce(grad, wide):
    chips_x, core, xpos, zhi = wide_layout(wide)
    rows, cols = grad.shape
    half = rows // 2
    quarter = half // chips_x
    eighth = quarter // 2
    keep = lax.dynamic_slice_in_dim(grad, core * half, half, 0)
    send = lax.dynamic_slice_in_dim(grad, (1 - core) * half, half, 0)
    summed = keep.astype(F32) + lax.ppermute(send, "wide", wide_map(wide, flip_core=True)).astype(F32)
    acc = lax.dynamic_slice_in_dim(summed, xpos * quarter, quarter, 0)
    for k in range(1, chips_x):
        piece = lax.dynamic_slice_in_dim(summed, ((xpos + k) % chips_x) * quarter, quarter, 0)
        acc = acc + lax.ppermute(piece.astype(BF16), "wide", wide_map(wide, dx=k)).astype(F32)
    mine = lax.dynamic_slice_in_dim(acc, zhi * eighth, eighth, 0)
    other = lax.dynamic_slice_in_dim(acc, (1 - zhi) * eighth, eighth, 0)
    final = (mine + lax.ppermute(other.astype(BF16), "wide", wide_map(wide, dz=1)).astype(F32)).astype(BF16)
    part = jnp.zeros((quarter, cols), BF16)
    part = lax.dynamic_update_slice_in_dim(part, final, zhi * eighth, 0)
    part = lax.dynamic_update_slice_in_dim(
        part, lax.ppermute(final, "wide", wide_map(wide, dz=1)), (1 - zhi) * eighth, 0
    )
    halfrows = jnp.zeros((half, cols), BF16)
    halfrows = lax.dynamic_update_slice_in_dim(halfrows, part, xpos * quarter, 0)
    for k in range(1, chips_x):
        got = lax.ppermute(part, "wide", wide_map(wide, dx=chips_x - k))
        halfrows = lax.dynamic_update_slice_in_dim(
            halfrows, got, ((xpos + k) % chips_x) * quarter, 0
        )
    whole = jnp.zeros((rows, cols), BF16)
    whole = lax.dynamic_update_slice_in_dim(whole, halfrows, core * half, 0)
    whole = lax.dynamic_update_slice_in_dim(
        whole, lax.ppermute(halfrows, "wide", wide_map(wide, flip_core=True)), (1 - core) * half, 0
    )
    return whole.astype(F32)


def wide_allreduce_small(values, wide):
    chips_x = wide // 4
    values = values + lax.ppermute(values, "wide", wide_map(wide, flip_core=True))
    values = values + lax.ppermute(values, "wide", wide_map(wide, xor_x=1))
    if chips_x > 2:
        values = values + lax.ppermute(values, "wide", wide_map(wide, xor_x=2))
    return values + lax.ppermute(values, "wide", wide_map(wide, dz=1))


def per_device(
    tokens,
    cotangent,
    segments,
    w_query,
    w_key,
    w_value,
    w_out,
    w_gate,
    w_up,
    w_down,
    gain_one,
    bias_one,
    gain_two,
    bias_two,
):
    count = lax.axis_size("narrow")
    wide = lax.axis_size("wide")
    block, d_model = tokens.shape
    narrow_index = lax.axis_index("narrow")
    own_rows = narrow_index * block

    seg = segments[0]
    length = seg.shape[0]
    column = lax.broadcasted_iota(jnp.int32, (length, length), 1)
    same_segment = seg[:, None] == seg[None, :]
    first_index = jnp.min(jnp.where(same_segment, column, length), axis=-1)
    position = (jnp.arange(length, dtype=jnp.int32) - first_index).astype(F32)
    inverse = 10000.0 ** (-(2.0 * jnp.arange(HD // 2).astype(F32) / HD))
    angles = position[:, None] * inverse
    cosine_table, sine_table = jnp.cos(angles), jnp.sin(angles)

    head_rows = w_out.shape[0]
    rows_first = tree_gather_rows(jnp.concatenate([tokens, cotangent], axis=0), count)
    tok_full = rows_first[:, :block].reshape(length, d_model)
    cot_full = rows_first[:, block:].reshape(length, d_model)
    w_out_slots = tree_gather(w_out, count)

    inputs = tok_full.astype(F32)
    normed_float, scaled_one, inverse_one = normalize(inputs, gain_one, bias_one)
    normed_one = normed_float.astype(BF16)
    own_scaled_one = lax.dynamic_slice_in_dim(scaled_one, own_rows, block, 0)
    own_inverse_one = lax.dynamic_slice_in_dim(inverse_one, own_rows, block, 0)

    heads = w_query.shape[1] // HD
    head_shape = (length, heads, HD)
    queries = rotate(
        jnp.dot(normed_one, w_query, preferred_element_type=F32).reshape(head_shape),
        cosine_table,
        sine_table,
    ).astype(BF16)
    key_rows = rotate(
        jnp.dot(normed_one, w_key, preferred_element_type=F32).reshape(head_shape),
        cosine_table,
        sine_table,
    ).astype(BF16)
    value_rows = (
        jnp.dot(normed_one, w_value, preferred_element_type=F32).astype(BF16).reshape(head_shape)
    )
    score_scale = 1.0 / math.sqrt(HD)
    scores = (
        jnp.einsum("qhd,khd->hqk", queries, key_rows, preferred_element_type=F32) * score_scale
    )
    scores = jnp.where(same_segment[None], scores, MASKED)
    row_peak = jnp.max(scores, axis=-1, keepdims=True)
    exponent = jnp.exp(scores - row_peak)
    row_total = jnp.sum(exponent, axis=-1, keepdims=True)
    probs = exponent / row_total
    probs_low = probs.astype(BF16)
    attended = (
        jnp.einsum("hqk,khd->qhd", probs_low, value_rows, preferred_element_type=F32)
        .astype(BF16)
        .reshape(length, -1)
    )

    attended_slots = tree_gather(attended, count)
    branch = jnp.einsum(
        "jtc,jcd->td", attended_slots, w_out_slots, preferred_element_type=F32
    )
    middle = inputs + branch
    normed_two_float, scaled_two, inverse_two = normalize(middle, gain_two, bias_two)
    normed_two = normed_two_float.astype(BF16)

    gate_pre = jnp.dot(normed_two, w_gate, preferred_element_type=F32)
    up_pre = jnp.dot(normed_two, w_up, preferred_element_type=F32)
    sigmoid_gate = jax.nn.sigmoid(gate_pre)
    active = gate_pre * sigmoid_gate
    hidden = (active * up_pre).astype(BF16)
    ffn_partial = jnp.dot(hidden, w_down, preferred_element_type=F32).astype(BF16)

    hidden_grad = contract_last(cot_full, w_down)
    gate_grad = (
        hidden_grad * up_pre * sigmoid_gate * (1.0 + gate_pre * (1.0 - sigmoid_gate))
    ).astype(BF16)
    up_grad = (hidden_grad * active).astype(BF16)
    ffn_grads = jnp.concatenate(
        [
            contract_first(normed_two, jnp.concatenate([gate_grad, up_grad], axis=1)),
            contract_first(hidden, cot_full),
        ],
        axis=0,
    ).astype(BF16)
    ffn_total = lax.psum(ffn_grads, "wide").astype(F32)
    two_partial = (contract_last(gate_grad, w_gate) + contract_last(up_grad, w_up)).astype(BF16)
    both = narrow_scatter(jnp.concatenate([ffn_partial, two_partial], axis=1), count)
    layer_out = lax.dynamic_slice_in_dim(middle, own_rows, block, 0) + both[:, :d_model]
    own_two_grad = both[:, d_model:]
    own_scaled_two = lax.dynamic_slice_in_dim(scaled_two, own_rows, block, 0)
    own_inverse_two = lax.dynamic_slice_in_dim(inverse_two, own_rows, block, 0)

    middle_grad = cotangent.astype(F32) + normalize_back(
        own_two_grad, own_scaled_two, own_inverse_two, gain_two
    )
    branch_grad = tree_gather_rows(middle_grad.astype(BF16), count).reshape(length, d_model)

    attended_grad = contract_last(branch_grad, w_out).astype(BF16).reshape(head_shape)
    prob_grad = jnp.einsum(
        "qhd,khd->hqk", attended_grad, value_rows, preferred_element_type=F32
    )
    score_grad = (
        probs * (prob_grad - jnp.sum(probs * prob_grad, axis=-1, keepdims=True))
    ).astype(BF16)
    query_grad = score_scale * jnp.einsum(
        "hqk,khd->qhd", score_grad, key_rows, preferred_element_type=F32
    )
    key_grad = score_scale * jnp.einsum(
        "hqk,qhd->khd", score_grad, queries, preferred_element_type=F32
    )
    value_grad = jnp.einsum(
        "hqk,qhd->khd", probs_low, attended_grad, preferred_element_type=F32
    ).astype(BF16).reshape(length, -1)
    query_grad = unrotate(query_grad, cosine_table, sine_table).astype(BF16).reshape(length, -1)
    key_grad = unrotate(key_grad, cosine_table, sine_table).astype(BF16).reshape(length, -1)
    projection_grads = jnp.concatenate([query_grad, key_grad, value_grad], axis=1)
    projections = w_query.shape[1]
    qkv_grads = contract_first(normed_one, projection_grads).astype(BF16)
    attn_grads = jnp.concatenate(
        [qkv_grads, contract_first(branch_grad, attended).astype(BF16)], axis=1
    )
    attn_total = wide_allreduce(attn_grads, wide)
    one_float = contract_last(
        projection_grads, jnp.concatenate([w_query, w_key, w_value], axis=1)
    )
    norm_one = jnp.stack(
        [jnp.sum(one_float * scaled_one, axis=0), jnp.sum(one_float, axis=0)]
    )
    norm_two = jnp.stack(
        [jnp.sum(own_two_grad * own_scaled_two, axis=0), jnp.sum(own_two_grad, axis=0)]
    )
    norm_parts = jnp.concatenate([norm_one, norm_two], axis=0)
    high, low = split_hi_lo(norm_parts)
    extra = jnp.concatenate([high, low, jnp.zeros((8, d_model), BF16)], axis=0)
    one_blocks = one_float.astype(BF16).reshape(count, block, d_model)
    payload = jnp.concatenate(
        [one_blocks, jnp.broadcast_to(extra[None], (count,) + extra.shape)], axis=1
    )
    got = lax.all_to_all(payload, "narrow", 0, 0, tiled=False).astype(F32)
    summed = jnp.sum(got, axis=0)
    own_one_grad = summed[:block]
    norm_narrow = summed[block : block + 4] + summed[block + 4 : block + 8]
    norm_total = wide_allreduce_small(norm_narrow, wide)
    input_grad = middle_grad + normalize_back(
        own_one_grad, own_scaled_one, own_inverse_one, gain_one
    )
    ff_cols = w_gate.shape[1]
    return (
        layer_out,
        input_grad,
        attn_total[:, :projections],
        attn_total[:, projections : 2 * projections],
        attn_total[:, 2 * projections : 3 * projections],
        attn_total[:, 3 * projections :].T,
        ffn_total[:d_model, :ff_cols],
        ffn_total[:d_model, ff_cols:],
        ffn_total[d_model:],
        norm_total[0],
        norm_total[1],
        norm_total[2],
        norm_total[3],
    )


def solution(mesh):
    placed = (
        P(("wide", "narrow"), None),
        P(("wide", "narrow"), None),
        P("wide", None),
        P(None, "narrow"),
        P(None, "narrow"),
        P(None, "narrow"),
        P("narrow", None),
        P(None, "narrow"),
        P(None, "narrow"),
        P("narrow", None),
        P(),
        P(),
        P(),
        P(),
    )
    return jax.shard_map(
        per_device,
        mesh=mesh,
        in_specs=placed,
        out_specs=(
            P(("wide", "narrow"), None),
            P(("wide", "narrow"), None),
            P(None, "narrow"),
            P(None, "narrow"),
            P(None, "narrow"),
            P("narrow", None),
            P(None, "narrow"),
            P(None, "narrow"),
            P("narrow", None),
            P(),
            P(),
            P(),
            P(),
        ),
        check_vma=False,
    )
```

```python
import math

import jax
import jax.numpy as jnp
from jax import lax
from jax.sharding import PartitionSpec as P

HD = 64
EPS = 1e-05
MASKED = -1e30
F32 = jnp.float32
BF16 = jnp.bfloat16


def normalize(values, gain_vec, bias_vec):
    centred = values - jnp.mean(values, axis=-1, keepdims=True)
    inverse = lax.rsqrt(jnp.mean(centred * centred, axis=-1, keepdims=True) + EPS)
    scaled = centred * inverse
    return (scaled * gain_vec + bias_vec, scaled, inverse)


def normalize_back(grad_in, scaled, inverse, gain_vec):
    along = grad_in * gain_vec
    return inverse * (
        along
        - jnp.mean(along, axis=-1, keepdims=True)
        - scaled * jnp.mean(along * scaled, axis=-1, keepdims=True)
    )


def contract_last(left_side, right_side):
    return lax.dot_general(
        left_side, right_side, (((1,), (1,)), ((), ())), preferred_element_type=F32
    )


def contract_first(left_side, right_side):
    return lax.dot_general(
        left_side, right_side, (((0,), (0,)), ((), ())), preferred_element_type=F32
    )


def rotate(values, cosine_table, sine_table):
    half_width = values.shape[-1] // 2
    first_half = values[..., :half_width]
    second_half = values[..., half_width:]
    cosine = cosine_table[:, None, :]
    sine_part = sine_table[:, None, :]
    return jnp.concatenate(
        [
            first_half * cosine - second_half * sine_part,
            second_half * cosine + first_half * sine_part,
        ],
        axis=-1,
    )


def unrotate(values, cosine_table, sine_table):
    half_width = values.shape[-1] // 2
    first_half = values[..., :half_width]
    second_half = values[..., half_width:]
    cosine = cosine_table[:, None, :]
    sine_part = sine_table[:, None, :]
    return jnp.concatenate(
        [
            first_half * cosine + second_half * sine_part,
            second_half * cosine - first_half * sine_part,
        ],
        axis=-1,
    )


def narrow_gather(own, count):
    slots = jnp.broadcast_to(own[None], (count,) + own.shape)
    got = lax.all_to_all(slots, "narrow", 0, 0, tiled=False)
    return got.reshape(count * own.shape[0], own.shape[1])


def narrow_scatter(partial, count):
    blocks = partial.reshape(count, partial.shape[0] // count, partial.shape[1])
    got = lax.all_to_all(blocks, "narrow", 0, 0, tiled=False)
    return jnp.sum(got.astype(F32), axis=0)


def narrow_gather_async(own, count):
    index = lax.axis_index("narrow")
    rows = own.shape[0]
    whole = jnp.zeros((count * rows, own.shape[1]), own.dtype)
    whole = lax.dynamic_update_slice_in_dim(whole, own, index * rows, 0)
    for k in range(1, count):
        got = lax.ppermute(own, "narrow", [((i + k) % count, i) for i in range(count)])
        whole = lax.dynamic_update_slice_in_dim(whole, got, ((index + k) % count) * rows, 0)
    return whole


def split_hi_lo(values):
    high = values.astype(BF16)
    return high, (values - high.astype(F32)).astype(BF16)


def wide_layout(wide):
    chips_x = wide // 4
    w = lax.axis_index("wide")
    return chips_x, w % 2, (w // 2) % chips_x, w // (2 * chips_x)


def wide_map(wide, dcore=0, dx=0, dz=0, flip_core=False, xor_x=0):
    chips_x = wide // 4
    pairs = []
    for v in range(wide):
        c, xx, zz = v % 2, (v // 2) % chips_x, v // (2 * chips_x)
        c2 = (1 - c) if flip_core else c
        x2 = ((xx ^ xor_x) + dx) % chips_x
        z2 = (zz + dz) % 2
        pairs.append((v, z2 * 2 * chips_x + x2 * 2 + c2))
    return pairs


def tie(value, anchor):
    if anchor is None:
        return value
    return lax.optimization_barrier((value, anchor))[0]


def wide_allreduce(grad, wide, anchors=(None,) * 6):
    chips_x, core, xpos, zhi = wide_layout(wide)
    rows, cols = grad.shape
    half = rows // 2
    quarter = half // chips_x
    eighth = quarter // 2
    grad = tie(grad, anchors[0])
    keep = lax.dynamic_slice_in_dim(grad, core * half, half, 0)
    send = lax.dynamic_slice_in_dim(grad, (1 - core) * half, half, 0)
    summed = keep.astype(F32) + lax.ppermute(send, "wide", wide_map(wide, flip_core=True)).astype(F32)
    summed = tie(summed, anchors[1])
    acc = lax.dynamic_slice_in_dim(summed, xpos * quarter, quarter, 0)
    for k in range(1, chips_x):
        piece = lax.dynamic_slice_in_dim(summed, ((xpos + k) % chips_x) * quarter, quarter, 0)
        acc = acc + lax.ppermute(piece.astype(BF16), "wide", wide_map(wide, dx=k)).astype(F32)
    acc = tie(acc, anchors[2])
    mine = lax.dynamic_slice_in_dim(acc, zhi * eighth, eighth, 0)
    other = lax.dynamic_slice_in_dim(acc, (1 - zhi) * eighth, eighth, 0)
    final = (mine + lax.ppermute(other.astype(BF16), "wide", wide_map(wide, dz=1)).astype(F32)).astype(BF16)
    final = tie(final, anchors[3])
    part = jnp.zeros((quarter, cols), BF16)
    part = lax.dynamic_update_slice_in_dim(part, final, zhi * eighth, 0)
    part = lax.dynamic_update_slice_in_dim(
        part, lax.ppermute(final, "wide", wide_map(wide, dz=1)), (1 - zhi) * eighth, 0
    )
    part = tie(part, anchors[4])
    halfrows = jnp.zeros((half, cols), BF16)
    halfrows = lax.dynamic_update_slice_in_dim(halfrows, part, xpos * quarter, 0)
    for k in range(1, chips_x):
        got = lax.ppermute(part, "wide", wide_map(wide, dx=chips_x - k))
        halfrows = lax.dynamic_update_slice_in_dim(
            halfrows, got, ((xpos + k) % chips_x) * quarter, 0
        )
    halfrows = tie(halfrows, anchors[5])
    whole = jnp.zeros((rows, cols), BF16)
    whole = lax.dynamic_update_slice_in_dim(whole, halfrows, core * half, 0)
    whole = lax.dynamic_update_slice_in_dim(
        whole, lax.ppermute(halfrows, "wide", wide_map(wide, flip_core=True)), (1 - core) * half, 0
    )
    return whole.astype(F32)


def wide_allreduce_small(values, wide):
    chips_x = wide // 4
    values = values + lax.ppermute(values, "wide", wide_map(wide, flip_core=True))
    values = values + lax.ppermute(values, "wide", wide_map(wide, xor_x=1))
    if chips_x > 2:
        values = values + lax.ppermute(values, "wide", wide_map(wide, xor_x=2))
    return values + lax.ppermute(values, "wide", wide_map(wide, dz=1))


def per_device(
    tokens,
    cotangent,
    segments,
    w_query,
    w_key,
    w_value,
    w_out,
    w_gate,
    w_up,
    w_down,
    gain_one,
    bias_one,
    gain_two,
    bias_two,
):
    count = lax.axis_size("narrow")
    wide = lax.axis_size("wide")
    block, d_model = tokens.shape
    narrow_index = lax.axis_index("narrow")
    own_rows = narrow_index * block

    seg = segments[0]
    length = seg.shape[0]
    column = lax.broadcasted_iota(jnp.int32, (length, length), 1)
    same_segment = seg[:, None] == seg[None, :]
    first_index = jnp.min(jnp.where(same_segment, column, length), axis=-1)
    position = (jnp.arange(length, dtype=jnp.int32) - first_index).astype(F32)
    inverse = 10000.0 ** (-(2.0 * jnp.arange(HD // 2).astype(F32) / HD))
    angles = position[:, None] * inverse
    cosine_table, sine_table = jnp.cos(angles), jnp.sin(angles)

    head_rows = w_out.shape[0]
    first = narrow_gather(
        jnp.concatenate([tokens, cotangent, w_out], axis=0), count
    ).reshape(count, 2 * block + head_rows, d_model)
    tok_full = first[:, :block].reshape(length, d_model)
    cot_full = first[:, block : 2 * block].reshape(length, d_model)
    w_out_full = first[:, 2 * block :]

    inputs = tok_full.astype(F32)
    normed_float, scaled_one, inverse_one = normalize(inputs, gain_one, bias_one)
    normed_one = normed_float.astype(BF16)
    own_scaled_one = lax.dynamic_slice_in_dim(scaled_one, own_rows, block, 0)
    own_inverse_one = lax.dynamic_slice_in_dim(inverse_one, own_rows, block, 0)

    heads = w_query.shape[1] // HD
    head_shape = (length, heads, HD)
    queries = rotate(
        jnp.dot(normed_one, w_query, preferred_element_type=F32).reshape(head_shape),
        cosine_table,
        sine_table,
    ).astype(BF16)
    key_rows = rotate(
        jnp.dot(normed_one, w_key, preferred_element_type=F32).reshape(head_shape),
        cosine_table,
        sine_table,
    ).astype(BF16)
    value_rows = (
        jnp.dot(normed_one, w_value, preferred_element_type=F32).astype(BF16).reshape(head_shape)
    )
    score_scale = 1.0 / math.sqrt(HD)
    scores = (
        jnp.einsum("qhd,khd->hqk", queries, key_rows, preferred_element_type=F32) * score_scale
    )
    scores = jnp.where(same_segment[None], scores, MASKED)
    row_peak = jnp.max(scores, axis=-1, keepdims=True)
    exponent = jnp.exp(scores - row_peak)
    row_total = jnp.sum(exponent, axis=-1, keepdims=True)
    probs = exponent / row_total
    probs_low = probs.astype(BF16)
    attended = (
        jnp.einsum("hqk,khd->qhd", probs_low, value_rows, preferred_element_type=F32)
        .astype(BF16)
        .reshape(length, -1)
    )

    attended_all = lax.all_to_all(
        jnp.broadcast_to(attended[None], (count,) + attended.shape), "narrow", 0, 0, tiled=False
    )
    branch = jnp.einsum(
        "jtc,jcd->td", attended_all, w_out_full, preferred_element_type=F32
    )
    middle = inputs + branch
    normed_two_float, scaled_two, inverse_two = normalize(middle, gain_two, bias_two)
    normed_two = normed_two_float.astype(BF16)

    gate_pre = jnp.dot(normed_two, w_gate, preferred_element_type=F32)
    up_pre = jnp.dot(normed_two, w_up, preferred_element_type=F32)
    sigmoid_gate = jax.nn.sigmoid(gate_pre)
    active = gate_pre * sigmoid_gate
    hidden = (active * up_pre).astype(BF16)
    ffn_partial = jnp.dot(hidden, w_down, preferred_element_type=F32).astype(BF16)

    hidden_grad = contract_last(cot_full, w_down)
    gate_grad = (
        hidden_grad * up_pre * sigmoid_gate * (1.0 + gate_pre * (1.0 - sigmoid_gate))
    ).astype(BF16)
    up_grad = (hidden_grad * active).astype(BF16)
    ffn_grads = jnp.concatenate(
        [
            contract_first(normed_two, jnp.concatenate([gate_grad, up_grad], axis=1)),
            contract_first(hidden, cot_full),
        ],
        axis=0,
    ).astype(BF16)
    two_partial = (contract_last(gate_grad, w_gate) + contract_last(up_grad, w_up)).astype(BF16)
    both = narrow_scatter(jnp.concatenate([ffn_partial, two_partial], axis=1), count)
    layer_out = lax.dynamic_slice_in_dim(middle, own_rows, block, 0) + both[:, :d_model]
    own_two_grad = both[:, d_model:]
    own_scaled_two = lax.dynamic_slice_in_dim(scaled_two, own_rows, block, 0)
    own_inverse_two = lax.dynamic_slice_in_dim(inverse_two, own_rows, block, 0)

    middle_grad = cotangent.astype(F32) + normalize_back(
        own_two_grad, own_scaled_two, own_inverse_two, gain_two
    )
    branch_grad = narrow_gather(middle_grad.astype(BF16), count)

    attended_grad = contract_last(branch_grad, w_out).astype(BF16).reshape(head_shape)
    prob_grad = jnp.einsum(
        "qhd,khd->hqk", attended_grad, value_rows, preferred_element_type=F32
    )
    score_grad = (
        probs * (prob_grad - jnp.sum(probs * prob_grad, axis=-1, keepdims=True))
    ).astype(BF16)
    query_grad = score_scale * jnp.einsum(
        "hqk,khd->qhd", score_grad, key_rows, preferred_element_type=F32
    )
    key_grad = score_scale * jnp.einsum(
        "hqk,qhd->khd", score_grad, queries, preferred_element_type=F32
    )
    value_grad = jnp.einsum(
        "hqk,qhd->khd", probs_low, attended_grad, preferred_element_type=F32
    ).astype(BF16).reshape(length, -1)
    query_grad = unrotate(query_grad, cosine_table, sine_table).astype(BF16).reshape(length, -1)
    key_grad = unrotate(key_grad, cosine_table, sine_table).astype(BF16).reshape(length, -1)
    projection_grads = jnp.concatenate([query_grad, key_grad, value_grad], axis=1)
    projections = w_query.shape[1]
    qkv_grads = contract_first(normed_one, projection_grads).astype(BF16)
    attn_grads = jnp.concatenate(
        [qkv_grads, contract_first(branch_grad, attended).astype(BF16)], axis=1
    )
    one_float = contract_last(
        projection_grads, jnp.concatenate([w_query, w_key, w_value], axis=1)
    )
    norm_one = jnp.stack(
        [jnp.sum(one_float * scaled_one, axis=0), jnp.sum(one_float, axis=0)]
    )
    norm_two = jnp.stack(
        [jnp.sum(own_two_grad * own_scaled_two, axis=0), jnp.sum(own_two_grad, axis=0)]
    )
    norm_parts = jnp.concatenate([norm_one, norm_two], axis=0)
    high, low = split_hi_lo(norm_parts)
    extra = jnp.concatenate([high, low, jnp.zeros((8, d_model), BF16)], axis=0)
    one_blocks = one_float.astype(BF16).reshape(count, block, d_model)
    payload = jnp.concatenate(
        [one_blocks, jnp.broadcast_to(extra[None], (count,) + extra.shape)], axis=1
    )
    got = lax.all_to_all(payload, "narrow", 0, 0, tiled=False).astype(F32)
    summed = jnp.sum(got, axis=0)
    ffn_total = wide_allreduce(
        ffn_grads, wide, (None, both, branch_grad, projection_grads, one_float, got)
    )
    attn_total = wide_allreduce(attn_grads, wide)
    own_one_grad = summed[:block]
    norm_narrow = summed[block : block + 4] + summed[block + 4 : block + 8]
    norm_total = wide_allreduce_small(norm_narrow, wide)
    input_grad = middle_grad + normalize_back(
        own_one_grad, own_scaled_one, own_inverse_one, gain_one
    )
    ff_cols = w_gate.shape[1]
    return (
        layer_out,
        input_grad,
        attn_total[:, :projections],
        attn_total[:, projections : 2 * projections],
        attn_total[:, 2 * projections : 3 * projections],
        attn_total[:, 3 * projections :].T,
        ffn_total[:d_model, :ff_cols],
        ffn_total[:d_model, ff_cols:],
        ffn_total[d_model:],
        norm_total[0],
        norm_total[1],
        norm_total[2],
        norm_total[3],
    )


def solution(mesh):
    placed = (
        P(("wide", "narrow"), None),
        P(("wide", "narrow"), None),
        P("wide", None),
        P(None, "narrow"),
        P(None, "narrow"),
        P(None, "narrow"),
        P("narrow", None),
        P(None, "narrow"),
        P(None, "narrow"),
        P("narrow", None),
        P(),
        P(),
        P(),
        P(),
    )
    return jax.shard_map(
        per_device,
        mesh=mesh,
        in_specs=placed,
        out_specs=(
            P(("wide", "narrow"), None),
            P(("wide", "narrow"), None),
            P(None, "narrow"),
            P(None, "narrow"),
            P(None, "narrow"),
            P("narrow", None),
            P(None, "narrow"),
            P(None, "narrow"),
            P("narrow", None),
            P(),
            P(),
            P(),
            P(),
        ),
        check_vma=False,
    )
```

```python
import math

import jax
import jax.numpy as jnp
from jax import lax
from jax.sharding import PartitionSpec as P

HD = 64
EPS = 1e-05
MASKED = -1e30
F32 = jnp.float32
BF16 = jnp.bfloat16


def normalize(values, gain_vec, bias_vec):
    centred = values - jnp.mean(values, axis=-1, keepdims=True)
    inverse = lax.rsqrt(jnp.mean(centred * centred, axis=-1, keepdims=True) + EPS)
    scaled = centred * inverse
    return (scaled * gain_vec + bias_vec, scaled, inverse)


def normalize_back(grad_in, scaled, inverse, gain_vec):
    along = grad_in * gain_vec
    return inverse * (
        along
        - jnp.mean(along, axis=-1, keepdims=True)
        - scaled * jnp.mean(along * scaled, axis=-1, keepdims=True)
    )


def contract_last(left_side, right_side):
    return lax.dot_general(
        left_side, right_side, (((1,), (1,)), ((), ())), preferred_element_type=F32
    )


def contract_first(left_side, right_side):
    return lax.dot_general(
        left_side, right_side, (((0,), (0,)), ((), ())), preferred_element_type=F32
    )


def rotate(values, cosine_table, sine_table):
    half_width = values.shape[-1] // 2
    first_half = values[..., :half_width]
    second_half = values[..., half_width:]
    cosine = cosine_table[:, None, :]
    sine_part = sine_table[:, None, :]
    return jnp.concatenate(
        [
            first_half * cosine - second_half * sine_part,
            second_half * cosine + first_half * sine_part,
        ],
        axis=-1,
    )


def unrotate(values, cosine_table, sine_table):
    half_width = values.shape[-1] // 2
    first_half = values[..., :half_width]
    second_half = values[..., half_width:]
    cosine = cosine_table[:, None, :]
    sine_part = sine_table[:, None, :]
    return jnp.concatenate(
        [
            first_half * cosine + second_half * sine_part,
            second_half * cosine - first_half * sine_part,
        ],
        axis=-1,
    )


def narrow_gather(own, count):
    slots = jnp.broadcast_to(own[None], (count,) + own.shape)
    got = lax.all_to_all(slots, "narrow", 0, 0, tiled=False)
    return got.reshape(count * own.shape[0], own.shape[1])


def narrow_scatter(partial, count):
    blocks = partial.reshape(count, partial.shape[0] // count, partial.shape[1])
    got = lax.all_to_all(blocks, "narrow", 0, 0, tiled=False)
    return jnp.sum(got.astype(F32), axis=0)


def narrow_gather_async(own, count):
    index = lax.axis_index("narrow")
    rows = own.shape[0]
    whole = jnp.zeros((count * rows, own.shape[1]), own.dtype)
    whole = lax.dynamic_update_slice_in_dim(whole, own, index * rows, 0)
    for k in range(1, count):
        got = lax.ppermute(own, "narrow", [((i + k) % count, i) for i in range(count)])
        whole = lax.dynamic_update_slice_in_dim(whole, got, ((index + k) % count) * rows, 0)
    return whole


def split_hi_lo(values):
    high = values.astype(BF16)
    return high, (values - high.astype(F32)).astype(BF16)


def wide_layout(wide):
    chips_x = wide // 4
    w = lax.axis_index("wide")
    return chips_x, w % 2, (w // 2) % chips_x, w // (2 * chips_x)


def wide_map(wide, dcore=0, dx=0, dz=0, flip_core=False, xor_x=0):
    chips_x = wide // 4
    pairs = []
    for v in range(wide):
        c, xx, zz = v % 2, (v // 2) % chips_x, v // (2 * chips_x)
        c2 = (1 - c) if flip_core else c
        x2 = ((xx ^ xor_x) + dx) % chips_x
        z2 = (zz + dz) % 2
        pairs.append((v, z2 * 2 * chips_x + x2 * 2 + c2))
    return pairs


def tie(value, anchor):
    if anchor is None:
        return value
    return lax.optimization_barrier((value, anchor))[0]


def wide_allreduce(grad, wide, anchors=(None,) * 6):
    chips_x, core, xpos, zhi = wide_layout(wide)
    rows, cols = grad.shape
    half = rows // 2
    quarter = half // chips_x
    eighth = quarter // 2
    grad = tie(grad, anchors[0])
    keep = lax.dynamic_slice_in_dim(grad, core * half, half, 0)
    send = lax.dynamic_slice_in_dim(grad, (1 - core) * half, half, 0)
    summed = keep.astype(F32) + lax.ppermute(send, "wide", wide_map(wide, flip_core=True)).astype(F32)
    summed = tie(summed, anchors[1])
    acc = lax.dynamic_slice_in_dim(summed, xpos * quarter, quarter, 0)
    for k in range(1, chips_x):
        piece = lax.dynamic_slice_in_dim(summed, ((xpos + k) % chips_x) * quarter, quarter, 0)
        acc = acc + lax.ppermute(piece.astype(BF16), "wide", wide_map(wide, dx=k)).astype(F32)
    acc = tie(acc, anchors[2])
    mine = lax.dynamic_slice_in_dim(acc, zhi * eighth, eighth, 0)
    other = lax.dynamic_slice_in_dim(acc, (1 - zhi) * eighth, eighth, 0)
    final = (mine + lax.ppermute(other.astype(BF16), "wide", wide_map(wide, dz=1)).astype(F32)).astype(BF16)
    final = tie(final, anchors[3])
    part = jnp.zeros((quarter, cols), BF16)
    part = lax.dynamic_update_slice_in_dim(part, final, zhi * eighth, 0)
    part = lax.dynamic_update_slice_in_dim(
        part, lax.ppermute(final, "wide", wide_map(wide, dz=1)), (1 - zhi) * eighth, 0
    )
    part = tie(part, anchors[4])
    halfrows = jnp.zeros((half, cols), BF16)
    halfrows = lax.dynamic_update_slice_in_dim(halfrows, part, xpos * quarter, 0)
    for k in range(1, chips_x):
        got = lax.ppermute(part, "wide", wide_map(wide, dx=chips_x - k))
        halfrows = lax.dynamic_update_slice_in_dim(
            halfrows, got, ((xpos + k) % chips_x) * quarter, 0
        )
    halfrows = tie(halfrows, anchors[5])
    whole = jnp.zeros((rows, cols), BF16)
    whole = lax.dynamic_update_slice_in_dim(whole, halfrows, core * half, 0)
    whole = lax.dynamic_update_slice_in_dim(
        whole, lax.ppermute(halfrows, "wide", wide_map(wide, flip_core=True)), (1 - core) * half, 0
    )
    return whole.astype(F32)


def wide_allreduce_small(values, wide):
    chips_x = wide // 4
    values = values + lax.ppermute(values, "wide", wide_map(wide, flip_core=True))
    values = values + lax.ppermute(values, "wide", wide_map(wide, xor_x=1))
    if chips_x > 2:
        values = values + lax.ppermute(values, "wide", wide_map(wide, xor_x=2))
    return values + lax.ppermute(values, "wide", wide_map(wide, dz=1))


def per_device(
    tokens,
    cotangent,
    segments,
    w_query,
    w_key,
    w_value,
    w_out,
    w_gate,
    w_up,
    w_down,
    gain_one,
    bias_one,
    gain_two,
    bias_two,
):
    count = lax.axis_size("narrow")
    wide = lax.axis_size("wide")
    block, d_model = tokens.shape
    narrow_index = lax.axis_index("narrow")
    own_rows = narrow_index * block

    seg = segments[0]
    length = seg.shape[0]
    column = lax.broadcasted_iota(jnp.int32, (length, length), 1)
    same_segment = seg[:, None] == seg[None, :]
    first_index = jnp.min(jnp.where(same_segment, column, length), axis=-1)
    position = (jnp.arange(length, dtype=jnp.int32) - first_index).astype(F32)
    inverse = 10000.0 ** (-(2.0 * jnp.arange(HD // 2).astype(F32) / HD))
    angles = position[:, None] * inverse
    cosine_table, sine_table = jnp.cos(angles), jnp.sin(angles)

    head_rows = w_out.shape[0]
    first = narrow_gather(
        jnp.concatenate([tokens, cotangent, w_out], axis=0), count
    ).reshape(count, 2 * block + head_rows, d_model)
    tok_full = first[:, :block].reshape(length, d_model)
    cot_full = first[:, block : 2 * block].reshape(length, d_model)
    w_out_full = first[:, 2 * block :]

    inputs = tok_full.astype(F32)
    normed_float, scaled_one, inverse_one = normalize(inputs, gain_one, bias_one)
    normed_one = normed_float.astype(BF16)
    own_scaled_one = lax.dynamic_slice_in_dim(scaled_one, own_rows, block, 0)
    own_inverse_one = lax.dynamic_slice_in_dim(inverse_one, own_rows, block, 0)

    heads = w_query.shape[1] // HD
    head_shape = (length, heads, HD)
    queries = rotate(
        jnp.dot(normed_one, w_query, preferred_element_type=F32).reshape(head_shape),
        cosine_table,
        sine_table,
    ).astype(BF16)
    key_rows = rotate(
        jnp.dot(normed_one, w_key, preferred_element_type=F32).reshape(head_shape),
        cosine_table,
        sine_table,
    ).astype(BF16)
    value_rows = (
        jnp.dot(normed_one, w_value, preferred_element_type=F32).astype(BF16).reshape(head_shape)
    )
    score_scale = 1.0 / math.sqrt(HD)
    scores = (
        jnp.einsum("qhd,khd->hqk", queries, key_rows, preferred_element_type=F32) * score_scale
    )
    scores = jnp.where(same_segment[None], scores, MASKED)
    row_peak = jnp.max(scores, axis=-1, keepdims=True)
    exponent = jnp.exp(scores - row_peak)
    row_total = jnp.sum(exponent, axis=-1, keepdims=True)
    probs = exponent / row_total
    probs_low = probs.astype(BF16)
    attended = (
        jnp.einsum("hqk,khd->qhd", probs_low, value_rows, preferred_element_type=F32)
        .astype(BF16)
        .reshape(length, -1)
    )

    attended_all = lax.all_to_all(
        jnp.broadcast_to(attended[None], (count,) + attended.shape), "narrow", 0, 0, tiled=False
    )
    branch = jnp.einsum(
        "jtc,jcd->td", attended_all, w_out_full, preferred_element_type=F32
    )
    middle = inputs + branch
    normed_two_float, scaled_two, inverse_two = normalize(middle, gain_two, bias_two)
    normed_two = normed_two_float.astype(BF16)

    gate_pre = jnp.dot(normed_two, w_gate, preferred_element_type=F32)
    up_pre = jnp.dot(normed_two, w_up, preferred_element_type=F32)
    sigmoid_gate = jax.nn.sigmoid(gate_pre)
    active = gate_pre * sigmoid_gate
    hidden = (active * up_pre).astype(BF16)
    ffn_partial = jnp.dot(hidden, w_down, preferred_element_type=F32).astype(BF16)

    hidden_grad = contract_last(cot_full, w_down)
    gate_grad = (
        hidden_grad * up_pre * sigmoid_gate * (1.0 + gate_pre * (1.0 - sigmoid_gate))
    ).astype(BF16)
    up_grad = (hidden_grad * active).astype(BF16)
    ffn_grads = jnp.concatenate(
        [
            contract_first(normed_two, jnp.concatenate([gate_grad, up_grad], axis=1)),
            contract_first(hidden, cot_full),
        ],
        axis=0,
    ).astype(BF16)
    two_partial = (contract_last(gate_grad, w_gate) + contract_last(up_grad, w_up)).astype(BF16)
    both = narrow_scatter(jnp.concatenate([ffn_partial, two_partial], axis=1), count)
    layer_out = lax.dynamic_slice_in_dim(middle, own_rows, block, 0) + both[:, :d_model]
    own_two_grad = both[:, d_model:]
    own_scaled_two = lax.dynamic_slice_in_dim(scaled_two, own_rows, block, 0)
    own_inverse_two = lax.dynamic_slice_in_dim(inverse_two, own_rows, block, 0)

    middle_grad = cotangent.astype(F32) + normalize_back(
        own_two_grad, own_scaled_two, own_inverse_two, gain_two
    )
    branch_grad = narrow_gather(middle_grad.astype(BF16), count)

    attended_grad = contract_last(branch_grad, w_out).astype(BF16).reshape(head_shape)
    prob_grad = jnp.einsum(
        "qhd,khd->hqk", attended_grad, value_rows, preferred_element_type=F32
    )
    score_grad = (
        probs * (prob_grad - jnp.sum(probs * prob_grad, axis=-1, keepdims=True))
    ).astype(BF16)
    query_grad = score_scale * jnp.einsum(
        "hqk,khd->qhd", score_grad, key_rows, preferred_element_type=F32
    )
    key_grad = score_scale * jnp.einsum(
        "hqk,qhd->khd", score_grad, queries, preferred_element_type=F32
    )
    value_grad = jnp.einsum(
        "hqk,qhd->khd", probs_low, attended_grad, preferred_element_type=F32
    ).astype(BF16).reshape(length, -1)
    query_grad = unrotate(query_grad, cosine_table, sine_table).astype(BF16).reshape(length, -1)
    key_grad = unrotate(key_grad, cosine_table, sine_table).astype(BF16).reshape(length, -1)
    projection_grads = jnp.concatenate([query_grad, key_grad, value_grad], axis=1)
    projections = w_query.shape[1]
    qkv_grads = contract_first(normed_one, projection_grads).astype(BF16)
    attn_grads = jnp.concatenate(
        [qkv_grads, contract_first(branch_grad, attended).astype(BF16)], axis=1
    )
    one_float = contract_last(
        projection_grads, jnp.concatenate([w_query, w_key, w_value], axis=1)
    )
    norm_one = jnp.stack(
        [jnp.sum(one_float * scaled_one, axis=0), jnp.sum(one_float, axis=0)]
    )
    norm_two = jnp.stack(
        [jnp.sum(own_two_grad * own_scaled_two, axis=0), jnp.sum(own_two_grad, axis=0)]
    )
    norm_parts = jnp.concatenate([norm_one, norm_two], axis=0)
    high, low = split_hi_lo(norm_parts)
    extra = jnp.concatenate([high, low, jnp.zeros((8, d_model), BF16)], axis=0)
    one_blocks = one_float.astype(BF16).reshape(count, block, d_model)
    payload = jnp.concatenate(
        [one_blocks, jnp.broadcast_to(extra[None], (count,) + extra.shape)], axis=1
    )
    got = lax.all_to_all(payload, "narrow", 0, 0, tiled=False).astype(F32)
    summed = jnp.sum(got, axis=0)
    attn_total = wide_allreduce(attn_grads, wide, (None, payload, None, None, None, None))
    ffn_total = tie(lax.psum(ffn_grads, "wide"), got).astype(F32)
    own_one_grad = summed[:block]
    norm_narrow = summed[block : block + 4] + summed[block + 4 : block + 8]
    norm_total = wide_allreduce_small(norm_narrow, wide)
    input_grad = middle_grad + normalize_back(
        own_one_grad, own_scaled_one, own_inverse_one, gain_one
    )
    ff_cols = w_gate.shape[1]
    return (
        layer_out,
        input_grad,
        attn_total[:, :projections],
        attn_total[:, projections : 2 * projections],
        attn_total[:, 2 * projections : 3 * projections],
        attn_total[:, 3 * projections :].T,
        ffn_total[:d_model, :ff_cols],
        ffn_total[:d_model, ff_cols:],
        ffn_total[d_model:],
        norm_total[0],
        norm_total[1],
        norm_total[2],
        norm_total[3],
    )


def solution(mesh):
    placed = (
        P(("wide", "narrow"), None),
        P(("wide", "narrow"), None),
        P("wide", None),
        P(None, "narrow"),
        P(None, "narrow"),
        P(None, "narrow"),
        P("narrow", None),
        P(None, "narrow"),
        P(None, "narrow"),
        P("narrow", None),
        P(),
        P(),
        P(),
        P(),
    )
    return jax.shard_map(
        per_device,
        mesh=mesh,
        in_specs=placed,
        out_specs=(
            P(("wide", "narrow"), None),
            P(("wide", "narrow"), None),
            P(None, "narrow"),
            P(None, "narrow"),
            P(None, "narrow"),
            P("narrow", None),
            P(None, "narrow"),
            P(None, "narrow"),
            P("narrow", None),
            P(),
            P(),
            P(),
            P(),
        ),
        check_vma=False,
    )
```

```python
import math

import jax
import jax.numpy as jnp
from jax import lax
from jax.sharding import PartitionSpec as P

HD = 64
EPS = 1e-05
MASKED = -1e30
F32 = jnp.float32
BF16 = jnp.bfloat16


def normalize(values, gain_vec, bias_vec):
    centred = values - jnp.mean(values, axis=-1, keepdims=True)
    inverse = lax.rsqrt(jnp.mean(centred * centred, axis=-1, keepdims=True) + EPS)
    scaled = centred * inverse
    return (scaled * gain_vec + bias_vec, scaled, inverse)


def normalize_back(grad_in, scaled, inverse, gain_vec):
    along = grad_in * gain_vec
    return inverse * (
        along
        - jnp.mean(along, axis=-1, keepdims=True)
        - scaled * jnp.mean(along * scaled, axis=-1, keepdims=True)
    )


def contract_last(left_side, right_side):
    return lax.dot_general(
        left_side, right_side, (((1,), (1,)), ((), ())), preferred_element_type=F32
    )


def contract_first(left_side, right_side):
    return lax.dot_general(
        left_side, right_side, (((0,), (0,)), ((), ())), preferred_element_type=F32
    )


def rotate(values, cosine_table, sine_table):
    half_width = values.shape[-1] // 2
    first_half = values[..., :half_width]
    second_half = values[..., half_width:]
    cosine = cosine_table[:, None, :]
    sine_part = sine_table[:, None, :]
    return jnp.concatenate(
        [
            first_half * cosine - second_half * sine_part,
            second_half * cosine + first_half * sine_part,
        ],
        axis=-1,
    )


def unrotate(values, cosine_table, sine_table):
    half_width = values.shape[-1] // 2
    first_half = values[..., :half_width]
    second_half = values[..., half_width:]
    cosine = cosine_table[:, None, :]
    sine_part = sine_table[:, None, :]
    return jnp.concatenate(
        [
            first_half * cosine + second_half * sine_part,
            second_half * cosine - first_half * sine_part,
        ],
        axis=-1,
    )


def narrow_gather(own, count):
    slots = jnp.broadcast_to(own[None], (count,) + own.shape)
    got = lax.all_to_all(slots, "narrow", 0, 0, tiled=False)
    return got.reshape(count * own.shape[0], own.shape[1])


def narrow_scatter(partial, count):
    blocks = partial.reshape(count, partial.shape[0] // count, partial.shape[1])
    got = lax.all_to_all(blocks, "narrow", 0, 0, tiled=False)
    return jnp.sum(got.astype(F32), axis=0)


def narrow_gather_async(own, count):
    index = lax.axis_index("narrow")
    rows = own.shape[0]
    whole = jnp.zeros((count * rows, own.shape[1]), own.dtype)
    whole = lax.dynamic_update_slice_in_dim(whole, own, index * rows, 0)
    for k in range(1, count):
        got = lax.ppermute(own, "narrow", [((i + k) % count, i) for i in range(count)])
        whole = lax.dynamic_update_slice_in_dim(whole, got, ((index + k) % count) * rows, 0)
    return whole


def split_hi_lo(values):
    high = values.astype(BF16)
    return high, (values - high.astype(F32)).astype(BF16)


def wide_layout(wide):
    chips_x = wide // 4
    w = lax.axis_index("wide")
    return chips_x, w % 2, (w // 2) % chips_x, w // (2 * chips_x)


def wide_map(wide, dcore=0, dx=0, dz=0, flip_core=False, xor_x=0):
    chips_x = wide // 4
    pairs = []
    for v in range(wide):
        c, xx, zz = v % 2, (v // 2) % chips_x, v // (2 * chips_x)
        c2 = (1 - c) if flip_core else c
        x2 = ((xx ^ xor_x) + dx) % chips_x
        z2 = (zz + dz) % 2
        pairs.append((v, z2 * 2 * chips_x + x2 * 2 + c2))
    return pairs


def tie(value, anchor):
    return lax.optimization_barrier((value, anchor))[0]


def core_reduce(grad, wide):
    _, core, _, _ = wide_layout(wide)
    half = grad.shape[0] // 2
    keep = lax.dynamic_slice_in_dim(grad, core * half, half, 0)
    send = lax.dynamic_slice_in_dim(grad, (1 - core) * half, half, 0)
    return keep.astype(F32) + lax.ppermute(send, "wide", wide_map(wide, flip_core=True)).astype(F32)


def x_reduce(summed, wide):
    chips_x, _, xpos, _ = wide_layout(wide)
    quarter = summed.shape[0] // chips_x
    acc = lax.dynamic_slice_in_dim(summed, xpos * quarter, quarter, 0)
    for k in range(1, chips_x):
        piece = lax.dynamic_slice_in_dim(summed, ((xpos + k) % chips_x) * quarter, quarter, 0)
        acc = acc + lax.ppermute(piece.astype(BF16), "wide", wide_map(wide, dx=k)).astype(F32)
    return acc


def z_reduce(acc, wide):
    _, _, _, zhi = wide_layout(wide)
    eighth = acc.shape[0] // 2
    mine = lax.dynamic_slice_in_dim(acc, zhi * eighth, eighth, 0)
    other = lax.dynamic_slice_in_dim(acc, (1 - zhi) * eighth, eighth, 0)
    got = lax.ppermute(other.astype(BF16), "wide", wide_map(wide, dz=1)).astype(F32)
    return (mine + got).astype(BF16)


def z_gather(final, wide):
    _, _, _, zhi = wide_layout(wide)
    eighth = final.shape[0]
    part = jnp.zeros((2 * eighth, final.shape[1]), BF16)
    part = lax.dynamic_update_slice_in_dim(part, final, zhi * eighth, 0)
    return lax.dynamic_update_slice_in_dim(
        part, lax.ppermute(final, "wide", wide_map(wide, dz=1)), (1 - zhi) * eighth, 0
    )


def x_gather(part, wide):
    chips_x, _, xpos, _ = wide_layout(wide)
    quarter = part.shape[0]
    halfrows = jnp.zeros((chips_x * quarter, part.shape[1]), BF16)
    halfrows = lax.dynamic_update_slice_in_dim(halfrows, part, xpos * quarter, 0)
    for k in range(1, chips_x):
        got = lax.ppermute(part, "wide", wide_map(wide, dx=chips_x - k))
        halfrows = lax.dynamic_update_slice_in_dim(
            halfrows, got, ((xpos + k) % chips_x) * quarter, 0
        )
    return halfrows


def core_gather(halfrows, wide):
    _, core, _, _ = wide_layout(wide)
    half = halfrows.shape[0]
    whole = jnp.zeros((2 * half, halfrows.shape[1]), BF16)
    whole = lax.dynamic_update_slice_in_dim(whole, halfrows, core * half, 0)
    return lax.dynamic_update_slice_in_dim(
        whole, lax.ppermute(halfrows, "wide", wide_map(wide, flip_core=True)), (1 - core) * half, 0
    )


def wide_allreduce(grad, wide):
    stage = z_gather(z_reduce(x_reduce(core_reduce(grad, wide), wide), wide), wide)
    return core_gather(x_gather(stage, wide), wide).astype(F32)


def wide_allreduce_small(values, wide):
    chips_x = wide // 4
    values = values + lax.ppermute(values, "wide", wide_map(wide, flip_core=True))
    values = values + lax.ppermute(values, "wide", wide_map(wide, xor_x=1))
    if chips_x > 2:
        values = values + lax.ppermute(values, "wide", wide_map(wide, xor_x=2))
    return values + lax.ppermute(values, "wide", wide_map(wide, dz=1))


def per_device(
    tokens,
    cotangent,
    segments,
    w_query,
    w_key,
    w_value,
    w_out,
    w_gate,
    w_up,
    w_down,
    gain_one,
    bias_one,
    gain_two,
    bias_two,
):
    count = lax.axis_size("narrow")
    wide = lax.axis_size("wide")
    block, d_model = tokens.shape
    narrow_index = lax.axis_index("narrow")
    own_rows = narrow_index * block

    seg = segments[0]
    length = seg.shape[0]
    column = lax.broadcasted_iota(jnp.int32, (length, length), 1)
    same_segment = seg[:, None] == seg[None, :]
    first_index = jnp.min(jnp.where(same_segment, column, length), axis=-1)
    position = (jnp.arange(length, dtype=jnp.int32) - first_index).astype(F32)
    inverse = 10000.0 ** (-(2.0 * jnp.arange(HD // 2).astype(F32) / HD))
    angles = position[:, None] * inverse
    cosine_table, sine_table = jnp.cos(angles), jnp.sin(angles)

    head_rows = w_out.shape[0]
    first = narrow_gather(
        jnp.concatenate([tokens, cotangent, w_out], axis=0), count
    ).reshape(count, 2 * block + head_rows, d_model)
    tok_full = first[:, :block].reshape(length, d_model)
    cot_full = first[:, block : 2 * block].reshape(length, d_model)
    w_out_full = first[:, 2 * block :]

    inputs = tok_full.astype(F32)
    normed_float, scaled_one, inverse_one = normalize(inputs, gain_one, bias_one)
    normed_one = normed_float.astype(BF16)
    own_scaled_one = lax.dynamic_slice_in_dim(scaled_one, own_rows, block, 0)
    own_inverse_one = lax.dynamic_slice_in_dim(inverse_one, own_rows, block, 0)

    heads = w_query.shape[1] // HD
    head_shape = (length, heads, HD)
    queries = rotate(
        jnp.dot(normed_one, w_query, preferred_element_type=F32).reshape(head_shape),
        cosine_table,
        sine_table,
    ).astype(BF16)
    key_rows = rotate(
        jnp.dot(normed_one, w_key, preferred_element_type=F32).reshape(head_shape),
        cosine_table,
        sine_table,
    ).astype(BF16)
    value_rows = (
        jnp.dot(normed_one, w_value, preferred_element_type=F32).astype(BF16).reshape(head_shape)
    )
    score_scale = 1.0 / math.sqrt(HD)
    scores = (
        jnp.einsum("qhd,khd->hqk", queries, key_rows, preferred_element_type=F32) * score_scale
    )
    scores = jnp.where(same_segment[None], scores, MASKED)
    row_peak = jnp.max(scores, axis=-1, keepdims=True)
    exponent = jnp.exp(scores - row_peak)
    row_total = jnp.sum(exponent, axis=-1, keepdims=True)
    probs = exponent / row_total
    probs_low = probs.astype(BF16)
    attended = (
        jnp.einsum("hqk,khd->qhd", probs_low, value_rows, preferred_element_type=F32)
        .astype(BF16)
        .reshape(length, -1)
    )

    attended_all = lax.all_to_all(
        jnp.broadcast_to(attended[None], (count,) + attended.shape), "narrow", 0, 0, tiled=False
    )
    branch = jnp.einsum(
        "jtc,jcd->td", attended_all, w_out_full, preferred_element_type=F32
    )
    middle = inputs + branch
    normed_two_float, scaled_two, inverse_two = normalize(middle, gain_two, bias_two)
    normed_two = normed_two_float.astype(BF16)

    gate_pre = jnp.dot(normed_two, w_gate, preferred_element_type=F32)
    up_pre = jnp.dot(normed_two, w_up, preferred_element_type=F32)
    sigmoid_gate = jax.nn.sigmoid(gate_pre)
    active = gate_pre * sigmoid_gate
    hidden = (active * up_pre).astype(BF16)
    ffn_partial = jnp.dot(hidden, w_down, preferred_element_type=F32).astype(BF16)

    hidden_grad = contract_last(cot_full, w_down)
    gate_grad = (
        hidden_grad * up_pre * sigmoid_gate * (1.0 + gate_pre * (1.0 - sigmoid_gate))
    ).astype(BF16)
    up_grad = (hidden_grad * active).astype(BF16)
    ffn_grads = jnp.concatenate(
        [
            contract_first(normed_two, jnp.concatenate([gate_grad, up_grad], axis=1)),
            contract_first(hidden, cot_full),
        ],
        axis=0,
    ).astype(BF16)
    ffn_core = core_reduce(ffn_grads, wide)
    two_partial = (contract_last(gate_grad, w_gate) + contract_last(up_grad, w_up)).astype(BF16)
    both = narrow_scatter(jnp.concatenate([ffn_partial, two_partial], axis=1), count)
    layer_out = lax.dynamic_slice_in_dim(middle, own_rows, block, 0) + both[:, :d_model]
    own_two_grad = both[:, d_model:]
    own_scaled_two = lax.dynamic_slice_in_dim(scaled_two, own_rows, block, 0)
    own_inverse_two = lax.dynamic_slice_in_dim(inverse_two, own_rows, block, 0)

    middle_grad = cotangent.astype(F32) + normalize_back(
        own_two_grad, own_scaled_two, own_inverse_two, gain_two
    )
    ffn_x = x_reduce(ffn_core, wide)
    branch_grad = narrow_gather(tie(middle_grad.astype(BF16), ffn_core), count)
    ffn_rows = x_gather(z_gather(z_reduce(ffn_x, wide), wide), wide)

    attended_grad = contract_last(branch_grad, w_out).astype(BF16).reshape(head_shape)
    prob_grad = jnp.einsum(
        "qhd,khd->hqk", attended_grad, value_rows, preferred_element_type=F32
    )
    score_grad = (
        probs * (prob_grad - jnp.sum(probs * prob_grad, axis=-1, keepdims=True))
    ).astype(BF16)
    query_grad = score_scale * jnp.einsum(
        "hqk,khd->qhd", score_grad, key_rows, preferred_element_type=F32
    )
    key_grad = score_scale * jnp.einsum(
        "hqk,qhd->khd", score_grad, queries, preferred_element_type=F32
    )
    value_grad = jnp.einsum(
        "hqk,qhd->khd", probs_low, attended_grad, preferred_element_type=F32
    ).astype(BF16).reshape(length, -1)
    query_grad = unrotate(query_grad, cosine_table, sine_table).astype(BF16).reshape(length, -1)
    key_grad = unrotate(key_grad, cosine_table, sine_table).astype(BF16).reshape(length, -1)
    projection_grads = jnp.concatenate([query_grad, key_grad, value_grad], axis=1)
    projections = w_query.shape[1]
    qkv_grads = contract_first(normed_one, projection_grads).astype(BF16)
    attn_grads = jnp.concatenate(
        [qkv_grads, contract_first(branch_grad, attended).astype(BF16)], axis=1
    )
    attn_total = wide_allreduce(attn_grads, wide)
    one_float = contract_last(
        projection_grads, jnp.concatenate([w_query, w_key, w_value], axis=1)
    )
    norm_one = jnp.stack(
        [jnp.sum(one_float * scaled_one, axis=0), jnp.sum(one_float, axis=0)]
    )
    norm_two = jnp.stack(
        [jnp.sum(own_two_grad * own_scaled_two, axis=0), jnp.sum(own_two_grad, axis=0)]
    )
    norm_parts = jnp.concatenate([norm_one, norm_two], axis=0)
    high, low = split_hi_lo(norm_parts)
    extra = jnp.concatenate([high, low, jnp.zeros((8, d_model), BF16)], axis=0)
    one_blocks = one_float.astype(BF16).reshape(count, block, d_model)
    payload = jnp.concatenate(
        [one_blocks, jnp.broadcast_to(extra[None], (count,) + extra.shape)], axis=1
    )
    got = lax.all_to_all(tie(payload, ffn_rows), "narrow", 0, 0, tiled=False).astype(F32)
    ffn_total = core_gather(ffn_rows, wide).astype(F32)
    summed = jnp.sum(got, axis=0)
    own_one_grad = summed[:block]
    norm_narrow = summed[block : block + 4] + summed[block + 4 : block + 8]
    norm_total = wide_allreduce_small(norm_narrow, wide)
    input_grad = middle_grad + normalize_back(
        own_one_grad, own_scaled_one, own_inverse_one, gain_one
    )
    ff_cols = w_gate.shape[1]
    return (
        layer_out,
        input_grad,
        attn_total[:, :projections],
        attn_total[:, projections : 2 * projections],
        attn_total[:, 2 * projections : 3 * projections],
        attn_total[:, 3 * projections :].T,
        ffn_total[:d_model, :ff_cols],
        ffn_total[:d_model, ff_cols:],
        ffn_total[d_model:],
        norm_total[0],
        norm_total[1],
        norm_total[2],
        norm_total[3],
    )


def solution(mesh):
    placed = (
        P(("wide", "narrow"), None),
        P(("wide", "narrow"), None),
        P("wide", None),
        P(None, "narrow"),
        P(None, "narrow"),
        P(None, "narrow"),
        P("narrow", None),
        P(None, "narrow"),
        P(None, "narrow"),
        P("narrow", None),
        P(),
        P(),
        P(),
        P(),
    )
    return jax.shard_map(
        per_device,
        mesh=mesh,
        in_specs=placed,
        out_specs=(
            P(("wide", "narrow"), None),
            P(("wide", "narrow"), None),
            P(None, "narrow"),
            P(None, "narrow"),
            P(None, "narrow"),
            P("narrow", None),
            P(None, "narrow"),
            P(None, "narrow"),
            P("narrow", None),
            P(),
            P(),
            P(),
            P(),
        ),
        check_vma=False,
    )
```

```python
import math

import jax
import jax.numpy as jnp
from jax import lax
from jax.sharding import PartitionSpec as P

HD = 64
EPS = 1e-05
MASKED = -1e30
F32 = jnp.float32
BF16 = jnp.bfloat16


def normalize(values, gain_vec, bias_vec):
    centred = values - jnp.mean(values, axis=-1, keepdims=True)
    inverse = lax.rsqrt(jnp.mean(centred * centred, axis=-1, keepdims=True) + EPS)
    scaled = centred * inverse
    return (scaled * gain_vec + bias_vec, scaled, inverse)


def normalize_back(grad_in, scaled, inverse, gain_vec):
    along = grad_in * gain_vec
    return inverse * (
        along
        - jnp.mean(along, axis=-1, keepdims=True)
        - scaled * jnp.mean(along * scaled, axis=-1, keepdims=True)
    )


def contract_last(left_side, right_side):
    return lax.dot_general(
        left_side, right_side, (((1,), (1,)), ((), ())), preferred_element_type=F32
    )


def contract_first(left_side, right_side):
    return lax.dot_general(
        left_side, right_side, (((0,), (0,)), ((), ())), preferred_element_type=F32
    )


def rotate(values, cosine_table, sine_table):
    half_width = values.shape[-1] // 2
    first_half = values[..., :half_width]
    second_half = values[..., half_width:]
    cosine = cosine_table[:, None, :]
    sine_part = sine_table[:, None, :]
    return jnp.concatenate(
        [
            first_half * cosine - second_half * sine_part,
            second_half * cosine + first_half * sine_part,
        ],
        axis=-1,
    )


def unrotate(values, cosine_table, sine_table):
    half_width = values.shape[-1] // 2
    first_half = values[..., :half_width]
    second_half = values[..., half_width:]
    cosine = cosine_table[:, None, :]
    sine_part = sine_table[:, None, :]
    return jnp.concatenate(
        [
            first_half * cosine + second_half * sine_part,
            second_half * cosine - first_half * sine_part,
        ],
        axis=-1,
    )


def narrow_gather(own, count):
    slots = jnp.broadcast_to(own[None], (count,) + own.shape)
    got = lax.all_to_all(slots, "narrow", 0, 0, tiled=False)
    return got.reshape(count * own.shape[0], own.shape[1])


def narrow_scatter(partial, count):
    blocks = partial.reshape(count, partial.shape[0] // count, partial.shape[1])
    got = lax.all_to_all(blocks, "narrow", 0, 0, tiled=False)
    return jnp.sum(got.astype(F32), axis=0)


def narrow_gather_async(own, count):
    index = lax.axis_index("narrow")
    rows = own.shape[0]
    whole = jnp.zeros((count * rows, own.shape[1]), own.dtype)
    whole = lax.dynamic_update_slice_in_dim(whole, own, index * rows, 0)
    for k in range(1, count):
        got = lax.ppermute(own, "narrow", [((i + k) % count, i) for i in range(count)])
        whole = lax.dynamic_update_slice_in_dim(whole, got, ((index + k) % count) * rows, 0)
    return whole


def split_hi_lo(values):
    high = values.astype(BF16)
    return high, (values - high.astype(F32)).astype(BF16)


def wide_layout(wide):
    chips_x = wide // 4
    w = lax.axis_index("wide")
    return chips_x, w % 2, (w // 2) % chips_x, w // (2 * chips_x)


def wide_map(wide, dcore=0, dx=0, dz=0, flip_core=False, xor_x=0):
    chips_x = wide // 4
    pairs = []
    for v in range(wide):
        c, xx, zz = v % 2, (v // 2) % chips_x, v // (2 * chips_x)
        c2 = (1 - c) if flip_core else c
        x2 = ((xx ^ xor_x) + dx) % chips_x
        z2 = (zz + dz) % 2
        pairs.append((v, z2 * 2 * chips_x + x2 * 2 + c2))
    return pairs


def tie(value, anchor):
    return lax.optimization_barrier((value, anchor))[0]


def core_reduce(grad, wide):
    _, core, _, _ = wide_layout(wide)
    half = grad.shape[0] // 2
    keep = lax.dynamic_slice_in_dim(grad, core * half, half, 0)
    send = lax.dynamic_slice_in_dim(grad, (1 - core) * half, half, 0)
    return keep.astype(F32) + lax.ppermute(send, "wide", wide_map(wide, flip_core=True)).astype(F32)


def x_reduce(summed, wide):
    chips_x, _, xpos, _ = wide_layout(wide)
    quarter = summed.shape[0] // chips_x
    acc = lax.dynamic_slice_in_dim(summed, xpos * quarter, quarter, 0)
    for k in range(1, chips_x):
        piece = lax.dynamic_slice_in_dim(summed, ((xpos + k) % chips_x) * quarter, quarter, 0)
        acc = acc + lax.ppermute(piece.astype(BF16), "wide", wide_map(wide, dx=k)).astype(F32)
    return acc


def z_reduce(acc, wide):
    _, _, _, zhi = wide_layout(wide)
    eighth = acc.shape[0] // 2
    mine = lax.dynamic_slice_in_dim(acc, zhi * eighth, eighth, 0)
    other = lax.dynamic_slice_in_dim(acc, (1 - zhi) * eighth, eighth, 0)
    got = lax.ppermute(other.astype(BF16), "wide", wide_map(wide, dz=1)).astype(F32)
    return (mine + got).astype(BF16)


def z_gather(final, wide):
    _, _, _, zhi = wide_layout(wide)
    eighth = final.shape[0]
    part = jnp.zeros((2 * eighth, final.shape[1]), BF16)
    part = lax.dynamic_update_slice_in_dim(part, final, zhi * eighth, 0)
    return lax.dynamic_update_slice_in_dim(
        part, lax.ppermute(final, "wide", wide_map(wide, dz=1)), (1 - zhi) * eighth, 0
    )


def x_gather(part, wide):
    chips_x, _, xpos, _ = wide_layout(wide)
    quarter = part.shape[0]
    halfrows = jnp.zeros((chips_x * quarter, part.shape[1]), BF16)
    halfrows = lax.dynamic_update_slice_in_dim(halfrows, part, xpos * quarter, 0)
    for k in range(1, chips_x):
        got = lax.ppermute(part, "wide", wide_map(wide, dx=chips_x - k))
        halfrows = lax.dynamic_update_slice_in_dim(
            halfrows, got, ((xpos + k) % chips_x) * quarter, 0
        )
    return halfrows


def core_gather(halfrows, wide):
    _, core, _, _ = wide_layout(wide)
    half = halfrows.shape[0]
    whole = jnp.zeros((2 * half, halfrows.shape[1]), BF16)
    whole = lax.dynamic_update_slice_in_dim(whole, halfrows, core * half, 0)
    return lax.dynamic_update_slice_in_dim(
        whole, lax.ppermute(halfrows, "wide", wide_map(wide, flip_core=True)), (1 - core) * half, 0
    )


def wide_allreduce(grad, wide):
    stage = z_gather(z_reduce(x_reduce(core_reduce(grad, wide), wide), wide), wide)
    return core_gather(x_gather(stage, wide), wide).astype(F32)


def wide_allreduce_small(values, wide):
    chips_x = wide // 4
    values = values + lax.ppermute(values, "wide", wide_map(wide, flip_core=True))
    values = values + lax.ppermute(values, "wide", wide_map(wide, xor_x=1))
    if chips_x > 2:
        values = values + lax.ppermute(values, "wide", wide_map(wide, xor_x=2))
    return values + lax.ppermute(values, "wide", wide_map(wide, dz=1))


def per_device(
    tokens,
    cotangent,
    segments,
    w_query,
    w_key,
    w_value,
    w_out,
    w_gate,
    w_up,
    w_down,
    gain_one,
    bias_one,
    gain_two,
    bias_two,
):
    count = lax.axis_size("narrow")
    wide = lax.axis_size("wide")
    block, d_model = tokens.shape
    narrow_index = lax.axis_index("narrow")
    own_rows = narrow_index * block

    seg = segments[0]
    length = seg.shape[0]
    column = lax.broadcasted_iota(jnp.int32, (length, length), 1)
    same_segment = seg[:, None] == seg[None, :]
    first_index = jnp.min(jnp.where(same_segment, column, length), axis=-1)
    position = (jnp.arange(length, dtype=jnp.int32) - first_index).astype(F32)
    inverse = 10000.0 ** (-(2.0 * jnp.arange(HD // 2).astype(F32) / HD))
    angles = position[:, None] * inverse
    cosine_table, sine_table = jnp.cos(angles), jnp.sin(angles)

    head_rows = w_out.shape[0]
    first = narrow_gather(
        jnp.concatenate([tokens, cotangent, w_out], axis=0), count
    ).reshape(count, 2 * block + head_rows, d_model)
    tok_full = first[:, :block].reshape(length, d_model)
    cot_full = first[:, block : 2 * block].reshape(length, d_model)
    w_out_full = first[:, 2 * block :]

    inputs = tok_full.astype(F32)
    normed_float, scaled_one, inverse_one = normalize(inputs, gain_one, bias_one)
    normed_one = normed_float.astype(BF16)
    own_scaled_one = lax.dynamic_slice_in_dim(scaled_one, own_rows, block, 0)
    own_inverse_one = lax.dynamic_slice_in_dim(inverse_one, own_rows, block, 0)

    heads = w_query.shape[1] // HD
    head_shape = (length, heads, HD)
    queries = rotate(
        jnp.dot(normed_one, w_query, preferred_element_type=F32).reshape(head_shape),
        cosine_table,
        sine_table,
    ).astype(BF16)
    key_rows = rotate(
        jnp.dot(normed_one, w_key, preferred_element_type=F32).reshape(head_shape),
        cosine_table,
        sine_table,
    ).astype(BF16)
    value_rows = (
        jnp.dot(normed_one, w_value, preferred_element_type=F32).astype(BF16).reshape(head_shape)
    )
    score_scale = 1.0 / math.sqrt(HD)
    scores = (
        jnp.einsum("qhd,khd->hqk", queries, key_rows, preferred_element_type=F32) * score_scale
    )
    scores = jnp.where(same_segment[None], scores, MASKED)
    row_peak = jnp.max(scores, axis=-1, keepdims=True)
    exponent = jnp.exp(scores - row_peak)
    row_total = jnp.sum(exponent, axis=-1, keepdims=True)
    probs = exponent / row_total
    probs_low = probs.astype(BF16)
    attended = (
        jnp.einsum("hqk,khd->qhd", probs_low, value_rows, preferred_element_type=F32)
        .astype(BF16)
        .reshape(length, -1)
    )

    attended_all = lax.all_to_all(
        jnp.broadcast_to(attended[None], (count,) + attended.shape), "narrow", 0, 0, tiled=False
    )
    branch = jnp.einsum(
        "jtc,jcd->td", attended_all, w_out_full, preferred_element_type=F32
    )
    middle = inputs + branch
    normed_two_float, scaled_two, inverse_two = normalize(middle, gain_two, bias_two)
    normed_two = normed_two_float.astype(BF16)

    gate_pre = jnp.dot(normed_two, w_gate, preferred_element_type=F32)
    up_pre = jnp.dot(normed_two, w_up, preferred_element_type=F32)
    sigmoid_gate = jax.nn.sigmoid(gate_pre)
    active = gate_pre * sigmoid_gate
    hidden = (active * up_pre).astype(BF16)
    ffn_partial = jnp.dot(hidden, w_down, preferred_element_type=F32).astype(BF16)

    hidden_grad = contract_last(cot_full, w_down)
    gate_grad = (
        hidden_grad * up_pre * sigmoid_gate * (1.0 + gate_pre * (1.0 - sigmoid_gate))
    ).astype(BF16)
    up_grad = (hidden_grad * active).astype(BF16)
    ffn_grads = jnp.concatenate(
        [
            contract_first(normed_two, jnp.concatenate([gate_grad, up_grad], axis=1)),
            contract_first(hidden, cot_full),
        ],
        axis=0,
    ).astype(BF16)
    ffn_core = core_reduce(ffn_grads, wide)
    two_partial = (contract_last(gate_grad, w_gate) + contract_last(up_grad, w_up)).astype(BF16)
    both = narrow_scatter(jnp.concatenate([ffn_partial, two_partial], axis=1), count)
    layer_out = lax.dynamic_slice_in_dim(middle, own_rows, block, 0) + both[:, :d_model]
    own_two_grad = both[:, d_model:]
    own_scaled_two = lax.dynamic_slice_in_dim(scaled_two, own_rows, block, 0)
    own_inverse_two = lax.dynamic_slice_in_dim(inverse_two, own_rows, block, 0)

    middle_grad = cotangent.astype(F32) + normalize_back(
        own_two_grad, own_scaled_two, own_inverse_two, gain_two
    )
    own_branch, ffn_core = lax.optimization_barrier((middle_grad.astype(BF16), ffn_core))
    ffn_x = x_reduce(ffn_core, wide)
    branch_grad = narrow_gather(own_branch, count)
    ffn_rows = x_gather(z_gather(z_reduce(ffn_x, wide), wide), wide)

    attended_grad = contract_last(branch_grad, w_out).astype(BF16).reshape(head_shape)
    prob_grad = jnp.einsum(
        "qhd,khd->hqk", attended_grad, value_rows, preferred_element_type=F32
    )
    score_grad = (
        probs * (prob_grad - jnp.sum(probs * prob_grad, axis=-1, keepdims=True))
    ).astype(BF16)
    query_grad = score_scale * jnp.einsum(
        "hqk,khd->qhd", score_grad, key_rows, preferred_element_type=F32
    )
    key_grad = score_scale * jnp.einsum(
        "hqk,qhd->khd", score_grad, queries, preferred_element_type=F32
    )
    value_grad = jnp.einsum(
        "hqk,qhd->khd", probs_low, attended_grad, preferred_element_type=F32
    ).astype(BF16).reshape(length, -1)
    query_grad = unrotate(query_grad, cosine_table, sine_table).astype(BF16).reshape(length, -1)
    key_grad = unrotate(key_grad, cosine_table, sine_table).astype(BF16).reshape(length, -1)
    projection_grads = jnp.concatenate([query_grad, key_grad, value_grad], axis=1)
    projections = w_query.shape[1]
    qkv_grads = contract_first(normed_one, projection_grads).astype(BF16)
    attn_grads = jnp.concatenate(
        [qkv_grads, contract_first(branch_grad, attended).astype(BF16)], axis=1
    )
    one_float = contract_last(
        projection_grads, jnp.concatenate([w_query, w_key, w_value], axis=1)
    )
    norm_one = jnp.stack(
        [jnp.sum(one_float * scaled_one, axis=0), jnp.sum(one_float, axis=0)]
    )
    norm_two = jnp.stack(
        [jnp.sum(own_two_grad * own_scaled_two, axis=0), jnp.sum(own_two_grad, axis=0)]
    )
    norm_parts = jnp.concatenate([norm_one, norm_two], axis=0)
    high, low = split_hi_lo(norm_parts)
    extra = jnp.concatenate([high, low, jnp.zeros((8, d_model), BF16)], axis=0)
    one_blocks = one_float.astype(BF16).reshape(count, block, d_model)
    payload = jnp.concatenate(
        [one_blocks, jnp.broadcast_to(extra[None], (count,) + extra.shape)], axis=1
    )
    payload, ffn_rows = lax.optimization_barrier((payload, ffn_rows))
    got = lax.all_to_all(payload, "narrow", 0, 0, tiled=False)
    attn_core = core_reduce(attn_grads, wide)
    got, attn_core = lax.optimization_barrier((got, attn_core))
    got = got.astype(F32)
    attn_stage = z_gather(z_reduce(x_reduce(attn_core, wide), wide), wide)
    attn_total = core_gather(x_gather(attn_stage, wide), wide).astype(F32)
    ffn_total = core_gather(ffn_rows, wide).astype(F32)
    summed = jnp.sum(got, axis=0)
    own_one_grad = summed[:block]
    norm_narrow = summed[block : block + 4] + summed[block + 4 : block + 8]
    norm_total = wide_allreduce_small(norm_narrow, wide)
    input_grad = middle_grad + normalize_back(
        own_one_grad, own_scaled_one, own_inverse_one, gain_one
    )
    ff_cols = w_gate.shape[1]
    return (
        layer_out,
        input_grad,
        attn_total[:, :projections],
        attn_total[:, projections : 2 * projections],
        attn_total[:, 2 * projections : 3 * projections],
        attn_total[:, 3 * projections :].T,
        ffn_total[:d_model, :ff_cols],
        ffn_total[:d_model, ff_cols:],
        ffn_total[d_model:],
        norm_total[0],
        norm_total[1],
        norm_total[2],
        norm_total[3],
    )


def solution(mesh):
    placed = (
        P(("wide", "narrow"), None),
        P(("wide", "narrow"), None),
        P("wide", None),
        P(None, "narrow"),
        P(None, "narrow"),
        P(None, "narrow"),
        P("narrow", None),
        P(None, "narrow"),
        P(None, "narrow"),
        P("narrow", None),
        P(),
        P(),
        P(),
        P(),
    )
    return jax.shard_map(
        per_device,
        mesh=mesh,
        in_specs=placed,
        out_specs=(
            P(("wide", "narrow"), None),
            P(("wide", "narrow"), None),
            P(None, "narrow"),
            P(None, "narrow"),
            P(None, "narrow"),
            P("narrow", None),
            P(None, "narrow"),
            P(None, "narrow"),
            P("narrow", None),
            P(),
            P(),
            P(),
            P(),
        ),
        check_vma=False,
    )
```

```python
import math

import jax
import jax.numpy as jnp
from jax import lax
from jax.sharding import PartitionSpec as P

HD = 64
EPS = 1e-05
MASKED = -1e30
F32 = jnp.float32
BF16 = jnp.bfloat16


def normalize(values, gain_vec, bias_vec):
    centred = values - jnp.mean(values, axis=-1, keepdims=True)
    inverse = lax.rsqrt(jnp.mean(centred * centred, axis=-1, keepdims=True) + EPS)
    scaled = centred * inverse
    return (scaled * gain_vec + bias_vec, scaled, inverse)


def normalize_back(grad_in, scaled, inverse, gain_vec):
    along = grad_in * gain_vec
    return inverse * (
        along
        - jnp.mean(along, axis=-1, keepdims=True)
        - scaled * jnp.mean(along * scaled, axis=-1, keepdims=True)
    )


def contract_last(left_side, right_side):
    return lax.dot_general(
        left_side, right_side, (((1,), (1,)), ((), ())), preferred_element_type=F32
    )


def contract_first(left_side, right_side):
    return lax.dot_general(
        left_side, right_side, (((0,), (0,)), ((), ())), preferred_element_type=F32
    )


def rotate(values, cosine_table, sine_table):
    half_width = values.shape[-1] // 2
    first_half = values[..., :half_width]
    second_half = values[..., half_width:]
    cosine = cosine_table[:, None, :]
    sine_part = sine_table[:, None, :]
    return jnp.concatenate(
        [
            first_half * cosine - second_half * sine_part,
            second_half * cosine + first_half * sine_part,
        ],
        axis=-1,
    )


def unrotate(values, cosine_table, sine_table):
    half_width = values.shape[-1] // 2
    first_half = values[..., :half_width]
    second_half = values[..., half_width:]
    cosine = cosine_table[:, None, :]
    sine_part = sine_table[:, None, :]
    return jnp.concatenate(
        [
            first_half * cosine + second_half * sine_part,
            second_half * cosine - first_half * sine_part,
        ],
        axis=-1,
    )


def narrow_gather(own, count):
    slots = jnp.broadcast_to(own[None], (count,) + own.shape)
    got = lax.all_to_all(slots, "narrow", 0, 0, tiled=False)
    return got.reshape(count * own.shape[0], own.shape[1])


def narrow_scatter(partial, count):
    blocks = partial.reshape(count, partial.shape[0] // count, partial.shape[1])
    got = lax.all_to_all(blocks, "narrow", 0, 0, tiled=False)
    return jnp.sum(got.astype(F32), axis=0)


def narrow_gather_async(own, count):
    index = lax.axis_index("narrow")
    rows = own.shape[0]
    whole = jnp.zeros((count * rows, own.shape[1]), own.dtype)
    whole = lax.dynamic_update_slice_in_dim(whole, own, index * rows, 0)
    for k in range(1, count):
        got = lax.ppermute(own, "narrow", [((i + k) % count, i) for i in range(count)])
        whole = lax.dynamic_update_slice_in_dim(whole, got, ((index + k) % count) * rows, 0)
    return whole


def split_hi_lo(values):
    high = values.astype(BF16)
    return high, (values - high.astype(F32)).astype(BF16)


def narrow_maps(count):
    plane = count // 2

    def build(mapping):
        return [(z * plane + y, mapping(z, y)) for z in range(2) for y in range(plane)]

    up = build(lambda z, y: z * plane + (y + 1) % plane)
    down = build(lambda z, y: z * plane + (y - 1) % plane)
    across = build(lambda z, y: (1 - z) * plane + y)
    return up, down, across


def tree_gather(own, count):
    up, down, across = narrow_maps(count)
    from_below = lax.ppermute(own, "narrow", up)
    from_above = lax.ppermute(own, "narrow", down)
    from_across = lax.ppermute(own, "narrow", across)
    two_above = lax.ppermute(from_below, "narrow", up)
    across_above = lax.ppermute(from_across, "narrow", down)
    across_below = lax.ppermute(from_below, "narrow", across)
    across_two = lax.ppermute(two_above, "narrow", across)
    return [own, from_below, from_above, from_across, two_above, across_above, across_below, across_two]


def tree_scatter(blocks, count):
    up, down, across = narrow_maps(count)

    def send(value, pairs):
        return lax.ppermute(value.astype(BF16), "narrow", pairs).astype(F32)

    part = [blocks[s].astype(F32) for s in range(count)]
    first = send(part[7], across)
    below = send(part[4] + first, down)
    side = send(part[6], across)
    over = send(part[5], up)
    total = part[0] + send(part[1] + below + side, down)
    total = total + send(part[3] + over, across)
    return total + send(part[2], up)


def slot_sources(count):
    plane = count // 2
    index = lax.axis_index("narrow")
    z, y = index // plane, index % plane
    dz = jnp.array([0, 0, 0, 1, 0, 1, 1, 1], jnp.int32)
    dy = jnp.array([0, -1, 1, 0, 2, 1, -1, 2], jnp.int32)
    return ((z + dz) % 2) * plane + (y + dy) % plane


def source_slots(count):
    plane = count // 2
    index = lax.axis_index("narrow")
    z, y = index // plane, index % plane
    block = jnp.arange(count)
    dz = (block // plane - z) % 2
    dy = (block % plane - y) % plane
    same = jnp.array([0, 2, 4, 1], jnp.int32)
    other = jnp.array([3, 5, 7, 6], jnp.int32)
    return jnp.where(dz == 0, same[dy], other[dy])


def wide_layout(wide):
    chips_x = wide // 4
    w = lax.axis_index("wide")
    return chips_x, w % 2, (w // 2) % chips_x, w // (2 * chips_x)


def wide_map(wide, dcore=0, dx=0, dz=0, flip_core=False, xor_x=0):
    chips_x = wide // 4
    pairs = []
    for v in range(wide):
        c, xx, zz = v % 2, (v // 2) % chips_x, v // (2 * chips_x)
        c2 = (1 - c) if flip_core else c
        x2 = ((xx ^ xor_x) + dx) % chips_x
        z2 = (zz + dz) % 2
        pairs.append((v, z2 * 2 * chips_x + x2 * 2 + c2))
    return pairs


def tie(value, anchor):
    return lax.optimization_barrier((value, anchor))[0]


def core_reduce(grad, wide):
    _, core, _, _ = wide_layout(wide)
    half = grad.shape[0] // 2
    keep = lax.dynamic_slice_in_dim(grad, core * half, half, 0)
    send = lax.dynamic_slice_in_dim(grad, (1 - core) * half, half, 0)
    return keep.astype(F32) + lax.ppermute(send, "wide", wide_map(wide, flip_core=True)).astype(F32)


def x_reduce(summed, wide):
    chips_x, _, xpos, _ = wide_layout(wide)
    quarter = summed.shape[0] // chips_x
    acc = lax.dynamic_slice_in_dim(summed, xpos * quarter, quarter, 0)
    for k in range(1, chips_x):
        piece = lax.dynamic_slice_in_dim(summed, ((xpos + k) % chips_x) * quarter, quarter, 0)
        acc = acc + lax.ppermute(piece.astype(BF16), "wide", wide_map(wide, dx=k)).astype(F32)
    return acc


def z_reduce(acc, wide):
    _, _, _, zhi = wide_layout(wide)
    eighth = acc.shape[0] // 2
    mine = lax.dynamic_slice_in_dim(acc, zhi * eighth, eighth, 0)
    other = lax.dynamic_slice_in_dim(acc, (1 - zhi) * eighth, eighth, 0)
    got = lax.ppermute(other.astype(BF16), "wide", wide_map(wide, dz=1)).astype(F32)
    return (mine + got).astype(BF16)


def z_gather(final, wide):
    _, _, _, zhi = wide_layout(wide)
    eighth = final.shape[0]
    part = jnp.zeros((2 * eighth, final.shape[1]), BF16)
    part = lax.dynamic_update_slice_in_dim(part, final, zhi * eighth, 0)
    return lax.dynamic_update_slice_in_dim(
        part, lax.ppermute(final, "wide", wide_map(wide, dz=1)), (1 - zhi) * eighth, 0
    )


def x_gather(part, wide):
    chips_x, _, xpos, _ = wide_layout(wide)
    quarter = part.shape[0]
    halfrows = jnp.zeros((chips_x * quarter, part.shape[1]), BF16)
    halfrows = lax.dynamic_update_slice_in_dim(halfrows, part, xpos * quarter, 0)
    for k in range(1, chips_x):
        got = lax.ppermute(part, "wide", wide_map(wide, dx=chips_x - k))
        halfrows = lax.dynamic_update_slice_in_dim(
            halfrows, got, ((xpos + k) % chips_x) * quarter, 0
        )
    return halfrows


def core_gather(halfrows, wide):
    _, core, _, _ = wide_layout(wide)
    half = halfrows.shape[0]
    whole = jnp.zeros((2 * half, halfrows.shape[1]), BF16)
    whole = lax.dynamic_update_slice_in_dim(whole, halfrows, core * half, 0)
    return lax.dynamic_update_slice_in_dim(
        whole, lax.ppermute(halfrows, "wide", wide_map(wide, flip_core=True)), (1 - core) * half, 0
    )


def wide_allreduce(grad, wide):
    stage = z_gather(z_reduce(x_reduce(core_reduce(grad, wide), wide), wide), wide)
    return core_gather(x_gather(stage, wide), wide).astype(F32)


def wide_allreduce_small(values, wide):
    chips_x = wide // 4
    values = values + lax.ppermute(values, "wide", wide_map(wide, flip_core=True))
    values = values + lax.ppermute(values, "wide", wide_map(wide, xor_x=1))
    if chips_x > 2:
        values = values + lax.ppermute(values, "wide", wide_map(wide, xor_x=2))
    return values + lax.ppermute(values, "wide", wide_map(wide, dz=1))


def per_device(
    tokens,
    cotangent,
    segments,
    w_query,
    w_key,
    w_value,
    w_out,
    w_gate,
    w_up,
    w_down,
    gain_one,
    bias_one,
    gain_two,
    bias_two,
):
    count = lax.axis_size("narrow")
    wide = lax.axis_size("wide")
    block, d_model = tokens.shape
    narrow_index = lax.axis_index("narrow")
    own_rows = narrow_index * block

    seg = segments[0]
    length = seg.shape[0]
    column = lax.broadcasted_iota(jnp.int32, (length, length), 1)
    same_orig = seg[:, None] == seg[None, :]
    first_index = jnp.min(jnp.where(same_orig, column, length), axis=-1)
    position = jnp.arange(length, dtype=jnp.int32) - first_index
    order = slot_sources(count)
    seg = jnp.take(seg.reshape(count, block), order, axis=0).reshape(length)
    position = jnp.take(position.reshape(count, block), order, axis=0).reshape(length)
    same_segment = seg[:, None] == seg[None, :]
    inverse = 10000.0 ** (-(2.0 * jnp.arange(HD // 2).astype(F32) / HD))
    angles = position.astype(F32)[:, None] * inverse
    cosine_table, sine_table = jnp.cos(angles), jnp.sin(angles)

    head_rows = w_out.shape[0]
    first = tree_gather(jnp.concatenate([tokens, cotangent, w_out], axis=0), count)
    tok_full = jnp.concatenate([piece[:block] for piece in first], axis=0)
    cot_full = jnp.concatenate([piece[block : 2 * block] for piece in first], axis=0)
    w_out_slots = jnp.stack([piece[2 * block :] for piece in first])

    inputs = tok_full.astype(F32)
    normed_float, scaled_one, inverse_one = normalize(inputs, gain_one, bias_one)
    normed_one = normed_float.astype(BF16)
    own_scaled_one = scaled_one[:block]
    own_inverse_one = inverse_one[:block]

    heads = w_query.shape[1] // HD
    head_shape = (length, heads, HD)
    queries = rotate(
        jnp.dot(normed_one, w_query, preferred_element_type=F32).reshape(head_shape),
        cosine_table,
        sine_table,
    ).astype(BF16)
    key_rows = rotate(
        jnp.dot(normed_one, w_key, preferred_element_type=F32).reshape(head_shape),
        cosine_table,
        sine_table,
    ).astype(BF16)
    value_rows = (
        jnp.dot(normed_one, w_value, preferred_element_type=F32).astype(BF16).reshape(head_shape)
    )
    score_scale = 1.0 / math.sqrt(HD)
    scores = (
        jnp.einsum("qhd,khd->hqk", queries, key_rows, preferred_element_type=F32) * score_scale
    )
    scores = jnp.where(same_segment[None], scores, MASKED)
    row_peak = jnp.max(scores, axis=-1, keepdims=True)
    exponent = jnp.exp(scores - row_peak)
    row_total = jnp.sum(exponent, axis=-1, keepdims=True)
    probs = exponent / row_total
    probs_low = probs.astype(BF16)
    attended = (
        jnp.einsum("hqk,khd->qhd", probs_low, value_rows, preferred_element_type=F32)
        .astype(BF16)
        .reshape(length, -1)
    )

    heads_cols = attended.shape[1]
    attended_orig = jnp.take(
        attended.reshape(count, block, heads_cols), source_slots(count), axis=0
    ).reshape(length, heads_cols)
    attended_all = jnp.take(
        jnp.stack(tree_gather(attended_orig, count)).reshape(count, count, block, heads_cols),
        order,
        axis=1,
    ).reshape(count, length, heads_cols)
    branch = jnp.einsum(
        "jtc,jcd->td", attended_all, w_out_slots, preferred_element_type=F32
    )
    middle = inputs + branch
    normed_two_float, scaled_two, inverse_two = normalize(middle, gain_two, bias_two)
    normed_two = normed_two_float.astype(BF16)

    gate_pre = jnp.dot(normed_two, w_gate, preferred_element_type=F32)
    up_pre = jnp.dot(normed_two, w_up, preferred_element_type=F32)
    sigmoid_gate = jax.nn.sigmoid(gate_pre)
    active = gate_pre * sigmoid_gate
    hidden = (active * up_pre).astype(BF16)
    ffn_partial = jnp.dot(hidden, w_down, preferred_element_type=F32).astype(BF16)

    hidden_grad = contract_last(cot_full, w_down)
    gate_grad = (
        hidden_grad * up_pre * sigmoid_gate * (1.0 + gate_pre * (1.0 - sigmoid_gate))
    ).astype(BF16)
    up_grad = (hidden_grad * active).astype(BF16)
    ffn_grads = jnp.concatenate(
        [
            contract_first(normed_two, jnp.concatenate([gate_grad, up_grad], axis=1)),
            contract_first(hidden, cot_full),
        ],
        axis=0,
    ).astype(BF16)
    ffn_core = core_reduce(ffn_grads, wide)
    two_partial = (contract_last(gate_grad, w_gate) + contract_last(up_grad, w_up)).astype(BF16)
    both = tree_scatter(
        jnp.concatenate([ffn_partial, two_partial], axis=1).reshape(count, block, 2 * d_model), count
    )
    layer_out = middle[:block] + both[:, :d_model]
    own_two_grad = both[:, d_model:]
    own_scaled_two = scaled_two[:block]
    own_inverse_two = inverse_two[:block]

    middle_grad = cotangent.astype(F32) + normalize_back(
        own_two_grad, own_scaled_two, own_inverse_two, gain_two
    )
    ffn_x = x_reduce(ffn_core, wide)
    branch_grad = jnp.concatenate(tree_gather(middle_grad.astype(BF16), count), axis=0)
    ffn_rows = x_gather(z_gather(z_reduce(ffn_x, wide), wide), wide)

    attended_grad = contract_last(branch_grad, w_out).astype(BF16).reshape(head_shape)
    prob_grad = jnp.einsum(
        "qhd,khd->hqk", attended_grad, value_rows, preferred_element_type=F32
    )
    score_grad = (
        probs * (prob_grad - jnp.sum(probs * prob_grad, axis=-1, keepdims=True))
    ).astype(BF16)
    query_grad = score_scale * jnp.einsum(
        "hqk,khd->qhd", score_grad, key_rows, preferred_element_type=F32
    )
    key_grad = score_scale * jnp.einsum(
        "hqk,qhd->khd", score_grad, queries, preferred_element_type=F32
    )
    value_grad = jnp.einsum(
        "hqk,qhd->khd", probs_low, attended_grad, preferred_element_type=F32
    ).astype(BF16).reshape(length, -1)
    query_grad = unrotate(query_grad, cosine_table, sine_table).astype(BF16).reshape(length, -1)
    key_grad = unrotate(key_grad, cosine_table, sine_table).astype(BF16).reshape(length, -1)
    projection_grads = jnp.concatenate([query_grad, key_grad, value_grad], axis=1)
    projections = w_query.shape[1]
    qkv_grads = contract_first(normed_one, projection_grads).astype(BF16)
    attn_grads = jnp.concatenate(
        [qkv_grads, contract_first(branch_grad, attended).astype(BF16)], axis=1
    )
    attn_total = wide_allreduce(attn_grads, wide)
    one_float = contract_last(
        projection_grads, jnp.concatenate([w_query, w_key, w_value], axis=1)
    )
    norm_one = jnp.stack(
        [jnp.sum(one_float * scaled_one, axis=0), jnp.sum(one_float, axis=0)]
    )
    norm_two = jnp.stack(
        [jnp.sum(own_two_grad * own_scaled_two, axis=0), jnp.sum(own_two_grad, axis=0)]
    )
    norm_parts = jnp.concatenate([norm_one, norm_two], axis=0)
    high, low = split_hi_lo(norm_parts)
    extra = jnp.concatenate([high, low, jnp.zeros((8, d_model), BF16)], axis=0)
    one_blocks = one_float.astype(BF16).reshape(count, block, d_model)
    payload = jnp.concatenate(
        [one_blocks, jnp.broadcast_to(extra[None], (count,) + extra.shape)], axis=1
    )
    summed = tree_scatter(payload, count)
    ffn_total = core_gather(ffn_rows, wide).astype(F32)
    own_one_grad = summed[:block]
    norm_narrow = summed[block : block + 4] + summed[block + 4 : block + 8]
    norm_total = wide_allreduce_small(norm_narrow, wide)
    input_grad = middle_grad + normalize_back(
        own_one_grad, own_scaled_one, own_inverse_one, gain_one
    )
    ff_cols = w_gate.shape[1]
    return (
        layer_out,
        input_grad,
        attn_total[:, :projections],
        attn_total[:, projections : 2 * projections],
        attn_total[:, 2 * projections : 3 * projections],
        attn_total[:, 3 * projections :].T,
        ffn_total[:d_model, :ff_cols],
        ffn_total[:d_model, ff_cols:],
        ffn_total[d_model:],
        norm_total[0],
        norm_total[1],
        norm_total[2],
        norm_total[3],
    )


def solution(mesh):
    placed = (
        P(("wide", "narrow"), None),
        P(("wide", "narrow"), None),
        P("wide", None),
        P(None, "narrow"),
        P(None, "narrow"),
        P(None, "narrow"),
        P("narrow", None),
        P(None, "narrow"),
        P(None, "narrow"),
        P("narrow", None),
        P(),
        P(),
        P(),
        P(),
    )
    return jax.shard_map(
        per_device,
        mesh=mesh,
        in_specs=placed,
        out_specs=(
            P(("wide", "narrow"), None),
            P(("wide", "narrow"), None),
            P(None, "narrow"),
            P(None, "narrow"),
            P(None, "narrow"),
            P("narrow", None),
            P(None, "narrow"),
            P(None, "narrow"),
            P("narrow", None),
            P(),
            P(),
            P(),
            P(),
        ),
        check_vma=False,
    )
```

```python
import math

import jax
import jax.numpy as jnp
from jax import lax
from jax.sharding import PartitionSpec as P

HD = 64
EPS = 1e-05
MASKED = -1e30
F32 = jnp.float32
BF16 = jnp.bfloat16


def normalize(values, gain_vec, bias_vec):
    centred = values - jnp.mean(values, axis=-1, keepdims=True)
    inverse = lax.rsqrt(jnp.mean(centred * centred, axis=-1, keepdims=True) + EPS)
    scaled = centred * inverse
    return (scaled * gain_vec + bias_vec, scaled, inverse)


def normalize_back(grad_in, scaled, inverse, gain_vec):
    along = grad_in * gain_vec
    return inverse * (
        along
        - jnp.mean(along, axis=-1, keepdims=True)
        - scaled * jnp.mean(along * scaled, axis=-1, keepdims=True)
    )


def contract_last(left_side, right_side):
    return lax.dot_general(
        left_side, right_side, (((1,), (1,)), ((), ())), preferred_element_type=F32
    )


def contract_first(left_side, right_side):
    return lax.dot_general(
        left_side, right_side, (((0,), (0,)), ((), ())), preferred_element_type=F32
    )


def rotate(values, cosine_table, sine_table):
    half_width = values.shape[-1] // 2
    first_half = values[..., :half_width]
    second_half = values[..., half_width:]
    cosine = cosine_table[:, None, :]
    sine_part = sine_table[:, None, :]
    return jnp.concatenate(
        [
            first_half * cosine - second_half * sine_part,
            second_half * cosine + first_half * sine_part,
        ],
        axis=-1,
    )


def unrotate(values, cosine_table, sine_table):
    half_width = values.shape[-1] // 2
    first_half = values[..., :half_width]
    second_half = values[..., half_width:]
    cosine = cosine_table[:, None, :]
    sine_part = sine_table[:, None, :]
    return jnp.concatenate(
        [
            first_half * cosine + second_half * sine_part,
            second_half * cosine - first_half * sine_part,
        ],
        axis=-1,
    )


def narrow_gather(own, count):
    slots = jnp.broadcast_to(own[None], (count,) + own.shape)
    got = lax.all_to_all(slots, "narrow", 0, 0, tiled=False)
    return got.reshape(count * own.shape[0], own.shape[1])


def narrow_scatter(partial, count):
    blocks = partial.reshape(count, partial.shape[0] // count, partial.shape[1])
    got = lax.all_to_all(blocks, "narrow", 0, 0, tiled=False)
    return jnp.sum(got.astype(F32), axis=0)


def narrow_gather_async(own, count):
    index = lax.axis_index("narrow")
    rows = own.shape[0]
    whole = jnp.zeros((count * rows, own.shape[1]), own.dtype)
    whole = lax.dynamic_update_slice_in_dim(whole, own, index * rows, 0)
    for k in range(1, count):
        got = lax.ppermute(own, "narrow", [((i + k) % count, i) for i in range(count)])
        whole = lax.dynamic_update_slice_in_dim(whole, got, ((index + k) % count) * rows, 0)
    return whole


def split_hi_lo(values):
    high = values.astype(BF16)
    return high, (values - high.astype(F32)).astype(BF16)


def narrow_maps(count):
    plane = count // 2

    def build(mapping):
        return [(z * plane + y, mapping(z, y)) for z in range(2) for y in range(plane)]

    up = build(lambda z, y: z * plane + (y + 1) % plane)
    down = build(lambda z, y: z * plane + (y - 1) % plane)
    across = build(lambda z, y: (1 - z) * plane + y)
    return up, down, across


def tree_gather(own, count):
    up, down, across = narrow_maps(count)
    from_below = lax.ppermute(own, "narrow", up)
    from_above = lax.ppermute(own, "narrow", down)
    from_across = lax.ppermute(own, "narrow", across)
    two_above = lax.ppermute(from_below, "narrow", up)
    across_above = lax.ppermute(from_across, "narrow", down)
    across_below = lax.ppermute(from_below, "narrow", across)
    across_two = lax.ppermute(two_above, "narrow", across)
    return [own, from_below, from_above, from_across, two_above, across_above, across_below, across_two]


def tree_scatter(blocks, count):
    up, down, across = narrow_maps(count)

    def send(value, pairs):
        return lax.ppermute(value.astype(BF16), "narrow", pairs).astype(F32)

    part = [blocks[s].astype(F32) for s in range(count)]
    first = send(part[7], across)
    below = send(part[4] + first, down)
    side = send(part[6], across)
    over = send(part[5], up)
    total = part[0] + send(part[1] + below + side, down)
    total = total + send(part[3] + over, across)
    return total + send(part[2], up)


def slot_sources(count):
    plane = count // 2
    index = lax.axis_index("narrow")
    z, y = index // plane, index % plane
    dz = jnp.array([0, 0, 0, 1, 0, 1, 1, 1], jnp.int32)
    dy = jnp.array([0, -1, 1, 0, 2, 1, -1, 2], jnp.int32)
    return ((z + dz) % 2) * plane + (y + dy) % plane


def source_slots(count):
    plane = count // 2
    index = lax.axis_index("narrow")
    z, y = index // plane, index % plane
    block = jnp.arange(count)
    dz = (block // plane - z) % 2
    dy = (block % plane - y) % plane
    same = jnp.array([0, 2, 4, 1], jnp.int32)
    other = jnp.array([3, 5, 7, 6], jnp.int32)
    return jnp.where(dz == 0, same[dy], other[dy])


def wide_layout(wide):
    chips_x = wide // 4
    w = lax.axis_index("wide")
    return chips_x, w % 2, (w // 2) % chips_x, w // (2 * chips_x)


def wide_map(wide, dcore=0, dx=0, dz=0, flip_core=False, xor_x=0):
    chips_x = wide // 4
    pairs = []
    for v in range(wide):
        c, xx, zz = v % 2, (v // 2) % chips_x, v // (2 * chips_x)
        c2 = (1 - c) if flip_core else c
        x2 = ((xx ^ xor_x) + dx) % chips_x
        z2 = (zz + dz) % 2
        pairs.append((v, z2 * 2 * chips_x + x2 * 2 + c2))
    return pairs


def tie(value, anchor):
    return lax.optimization_barrier((value, anchor))[0]


def core_reduce(grad, wide):
    _, core, _, _ = wide_layout(wide)
    half = grad.shape[0] // 2
    keep = lax.dynamic_slice_in_dim(grad, core * half, half, 0)
    send = lax.dynamic_slice_in_dim(grad, (1 - core) * half, half, 0)
    return keep.astype(F32) + lax.ppermute(send, "wide", wide_map(wide, flip_core=True)).astype(F32)


def x_reduce(summed, wide):
    chips_x, _, xpos, _ = wide_layout(wide)
    quarter = summed.shape[0] // chips_x
    acc = lax.dynamic_slice_in_dim(summed, xpos * quarter, quarter, 0)
    for k in range(1, chips_x):
        piece = lax.dynamic_slice_in_dim(summed, ((xpos + k) % chips_x) * quarter, quarter, 0)
        acc = acc + lax.ppermute(piece.astype(BF16), "wide", wide_map(wide, dx=k)).astype(F32)
    return acc


def z_reduce(acc, wide):
    _, _, _, zhi = wide_layout(wide)
    eighth = acc.shape[0] // 2
    mine = lax.dynamic_slice_in_dim(acc, zhi * eighth, eighth, 0)
    other = lax.dynamic_slice_in_dim(acc, (1 - zhi) * eighth, eighth, 0)
    got = lax.ppermute(other.astype(BF16), "wide", wide_map(wide, dz=1)).astype(F32)
    return (mine + got).astype(BF16)


def z_gather(final, wide):
    return jnp.concatenate([final, lax.ppermute(final, "wide", wide_map(wide, dz=1))], axis=0)


def x_gather(part, wide):
    chips_x = wide // 4
    pieces = [part]
    for k in range(1, chips_x):
        pieces.append(lax.ppermute(part, "wide", wide_map(wide, dx=chips_x - k)))
    return jnp.concatenate(pieces, axis=0)


def core_gather(halfrows, wide):
    partner = lax.ppermute(halfrows, "wide", wide_map(wide, flip_core=True))
    return jnp.concatenate([halfrows, partner], axis=0)


def unrotate_rows(rotated, wide):
    chips_x, core, xpos, zhi = wide_layout(wide)
    count = 4 * chips_x
    block = jnp.arange(count)
    half, quarter, eighth = block // (2 * chips_x), (block // 2) % chips_x, block % 2
    position = ((half - core) % 2) * (2 * chips_x) + ((quarter - xpos) % chips_x) * 2 + (eighth - zhi) % 2
    rows, cols = rotated.shape
    return jnp.take(rotated.reshape(count, rows // count, cols), position, axis=0).reshape(rows, cols)


def wide_allreduce(grad, wide):
    stage = z_gather(z_reduce(x_reduce(core_reduce(grad, wide), wide), wide), wide)
    return unrotate_rows(core_gather(x_gather(stage, wide), wide), wide).astype(F32)


def wide_allreduce_small(values, wide):
    chips_x = wide // 4
    values = values + lax.ppermute(values, "wide", wide_map(wide, flip_core=True))
    values = values + lax.ppermute(values, "wide", wide_map(wide, xor_x=1))
    if chips_x > 2:
        values = values + lax.ppermute(values, "wide", wide_map(wide, xor_x=2))
    return values + lax.ppermute(values, "wide", wide_map(wide, dz=1))


def per_device(
    tokens,
    cotangent,
    segments,
    w_query,
    w_key,
    w_value,
    w_out,
    w_gate,
    w_up,
    w_down,
    gain_one,
    bias_one,
    gain_two,
    bias_two,
):
    count = lax.axis_size("narrow")
    wide = lax.axis_size("wide")
    block, d_model = tokens.shape
    narrow_index = lax.axis_index("narrow")
    own_rows = narrow_index * block

    seg = segments[0]
    length = seg.shape[0]
    column = lax.broadcasted_iota(jnp.int32, (length, length), 1)
    same_orig = seg[:, None] == seg[None, :]
    first_index = jnp.min(jnp.where(same_orig, column, length), axis=-1)
    position = jnp.arange(length, dtype=jnp.int32) - first_index
    order = slot_sources(count)
    seg = jnp.take(seg.reshape(count, block), order, axis=0).reshape(length)
    position = jnp.take(position.reshape(count, block), order, axis=0).reshape(length)
    same_segment = seg[:, None] == seg[None, :]
    inverse = 10000.0 ** (-(2.0 * jnp.arange(HD // 2).astype(F32) / HD))
    angles = position.astype(F32)[:, None] * inverse
    cosine_table, sine_table = jnp.cos(angles), jnp.sin(angles)

    head_rows = w_out.shape[0]
    first = tree_gather(jnp.concatenate([tokens, cotangent, w_out], axis=0), count)
    tok_full = jnp.concatenate([piece[:block] for piece in first], axis=0)
    cot_full = jnp.concatenate([piece[block : 2 * block] for piece in first], axis=0)
    w_out_slots = jnp.stack([piece[2 * block :] for piece in first])

    inputs = tok_full.astype(F32)
    normed_float, scaled_one, inverse_one = normalize(inputs, gain_one, bias_one)
    normed_one = normed_float.astype(BF16)
    own_scaled_one = scaled_one[:block]
    own_inverse_one = inverse_one[:block]

    heads = w_query.shape[1] // HD
    head_shape = (length, heads, HD)
    queries = rotate(
        jnp.dot(normed_one, w_query, preferred_element_type=F32).reshape(head_shape),
        cosine_table,
        sine_table,
    ).astype(BF16)
    key_rows = rotate(
        jnp.dot(normed_one, w_key, preferred_element_type=F32).reshape(head_shape),
        cosine_table,
        sine_table,
    ).astype(BF16)
    value_rows = (
        jnp.dot(normed_one, w_value, preferred_element_type=F32).astype(BF16).reshape(head_shape)
    )
    score_scale = 1.0 / math.sqrt(HD)
    scores = (
        jnp.einsum("qhd,khd->hqk", queries, key_rows, preferred_element_type=F32) * score_scale
    )
    scores = jnp.where(same_segment[None], scores, MASKED)
    row_peak = jnp.max(scores, axis=-1, keepdims=True)
    exponent = jnp.exp(scores - row_peak)
    row_total = jnp.sum(exponent, axis=-1, keepdims=True)
    probs = exponent / row_total
    probs_low = probs.astype(BF16)
    attended = (
        jnp.einsum("hqk,khd->qhd", probs_low, value_rows, preferred_element_type=F32)
        .astype(BF16)
        .reshape(length, -1)
    )

    heads_cols = attended.shape[1]
    attended_orig = jnp.take(
        attended.reshape(count, block, heads_cols), source_slots(count), axis=0
    ).reshape(length, heads_cols)
    attended_all = jnp.take(
        jnp.stack(tree_gather(attended_orig, count)).reshape(count, count, block, heads_cols),
        order,
        axis=1,
    ).reshape(count, length, heads_cols)
    branch = jnp.einsum(
        "jtc,jcd->td", attended_all, w_out_slots, preferred_element_type=F32
    )
    middle = inputs + branch
    normed_two_float, scaled_two, inverse_two = normalize(middle, gain_two, bias_two)
    normed_two = normed_two_float.astype(BF16)

    gate_pre = jnp.dot(normed_two, w_gate, preferred_element_type=F32)
    up_pre = jnp.dot(normed_two, w_up, preferred_element_type=F32)
    sigmoid_gate = jax.nn.sigmoid(gate_pre)
    active = gate_pre * sigmoid_gate
    hidden = (active * up_pre).astype(BF16)
    ffn_partial = jnp.dot(hidden, w_down, preferred_element_type=F32).astype(BF16)

    hidden_grad = contract_last(cot_full, w_down)
    gate_grad = (
        hidden_grad * up_pre * sigmoid_gate * (1.0 + gate_pre * (1.0 - sigmoid_gate))
    ).astype(BF16)
    up_grad = (hidden_grad * active).astype(BF16)
    ffn_grads = jnp.concatenate(
        [
            contract_first(normed_two, jnp.concatenate([gate_grad, up_grad], axis=1)),
            contract_first(hidden, cot_full),
        ],
        axis=0,
    ).astype(BF16)
    ffn_core = core_reduce(ffn_grads, wide)
    two_partial = (contract_last(gate_grad, w_gate) + contract_last(up_grad, w_up)).astype(BF16)
    both = tree_scatter(
        jnp.concatenate([ffn_partial, two_partial], axis=1).reshape(count, block, 2 * d_model), count
    )
    layer_out = middle[:block] + both[:, :d_model]
    own_two_grad = both[:, d_model:]
    own_scaled_two = scaled_two[:block]
    own_inverse_two = inverse_two[:block]

    middle_grad = cotangent.astype(F32) + normalize_back(
        own_two_grad, own_scaled_two, own_inverse_two, gain_two
    )
    ffn_x = x_reduce(ffn_core, wide)
    branch_grad = jnp.concatenate(tree_gather(middle_grad.astype(BF16), count), axis=0)
    ffn_rows = x_gather(z_gather(z_reduce(ffn_x, wide), wide), wide)

    attended_grad = contract_last(branch_grad, w_out).astype(BF16).reshape(head_shape)
    prob_grad = jnp.einsum(
        "qhd,khd->hqk", attended_grad, value_rows, preferred_element_type=F32
    )
    score_grad = (
        probs * (prob_grad - jnp.sum(probs * prob_grad, axis=-1, keepdims=True))
    ).astype(BF16)
    query_grad = score_scale * jnp.einsum(
        "hqk,khd->qhd", score_grad, key_rows, preferred_element_type=F32
    )
    key_grad = score_scale * jnp.einsum(
        "hqk,qhd->khd", score_grad, queries, preferred_element_type=F32
    )
    value_grad = jnp.einsum(
        "hqk,qhd->khd", probs_low, attended_grad, preferred_element_type=F32
    ).astype(BF16).reshape(length, -1)
    query_grad = unrotate(query_grad, cosine_table, sine_table).astype(BF16).reshape(length, -1)
    key_grad = unrotate(key_grad, cosine_table, sine_table).astype(BF16).reshape(length, -1)
    projection_grads = jnp.concatenate([query_grad, key_grad, value_grad], axis=1)
    projections = w_query.shape[1]
    qkv_grads = contract_first(normed_one, projection_grads).astype(BF16)
    attn_grads = jnp.concatenate(
        [qkv_grads, contract_first(branch_grad, attended).astype(BF16)], axis=1
    )
    attn_total = wide_allreduce(attn_grads, wide)
    one_float = contract_last(
        projection_grads, jnp.concatenate([w_query, w_key, w_value], axis=1)
    )
    norm_one = jnp.stack(
        [jnp.sum(one_float * scaled_one, axis=0), jnp.sum(one_float, axis=0)]
    )
    norm_two = jnp.stack(
        [jnp.sum(own_two_grad * own_scaled_two, axis=0), jnp.sum(own_two_grad, axis=0)]
    )
    norm_parts = jnp.concatenate([norm_one, norm_two], axis=0)
    high, low = split_hi_lo(norm_parts)
    extra = jnp.concatenate([high, low, jnp.zeros((8, d_model), BF16)], axis=0)
    one_blocks = one_float.astype(BF16).reshape(count, block, d_model)
    payload = jnp.concatenate(
        [one_blocks, jnp.broadcast_to(extra[None], (count,) + extra.shape)], axis=1
    )
    summed = tree_scatter(payload, count)
    ffn_total = unrotate_rows(core_gather(ffn_rows, wide), wide).astype(F32)
    own_one_grad = summed[:block]
    norm_narrow = summed[block : block + 4] + summed[block + 4 : block + 8]
    norm_total = wide_allreduce_small(norm_narrow, wide)
    input_grad = middle_grad + normalize_back(
        own_one_grad, own_scaled_one, own_inverse_one, gain_one
    )
    ff_cols = w_gate.shape[1]
    return (
        layer_out,
        input_grad,
        attn_total[:, :projections],
        attn_total[:, projections : 2 * projections],
        attn_total[:, 2 * projections : 3 * projections],
        attn_total[:, 3 * projections :].T,
        ffn_total[:d_model, :ff_cols],
        ffn_total[:d_model, ff_cols:],
        ffn_total[d_model:],
        norm_total[0],
        norm_total[1],
        norm_total[2],
        norm_total[3],
    )


def solution(mesh):
    placed = (
        P(("wide", "narrow"), None),
        P(("wide", "narrow"), None),
        P("wide", None),
        P(None, "narrow"),
        P(None, "narrow"),
        P(None, "narrow"),
        P("narrow", None),
        P(None, "narrow"),
        P(None, "narrow"),
        P("narrow", None),
        P(),
        P(),
        P(),
        P(),
    )
    return jax.shard_map(
        per_device,
        mesh=mesh,
        in_specs=placed,
        out_specs=(
            P(("wide", "narrow"), None),
            P(("wide", "narrow"), None),
            P(None, "narrow"),
            P(None, "narrow"),
            P(None, "narrow"),
            P("narrow", None),
            P(None, "narrow"),
            P(None, "narrow"),
            P("narrow", None),
            P(),
            P(),
            P(),
            P(),
        ),
        check_vma=False,
    )
```

```python
import math

import jax
import jax.numpy as jnp
from jax import lax
from jax.experimental import pallas as pl
from jax.sharding import PartitionSpec as P

HD = 64
EPS = 1e-05
MASKED = -1e30
F32 = jnp.float32
BF16 = jnp.bfloat16


def normalize(values, gain_vec, bias_vec):
    centred = values - jnp.mean(values, axis=-1, keepdims=True)
    inverse = lax.rsqrt(jnp.mean(centred * centred, axis=-1, keepdims=True) + EPS)
    scaled = centred * inverse
    return (scaled * gain_vec + bias_vec, scaled, inverse)


def normalize_back(grad_in, scaled, inverse, gain_vec):
    along = grad_in * gain_vec
    return inverse * (
        along
        - jnp.mean(along, axis=-1, keepdims=True)
        - scaled * jnp.mean(along * scaled, axis=-1, keepdims=True)
    )


def contract_last(left_side, right_side):
    return lax.dot_general(
        left_side, right_side, (((1,), (1,)), ((), ())), preferred_element_type=F32
    )


def contract_first(left_side, right_side):
    return lax.dot_general(
        left_side, right_side, (((0,), (0,)), ((), ())), preferred_element_type=F32
    )


def rotate(values, cosine_table, sine_table):
    half_width = values.shape[-1] // 2
    first_half = values[..., :half_width]
    second_half = values[..., half_width:]
    cosine = cosine_table[:, None, :]
    sine_part = sine_table[:, None, :]
    return jnp.concatenate(
        [
            first_half * cosine - second_half * sine_part,
            second_half * cosine + first_half * sine_part,
        ],
        axis=-1,
    )


def unrotate(values, cosine_table, sine_table):
    half_width = values.shape[-1] // 2
    first_half = values[..., :half_width]
    second_half = values[..., half_width:]
    cosine = cosine_table[:, None, :]
    sine_part = sine_table[:, None, :]
    return jnp.concatenate(
        [
            first_half * cosine + second_half * sine_part,
            second_half * cosine - first_half * sine_part,
        ],
        axis=-1,
    )


def _probs(q, k, same, scale):
    s = lax.dot_general(q, k, (((1,), (1,)), ((), ())), preferred_element_type=F32) * scale
    s = jnp.where(same, s, MASKED)
    e = jnp.exp(s - jnp.max(s, axis=1, keepdims=True))
    return e / jnp.sum(e, axis=1, keepdims=True)

def attn_fwd_kernel(q_ref, k_ref, v_ref, sq_ref, sk_ref, o_ref):
    same = sq_ref[...] == sk_ref[...]
    scale = 1.0 / math.sqrt(HD)
    for h in range(q_ref.shape[1] // HD):
        cols = slice(h * HD, (h + 1) * HD)
        p = _probs(q_ref[:, cols], k_ref[:, cols], same, scale).astype(BF16)
        o_ref[:, cols] = jnp.dot(p, v_ref[:, cols], preferred_element_type=F32).astype(BF16)

def attn_bwd_kernel(q_ref, k_ref, v_ref, g_ref, sq_ref, sk_ref, dq_ref, dk_ref, dv_ref):
    same = sq_ref[...] == sk_ref[...]
    scale = 1.0 / math.sqrt(HD)
    for h in range(q_ref.shape[1] // HD):
        cols = slice(h * HD, (h + 1) * HD)
        q, k, g = q_ref[:, cols], k_ref[:, cols], g_ref[:, cols]
        p = _probs(q, k, same, scale)
        dp = lax.dot_general(g, v_ref[:, cols], (((1,), (1,)), ((), ())), preferred_element_type=F32)
        ds = (p * (dp - jnp.sum(p * dp, axis=1, keepdims=True))).astype(BF16)
        dq_ref[:, cols] = scale * jnp.dot(ds, k, preferred_element_type=F32)
        dk_ref[:, cols] = scale * lax.dot_general(ds, q, (((0,), (0,)), ((), ())), preferred_element_type=F32)
        dv_ref[:, cols] = lax.dot_general(p.astype(BF16), g, (((0,), (0,)), ((), ())), preferred_element_type=F32).astype(BF16)

def attn_fwd(q, k, v, seg):
    n, c = q.shape
    return pl.pallas_call(
        attn_fwd_kernel,
        out_shape=jax.ShapeDtypeStruct((n, c), BF16),
        cost_estimate=pl.CostEstimate(
            flops=4 * n * n * c, transcendentals=n * n * c // HD, bytes_accessed=8 * n * c
        ),
    )(q, k, v, seg.reshape(n, 1), seg.reshape(1, n))

def attn_bwd(q, k, v, g, seg):
    n, c = q.shape
    return pl.pallas_call(
        attn_bwd_kernel,
        out_shape=(
            jax.ShapeDtypeStruct((n, c), F32),
            jax.ShapeDtypeStruct((n, c), F32),
            jax.ShapeDtypeStruct((n, c), BF16),
        ),
        cost_estimate=pl.CostEstimate(
            flops=12 * n * n * c, transcendentals=n * n * c // HD, bytes_accessed=20 * n * c
        ),
    )(q, k, v, g, seg.reshape(n, 1), seg.reshape(1, n))


def narrow_gather(own, count):
    slots = jnp.broadcast_to(own[None], (count,) + own.shape)
    got = lax.all_to_all(slots, "narrow", 0, 0, tiled=False)
    return got.reshape(count * own.shape[0], own.shape[1])


def narrow_scatter(partial, count):
    blocks = partial.reshape(count, partial.shape[0] // count, partial.shape[1])
    got = lax.all_to_all(blocks, "narrow", 0, 0, tiled=False)
    return jnp.sum(got.astype(F32), axis=0)


def narrow_gather_async(own, count):
    index = lax.axis_index("narrow")
    rows = own.shape[0]
    whole = jnp.zeros((count * rows, own.shape[1]), own.dtype)
    whole = lax.dynamic_update_slice_in_dim(whole, own, index * rows, 0)
    for k in range(1, count):
        got = lax.ppermute(own, "narrow", [((i + k) % count, i) for i in range(count)])
        whole = lax.dynamic_update_slice_in_dim(whole, got, ((index + k) % count) * rows, 0)
    return whole


def split_hi_lo(values):
    high = values.astype(BF16)
    return high, (values - high.astype(F32)).astype(BF16)


def narrow_maps(count):
    plane = count // 2

    def build(mapping):
        return [(z * plane + y, mapping(z, y)) for z in range(2) for y in range(plane)]

    up = build(lambda z, y: z * plane + (y + 1) % plane)
    down = build(lambda z, y: z * plane + (y - 1) % plane)
    across = build(lambda z, y: (1 - z) * plane + y)
    return up, down, across


def tree_gather(own, count):
    up, down, across = narrow_maps(count)
    from_below = lax.ppermute(own, "narrow", up)
    from_above = lax.ppermute(own, "narrow", down)
    from_across = lax.ppermute(own, "narrow", across)
    two_above = lax.ppermute(from_below, "narrow", up)
    across_above = lax.ppermute(from_across, "narrow", down)
    across_below = lax.ppermute(from_below, "narrow", across)
    across_two = lax.ppermute(two_above, "narrow", across)
    return [own, from_below, from_above, from_across, two_above, across_above, across_below, across_two]


def tree_scatter(blocks, count):
    up, down, across = narrow_maps(count)

    def send(value, pairs):
        return lax.ppermute(value.astype(BF16), "narrow", pairs).astype(F32)

    part = [blocks[s].astype(F32) for s in range(count)]
    first = send(part[7], across)
    below = send(part[4] + first, down)
    side = send(part[6], across)
    over = send(part[5], up)
    total = part[0] + send(part[1] + below + side, down)
    total = total + send(part[3] + over, across)
    return total + send(part[2], up)


def slot_sources(count):
    plane = count // 2
    index = lax.axis_index("narrow")
    z, y = index // plane, index % plane
    dz = jnp.array([0, 0, 0, 1, 0, 1, 1, 1], jnp.int32)
    dy = jnp.array([0, -1, 1, 0, 2, 1, -1, 2], jnp.int32)
    return ((z + dz) % 2) * plane + (y + dy) % plane


def source_slots(count):
    plane = count // 2
    index = lax.axis_index("narrow")
    z, y = index // plane, index % plane
    block = jnp.arange(count)
    dz = (block // plane - z) % 2
    dy = (block % plane - y) % plane
    same = jnp.array([0, 2, 4, 1], jnp.int32)
    other = jnp.array([3, 5, 7, 6], jnp.int32)
    return jnp.where(dz == 0, same[dy], other[dy])


def wide_layout(wide):
    chips_x = wide // 4
    w = lax.axis_index("wide")
    return chips_x, w % 2, (w // 2) % chips_x, w // (2 * chips_x)


def wide_map(wide, dcore=0, dx=0, dz=0, flip_core=False, xor_x=0):
    chips_x = wide // 4
    pairs = []
    for v in range(wide):
        c, xx, zz = v % 2, (v // 2) % chips_x, v // (2 * chips_x)
        c2 = (1 - c) if flip_core else c
        x2 = ((xx ^ xor_x) + dx) % chips_x
        z2 = (zz + dz) % 2
        pairs.append((v, z2 * 2 * chips_x + x2 * 2 + c2))
    return pairs


def tie(value, anchor):
    return lax.optimization_barrier((value, anchor))[0]


def core_reduce(grad, wide):
    _, core, _, _ = wide_layout(wide)
    half = grad.shape[0] // 2
    keep = lax.dynamic_slice_in_dim(grad, core * half, half, 0)
    send = lax.dynamic_slice_in_dim(grad, (1 - core) * half, half, 0)
    return keep.astype(F32) + lax.ppermute(send, "wide", wide_map(wide, flip_core=True)).astype(F32)


def x_reduce(summed, wide):
    chips_x, _, xpos, _ = wide_layout(wide)
    quarter = summed.shape[0] // chips_x
    acc = lax.dynamic_slice_in_dim(summed, xpos * quarter, quarter, 0)
    for k in range(1, chips_x):
        piece = lax.dynamic_slice_in_dim(summed, ((xpos + k) % chips_x) * quarter, quarter, 0)
        acc = acc + lax.ppermute(piece.astype(BF16), "wide", wide_map(wide, dx=k)).astype(F32)
    return acc


def z_reduce(acc, wide):
    _, _, _, zhi = wide_layout(wide)
    eighth = acc.shape[0] // 2
    mine = lax.dynamic_slice_in_dim(acc, zhi * eighth, eighth, 0)
    other = lax.dynamic_slice_in_dim(acc, (1 - zhi) * eighth, eighth, 0)
    got = lax.ppermute(other.astype(BF16), "wide", wide_map(wide, dz=1)).astype(F32)
    return (mine + got).astype(BF16)


def z_gather(final, wide):
    return jnp.concatenate([final, lax.ppermute(final, "wide", wide_map(wide, dz=1))], axis=0)


def x_gather(part, wide):
    chips_x = wide // 4
    pieces = [part]
    for k in range(1, chips_x):
        pieces.append(lax.ppermute(part, "wide", wide_map(wide, dx=chips_x - k)))
    return jnp.concatenate(pieces, axis=0)


def core_gather(halfrows, wide):
    partner = lax.ppermute(halfrows, "wide", wide_map(wide, flip_core=True))
    return jnp.concatenate([halfrows, partner], axis=0)


def unrotate_rows(rotated, wide):
    chips_x, core, xpos, zhi = wide_layout(wide)
    count = 4 * chips_x
    block = jnp.arange(count)
    half, quarter, eighth = block // (2 * chips_x), (block // 2) % chips_x, block % 2
    position = ((half - core) % 2) * (2 * chips_x) + ((quarter - xpos) % chips_x) * 2 + (eighth - zhi) % 2
    rows, cols = rotated.shape
    return jnp.take(rotated.reshape(count, rows // count, cols), position, axis=0).reshape(rows, cols)


def wide_allreduce(grad, wide):
    stage = z_gather(z_reduce(x_reduce(core_reduce(grad, wide), wide), wide), wide)
    return unrotate_rows(core_gather(x_gather(stage, wide), wide), wide).astype(F32)


def wide_allreduce_small(values, wide):
    chips_x = wide // 4
    values = values + lax.ppermute(values, "wide", wide_map(wide, flip_core=True))
    values = values + lax.ppermute(values, "wide", wide_map(wide, xor_x=1))
    if chips_x > 2:
        values = values + lax.ppermute(values, "wide", wide_map(wide, xor_x=2))
    return values + lax.ppermute(values, "wide", wide_map(wide, dz=1))


def per_device(
    tokens,
    cotangent,
    segments,
    w_query,
    w_key,
    w_value,
    w_out,
    w_gate,
    w_up,
    w_down,
    gain_one,
    bias_one,
    gain_two,
    bias_two,
):
    count = lax.axis_size("narrow")
    wide = lax.axis_size("wide")
    block, d_model = tokens.shape
    narrow_index = lax.axis_index("narrow")
    own_rows = narrow_index * block

    seg = segments[0]
    length = seg.shape[0]
    column = lax.broadcasted_iota(jnp.int32, (length, length), 1)
    same_orig = seg[:, None] == seg[None, :]
    first_index = jnp.min(jnp.where(same_orig, column, length), axis=-1)
    position = jnp.arange(length, dtype=jnp.int32) - first_index
    order = slot_sources(count)
    seg = jnp.take(seg.reshape(count, block), order, axis=0).reshape(length)
    position = jnp.take(position.reshape(count, block), order, axis=0).reshape(length)
    same_segment = seg[:, None] == seg[None, :]
    inverse = 10000.0 ** (-(2.0 * jnp.arange(HD // 2).astype(F32) / HD))
    angles = position.astype(F32)[:, None] * inverse
    cosine_table, sine_table = jnp.cos(angles), jnp.sin(angles)

    head_rows = w_out.shape[0]
    first = tree_gather(jnp.concatenate([tokens, cotangent, w_out], axis=0), count)
    tok_full = jnp.concatenate([piece[:block] for piece in first], axis=0)
    cot_full = jnp.concatenate([piece[block : 2 * block] for piece in first], axis=0)
    w_out_slots = jnp.stack([piece[2 * block :] for piece in first])

    inputs = tok_full.astype(F32)
    normed_float, scaled_one, inverse_one = normalize(inputs, gain_one, bias_one)
    normed_one = normed_float.astype(BF16)
    own_scaled_one = scaled_one[:block]
    own_inverse_one = inverse_one[:block]

    heads = w_query.shape[1] // HD
    head_shape = (length, heads, HD)
    queries = rotate(
        jnp.dot(normed_one, w_query, preferred_element_type=F32).reshape(head_shape),
        cosine_table,
        sine_table,
    ).astype(BF16)
    key_rows = rotate(
        jnp.dot(normed_one, w_key, preferred_element_type=F32).reshape(head_shape),
        cosine_table,
        sine_table,
    ).astype(BF16)
    value_rows = (
        jnp.dot(normed_one, w_value, preferred_element_type=F32).astype(BF16).reshape(head_shape)
    )
    flat = (length, heads * HD)
    query_flat = queries.reshape(flat)
    key_flat = key_rows.reshape(flat)
    value_flat = value_rows.reshape(flat)
    attended = attn_fwd(query_flat, key_flat, value_flat, seg)

    heads_cols = attended.shape[1]
    attended_orig = jnp.take(
        attended.reshape(count, block, heads_cols), source_slots(count), axis=0
    ).reshape(length, heads_cols)
    attended_all = jnp.take(
        jnp.stack(tree_gather(attended_orig, count)).reshape(count, count, block, heads_cols),
        order,
        axis=1,
    ).reshape(count, length, heads_cols)
    branch = jnp.einsum(
        "jtc,jcd->td", attended_all, w_out_slots, preferred_element_type=F32
    )
    middle = inputs + branch
    normed_two_float, scaled_two, inverse_two = normalize(middle, gain_two, bias_two)
    normed_two = normed_two_float.astype(BF16)

    gate_pre = jnp.dot(normed_two, w_gate, preferred_element_type=F32)
    up_pre = jnp.dot(normed_two, w_up, preferred_element_type=F32)
    sigmoid_gate = jax.nn.sigmoid(gate_pre)
    active = gate_pre * sigmoid_gate
    hidden = (active * up_pre).astype(BF16)
    ffn_partial = jnp.dot(hidden, w_down, preferred_element_type=F32).astype(BF16)

    hidden_grad = contract_last(cot_full, w_down)
    gate_grad = (
        hidden_grad * up_pre * sigmoid_gate * (1.0 + gate_pre * (1.0 - sigmoid_gate))
    ).astype(BF16)
    up_grad = (hidden_grad * active).astype(BF16)
    ffn_grads = jnp.concatenate(
        [
            contract_first(normed_two, jnp.concatenate([gate_grad, up_grad], axis=1)),
            contract_first(hidden, cot_full),
        ],
        axis=0,
    ).astype(BF16)
    ffn_core = core_reduce(ffn_grads, wide)
    two_partial = (contract_last(gate_grad, w_gate) + contract_last(up_grad, w_up)).astype(BF16)
    both = tree_scatter(
        jnp.concatenate([ffn_partial, two_partial], axis=1).reshape(count, block, 2 * d_model), count
    )
    layer_out = middle[:block] + both[:, :d_model]
    own_two_grad = both[:, d_model:]
    own_scaled_two = scaled_two[:block]
    own_inverse_two = inverse_two[:block]

    middle_grad = cotangent.astype(F32) + normalize_back(
        own_two_grad, own_scaled_two, own_inverse_two, gain_two
    )
    ffn_x = x_reduce(ffn_core, wide)
    branch_grad = jnp.concatenate(tree_gather(middle_grad.astype(BF16), count), axis=0)
    ffn_rows = x_gather(z_gather(z_reduce(ffn_x, wide), wide), wide)

    attended_grad = contract_last(branch_grad, w_out).astype(BF16)
    query_grad, key_grad, value_grad = attn_bwd(query_flat, key_flat, value_flat, attended_grad, seg)
    query_grad = unrotate(query_grad.reshape(head_shape), cosine_table, sine_table)
    key_grad = unrotate(key_grad.reshape(head_shape), cosine_table, sine_table)
    query_grad = query_grad.astype(BF16).reshape(flat)
    key_grad = key_grad.astype(BF16).reshape(flat)
    projection_grads = jnp.concatenate([query_grad, key_grad, value_grad], axis=1)
    projections = w_query.shape[1]
    qkv_grads = contract_first(normed_one, projection_grads).astype(BF16)
    attn_grads = jnp.concatenate(
        [qkv_grads, contract_first(branch_grad, attended).astype(BF16)], axis=1
    )
    attn_total = wide_allreduce(attn_grads, wide)
    one_float = contract_last(
        projection_grads, jnp.concatenate([w_query, w_key, w_value], axis=1)
    )
    norm_one = jnp.stack(
        [jnp.sum(one_float * scaled_one, axis=0), jnp.sum(one_float, axis=0)]
    )
    norm_two = jnp.stack(
        [jnp.sum(own_two_grad * own_scaled_two, axis=0), jnp.sum(own_two_grad, axis=0)]
    )
    norm_parts = jnp.concatenate([norm_one, norm_two], axis=0)
    high, low = split_hi_lo(norm_parts)
    extra = jnp.concatenate([high, low, jnp.zeros((8, d_model), BF16)], axis=0)
    one_blocks = one_float.astype(BF16).reshape(count, block, d_model)
    payload = jnp.concatenate(
        [one_blocks, jnp.broadcast_to(extra[None], (count,) + extra.shape)], axis=1
    )
    summed = tree_scatter(payload, count)
    ffn_total = unrotate_rows(core_gather(ffn_rows, wide), wide).astype(F32)
    own_one_grad = summed[:block]
    norm_narrow = summed[block : block + 4] + summed[block + 4 : block + 8]
    norm_total = wide_allreduce_small(norm_narrow, wide)
    input_grad = middle_grad + normalize_back(
        own_one_grad, own_scaled_one, own_inverse_one, gain_one
    )
    ff_cols = w_gate.shape[1]
    return (
        layer_out,
        input_grad,
        attn_total[:, :projections],
        attn_total[:, projections : 2 * projections],
        attn_total[:, 2 * projections : 3 * projections],
        attn_total[:, 3 * projections :].T,
        ffn_total[:d_model, :ff_cols],
        ffn_total[:d_model, ff_cols:],
        ffn_total[d_model:],
        norm_total[0],
        norm_total[1],
        norm_total[2],
        norm_total[3],
    )


def solution(mesh):
    placed = (
        P(("wide", "narrow"), None),
        P(("wide", "narrow"), None),
        P("wide", None),
        P(None, "narrow"),
        P(None, "narrow"),
        P(None, "narrow"),
        P("narrow", None),
        P(None, "narrow"),
        P(None, "narrow"),
        P("narrow", None),
        P(),
        P(),
        P(),
        P(),
    )
    return jax.shard_map(
        per_device,
        mesh=mesh,
        in_specs=placed,
        out_specs=(
            P(("wide", "narrow"), None),
            P(("wide", "narrow"), None),
            P(None, "narrow"),
            P(None, "narrow"),
            P(None, "narrow"),
            P("narrow", None),
            P(None, "narrow"),
            P(None, "narrow"),
            P("narrow", None),
            P(),
            P(),
            P(),
            P(),
        ),
        check_vma=False,
    )
```

```python
import math

import jax
import jax.numpy as jnp
from jax import lax
from jax.sharding import PartitionSpec as P

HD = 64
EPS = 1e-05
MASKED = -1e30
F32 = jnp.float32
BF16 = jnp.bfloat16


def normalize(values, gain_vec, bias_vec):
    centred = values - jnp.mean(values, axis=-1, keepdims=True)
    inverse = lax.rsqrt(jnp.mean(centred * centred, axis=-1, keepdims=True) + EPS)
    scaled = centred * inverse
    return (scaled * gain_vec + bias_vec, scaled, inverse)


def normalize_back(grad_in, scaled, inverse, gain_vec):
    along = grad_in * gain_vec
    return inverse * (
        along
        - jnp.mean(along, axis=-1, keepdims=True)
        - scaled * jnp.mean(along * scaled, axis=-1, keepdims=True)
    )


def contract_last(left_side, right_side):
    return lax.dot_general(
        left_side, right_side, (((1,), (1,)), ((), ())), preferred_element_type=F32
    )


def contract_first(left_side, right_side):
    return lax.dot_general(
        left_side, right_side, (((0,), (0,)), ((), ())), preferred_element_type=F32
    )


def rotate(values, cosine_table, sine_table):
    half_width = values.shape[-1] // 2
    first_half = values[..., :half_width]
    second_half = values[..., half_width:]
    cosine = cosine_table[:, None, :]
    sine_part = sine_table[:, None, :]
    return jnp.concatenate(
        [
            first_half * cosine - second_half * sine_part,
            second_half * cosine + first_half * sine_part,
        ],
        axis=-1,
    )


def unrotate(values, cosine_table, sine_table):
    half_width = values.shape[-1] // 2
    first_half = values[..., :half_width]
    second_half = values[..., half_width:]
    cosine = cosine_table[:, None, :]
    sine_part = sine_table[:, None, :]
    return jnp.concatenate(
        [
            first_half * cosine + second_half * sine_part,
            second_half * cosine - first_half * sine_part,
        ],
        axis=-1,
    )


def narrow_gather(own, count):
    slots = jnp.broadcast_to(own[None], (count,) + own.shape)
    got = lax.all_to_all(slots, "narrow", 0, 0, tiled=False)
    return got.reshape(count * own.shape[0], own.shape[1])


def narrow_scatter(partial, count):
    blocks = partial.reshape(count, partial.shape[0] // count, partial.shape[1])
    got = lax.all_to_all(blocks, "narrow", 0, 0, tiled=False)
    return jnp.sum(got.astype(F32), axis=0)


def narrow_gather_async(own, count):
    index = lax.axis_index("narrow")
    rows = own.shape[0]
    whole = jnp.zeros((count * rows, own.shape[1]), own.dtype)
    whole = lax.dynamic_update_slice_in_dim(whole, own, index * rows, 0)
    for k in range(1, count):
        got = lax.ppermute(own, "narrow", [((i + k) % count, i) for i in range(count)])
        whole = lax.dynamic_update_slice_in_dim(whole, got, ((index + k) % count) * rows, 0)
    return whole


def split_hi_lo(values):
    high = values.astype(BF16)
    return high, (values - high.astype(F32)).astype(BF16)


def narrow_maps(count):
    plane = count // 2

    def build(mapping):
        return [(z * plane + y, mapping(z, y)) for z in range(2) for y in range(plane)]

    up = build(lambda z, y: z * plane + (y + 1) % plane)
    down = build(lambda z, y: z * plane + (y - 1) % plane)
    across = build(lambda z, y: (1 - z) * plane + y)
    return up, down, across


def tree_gather(own, count):
    up, down, across = narrow_maps(count)
    from_below = lax.ppermute(own, "narrow", up)
    from_above = lax.ppermute(own, "narrow", down)
    from_across = lax.ppermute(own, "narrow", across)
    two_above = lax.ppermute(from_below, "narrow", up)
    across_above = lax.ppermute(from_across, "narrow", down)
    across_below = lax.ppermute(from_below, "narrow", across)
    across_two = lax.ppermute(two_above, "narrow", across)
    return [own, from_below, from_above, from_across, two_above, across_above, across_below, across_two]


def tree_scatter(blocks, count):
    up, down, across = narrow_maps(count)

    def send(value, pairs):
        return lax.ppermute(value.astype(BF16), "narrow", pairs).astype(F32)

    part = [blocks[s].astype(F32) for s in range(count)]
    first = send(part[7], across)
    below = send(part[4] + first, down)
    side = send(part[6], across)
    over = send(part[5], up)
    total = part[0] + send(part[1] + below + side, down)
    total = total + send(part[3] + over, across)
    return total + send(part[2], up)


def slot_sources(count):
    plane = count // 2
    index = lax.axis_index("narrow")
    z, y = index // plane, index % plane
    dz = jnp.array([0, 0, 0, 1, 0, 1, 1, 1], jnp.int32)
    dy = jnp.array([0, -1, 1, 0, 2, 1, -1, 2], jnp.int32)
    return ((z + dz) % 2) * plane + (y + dy) % plane


def source_slots(count):
    plane = count // 2
    index = lax.axis_index("narrow")
    z, y = index // plane, index % plane
    block = jnp.arange(count)
    dz = (block // plane - z) % 2
    dy = (block % plane - y) % plane
    same = jnp.array([0, 2, 4, 1], jnp.int32)
    other = jnp.array([3, 5, 7, 6], jnp.int32)
    return jnp.where(dz == 0, same[dy], other[dy])


def wide_layout(wide):
    chips_x = wide // 4
    w = lax.axis_index("wide")
    return chips_x, w % 2, (w // 2) % chips_x, w // (2 * chips_x)


def wide_map(wide, dcore=0, dx=0, dz=0, flip_core=False, xor_x=0):
    chips_x = wide // 4
    pairs = []
    for v in range(wide):
        c, xx, zz = v % 2, (v // 2) % chips_x, v // (2 * chips_x)
        c2 = (1 - c) if flip_core else c
        x2 = ((xx ^ xor_x) + dx) % chips_x
        z2 = (zz + dz) % 2
        pairs.append((v, z2 * 2 * chips_x + x2 * 2 + c2))
    return pairs


def tie(value, anchor):
    return lax.optimization_barrier((value, anchor))[0]


def core_reduce(grad, wide):
    _, core, _, _ = wide_layout(wide)
    half = grad.shape[0] // 2
    keep = lax.dynamic_slice_in_dim(grad, core * half, half, 0)
    send = lax.dynamic_slice_in_dim(grad, (1 - core) * half, half, 0)
    return keep.astype(F32) + lax.ppermute(send, "wide", wide_map(wide, flip_core=True)).astype(F32)


def x_reduce(summed, wide):
    chips_x, _, xpos, _ = wide_layout(wide)
    quarter = summed.shape[0] // chips_x
    acc = lax.dynamic_slice_in_dim(summed, xpos * quarter, quarter, 0)
    for k in range(1, chips_x):
        piece = lax.dynamic_slice_in_dim(summed, ((xpos + k) % chips_x) * quarter, quarter, 0)
        acc = acc + lax.ppermute(piece.astype(BF16), "wide", wide_map(wide, dx=k)).astype(F32)
    return acc


def z_reduce(acc, wide):
    _, _, _, zhi = wide_layout(wide)
    eighth = acc.shape[0] // 2
    mine = lax.dynamic_slice_in_dim(acc, zhi * eighth, eighth, 0)
    other = lax.dynamic_slice_in_dim(acc, (1 - zhi) * eighth, eighth, 0)
    got = lax.ppermute(other.astype(BF16), "wide", wide_map(wide, dz=1)).astype(F32)
    return (mine + got).astype(BF16)


def z_gather(final, wide):
    return jnp.concatenate([final, lax.ppermute(final, "wide", wide_map(wide, dz=1))], axis=0)


def x_gather(part, wide):
    chips_x = wide // 4
    pieces = [part]
    for k in range(1, chips_x):
        pieces.append(lax.ppermute(part, "wide", wide_map(wide, dx=chips_x - k)))
    return jnp.concatenate(pieces, axis=0)


def core_gather(halfrows, wide):
    partner = lax.ppermute(halfrows, "wide", wide_map(wide, flip_core=True))
    return jnp.concatenate([halfrows, partner], axis=0)


def unrotate_rows(rotated, wide):
    chips_x, core, xpos, zhi = wide_layout(wide)
    count = 4 * chips_x
    block = jnp.arange(count)
    half, quarter, eighth = block // (2 * chips_x), (block // 2) % chips_x, block % 2
    position = ((half - core) % 2) * (2 * chips_x) + ((quarter - xpos) % chips_x) * 2 + (eighth - zhi) % 2
    rows, cols = rotated.shape
    return jnp.take(rotated.reshape(count, rows // count, cols), position, axis=0).reshape(rows, cols)


def wide_allreduce(grad, wide):
    stage = z_gather(z_reduce(x_reduce(core_reduce(grad, wide), wide), wide), wide)
    return unrotate_rows(core_gather(x_gather(stage, wide), wide), wide).astype(F32)


def wide_allreduce_small(values, wide):
    chips_x = wide // 4
    values = values + lax.ppermute(values, "wide", wide_map(wide, flip_core=True))
    values = values + lax.ppermute(values, "wide", wide_map(wide, xor_x=1))
    if chips_x > 2:
        values = values + lax.ppermute(values, "wide", wide_map(wide, xor_x=2))
    return values + lax.ppermute(values, "wide", wide_map(wide, dz=1))


def per_device(
    tokens,
    cotangent,
    segments,
    w_query,
    w_key,
    w_value,
    w_out,
    w_gate,
    w_up,
    w_down,
    gain_one,
    bias_one,
    gain_two,
    bias_two,
):
    count = lax.axis_size("narrow")
    wide = lax.axis_size("wide")
    block, d_model = tokens.shape
    narrow_index = lax.axis_index("narrow")
    own_rows = narrow_index * block

    seg = segments[0]
    length = seg.shape[0]
    column = lax.broadcasted_iota(jnp.int32, (length, length), 1)
    same_orig = seg[:, None] == seg[None, :]
    first_index = jnp.min(jnp.where(same_orig, column, length), axis=-1)
    position = jnp.arange(length, dtype=jnp.int32) - first_index
    order = slot_sources(count)
    seg = jnp.take(seg.reshape(count, block), order, axis=0).reshape(length)
    position = jnp.take(position.reshape(count, block), order, axis=0).reshape(length)
    same_segment = seg[:, None] == seg[None, :]
    inverse = 10000.0 ** (-(2.0 * jnp.arange(HD // 2).astype(F32) / HD))
    angles = position.astype(F32)[:, None] * inverse
    cosine_table, sine_table = jnp.cos(angles), jnp.sin(angles)

    head_rows = w_out.shape[0]
    first = tree_gather(jnp.concatenate([tokens, cotangent, w_out], axis=0), count)
    tok_full = jnp.concatenate([piece[:block] for piece in first], axis=0)
    cot_full = jnp.concatenate([piece[block : 2 * block] for piece in first], axis=0)
    w_out_slots = jnp.stack([piece[2 * block :] for piece in first])

    inputs = tok_full.astype(F32)
    normed_float, scaled_one, inverse_one = normalize(inputs, gain_one, bias_one)
    normed_one = normed_float.astype(BF16)
    own_scaled_one = scaled_one[:block]
    own_inverse_one = inverse_one[:block]

    heads = w_query.shape[1] // HD
    head_shape = (length, heads, HD)
    queries = rotate(
        jnp.dot(normed_one, w_query, preferred_element_type=F32).reshape(head_shape),
        cosine_table,
        sine_table,
    ).astype(BF16)
    key_rows = rotate(
        jnp.dot(normed_one, w_key, preferred_element_type=F32).reshape(head_shape),
        cosine_table,
        sine_table,
    ).astype(BF16)
    value_rows = (
        jnp.dot(normed_one, w_value, preferred_element_type=F32).astype(BF16).reshape(head_shape)
    )
    score_scale = 1.0 / math.sqrt(HD)
    scores = (
        jnp.einsum("qhd,khd->hqk", queries, key_rows, preferred_element_type=F32) * score_scale
    )
    scores = jnp.where(same_segment[None], scores, MASKED)
    row_peak = jnp.max(scores, axis=-1, keepdims=True)
    exponent = jnp.exp(scores - row_peak)
    row_total = jnp.sum(exponent, axis=-1, keepdims=True)
    probs = exponent / row_total
    probs_low = probs.astype(BF16)
    attended = (
        jnp.einsum("hqk,khd->qhd", probs_low, value_rows, preferred_element_type=F32)
        .astype(BF16)
        .reshape(length, -1)
    )

    heads_cols = attended.shape[1]
    attended_orig = jnp.take(
        attended.reshape(count, block, heads_cols), source_slots(count), axis=0
    ).reshape(length, heads_cols)
    attended_all = jnp.take(
        jnp.stack(tree_gather(attended_orig, count)).reshape(count, count, block, heads_cols),
        order,
        axis=1,
    ).reshape(count, length, heads_cols)
    branch = jnp.einsum(
        "jtc,jcd->td", attended_all, w_out_slots, preferred_element_type=F32
    )
    middle = inputs + branch
    normed_two_float, scaled_two, inverse_two = normalize(middle, gain_two, bias_two)
    normed_two = normed_two_float.astype(BF16)

    gate_pre = jnp.dot(normed_two, w_gate, preferred_element_type=F32)
    up_pre = jnp.dot(normed_two, w_up, preferred_element_type=F32)
    sigmoid_gate = jax.nn.sigmoid(gate_pre)
    active = gate_pre * sigmoid_gate
    hidden = (active * up_pre).astype(BF16)
    ffn_partial = jnp.dot(hidden, w_down, preferred_element_type=F32).astype(BF16)

    hidden_grad = contract_last(cot_full, w_down)
    gate_grad = (
        hidden_grad * up_pre * sigmoid_gate * (1.0 + gate_pre * (1.0 - sigmoid_gate))
    ).astype(BF16)
    up_grad = (hidden_grad * active).astype(BF16)
    ffn_grads = jnp.concatenate(
        [
            contract_first(normed_two, jnp.concatenate([gate_grad, up_grad], axis=1)),
            contract_first(hidden, cot_full),
        ],
        axis=0,
    ).astype(BF16)
    ffn_core = core_reduce(ffn_grads, wide)
    two_partial = (contract_last(gate_grad, w_gate) + contract_last(up_grad, w_up)).astype(BF16)
    both = tree_scatter(
        jnp.concatenate([ffn_partial, two_partial], axis=1).reshape(count, block, 2 * d_model), count
    )
    layer_out = middle[:block] + both[:, :d_model]
    own_two_grad = both[:, d_model:]
    own_scaled_two = scaled_two[:block]
    own_inverse_two = inverse_two[:block]

    middle_grad = cotangent.astype(F32) + normalize_back(
        own_two_grad, own_scaled_two, own_inverse_two, gain_two
    )
    ffn_x = x_reduce(ffn_core, wide)
    branch_grad = jnp.concatenate(tree_gather(middle_grad.astype(BF16), count), axis=0)
    ffn_rows = x_gather(z_gather(z_reduce(ffn_x, wide), wide), wide)

    attended_grad = contract_last(branch_grad, w_out).astype(BF16).reshape(head_shape)
    prob_grad = jnp.einsum(
        "qhd,khd->hqk", attended_grad, value_rows, preferred_element_type=F32
    )
    score_grad = (
        probs * (prob_grad - jnp.sum(probs * prob_grad, axis=-1, keepdims=True))
    ).astype(BF16)
    query_grad = score_scale * jnp.einsum(
        "hqk,khd->qhd", score_grad, key_rows, preferred_element_type=F32
    )
    key_grad = score_scale * jnp.einsum(
        "hqk,qhd->khd", score_grad, queries, preferred_element_type=F32
    )
    value_grad = jnp.einsum(
        "hqk,qhd->khd", probs_low, attended_grad, preferred_element_type=F32
    ).astype(BF16).reshape(length, -1)
    query_grad = unrotate(query_grad, cosine_table, sine_table).astype(BF16).reshape(length, -1)
    key_grad = unrotate(key_grad, cosine_table, sine_table).astype(BF16).reshape(length, -1)
    projection_grads = jnp.concatenate([query_grad, key_grad, value_grad], axis=1)
    projections = w_query.shape[1]
    qkv_grads = contract_first(normed_one, projection_grads).astype(BF16)
    attn_grads = jnp.concatenate(
        [qkv_grads, contract_first(branch_grad, attended).astype(BF16)], axis=1
    )
    attn_total = wide_allreduce(attn_grads, wide)
    one_float = contract_last(
        projection_grads, jnp.concatenate([w_query, w_key, w_value], axis=1)
    )
    norm_one = jnp.stack(
        [jnp.sum(one_float * scaled_one, axis=0), jnp.sum(one_float, axis=0)]
    )
    norm_two = jnp.stack(
        [jnp.sum(own_two_grad * own_scaled_two, axis=0), jnp.sum(own_two_grad, axis=0)]
    )
    norm_parts = jnp.concatenate([norm_one, norm_two], axis=0)
    high, low = split_hi_lo(norm_parts)
    extra = jnp.concatenate([high, low, jnp.zeros((8, d_model), BF16)], axis=0)
    one_blocks = one_float.astype(BF16).reshape(count, block, d_model)
    payload = jnp.concatenate(
        [one_blocks, jnp.broadcast_to(extra[None], (count,) + extra.shape)], axis=1
    )
    ffn_total = unrotate_rows(core_gather(ffn_rows, wide), wide).astype(F32)
    ff_cols = w_gate.shape[1]
    ffn_outputs = (ffn_total[:d_model, :ff_cols], ffn_total[:d_model, ff_cols:], ffn_total[d_model:])
    payload, ffn_outputs = lax.optimization_barrier((payload, ffn_outputs))
    summed = tree_scatter(payload, count)
    own_one_grad = summed[:block]
    norm_narrow = summed[block : block + 4] + summed[block + 4 : block + 8]
    norm_total = wide_allreduce_small(norm_narrow, wide)
    input_grad = middle_grad + normalize_back(
        own_one_grad, own_scaled_one, own_inverse_one, gain_one
    )
    return (
        layer_out,
        input_grad,
        attn_total[:, :projections],
        attn_total[:, projections : 2 * projections],
        attn_total[:, 2 * projections : 3 * projections],
        attn_total[:, 3 * projections :].T,
        ffn_outputs[0],
        ffn_outputs[1],
        ffn_outputs[2],
        norm_total[0],
        norm_total[1],
        norm_total[2],
        norm_total[3],
    )


def solution(mesh):
    placed = (
        P(("wide", "narrow"), None),
        P(("wide", "narrow"), None),
        P("wide", None),
        P(None, "narrow"),
        P(None, "narrow"),
        P(None, "narrow"),
        P("narrow", None),
        P(None, "narrow"),
        P(None, "narrow"),
        P("narrow", None),
        P(),
        P(),
        P(),
        P(),
    )
    return jax.shard_map(
        per_device,
        mesh=mesh,
        in_specs=placed,
        out_specs=(
            P(("wide", "narrow"), None),
            P(("wide", "narrow"), None),
            P(None, "narrow"),
            P(None, "narrow"),
            P(None, "narrow"),
            P("narrow", None),
            P(None, "narrow"),
            P(None, "narrow"),
            P("narrow", None),
            P(),
            P(),
            P(),
            P(),
        ),
        check_vma=False,
    )
```

```python
import math

import jax
import jax.numpy as jnp
from jax import lax
from jax.experimental import pallas as pl
from jax.sharding import PartitionSpec as P

HD = 64
EPS = 1e-05
MASKED = -1e30
F32 = jnp.float32
BF16 = jnp.bfloat16


def normalize(values, gain_vec, bias_vec):
    centred = values - jnp.mean(values, axis=-1, keepdims=True)
    inverse = lax.rsqrt(jnp.mean(centred * centred, axis=-1, keepdims=True) + EPS)
    scaled = centred * inverse
    return (scaled * gain_vec + bias_vec, scaled, inverse)


def normalize_back(grad_in, scaled, inverse, gain_vec):
    along = grad_in * gain_vec
    return inverse * (
        along
        - jnp.mean(along, axis=-1, keepdims=True)
        - scaled * jnp.mean(along * scaled, axis=-1, keepdims=True)
    )


def contract_last(left_side, right_side):
    return lax.dot_general(
        left_side, right_side, (((1,), (1,)), ((), ())), preferred_element_type=F32
    )


def contract_first(left_side, right_side):
    return lax.dot_general(
        left_side, right_side, (((0,), (0,)), ((), ())), preferred_element_type=F32
    )


def rotate(values, cosine_table, sine_table):
    half_width = values.shape[-1] // 2
    first_half = values[..., :half_width]
    second_half = values[..., half_width:]
    cosine = cosine_table[:, None, :]
    sine_part = sine_table[:, None, :]
    return jnp.concatenate(
        [
            first_half * cosine - second_half * sine_part,
            second_half * cosine + first_half * sine_part,
        ],
        axis=-1,
    )


def unrotate(values, cosine_table, sine_table):
    half_width = values.shape[-1] // 2
    first_half = values[..., :half_width]
    second_half = values[..., half_width:]
    cosine = cosine_table[:, None, :]
    sine_part = sine_table[:, None, :]
    return jnp.concatenate(
        [
            first_half * cosine + second_half * sine_part,
            second_half * cosine - first_half * sine_part,
        ],
        axis=-1,
    )


def join_rows(parts, splits=None):
    cols, dtype = parts[0].shape[1], parts[0].dtype
    if splits is None:
        pieces = [[(0, part.shape[0])] for part in parts]
        sizes = [sum(part.shape[0] for part in parts)]
        layout = [[(i, 0, part.shape[0]) for i, part in enumerate(parts)]]
    else:
        layout = []
        start = 0
        for size in splits:
            layout.append([(i, start, size) for i in range(len(parts))])
            start += size
        sizes = [len(parts) * size for size in splits]
    count = len(parts)

    def kernel(*refs):
        ins, outs = refs[:count], refs[count:]
        for out, plan in zip(outs, layout):
            row = 0
            for i, start, size in plan:
                out[row : row + size, :] = ins[i][start : start + size, :]
                row += size

    total = sum(part.shape[0] for part in parts)
    return pl.pallas_call(
        kernel,
        out_shape=[jax.ShapeDtypeStruct((size, cols), dtype) for size in sizes],
        cost_estimate=pl.CostEstimate(flops=0, transcendentals=0, bytes_accessed=4 * total * cols),
    )(*parts)


def narrow_gather(own, count):
    slots = jnp.broadcast_to(own[None], (count,) + own.shape)
    got = lax.all_to_all(slots, "narrow", 0, 0, tiled=False)
    return got.reshape(count * own.shape[0], own.shape[1])


def narrow_scatter(partial, count):
    blocks = partial.reshape(count, partial.shape[0] // count, partial.shape[1])
    got = lax.all_to_all(blocks, "narrow", 0, 0, tiled=False)
    return jnp.sum(got.astype(F32), axis=0)


def narrow_gather_async(own, count):
    index = lax.axis_index("narrow")
    rows = own.shape[0]
    whole = jnp.zeros((count * rows, own.shape[1]), own.dtype)
    whole = lax.dynamic_update_slice_in_dim(whole, own, index * rows, 0)
    for k in range(1, count):
        got = lax.ppermute(own, "narrow", [((i + k) % count, i) for i in range(count)])
        whole = lax.dynamic_update_slice_in_dim(whole, got, ((index + k) % count) * rows, 0)
    return whole


def split_hi_lo(values):
    high = values.astype(BF16)
    return high, (values - high.astype(F32)).astype(BF16)


def narrow_maps(count):
    plane = count // 2

    def build(mapping):
        return [(z * plane + y, mapping(z, y)) for z in range(2) for y in range(plane)]

    up = build(lambda z, y: z * plane + (y + 1) % plane)
    down = build(lambda z, y: z * plane + (y - 1) % plane)
    across = build(lambda z, y: (1 - z) * plane + y)
    return up, down, across


def tree_gather(own, count):
    up, down, across = narrow_maps(count)
    from_below = lax.ppermute(own, "narrow", up)
    from_above = lax.ppermute(own, "narrow", down)
    from_across = lax.ppermute(own, "narrow", across)
    two_above = lax.ppermute(from_below, "narrow", up)
    across_above = lax.ppermute(from_across, "narrow", down)
    across_below = lax.ppermute(from_below, "narrow", across)
    across_two = lax.ppermute(two_above, "narrow", across)
    return [own, from_below, from_above, from_across, two_above, across_above, across_below, across_two]


def tree_scatter(blocks, count):
    up, down, across = narrow_maps(count)

    def send(value, pairs):
        return lax.ppermute(value.astype(BF16), "narrow", pairs).astype(F32)

    part = [blocks[s].astype(F32) for s in range(count)]
    first = send(part[7], across)
    below = send(part[4] + first, down)
    side = send(part[6], across)
    over = send(part[5], up)
    total = part[0] + send(part[1] + below + side, down)
    total = total + send(part[3] + over, across)
    return total + send(part[2], up)


def slot_sources(count):
    plane = count // 2
    index = lax.axis_index("narrow")
    z, y = index // plane, index % plane
    dz = jnp.array([0, 0, 0, 1, 0, 1, 1, 1], jnp.int32)
    dy = jnp.array([0, -1, 1, 0, 2, 1, -1, 2], jnp.int32)
    return ((z + dz) % 2) * plane + (y + dy) % plane


def source_slots(count):
    plane = count // 2
    index = lax.axis_index("narrow")
    z, y = index // plane, index % plane
    block = jnp.arange(count)
    dz = (block // plane - z) % 2
    dy = (block % plane - y) % plane
    same = jnp.array([0, 2, 4, 1], jnp.int32)
    other = jnp.array([3, 5, 7, 6], jnp.int32)
    return jnp.where(dz == 0, same[dy], other[dy])


def wide_layout(wide):
    chips_x = wide // 4
    w = lax.axis_index("wide")
    return chips_x, w % 2, (w // 2) % chips_x, w // (2 * chips_x)


def wide_map(wide, dcore=0, dx=0, dz=0, flip_core=False, xor_x=0):
    chips_x = wide // 4
    pairs = []
    for v in range(wide):
        c, xx, zz = v % 2, (v // 2) % chips_x, v // (2 * chips_x)
        c2 = (1 - c) if flip_core else c
        x2 = ((xx ^ xor_x) + dx) % chips_x
        z2 = (zz + dz) % 2
        pairs.append((v, z2 * 2 * chips_x + x2 * 2 + c2))
    return pairs


def tie(value, anchor):
    return lax.optimization_barrier((value, anchor))[0]


def core_reduce(grad, wide):
    _, core, _, _ = wide_layout(wide)
    half = grad.shape[0] // 2
    keep = lax.dynamic_slice_in_dim(grad, core * half, half, 0)
    send = lax.dynamic_slice_in_dim(grad, (1 - core) * half, half, 0)
    return keep.astype(F32) + lax.ppermute(send, "wide", wide_map(wide, flip_core=True)).astype(F32)


def x_reduce(summed, wide):
    chips_x, _, xpos, _ = wide_layout(wide)
    quarter = summed.shape[0] // chips_x
    acc = lax.dynamic_slice_in_dim(summed, xpos * quarter, quarter, 0)
    for k in range(1, chips_x):
        piece = lax.dynamic_slice_in_dim(summed, ((xpos + k) % chips_x) * quarter, quarter, 0)
        acc = acc + lax.ppermute(piece.astype(BF16), "wide", wide_map(wide, dx=k)).astype(F32)
    return acc


def z_reduce(acc, wide):
    _, _, _, zhi = wide_layout(wide)
    eighth = acc.shape[0] // 2
    mine = lax.dynamic_slice_in_dim(acc, zhi * eighth, eighth, 0)
    other = lax.dynamic_slice_in_dim(acc, (1 - zhi) * eighth, eighth, 0)
    got = lax.ppermute(other.astype(BF16), "wide", wide_map(wide, dz=1)).astype(F32)
    return (mine + got).astype(BF16)


def z_gather(final, wide):
    return jnp.concatenate([final, lax.ppermute(final, "wide", wide_map(wide, dz=1))], axis=0)


def x_gather(part, wide):
    chips_x = wide // 4
    pieces = [part]
    for k in range(1, chips_x):
        pieces.append(lax.ppermute(part, "wide", wide_map(wide, dx=chips_x - k)))
    return jnp.concatenate(pieces, axis=0)


def core_gather(halfrows, wide):
    partner = lax.ppermute(halfrows, "wide", wide_map(wide, flip_core=True))
    return jnp.concatenate([halfrows, partner], axis=0)


def unrotate_rows(rotated, wide):
    chips_x, core, xpos, zhi = wide_layout(wide)
    count = 4 * chips_x
    block = jnp.arange(count)
    half, quarter, eighth = block // (2 * chips_x), (block // 2) % chips_x, block % 2
    position = ((half - core) % 2) * (2 * chips_x) + ((quarter - xpos) % chips_x) * 2 + (eighth - zhi) % 2
    rows, cols = rotated.shape
    return jnp.take(rotated.reshape(count, rows // count, cols), position, axis=0).reshape(rows, cols)


def wide_allreduce(grad, wide):
    stage = z_gather(z_reduce(x_reduce(core_reduce(grad, wide), wide), wide), wide)
    return unrotate_rows(core_gather(x_gather(stage, wide), wide), wide).astype(F32)


def wide_allreduce_small(values, wide):
    chips_x = wide // 4
    values = values + lax.ppermute(values, "wide", wide_map(wide, flip_core=True))
    values = values + lax.ppermute(values, "wide", wide_map(wide, xor_x=1))
    if chips_x > 2:
        values = values + lax.ppermute(values, "wide", wide_map(wide, xor_x=2))
    return values + lax.ppermute(values, "wide", wide_map(wide, dz=1))


def per_device(
    tokens,
    cotangent,
    segments,
    w_query,
    w_key,
    w_value,
    w_out,
    w_gate,
    w_up,
    w_down,
    gain_one,
    bias_one,
    gain_two,
    bias_two,
):
    count = lax.axis_size("narrow")
    wide = lax.axis_size("wide")
    block, d_model = tokens.shape
    narrow_index = lax.axis_index("narrow")
    own_rows = narrow_index * block

    seg = segments[0]
    length = seg.shape[0]
    column = lax.broadcasted_iota(jnp.int32, (length, length), 1)
    same_orig = seg[:, None] == seg[None, :]
    first_index = jnp.min(jnp.where(same_orig, column, length), axis=-1)
    position = jnp.arange(length, dtype=jnp.int32) - first_index
    order = slot_sources(count)
    seg = jnp.take(seg.reshape(count, block), order, axis=0).reshape(length)
    position = jnp.take(position.reshape(count, block), order, axis=0).reshape(length)
    same_segment = seg[:, None] == seg[None, :]
    inverse = 10000.0 ** (-(2.0 * jnp.arange(HD // 2).astype(F32) / HD))
    angles = position.astype(F32)[:, None] * inverse
    cosine_table, sine_table = jnp.cos(angles), jnp.sin(angles)

    head_rows = w_out.shape[0]
    first = tree_gather(join_rows([tokens, cotangent, w_out])[0], count)
    tok_full, cot_full, w_out_rows = join_rows(first, [block, block, head_rows])
    w_out_slots = w_out_rows.reshape(count, head_rows, d_model)

    inputs = tok_full.astype(F32)
    normed_float, scaled_one, inverse_one = normalize(inputs, gain_one, bias_one)
    normed_one = normed_float.astype(BF16)
    own_scaled_one = scaled_one[:block]
    own_inverse_one = inverse_one[:block]

    heads = w_query.shape[1] // HD
    head_shape = (length, heads, HD)
    queries = rotate(
        jnp.dot(normed_one, w_query, preferred_element_type=F32).reshape(head_shape),
        cosine_table,
        sine_table,
    ).astype(BF16)
    key_rows = rotate(
        jnp.dot(normed_one, w_key, preferred_element_type=F32).reshape(head_shape),
        cosine_table,
        sine_table,
    ).astype(BF16)
    value_rows = (
        jnp.dot(normed_one, w_value, preferred_element_type=F32).astype(BF16).reshape(head_shape)
    )
    score_scale = 1.0 / math.sqrt(HD)
    scores = (
        jnp.einsum("qhd,khd->hqk", queries, key_rows, preferred_element_type=F32) * score_scale
    )
    scores = jnp.where(same_segment[None], scores, MASKED)
    row_peak = jnp.max(scores, axis=-1, keepdims=True)
    exponent = jnp.exp(scores - row_peak)
    row_total = jnp.sum(exponent, axis=-1, keepdims=True)
    probs = exponent / row_total
    probs_low = probs.astype(BF16)
    attended = (
        jnp.einsum("hqk,khd->qhd", probs_low, value_rows, preferred_element_type=F32)
        .astype(BF16)
        .reshape(length, -1)
    )

    heads_cols = attended.shape[1]
    attended_orig = jnp.take(
        attended.reshape(count, block, heads_cols), source_slots(count), axis=0
    ).reshape(length, heads_cols)
    attended_all = jnp.take(
        join_rows(tree_gather(attended_orig, count))[0].reshape(count, count, block, heads_cols),
        order,
        axis=1,
    ).reshape(count, length, heads_cols)
    branch = jnp.einsum(
        "jtc,jcd->td", attended_all, w_out_slots, preferred_element_type=F32
    )
    middle = inputs + branch
    normed_two_float, scaled_two, inverse_two = normalize(middle, gain_two, bias_two)
    normed_two = normed_two_float.astype(BF16)

    gate_pre = jnp.dot(normed_two, w_gate, preferred_element_type=F32)
    up_pre = jnp.dot(normed_two, w_up, preferred_element_type=F32)
    sigmoid_gate = jax.nn.sigmoid(gate_pre)
    active = gate_pre * sigmoid_gate
    hidden = (active * up_pre).astype(BF16)
    ffn_partial = jnp.dot(hidden, w_down, preferred_element_type=F32).astype(BF16)

    hidden_grad = contract_last(cot_full, w_down)
    gate_grad = (
        hidden_grad * up_pre * sigmoid_gate * (1.0 + gate_pre * (1.0 - sigmoid_gate))
    ).astype(BF16)
    up_grad = (hidden_grad * active).astype(BF16)
    ffn_grads = jnp.concatenate(
        [
            contract_first(normed_two, jnp.concatenate([gate_grad, up_grad], axis=1)),
            contract_first(hidden, cot_full),
        ],
        axis=0,
    ).astype(BF16)
    ffn_core = core_reduce(ffn_grads, wide)
    two_partial = (contract_last(gate_grad, w_gate) + contract_last(up_grad, w_up)).astype(BF16)
    both = tree_scatter(
        jnp.concatenate([ffn_partial, two_partial], axis=1).reshape(count, block, 2 * d_model), count
    )
    layer_out = middle[:block] + both[:, :d_model]
    own_two_grad = both[:, d_model:]
    own_scaled_two = scaled_two[:block]
    own_inverse_two = inverse_two[:block]

    middle_grad = cotangent.astype(F32) + normalize_back(
        own_two_grad, own_scaled_two, own_inverse_two, gain_two
    )
    ffn_x = x_reduce(ffn_core, wide)
    branch_grad = join_rows(tree_gather(middle_grad.astype(BF16), count))[0]
    ffn_rows = x_gather(z_gather(z_reduce(ffn_x, wide), wide), wide)

    attended_grad = contract_last(branch_grad, w_out).astype(BF16).reshape(head_shape)
    prob_grad = jnp.einsum(
        "qhd,khd->hqk", attended_grad, value_rows, preferred_element_type=F32
    )
    score_grad = (
        probs * (prob_grad - jnp.sum(probs * prob_grad, axis=-1, keepdims=True))
    ).astype(BF16)
    query_grad = score_scale * jnp.einsum(
        "hqk,khd->qhd", score_grad, key_rows, preferred_element_type=F32
    )
    key_grad = score_scale * jnp.einsum(
        "hqk,qhd->khd", score_grad, queries, preferred_element_type=F32
    )
    value_grad = jnp.einsum(
        "hqk,qhd->khd", probs_low, attended_grad, preferred_element_type=F32
    ).astype(BF16).reshape(length, -1)
    query_grad = unrotate(query_grad, cosine_table, sine_table).astype(BF16).reshape(length, -1)
    key_grad = unrotate(key_grad, cosine_table, sine_table).astype(BF16).reshape(length, -1)
    projection_grads = jnp.concatenate([query_grad, key_grad, value_grad], axis=1)
    projections = w_query.shape[1]
    qkv_grads = contract_first(normed_one, projection_grads).astype(BF16)
    attn_grads = jnp.concatenate(
        [qkv_grads, contract_first(branch_grad, attended).astype(BF16)], axis=1
    )
    attn_total = wide_allreduce(attn_grads, wide)
    one_float = contract_last(
        projection_grads, jnp.concatenate([w_query, w_key, w_value], axis=1)
    )
    norm_one = jnp.stack(
        [jnp.sum(one_float * scaled_one, axis=0), jnp.sum(one_float, axis=0)]
    )
    norm_two = jnp.stack(
        [jnp.sum(own_two_grad * own_scaled_two, axis=0), jnp.sum(own_two_grad, axis=0)]
    )
    norm_parts = jnp.concatenate([norm_one, norm_two], axis=0)
    high, low = split_hi_lo(norm_parts)
    extra = jnp.concatenate([high, low, jnp.zeros((8, d_model), BF16)], axis=0)
    one_blocks = one_float.astype(BF16).reshape(count, block, d_model)
    payload = jnp.concatenate(
        [one_blocks, jnp.broadcast_to(extra[None], (count,) + extra.shape)], axis=1
    )
    summed = tree_scatter(payload, count)
    ffn_total = unrotate_rows(core_gather(ffn_rows, wide), wide).astype(F32)
    own_one_grad = summed[:block]
    norm_narrow = summed[block : block + 4] + summed[block + 4 : block + 8]
    norm_total = wide_allreduce_small(norm_narrow, wide)
    input_grad = middle_grad + normalize_back(
        own_one_grad, own_scaled_one, own_inverse_one, gain_one
    )
    ff_cols = w_gate.shape[1]
    return (
        layer_out,
        input_grad,
        attn_total[:, :projections],
        attn_total[:, projections : 2 * projections],
        attn_total[:, 2 * projections : 3 * projections],
        attn_total[:, 3 * projections :].T,
        ffn_total[:d_model, :ff_cols],
        ffn_total[:d_model, ff_cols:],
        ffn_total[d_model:],
        norm_total[0],
        norm_total[1],
        norm_total[2],
        norm_total[3],
    )


def solution(mesh):
    placed = (
        P(("wide", "narrow"), None),
        P(("wide", "narrow"), None),
        P("wide", None),
        P(None, "narrow"),
        P(None, "narrow"),
        P(None, "narrow"),
        P("narrow", None),
        P(None, "narrow"),
        P(None, "narrow"),
        P("narrow", None),
        P(),
        P(),
        P(),
        P(),
    )
    return jax.shard_map(
        per_device,
        mesh=mesh,
        in_specs=placed,
        out_specs=(
            P(("wide", "narrow"), None),
            P(("wide", "narrow"), None),
            P(None, "narrow"),
            P(None, "narrow"),
            P(None, "narrow"),
            P("narrow", None),
            P(None, "narrow"),
            P(None, "narrow"),
            P("narrow", None),
            P(),
            P(),
            P(),
            P(),
        ),
        check_vma=False,
    )
```

```python
import math

import jax
import jax.numpy as jnp
from jax import lax
from jax.sharding import PartitionSpec as P

HD = 64
EPS = 1e-05
MASKED = -1e30
F32 = jnp.float32
BF16 = jnp.bfloat16


def normalize(values, gain_vec, bias_vec):
    centred = values - jnp.mean(values, axis=-1, keepdims=True)
    inverse = lax.rsqrt(jnp.mean(centred * centred, axis=-1, keepdims=True) + EPS)
    scaled = centred * inverse
    return (scaled * gain_vec + bias_vec, scaled, inverse)


def normalize_back(grad_in, scaled, inverse, gain_vec):
    along = grad_in * gain_vec
    return inverse * (
        along
        - jnp.mean(along, axis=-1, keepdims=True)
        - scaled * jnp.mean(along * scaled, axis=-1, keepdims=True)
    )


def contract_last(left_side, right_side):
    return lax.dot_general(
        left_side, right_side, (((1,), (1,)), ((), ())), preferred_element_type=F32
    )


def contract_first(left_side, right_side):
    return lax.dot_general(
        left_side, right_side, (((0,), (0,)), ((), ())), preferred_element_type=F32
    )


def rotate(values, cosine_table, sine_table):
    half_width = values.shape[-1] // 2
    first_half = values[..., :half_width]
    second_half = values[..., half_width:]
    cosine = cosine_table[:, None, :]
    sine_part = sine_table[:, None, :]
    return jnp.concatenate(
        [
            first_half * cosine - second_half * sine_part,
            second_half * cosine + first_half * sine_part,
        ],
        axis=-1,
    )


def unrotate(values, cosine_table, sine_table):
    half_width = values.shape[-1] // 2
    first_half = values[..., :half_width]
    second_half = values[..., half_width:]
    cosine = cosine_table[:, None, :]
    sine_part = sine_table[:, None, :]
    return jnp.concatenate(
        [
            first_half * cosine + second_half * sine_part,
            second_half * cosine - first_half * sine_part,
        ],
        axis=-1,
    )


def narrow_gather(own, count):
    slots = jnp.broadcast_to(own[None], (count,) + own.shape)
    got = lax.all_to_all(slots, "narrow", 0, 0, tiled=False)
    return got.reshape(count * own.shape[0], own.shape[1])


def narrow_scatter(partial, count):
    blocks = partial.reshape(count, partial.shape[0] // count, partial.shape[1])
    got = lax.all_to_all(blocks, "narrow", 0, 0, tiled=False)
    return jnp.sum(got.astype(F32), axis=0)


def narrow_gather_async(own, count):
    index = lax.axis_index("narrow")
    rows = own.shape[0]
    whole = jnp.zeros((count * rows, own.shape[1]), own.dtype)
    whole = lax.dynamic_update_slice_in_dim(whole, own, index * rows, 0)
    for k in range(1, count):
        got = lax.ppermute(own, "narrow", [((i + k) % count, i) for i in range(count)])
        whole = lax.dynamic_update_slice_in_dim(whole, got, ((index + k) % count) * rows, 0)
    return whole


def split_hi_lo(values):
    high = values.astype(BF16)
    return high, (values - high.astype(F32)).astype(BF16)


def narrow_maps(count):
    plane = count // 2

    def build(mapping):
        return [(z * plane + y, mapping(z, y)) for z in range(2) for y in range(plane)]

    up = build(lambda z, y: z * plane + (y + 1) % plane)
    down = build(lambda z, y: z * plane + (y - 1) % plane)
    across = build(lambda z, y: (1 - z) * plane + y)
    return up, down, across


def tree_gather(own, count):
    up, down, across = narrow_maps(count)
    from_below = lax.ppermute(own, "narrow", up)
    from_above = lax.ppermute(own, "narrow", down)
    from_across = lax.ppermute(own, "narrow", across)
    two_above = lax.ppermute(from_below, "narrow", up)
    across_above = lax.ppermute(from_across, "narrow", down)
    across_below = lax.ppermute(from_below, "narrow", across)
    across_two = lax.ppermute(two_above, "narrow", across)
    return [own, from_below, from_above, from_across, two_above, across_above, across_below, across_two]


def tree_scatter(blocks, count):
    up, down, across = narrow_maps(count)

    def send(value, pairs):
        return lax.ppermute(value.astype(BF16), "narrow", pairs).astype(F32)

    part = [blocks[s].astype(F32) for s in range(count)]
    first = send(part[7], across)
    below = send(part[4] + first, down)
    side = send(part[6], across)
    over = send(part[5], up)
    total = part[0] + send(part[1] + below + side, down)
    total = total + send(part[3] + over, across)
    return total + send(part[2], up)


def slot_sources(count):
    plane = count // 2
    index = lax.axis_index("narrow")
    z, y = index // plane, index % plane
    dz = jnp.array([0, 0, 0, 1, 0, 1, 1, 1], jnp.int32)
    dy = jnp.array([0, -1, 1, 0, 2, 1, -1, 2], jnp.int32)
    return ((z + dz) % 2) * plane + (y + dy) % plane


def source_slots(count):
    plane = count // 2
    index = lax.axis_index("narrow")
    z, y = index // plane, index % plane
    block = jnp.arange(count)
    dz = (block // plane - z) % 2
    dy = (block % plane - y) % plane
    same = jnp.array([0, 2, 4, 1], jnp.int32)
    other = jnp.array([3, 5, 7, 6], jnp.int32)
    return jnp.where(dz == 0, same[dy], other[dy])


def wide_layout(wide):
    chips_x = wide // 4
    w = lax.axis_index("wide")
    return chips_x, w % 2, (w // 2) % chips_x, w // (2 * chips_x)


def wide_map(wide, dcore=0, dx=0, dz=0, flip_core=False, xor_x=0):
    chips_x = wide // 4
    pairs = []
    for v in range(wide):
        c, xx, zz = v % 2, (v // 2) % chips_x, v // (2 * chips_x)
        c2 = (1 - c) if flip_core else c
        x2 = ((xx ^ xor_x) + dx) % chips_x
        z2 = (zz + dz) % 2
        pairs.append((v, z2 * 2 * chips_x + x2 * 2 + c2))
    return pairs


def tie(value, anchor):
    return lax.optimization_barrier((value, anchor))[0]


def core_reduce(grad, wide):
    _, core, _, _ = wide_layout(wide)
    half = grad.shape[0] // 2
    keep = lax.dynamic_slice_in_dim(grad, core * half, half, 0)
    send = lax.dynamic_slice_in_dim(grad, (1 - core) * half, half, 0)
    return keep.astype(F32) + lax.ppermute(send, "wide", wide_map(wide, flip_core=True)).astype(F32)


def x_reduce(summed, wide):
    chips_x, _, xpos, _ = wide_layout(wide)
    quarter = summed.shape[0] // chips_x
    acc = lax.dynamic_slice_in_dim(summed, xpos * quarter, quarter, 0)
    for k in range(1, chips_x):
        piece = lax.dynamic_slice_in_dim(summed, ((xpos + k) % chips_x) * quarter, quarter, 0)
        acc = acc + lax.ppermute(piece.astype(BF16), "wide", wide_map(wide, dx=k)).astype(F32)
    return acc


def z_reduce(acc, wide):
    _, _, _, zhi = wide_layout(wide)
    eighth = acc.shape[0] // 2
    mine = lax.dynamic_slice_in_dim(acc, zhi * eighth, eighth, 0)
    other = lax.dynamic_slice_in_dim(acc, (1 - zhi) * eighth, eighth, 0)
    got = lax.ppermute(other.astype(BF16), "wide", wide_map(wide, dz=1)).astype(F32)
    return (mine + got).astype(BF16)


def z_gather(final, wide):
    return jnp.concatenate([final, lax.ppermute(final, "wide", wide_map(wide, dz=1))], axis=0)


def x_gather(part, wide):
    chips_x = wide // 4
    pieces = [part]
    for k in range(1, chips_x):
        pieces.append(lax.ppermute(part, "wide", wide_map(wide, dx=chips_x - k)))
    return jnp.concatenate(pieces, axis=0)


def core_gather(halfrows, wide):
    partner = lax.ppermute(halfrows, "wide", wide_map(wide, flip_core=True))
    return jnp.concatenate([halfrows, partner], axis=0)


def unrotate_rows(rotated, wide):
    chips_x, core, xpos, zhi = wide_layout(wide)
    count = 4 * chips_x
    block = jnp.arange(count)
    half, quarter, eighth = block // (2 * chips_x), (block // 2) % chips_x, block % 2
    position = ((half - core) % 2) * (2 * chips_x) + ((quarter - xpos) % chips_x) * 2 + (eighth - zhi) % 2
    rows, cols = rotated.shape
    return jnp.take(rotated.reshape(count, rows // count, cols), position, axis=0).reshape(rows, cols)


def wide_allreduce(grad, wide):
    stage = z_gather(z_reduce(x_reduce(core_reduce(grad, wide), wide), wide), wide)
    return unrotate_rows(core_gather(x_gather(stage, wide), wide), wide).astype(F32)


def wide_allreduce_small(values, wide):
    chips_x = wide // 4
    values = values + lax.ppermute(values, "wide", wide_map(wide, flip_core=True))
    values = values + lax.ppermute(values, "wide", wide_map(wide, xor_x=1))
    if chips_x > 2:
        values = values + lax.ppermute(values, "wide", wide_map(wide, xor_x=2))
    return values + lax.ppermute(values, "wide", wide_map(wide, dz=1))


def per_device(
    tokens,
    cotangent,
    segments,
    w_query,
    w_key,
    w_value,
    w_out,
    w_gate,
    w_up,
    w_down,
    gain_one,
    bias_one,
    gain_two,
    bias_two,
):
    count = lax.axis_size("narrow")
    wide = lax.axis_size("wide")
    block, d_model = tokens.shape
    narrow_index = lax.axis_index("narrow")
    own_rows = narrow_index * block

    seg = segments[0]
    length = seg.shape[0]
    column = lax.broadcasted_iota(jnp.int32, (length, length), 1)
    same_orig = seg[:, None] == seg[None, :]
    first_index = jnp.min(jnp.where(same_orig, column, length), axis=-1)
    position = jnp.arange(length, dtype=jnp.int32) - first_index
    order = slot_sources(count)
    seg = jnp.take(seg.reshape(count, block), order, axis=0).reshape(length)
    position = jnp.take(position.reshape(count, block), order, axis=0).reshape(length)
    same_segment = seg[:, None] == seg[None, :]
    inverse = 10000.0 ** (-(2.0 * jnp.arange(HD // 2).astype(F32) / HD))
    angles = position.astype(F32)[:, None] * inverse
    cosine_table, sine_table = jnp.cos(angles), jnp.sin(angles)

    head_rows = w_out.shape[0]
    tok_full = jnp.concatenate(tree_gather(tokens, count), axis=0)
    side = tree_gather(jnp.concatenate([cotangent, w_out], axis=0), count)
    cot_full = jnp.concatenate([piece[:block] for piece in side], axis=0)
    w_out_slots = jnp.stack([piece[block:] for piece in side])

    inputs = tok_full.astype(F32)
    normed_float, scaled_one, inverse_one = normalize(inputs, gain_one, bias_one)
    normed_one = normed_float.astype(BF16)
    own_scaled_one = scaled_one[:block]
    own_inverse_one = inverse_one[:block]

    heads = w_query.shape[1] // HD
    head_shape = (length, heads, HD)
    queries = rotate(
        jnp.dot(normed_one, w_query, preferred_element_type=F32).reshape(head_shape),
        cosine_table,
        sine_table,
    ).astype(BF16)
    key_rows = rotate(
        jnp.dot(normed_one, w_key, preferred_element_type=F32).reshape(head_shape),
        cosine_table,
        sine_table,
    ).astype(BF16)
    value_rows = (
        jnp.dot(normed_one, w_value, preferred_element_type=F32).astype(BF16).reshape(head_shape)
    )
    score_scale = 1.0 / math.sqrt(HD)
    scores = (
        jnp.einsum("qhd,khd->hqk", queries, key_rows, preferred_element_type=F32) * score_scale
    )
    scores = jnp.where(same_segment[None], scores, MASKED)
    row_peak = jnp.max(scores, axis=-1, keepdims=True)
    exponent = jnp.exp(scores - row_peak)
    row_total = jnp.sum(exponent, axis=-1, keepdims=True)
    probs = exponent / row_total
    probs_low = probs.astype(BF16)
    attended = (
        jnp.einsum("hqk,khd->qhd", probs_low, value_rows, preferred_element_type=F32)
        .astype(BF16)
        .reshape(length, -1)
    )

    heads_cols = attended.shape[1]
    attended_orig = jnp.take(
        attended.reshape(count, block, heads_cols), source_slots(count), axis=0
    ).reshape(length, heads_cols)
    attended_all = jnp.take(
        jnp.stack(tree_gather(attended_orig, count)).reshape(count, count, block, heads_cols),
        order,
        axis=1,
    ).reshape(count, length, heads_cols)
    branch = jnp.einsum(
        "jtc,jcd->td", attended_all, w_out_slots, preferred_element_type=F32
    )
    middle = inputs + branch
    normed_two_float, scaled_two, inverse_two = normalize(middle, gain_two, bias_two)
    normed_two = normed_two_float.astype(BF16)

    gate_pre = jnp.dot(normed_two, w_gate, preferred_element_type=F32)
    up_pre = jnp.dot(normed_two, w_up, preferred_element_type=F32)
    sigmoid_gate = jax.nn.sigmoid(gate_pre)
    active = gate_pre * sigmoid_gate
    hidden = (active * up_pre).astype(BF16)
    ffn_partial = jnp.dot(hidden, w_down, preferred_element_type=F32).astype(BF16)

    hidden_grad = contract_last(cot_full, w_down)
    gate_grad = (
        hidden_grad * up_pre * sigmoid_gate * (1.0 + gate_pre * (1.0 - sigmoid_gate))
    ).astype(BF16)
    up_grad = (hidden_grad * active).astype(BF16)
    ffn_grads = jnp.concatenate(
        [
            contract_first(normed_two, jnp.concatenate([gate_grad, up_grad], axis=1)),
            contract_first(hidden, cot_full),
        ],
        axis=0,
    ).astype(BF16)
    ffn_core = core_reduce(ffn_grads, wide)
    two_partial = (contract_last(gate_grad, w_gate) + contract_last(up_grad, w_up)).astype(BF16)
    both = tree_scatter(
        jnp.concatenate([ffn_partial, two_partial], axis=1).reshape(count, block, 2 * d_model), count
    )
    layer_out = middle[:block] + both[:, :d_model]
    own_two_grad = both[:, d_model:]
    own_scaled_two = scaled_two[:block]
    own_inverse_two = inverse_two[:block]

    middle_grad = cotangent.astype(F32) + normalize_back(
        own_two_grad, own_scaled_two, own_inverse_two, gain_two
    )
    ffn_x = x_reduce(ffn_core, wide)
    branch_grad = jnp.concatenate(tree_gather(middle_grad.astype(BF16), count), axis=0)
    ffn_rows = x_gather(z_gather(z_reduce(ffn_x, wide), wide), wide)

    attended_grad = contract_last(branch_grad, w_out).astype(BF16).reshape(head_shape)
    prob_grad = jnp.einsum(
        "qhd,khd->hqk", attended_grad, value_rows, preferred_element_type=F32
    )
    score_grad = (
        probs * (prob_grad - jnp.sum(probs * prob_grad, axis=-1, keepdims=True))
    ).astype(BF16)
    query_grad = score_scale * jnp.einsum(
        "hqk,khd->qhd", score_grad, key_rows, preferred_element_type=F32
    )
    key_grad = score_scale * jnp.einsum(
        "hqk,qhd->khd", score_grad, queries, preferred_element_type=F32
    )
    value_grad = jnp.einsum(
        "hqk,qhd->khd", probs_low, attended_grad, preferred_element_type=F32
    ).astype(BF16).reshape(length, -1)
    query_grad = unrotate(query_grad, cosine_table, sine_table).astype(BF16).reshape(length, -1)
    key_grad = unrotate(key_grad, cosine_table, sine_table).astype(BF16).reshape(length, -1)
    projection_grads = jnp.concatenate([query_grad, key_grad, value_grad], axis=1)
    projections = w_query.shape[1]
    qkv_grads = contract_first(normed_one, projection_grads).astype(BF16)
    attn_grads = jnp.concatenate(
        [qkv_grads, contract_first(branch_grad, attended).astype(BF16)], axis=1
    )
    attn_total = wide_allreduce(attn_grads, wide)
    one_float = contract_last(
        projection_grads, jnp.concatenate([w_query, w_key, w_value], axis=1)
    )
    norm_one = jnp.stack(
        [jnp.sum(one_float * scaled_one, axis=0), jnp.sum(one_float, axis=0)]
    )
    norm_two = jnp.stack(
        [jnp.sum(own_two_grad * own_scaled_two, axis=0), jnp.sum(own_two_grad, axis=0)]
    )
    norm_parts = jnp.concatenate([norm_one, norm_two], axis=0)
    high, low = split_hi_lo(norm_parts)
    extra = jnp.concatenate([high, low, jnp.zeros((8, d_model), BF16)], axis=0)
    one_blocks = one_float.astype(BF16).reshape(count, block, d_model)
    payload = jnp.concatenate(
        [one_blocks, jnp.broadcast_to(extra[None], (count,) + extra.shape)], axis=1
    )
    summed = tree_scatter(payload, count)
    ffn_total = unrotate_rows(core_gather(ffn_rows, wide), wide).astype(F32)
    own_one_grad = summed[:block]
    norm_narrow = summed[block : block + 4] + summed[block + 4 : block + 8]
    norm_total = wide_allreduce_small(norm_narrow, wide)
    input_grad = middle_grad + normalize_back(
        own_one_grad, own_scaled_one, own_inverse_one, gain_one
    )
    ff_cols = w_gate.shape[1]
    return (
        layer_out,
        input_grad,
        attn_total[:, :projections],
        attn_total[:, projections : 2 * projections],
        attn_total[:, 2 * projections : 3 * projections],
        attn_total[:, 3 * projections :].T,
        ffn_total[:d_model, :ff_cols],
        ffn_total[:d_model, ff_cols:],
        ffn_total[d_model:],
        norm_total[0],
        norm_total[1],
        norm_total[2],
        norm_total[3],
    )


def solution(mesh):
    placed = (
        P(("wide", "narrow"), None),
        P(("wide", "narrow"), None),
        P("wide", None),
        P(None, "narrow"),
        P(None, "narrow"),
        P(None, "narrow"),
        P("narrow", None),
        P(None, "narrow"),
        P(None, "narrow"),
        P("narrow", None),
        P(),
        P(),
        P(),
        P(),
    )
    return jax.shard_map(
        per_device,
        mesh=mesh,
        in_specs=placed,
        out_specs=(
            P(("wide", "narrow"), None),
            P(("wide", "narrow"), None),
            P(None, "narrow"),
            P(None, "narrow"),
            P(None, "narrow"),
            P("narrow", None),
            P(None, "narrow"),
            P(None, "narrow"),
            P("narrow", None),
            P(),
            P(),
            P(),
            P(),
        ),
        check_vma=False,
    )
```

```python
import math

import jax
import jax.numpy as jnp
from jax import lax
from jax.sharding import PartitionSpec as P

HD = 64
EPS = 1e-05
MASKED = -1e30
F32 = jnp.float32
BF16 = jnp.bfloat16


def normalize(values, gain_vec, bias_vec):
    centred = values - jnp.mean(values, axis=-1, keepdims=True)
    inverse = lax.rsqrt(jnp.mean(centred * centred, axis=-1, keepdims=True) + EPS)
    scaled = centred * inverse
    return (scaled * gain_vec + bias_vec, scaled, inverse)


def normalize_back(grad_in, scaled, inverse, gain_vec):
    along = grad_in * gain_vec
    return inverse * (
        along
        - jnp.mean(along, axis=-1, keepdims=True)
        - scaled * jnp.mean(along * scaled, axis=-1, keepdims=True)
    )


def contract_last(left_side, right_side):
    return lax.dot_general(
        left_side, right_side, (((1,), (1,)), ((), ())), preferred_element_type=F32
    )


def contract_first(left_side, right_side):
    return lax.dot_general(
        left_side, right_side, (((0,), (0,)), ((), ())), preferred_element_type=F32
    )


def rotate(values, cosine_table, sine_table):
    half_width = values.shape[-1] // 2
    first_half = values[..., :half_width]
    second_half = values[..., half_width:]
    cosine = cosine_table[:, None, :]
    sine_part = sine_table[:, None, :]
    return jnp.concatenate(
        [
            first_half * cosine - second_half * sine_part,
            second_half * cosine + first_half * sine_part,
        ],
        axis=-1,
    )


def unrotate(values, cosine_table, sine_table):
    half_width = values.shape[-1] // 2
    first_half = values[..., :half_width]
    second_half = values[..., half_width:]
    cosine = cosine_table[:, None, :]
    sine_part = sine_table[:, None, :]
    return jnp.concatenate(
        [
            first_half * cosine + second_half * sine_part,
            second_half * cosine - first_half * sine_part,
        ],
        axis=-1,
    )


def narrow_gather(own, count):
    slots = jnp.broadcast_to(own[None], (count,) + own.shape)
    got = lax.all_to_all(slots, "narrow", 0, 0, tiled=False)
    return got.reshape(count * own.shape[0], own.shape[1])


def narrow_scatter(partial, count):
    blocks = partial.reshape(count, partial.shape[0] // count, partial.shape[1])
    got = lax.all_to_all(blocks, "narrow", 0, 0, tiled=False)
    return jnp.sum(got.astype(F32), axis=0)


def narrow_gather_async(own, count):
    index = lax.axis_index("narrow")
    rows = own.shape[0]
    whole = jnp.zeros((count * rows, own.shape[1]), own.dtype)
    whole = lax.dynamic_update_slice_in_dim(whole, own, index * rows, 0)
    for k in range(1, count):
        got = lax.ppermute(own, "narrow", [((i + k) % count, i) for i in range(count)])
        whole = lax.dynamic_update_slice_in_dim(whole, got, ((index + k) % count) * rows, 0)
    return whole


def split_hi_lo(values):
    high = values.astype(BF16)
    return high, (values - high.astype(F32)).astype(BF16)


def narrow_maps(count):
    plane = count // 2

    def build(mapping):
        return [(z * plane + y, mapping(z, y)) for z in range(2) for y in range(plane)]

    up = build(lambda z, y: z * plane + (y + 1) % plane)
    down = build(lambda z, y: z * plane + (y - 1) % plane)
    across = build(lambda z, y: (1 - z) * plane + y)
    return up, down, across


def tree_gather(own, count):
    up, down, across = narrow_maps(count)
    from_below = lax.ppermute(own, "narrow", up)
    from_above = lax.ppermute(own, "narrow", down)
    from_across = lax.ppermute(own, "narrow", across)
    two_above = lax.ppermute(from_below, "narrow", up)
    across_above = lax.ppermute(from_across, "narrow", down)
    across_below = lax.ppermute(from_below, "narrow", across)
    across_two = lax.ppermute(two_above, "narrow", across)
    return [own, from_below, from_above, from_across, two_above, across_above, across_below, across_two]


def tree_scatter(blocks, count):
    up, down, across = narrow_maps(count)

    def send(value, pairs):
        return lax.ppermute(value.astype(BF16), "narrow", pairs).astype(F32)

    part = [blocks[s].astype(F32) for s in range(count)]
    first = send(part[7], across)
    below = send(part[4] + first, down)
    side = send(part[6], across)
    over = send(part[5], up)
    total = part[0] + send(part[1] + below + side, down)
    total = total + send(part[3] + over, across)
    return total + send(part[2], up)


def slot_sources(count):
    plane = count // 2
    index = lax.axis_index("narrow")
    z, y = index // plane, index % plane
    dz = jnp.array([0, 0, 0, 1, 0, 1, 1, 1], jnp.int32)
    dy = jnp.array([0, -1, 1, 0, 2, 1, -1, 2], jnp.int32)
    return ((z + dz) % 2) * plane + (y + dy) % plane


def source_slots(count):
    plane = count // 2
    index = lax.axis_index("narrow")
    z, y = index // plane, index % plane
    block = jnp.arange(count)
    dz = (block // plane - z) % 2
    dy = (block % plane - y) % plane
    same = jnp.array([0, 2, 4, 1], jnp.int32)
    other = jnp.array([3, 5, 7, 6], jnp.int32)
    return jnp.where(dz == 0, same[dy], other[dy])


def wide_layout(wide):
    chips_x = wide // 4
    w = lax.axis_index("wide")
    return chips_x, w % 2, (w // 2) % chips_x, w // (2 * chips_x)


def wide_map(wide, dcore=0, dx=0, dz=0, flip_core=False, xor_x=0):
    chips_x = wide // 4
    pairs = []
    for v in range(wide):
        c, xx, zz = v % 2, (v // 2) % chips_x, v // (2 * chips_x)
        c2 = (1 - c) if flip_core else c
        x2 = ((xx ^ xor_x) + dx) % chips_x
        z2 = (zz + dz) % 2
        pairs.append((v, z2 * 2 * chips_x + x2 * 2 + c2))
    return pairs


def tie(value, anchor):
    return lax.optimization_barrier((value, anchor))[0]


def core_reduce(grad, wide):
    _, core, _, _ = wide_layout(wide)
    half = grad.shape[0] // 2
    keep = lax.dynamic_slice_in_dim(grad, core * half, half, 0)
    send = lax.dynamic_slice_in_dim(grad, (1 - core) * half, half, 0)
    return keep.astype(F32) + lax.ppermute(send, "wide", wide_map(wide, flip_core=True)).astype(F32)


def x_reduce(summed, wide):
    chips_x, _, xpos, _ = wide_layout(wide)
    quarter = summed.shape[0] // chips_x
    acc = lax.dynamic_slice_in_dim(summed, xpos * quarter, quarter, 0)
    for k in range(1, chips_x):
        piece = lax.dynamic_slice_in_dim(summed, ((xpos + k) % chips_x) * quarter, quarter, 0)
        acc = acc + lax.ppermute(piece.astype(BF16), "wide", wide_map(wide, dx=k)).astype(F32)
    return acc


def z_reduce(acc, wide):
    _, _, _, zhi = wide_layout(wide)
    eighth = acc.shape[0] // 2
    mine = lax.dynamic_slice_in_dim(acc, zhi * eighth, eighth, 0)
    other = lax.dynamic_slice_in_dim(acc, (1 - zhi) * eighth, eighth, 0)
    got = lax.ppermute(other.astype(BF16), "wide", wide_map(wide, dz=1)).astype(F32)
    return (mine + got).astype(BF16)


def z_gather(final, wide):
    return jnp.concatenate([final, lax.ppermute(final, "wide", wide_map(wide, dz=1))], axis=0)


def x_gather(part, wide):
    chips_x = wide // 4
    pieces = [part]
    for k in range(1, chips_x):
        pieces.append(lax.ppermute(part, "wide", wide_map(wide, dx=chips_x - k)))
    return jnp.concatenate(pieces, axis=0)


def core_gather(halfrows, wide):
    partner = lax.ppermute(halfrows, "wide", wide_map(wide, flip_core=True))
    return jnp.concatenate([halfrows, partner], axis=0)


def z_allreduce(acc, wide):
    mine = acc.astype(BF16)
    other = lax.ppermute(mine, "wide", wide_map(wide, dz=1))
    return (mine.astype(F32) + other.astype(F32)).astype(BF16)


def unrotate_rows(rotated, wide):
    chips_x, core, xpos, _ = wide_layout(wide)
    count = 2 * chips_x
    block = jnp.arange(count)
    half, quarter = block // chips_x, block % chips_x
    position = ((half - core) % 2) * chips_x + (quarter - xpos) % chips_x
    rows, cols = rotated.shape
    return jnp.take(rotated.reshape(count, rows // count, cols), position, axis=0).reshape(rows, cols)


def wide_allreduce(grad, wide):
    stage = z_allreduce(x_reduce(core_reduce(grad, wide), wide), wide)
    return unrotate_rows(core_gather(x_gather(stage, wide), wide), wide).astype(F32)


def wide_allreduce_small(values, wide):
    chips_x = wide // 4
    values = values + lax.ppermute(values, "wide", wide_map(wide, flip_core=True))
    values = values + lax.ppermute(values, "wide", wide_map(wide, xor_x=1))
    if chips_x > 2:
        values = values + lax.ppermute(values, "wide", wide_map(wide, xor_x=2))
    return values + lax.ppermute(values, "wide", wide_map(wide, dz=1))


def per_device(
    tokens,
    cotangent,
    segments,
    w_query,
    w_key,
    w_value,
    w_out,
    w_gate,
    w_up,
    w_down,
    gain_one,
    bias_one,
    gain_two,
    bias_two,
):
    count = lax.axis_size("narrow")
    wide = lax.axis_size("wide")
    block, d_model = tokens.shape
    narrow_index = lax.axis_index("narrow")
    own_rows = narrow_index * block

    seg = segments[0]
    length = seg.shape[0]
    column = lax.broadcasted_iota(jnp.int32, (length, length), 1)
    same_orig = seg[:, None] == seg[None, :]
    first_index = jnp.min(jnp.where(same_orig, column, length), axis=-1)
    position = jnp.arange(length, dtype=jnp.int32) - first_index
    order = slot_sources(count)
    seg = jnp.take(seg.reshape(count, block), order, axis=0).reshape(length)
    position = jnp.take(position.reshape(count, block), order, axis=0).reshape(length)
    same_segment = seg[:, None] == seg[None, :]
    inverse = 10000.0 ** (-(2.0 * jnp.arange(HD // 2).astype(F32) / HD))
    angles = position.astype(F32)[:, None] * inverse
    cosine_table, sine_table = jnp.cos(angles), jnp.sin(angles)

    head_rows = w_out.shape[0]
    first = tree_gather(jnp.concatenate([tokens, cotangent, w_out], axis=0), count)
    tok_full = jnp.concatenate([piece[:block] for piece in first], axis=0)
    cot_full = jnp.concatenate([piece[block : 2 * block] for piece in first], axis=0)
    w_out_slots = jnp.stack([piece[2 * block :] for piece in first])

    inputs = tok_full.astype(F32)
    normed_float, scaled_one, inverse_one = normalize(inputs, gain_one, bias_one)
    normed_one = normed_float.astype(BF16)
    own_scaled_one = scaled_one[:block]
    own_inverse_one = inverse_one[:block]

    heads = w_query.shape[1] // HD
    head_shape = (length, heads, HD)
    queries = rotate(
        jnp.dot(normed_one, w_query, preferred_element_type=F32).reshape(head_shape),
        cosine_table,
        sine_table,
    ).astype(BF16)
    key_rows = rotate(
        jnp.dot(normed_one, w_key, preferred_element_type=F32).reshape(head_shape),
        cosine_table,
        sine_table,
    ).astype(BF16)
    value_rows = (
        jnp.dot(normed_one, w_value, preferred_element_type=F32).astype(BF16).reshape(head_shape)
    )
    score_scale = 1.0 / math.sqrt(HD)
    scores = (
        jnp.einsum("qhd,khd->hqk", queries, key_rows, preferred_element_type=F32) * score_scale
    )
    scores = jnp.where(same_segment[None], scores, MASKED)
    row_peak = jnp.max(scores, axis=-1, keepdims=True)
    exponent = jnp.exp(scores - row_peak)
    row_total = jnp.sum(exponent, axis=-1, keepdims=True)
    probs = exponent / row_total
    probs_low = probs.astype(BF16)
    attended = (
        jnp.einsum("hqk,khd->qhd", probs_low, value_rows, preferred_element_type=F32)
        .astype(BF16)
        .reshape(length, -1)
    )

    heads_cols = attended.shape[1]
    attended_orig = jnp.take(
        attended.reshape(count, block, heads_cols), source_slots(count), axis=0
    ).reshape(length, heads_cols)
    attended_all = jnp.take(
        jnp.stack(tree_gather(attended_orig, count)).reshape(count, count, block, heads_cols),
        order,
        axis=1,
    ).reshape(count, length, heads_cols)
    branch = jnp.einsum(
        "jtc,jcd->td", attended_all, w_out_slots, preferred_element_type=F32
    )
    middle = inputs + branch
    normed_two_float, scaled_two, inverse_two = normalize(middle, gain_two, bias_two)
    normed_two = normed_two_float.astype(BF16)

    gate_pre = jnp.dot(normed_two, w_gate, preferred_element_type=F32)
    up_pre = jnp.dot(normed_two, w_up, preferred_element_type=F32)
    sigmoid_gate = jax.nn.sigmoid(gate_pre)
    active = gate_pre * sigmoid_gate
    hidden = (active * up_pre).astype(BF16)
    ffn_partial = jnp.dot(hidden, w_down, preferred_element_type=F32).astype(BF16)

    hidden_grad = contract_last(cot_full, w_down)
    gate_grad = (
        hidden_grad * up_pre * sigmoid_gate * (1.0 + gate_pre * (1.0 - sigmoid_gate))
    ).astype(BF16)
    up_grad = (hidden_grad * active).astype(BF16)
    ffn_grads = jnp.concatenate(
        [
            contract_first(normed_two, jnp.concatenate([gate_grad, up_grad], axis=1)),
            contract_first(hidden, cot_full),
        ],
        axis=0,
    ).astype(BF16)
    ffn_core = core_reduce(ffn_grads, wide)
    two_partial = (contract_last(gate_grad, w_gate) + contract_last(up_grad, w_up)).astype(BF16)
    both = tree_scatter(
        jnp.concatenate([ffn_partial, two_partial], axis=1).reshape(count, block, 2 * d_model), count
    )
    layer_out = middle[:block] + both[:, :d_model]
    own_two_grad = both[:, d_model:]
    own_scaled_two = scaled_two[:block]
    own_inverse_two = inverse_two[:block]

    middle_grad = cotangent.astype(F32) + normalize_back(
        own_two_grad, own_scaled_two, own_inverse_two, gain_two
    )
    ffn_x = x_reduce(ffn_core, wide)
    branch_grad = jnp.concatenate(tree_gather(middle_grad.astype(BF16), count), axis=0)
    ffn_rows = x_gather(z_allreduce(ffn_x, wide), wide)

    attended_grad = contract_last(branch_grad, w_out).astype(BF16).reshape(head_shape)
    prob_grad = jnp.einsum(
        "qhd,khd->hqk", attended_grad, value_rows, preferred_element_type=F32
    )
    score_grad = (
        probs * (prob_grad - jnp.sum(probs * prob_grad, axis=-1, keepdims=True))
    ).astype(BF16)
    query_grad = score_scale * jnp.einsum(
        "hqk,khd->qhd", score_grad, key_rows, preferred_element_type=F32
    )
    key_grad = score_scale * jnp.einsum(
        "hqk,qhd->khd", score_grad, queries, preferred_element_type=F32
    )
    value_grad = jnp.einsum(
        "hqk,qhd->khd", probs_low, attended_grad, preferred_element_type=F32
    ).astype(BF16).reshape(length, -1)
    query_grad = unrotate(query_grad, cosine_table, sine_table).astype(BF16).reshape(length, -1)
    key_grad = unrotate(key_grad, cosine_table, sine_table).astype(BF16).reshape(length, -1)
    projection_grads = jnp.concatenate([query_grad, key_grad, value_grad], axis=1)
    projections = w_query.shape[1]
    qkv_grads = contract_first(normed_one, projection_grads).astype(BF16)
    attn_grads = jnp.concatenate(
        [qkv_grads, contract_first(branch_grad, attended).astype(BF16)], axis=1
    )
    attn_total = wide_allreduce(attn_grads, wide)
    one_float = contract_last(
        projection_grads, jnp.concatenate([w_query, w_key, w_value], axis=1)
    )
    norm_one = jnp.stack(
        [jnp.sum(one_float * scaled_one, axis=0), jnp.sum(one_float, axis=0)]
    )
    norm_two = jnp.stack(
        [jnp.sum(own_two_grad * own_scaled_two, axis=0), jnp.sum(own_two_grad, axis=0)]
    )
    norm_parts = jnp.concatenate([norm_one, norm_two], axis=0)
    high, low = split_hi_lo(norm_parts)
    extra = jnp.concatenate([high, low, jnp.zeros((8, d_model), BF16)], axis=0)
    one_blocks = one_float.astype(BF16).reshape(count, block, d_model)
    payload = jnp.concatenate(
        [one_blocks, jnp.broadcast_to(extra[None], (count,) + extra.shape)], axis=1
    )
    summed = tree_scatter(payload, count)
    ffn_total = unrotate_rows(core_gather(ffn_rows, wide), wide).astype(F32)
    own_one_grad = summed[:block]
    norm_narrow = summed[block : block + 4] + summed[block + 4 : block + 8]
    norm_total = wide_allreduce_small(norm_narrow, wide)
    input_grad = middle_grad + normalize_back(
        own_one_grad, own_scaled_one, own_inverse_one, gain_one
    )
    ff_cols = w_gate.shape[1]
    return (
        layer_out,
        input_grad,
        attn_total[:, :projections],
        attn_total[:, projections : 2 * projections],
        attn_total[:, 2 * projections : 3 * projections],
        attn_total[:, 3 * projections :].T,
        ffn_total[:d_model, :ff_cols],
        ffn_total[:d_model, ff_cols:],
        ffn_total[d_model:],
        norm_total[0],
        norm_total[1],
        norm_total[2],
        norm_total[3],
    )


def solution(mesh):
    placed = (
        P(("wide", "narrow"), None),
        P(("wide", "narrow"), None),
        P("wide", None),
        P(None, "narrow"),
        P(None, "narrow"),
        P(None, "narrow"),
        P("narrow", None),
        P(None, "narrow"),
        P(None, "narrow"),
        P("narrow", None),
        P(),
        P(),
        P(),
        P(),
    )
    return jax.shard_map(
        per_device,
        mesh=mesh,
        in_specs=placed,
        out_specs=(
            P(("wide", "narrow"), None),
            P(("wide", "narrow"), None),
            P(None, "narrow"),
            P(None, "narrow"),
            P(None, "narrow"),
            P("narrow", None),
            P(None, "narrow"),
            P(None, "narrow"),
            P("narrow", None),
            P(),
            P(),
            P(),
            P(),
        ),
        check_vma=False,
    )
```

```python
import math

import jax
import jax.numpy as jnp
from jax import lax
from jax.experimental import pallas as pl
from jax.sharding import PartitionSpec as P

HD = 64
EPS = 1e-05
MASKED = -1e30
F32 = jnp.float32
BF16 = jnp.bfloat16


def normalize(values, gain_vec, bias_vec):
    centred = values - jnp.mean(values, axis=-1, keepdims=True)
    inverse = lax.rsqrt(jnp.mean(centred * centred, axis=-1, keepdims=True) + EPS)
    scaled = centred * inverse
    return (scaled * gain_vec + bias_vec, scaled, inverse)


def normalize_back(grad_in, scaled, inverse, gain_vec):
    along = grad_in * gain_vec
    return inverse * (
        along
        - jnp.mean(along, axis=-1, keepdims=True)
        - scaled * jnp.mean(along * scaled, axis=-1, keepdims=True)
    )


def contract_last(left_side, right_side):
    return lax.dot_general(
        left_side, right_side, (((1,), (1,)), ((), ())), preferred_element_type=F32
    )


def contract_first(left_side, right_side):
    return lax.dot_general(
        left_side, right_side, (((0,), (0,)), ((), ())), preferred_element_type=F32
    )


def rotate(values, cosine_table, sine_table):
    half_width = values.shape[-1] // 2
    first_half = values[..., :half_width]
    second_half = values[..., half_width:]
    cosine = cosine_table[:, None, :]
    sine_part = sine_table[:, None, :]
    return jnp.concatenate(
        [
            first_half * cosine - second_half * sine_part,
            second_half * cosine + first_half * sine_part,
        ],
        axis=-1,
    )


def unrotate(values, cosine_table, sine_table):
    half_width = values.shape[-1] // 2
    first_half = values[..., :half_width]
    second_half = values[..., half_width:]
    cosine = cosine_table[:, None, :]
    sine_part = sine_table[:, None, :]
    return jnp.concatenate(
        [
            first_half * cosine + second_half * sine_part,
            second_half * cosine - first_half * sine_part,
        ],
        axis=-1,
    )


def join_rows(parts, splits=None):
    cols, dtype = parts[0].shape[1], parts[0].dtype
    if splits is None:
        pieces = [[(0, part.shape[0])] for part in parts]
        sizes = [sum(part.shape[0] for part in parts)]
        layout = [[(i, 0, part.shape[0]) for i, part in enumerate(parts)]]
    else:
        layout = []
        start = 0
        for size in splits:
            layout.append([(i, start, size) for i in range(len(parts))])
            start += size
        sizes = [len(parts) * size for size in splits]
    count = len(parts)

    def kernel(*refs):
        ins, outs = refs[:count], refs[count:]
        for out, plan in zip(outs, layout):
            row = 0
            for i, start, size in plan:
                out[row : row + size, :] = ins[i][start : start + size, :]
                row += size

    total = sum(part.shape[0] for part in parts)
    return pl.pallas_call(
        kernel,
        out_shape=[jax.ShapeDtypeStruct((size, cols), dtype) for size in sizes],
        cost_estimate=pl.CostEstimate(flops=0, transcendentals=0, bytes_accessed=4 * total * cols),
    )(*parts)


def narrow_gather(own, count):
    slots = jnp.broadcast_to(own[None], (count,) + own.shape)
    got = lax.all_to_all(slots, "narrow", 0, 0, tiled=False)
    return got.reshape(count * own.shape[0], own.shape[1])


def narrow_scatter(partial, count):
    blocks = partial.reshape(count, partial.shape[0] // count, partial.shape[1])
    got = lax.all_to_all(blocks, "narrow", 0, 0, tiled=False)
    return jnp.sum(got.astype(F32), axis=0)


def narrow_gather_async(own, count):
    index = lax.axis_index("narrow")
    rows = own.shape[0]
    whole = jnp.zeros((count * rows, own.shape[1]), own.dtype)
    whole = lax.dynamic_update_slice_in_dim(whole, own, index * rows, 0)
    for k in range(1, count):
        got = lax.ppermute(own, "narrow", [((i + k) % count, i) for i in range(count)])
        whole = lax.dynamic_update_slice_in_dim(whole, got, ((index + k) % count) * rows, 0)
    return whole


def split_hi_lo(values):
    high = values.astype(BF16)
    return high, (values - high.astype(F32)).astype(BF16)


def narrow_maps(count):
    plane = count // 2

    def build(mapping):
        return [(z * plane + y, mapping(z, y)) for z in range(2) for y in range(plane)]

    up = build(lambda z, y: z * plane + (y + 1) % plane)
    down = build(lambda z, y: z * plane + (y - 1) % plane)
    across = build(lambda z, y: (1 - z) * plane + y)
    return up, down, across


def tree_gather(own, count):
    up, down, across = narrow_maps(count)
    from_below = lax.ppermute(own, "narrow", up)
    from_above = lax.ppermute(own, "narrow", down)
    from_across = lax.ppermute(own, "narrow", across)
    two_above = lax.ppermute(from_below, "narrow", up)
    across_above = lax.ppermute(from_across, "narrow", down)
    across_below = lax.ppermute(from_below, "narrow", across)
    across_two = lax.ppermute(two_above, "narrow", across)
    return [own, from_below, from_above, from_across, two_above, across_above, across_below, across_two]


def tree_scatter(blocks, count):
    up, down, across = narrow_maps(count)

    def send(value, pairs):
        return lax.ppermute(value.astype(BF16), "narrow", pairs).astype(F32)

    part = [blocks[s].astype(F32) for s in range(count)]
    first = send(part[7], across)
    below = send(part[4] + first, down)
    side = send(part[6], across)
    over = send(part[5], up)
    total = part[0] + send(part[1] + below + side, down)
    total = total + send(part[3] + over, across)
    return total + send(part[2], up)


def slot_sources(count):
    plane = count // 2
    index = lax.axis_index("narrow")
    z, y = index // plane, index % plane
    dz = jnp.array([0, 0, 0, 1, 0, 1, 1, 1], jnp.int32)
    dy = jnp.array([0, -1, 1, 0, 2, 1, -1, 2], jnp.int32)
    return ((z + dz) % 2) * plane + (y + dy) % plane


def source_slots(count):
    plane = count // 2
    index = lax.axis_index("narrow")
    z, y = index // plane, index % plane
    block = jnp.arange(count)
    dz = (block // plane - z) % 2
    dy = (block % plane - y) % plane
    same = jnp.array([0, 2, 4, 1], jnp.int32)
    other = jnp.array([3, 5, 7, 6], jnp.int32)
    return jnp.where(dz == 0, same[dy], other[dy])


def wide_layout(wide):
    chips_x = wide // 4
    w = lax.axis_index("wide")
    return chips_x, w % 2, (w // 2) % chips_x, w // (2 * chips_x)


def wide_map(wide, dcore=0, dx=0, dz=0, flip_core=False, xor_x=0):
    chips_x = wide // 4
    pairs = []
    for v in range(wide):
        c, xx, zz = v % 2, (v // 2) % chips_x, v // (2 * chips_x)
        c2 = (1 - c) if flip_core else c
        x2 = ((xx ^ xor_x) + dx) % chips_x
        z2 = (zz + dz) % 2
        pairs.append((v, z2 * 2 * chips_x + x2 * 2 + c2))
    return pairs


def tie(value, anchor):
    return lax.optimization_barrier((value, anchor))[0]


def core_reduce(grad, wide):
    _, core, _, _ = wide_layout(wide)
    half = grad.shape[0] // 2
    keep = lax.dynamic_slice_in_dim(grad, core * half, half, 0)
    send = lax.dynamic_slice_in_dim(grad, (1 - core) * half, half, 0)
    return keep.astype(F32) + lax.ppermute(send, "wide", wide_map(wide, flip_core=True)).astype(F32)


def x_reduce(summed, wide):
    chips_x, _, xpos, _ = wide_layout(wide)
    quarter = summed.shape[0] // chips_x
    acc = lax.dynamic_slice_in_dim(summed, xpos * quarter, quarter, 0)
    for k in range(1, chips_x):
        piece = lax.dynamic_slice_in_dim(summed, ((xpos + k) % chips_x) * quarter, quarter, 0)
        acc = acc + lax.ppermute(piece.astype(BF16), "wide", wide_map(wide, dx=k)).astype(F32)
    return acc


def z_reduce(acc, wide):
    _, _, _, zhi = wide_layout(wide)
    eighth = acc.shape[0] // 2
    mine = lax.dynamic_slice_in_dim(acc, zhi * eighth, eighth, 0)
    other = lax.dynamic_slice_in_dim(acc, (1 - zhi) * eighth, eighth, 0)
    got = lax.ppermute(other.astype(BF16), "wide", wide_map(wide, dz=1)).astype(F32)
    return (mine + got).astype(BF16)


def z_gather(final, wide):
    return jnp.concatenate([final, lax.ppermute(final, "wide", wide_map(wide, dz=1))], axis=0)


def x_gather(part, wide):
    chips_x = wide // 4
    pieces = [part]
    for k in range(1, chips_x):
        pieces.append(lax.ppermute(part, "wide", wide_map(wide, dx=chips_x - k)))
    return jnp.concatenate(pieces, axis=0)


def core_gather(halfrows, wide):
    partner = lax.ppermute(halfrows, "wide", wide_map(wide, flip_core=True))
    return jnp.concatenate([halfrows, partner], axis=0)


def unrotate_rows(rotated, wide):
    chips_x, core, xpos, zhi = wide_layout(wide)
    count = 4 * chips_x
    block = jnp.arange(count)
    half, quarter, eighth = block // (2 * chips_x), (block // 2) % chips_x, block % 2
    position = ((half - core) % 2) * (2 * chips_x) + ((quarter - xpos) % chips_x) * 2 + (eighth - zhi) % 2
    rows, cols = rotated.shape
    return jnp.take(rotated.reshape(count, rows // count, cols), position, axis=0).reshape(rows, cols)


def wide_allreduce(grad, wide):
    stage = z_gather(z_reduce(x_reduce(core_reduce(grad, wide), wide), wide), wide)
    return unrotate_rows(core_gather(x_gather(stage, wide), wide), wide).astype(F32)


def wide_allreduce_small(values, wide):
    chips_x = wide // 4
    values = values + lax.ppermute(values, "wide", wide_map(wide, flip_core=True))
    values = values + lax.ppermute(values, "wide", wide_map(wide, xor_x=1))
    if chips_x > 2:
        values = values + lax.ppermute(values, "wide", wide_map(wide, xor_x=2))
    return values + lax.ppermute(values, "wide", wide_map(wide, dz=1))


def per_device(
    tokens,
    cotangent,
    segments,
    w_query,
    w_key,
    w_value,
    w_out,
    w_gate,
    w_up,
    w_down,
    gain_one,
    bias_one,
    gain_two,
    bias_two,
):
    count = lax.axis_size("narrow")
    wide = lax.axis_size("wide")
    block, d_model = tokens.shape
    narrow_index = lax.axis_index("narrow")
    own_rows = narrow_index * block

    seg = segments[0]
    length = seg.shape[0]
    column = lax.broadcasted_iota(jnp.int32, (length, length), 1)
    same_orig = seg[:, None] == seg[None, :]
    first_index = jnp.min(jnp.where(same_orig, column, length), axis=-1)
    position = jnp.arange(length, dtype=jnp.int32) - first_index
    order = slot_sources(count)
    seg = jnp.take(seg.reshape(count, block), order, axis=0).reshape(length)
    position = jnp.take(position.reshape(count, block), order, axis=0).reshape(length)
    same_segment = seg[:, None] == seg[None, :]
    inverse = 10000.0 ** (-(2.0 * jnp.arange(HD // 2).astype(F32) / HD))
    angles = position.astype(F32)[:, None] * inverse
    cosine_table, sine_table = jnp.cos(angles), jnp.sin(angles)

    head_rows = w_out.shape[0]
    first = tree_gather(join_rows([tokens, cotangent, w_out])[0], count)
    tok_full = jnp.concatenate([piece[:block] for piece in first], axis=0)
    cot_full = jnp.concatenate([piece[block : 2 * block] for piece in first], axis=0)
    w_out_slots = jnp.stack([piece[2 * block :] for piece in first])

    inputs = tok_full.astype(F32)
    normed_float, scaled_one, inverse_one = normalize(inputs, gain_one, bias_one)
    normed_one = normed_float.astype(BF16)
    own_scaled_one = scaled_one[:block]
    own_inverse_one = inverse_one[:block]

    heads = w_query.shape[1] // HD
    head_shape = (length, heads, HD)
    queries = rotate(
        jnp.dot(normed_one, w_query, preferred_element_type=F32).reshape(head_shape),
        cosine_table,
        sine_table,
    ).astype(BF16)
    key_rows = rotate(
        jnp.dot(normed_one, w_key, preferred_element_type=F32).reshape(head_shape),
        cosine_table,
        sine_table,
    ).astype(BF16)
    value_rows = (
        jnp.dot(normed_one, w_value, preferred_element_type=F32).astype(BF16).reshape(head_shape)
    )
    score_scale = 1.0 / math.sqrt(HD)
    scores = (
        jnp.einsum("qhd,khd->hqk", queries, key_rows, preferred_element_type=F32) * score_scale
    )
    scores = jnp.where(same_segment[None], scores, MASKED)
    row_peak = jnp.max(scores, axis=-1, keepdims=True)
    exponent = jnp.exp(scores - row_peak)
    row_total = jnp.sum(exponent, axis=-1, keepdims=True)
    probs = exponent / row_total
    probs_low = probs.astype(BF16)
    attended = (
        jnp.einsum("hqk,khd->qhd", probs_low, value_rows, preferred_element_type=F32)
        .astype(BF16)
        .reshape(length, -1)
    )

    heads_cols = attended.shape[1]
    attended_orig = jnp.take(
        attended.reshape(count, block, heads_cols), source_slots(count), axis=0
    ).reshape(length, heads_cols)
    attended_all = jnp.take(
        jnp.stack(tree_gather(attended_orig, count)).reshape(count, count, block, heads_cols),
        order,
        axis=1,
    ).reshape(count, length, heads_cols)
    branch = jnp.einsum(
        "jtc,jcd->td", attended_all, w_out_slots, preferred_element_type=F32
    )
    middle = inputs + branch
    normed_two_float, scaled_two, inverse_two = normalize(middle, gain_two, bias_two)
    normed_two = normed_two_float.astype(BF16)

    gate_pre = jnp.dot(normed_two, w_gate, preferred_element_type=F32)
    up_pre = jnp.dot(normed_two, w_up, preferred_element_type=F32)
    sigmoid_gate = jax.nn.sigmoid(gate_pre)
    active = gate_pre * sigmoid_gate
    hidden = (active * up_pre).astype(BF16)
    ffn_partial = jnp.dot(hidden, w_down, preferred_element_type=F32).astype(BF16)

    hidden_grad = contract_last(cot_full, w_down)
    gate_grad = (
        hidden_grad * up_pre * sigmoid_gate * (1.0 + gate_pre * (1.0 - sigmoid_gate))
    ).astype(BF16)
    up_grad = (hidden_grad * active).astype(BF16)
    ffn_grads = jnp.concatenate(
        [
            contract_first(normed_two, jnp.concatenate([gate_grad, up_grad], axis=1)),
            contract_first(hidden, cot_full),
        ],
        axis=0,
    ).astype(BF16)
    ffn_core = core_reduce(ffn_grads, wide)
    two_partial = (contract_last(gate_grad, w_gate) + contract_last(up_grad, w_up)).astype(BF16)
    both = tree_scatter(
        jnp.concatenate([ffn_partial, two_partial], axis=1).reshape(count, block, 2 * d_model), count
    )
    layer_out = middle[:block] + both[:, :d_model]
    own_two_grad = both[:, d_model:]
    own_scaled_two = scaled_two[:block]
    own_inverse_two = inverse_two[:block]

    middle_grad = cotangent.astype(F32) + normalize_back(
        own_two_grad, own_scaled_two, own_inverse_two, gain_two
    )
    ffn_x = x_reduce(ffn_core, wide)
    branch_grad = jnp.concatenate(tree_gather(middle_grad.astype(BF16), count), axis=0)
    ffn_rows = x_gather(z_gather(z_reduce(ffn_x, wide), wide), wide)

    attended_grad = contract_last(branch_grad, w_out).astype(BF16).reshape(head_shape)
    prob_grad = jnp.einsum(
        "qhd,khd->hqk", attended_grad, value_rows, preferred_element_type=F32
    )
    score_grad = (
        probs * (prob_grad - jnp.sum(probs * prob_grad, axis=-1, keepdims=True))
    ).astype(BF16)
    query_grad = score_scale * jnp.einsum(
        "hqk,khd->qhd", score_grad, key_rows, preferred_element_type=F32
    )
    key_grad = score_scale * jnp.einsum(
        "hqk,qhd->khd", score_grad, queries, preferred_element_type=F32
    )
    value_grad = jnp.einsum(
        "hqk,qhd->khd", probs_low, attended_grad, preferred_element_type=F32
    ).astype(BF16).reshape(length, -1)
    query_grad = unrotate(query_grad, cosine_table, sine_table).astype(BF16).reshape(length, -1)
    key_grad = unrotate(key_grad, cosine_table, sine_table).astype(BF16).reshape(length, -1)
    projection_grads = jnp.concatenate([query_grad, key_grad, value_grad], axis=1)
    projections = w_query.shape[1]
    qkv_grads = contract_first(normed_one, projection_grads).astype(BF16)
    attn_grads = jnp.concatenate(
        [qkv_grads, contract_first(branch_grad, attended).astype(BF16)], axis=1
    )
    attn_total = wide_allreduce(attn_grads, wide)
    one_float = contract_last(
        projection_grads, jnp.concatenate([w_query, w_key, w_value], axis=1)
    )
    norm_one = jnp.stack(
        [jnp.sum(one_float * scaled_one, axis=0), jnp.sum(one_float, axis=0)]
    )
    norm_two = jnp.stack(
        [jnp.sum(own_two_grad * own_scaled_two, axis=0), jnp.sum(own_two_grad, axis=0)]
    )
    norm_parts = jnp.concatenate([norm_one, norm_two], axis=0)
    high, low = split_hi_lo(norm_parts)
    extra = jnp.concatenate([high, low, jnp.zeros((8, d_model), BF16)], axis=0)
    one_blocks = one_float.astype(BF16).reshape(count, block, d_model)
    payload = jnp.concatenate(
        [one_blocks, jnp.broadcast_to(extra[None], (count,) + extra.shape)], axis=1
    )
    summed = tree_scatter(payload, count)
    ffn_total = unrotate_rows(core_gather(ffn_rows, wide), wide).astype(F32)
    own_one_grad = summed[:block]
    norm_narrow = summed[block : block + 4] + summed[block + 4 : block + 8]
    norm_total = wide_allreduce_small(norm_narrow, wide)
    input_grad = middle_grad + normalize_back(
        own_one_grad, own_scaled_one, own_inverse_one, gain_one
    )
    ff_cols = w_gate.shape[1]
    return (
        layer_out,
        input_grad,
        attn_total[:, :projections],
        attn_total[:, projections : 2 * projections],
        attn_total[:, 2 * projections : 3 * projections],
        attn_total[:, 3 * projections :].T,
        ffn_total[:d_model, :ff_cols],
        ffn_total[:d_model, ff_cols:],
        ffn_total[d_model:],
        norm_total[0],
        norm_total[1],
        norm_total[2],
        norm_total[3],
    )


def solution(mesh):
    placed = (
        P(("wide", "narrow"), None),
        P(("wide", "narrow"), None),
        P("wide", None),
        P(None, "narrow"),
        P(None, "narrow"),
        P(None, "narrow"),
        P("narrow", None),
        P(None, "narrow"),
        P(None, "narrow"),
        P("narrow", None),
        P(),
        P(),
        P(),
        P(),
    )
    return jax.shard_map(
        per_device,
        mesh=mesh,
        in_specs=placed,
        out_specs=(
            P(("wide", "narrow"), None),
            P(("wide", "narrow"), None),
            P(None, "narrow"),
            P(None, "narrow"),
            P(None, "narrow"),
            P("narrow", None),
            P(None, "narrow"),
            P(None, "narrow"),
            P("narrow", None),
            P(),
            P(),
            P(),
            P(),
        ),
        check_vma=False,
    )
```

```python
import math

import jax
import jax.numpy as jnp
from jax import lax
from jax.sharding import PartitionSpec as P

HD = 64
EPS = 1e-05
MASKED = -1e30
F32 = jnp.float32
BF16 = jnp.bfloat16


def normalize(values, gain_vec, bias_vec):
    centred = values - jnp.mean(values, axis=-1, keepdims=True)
    inverse = lax.rsqrt(jnp.mean(centred * centred, axis=-1, keepdims=True) + EPS)
    scaled = centred * inverse
    return (scaled * gain_vec + bias_vec, scaled, inverse)


def normalize_back(grad_in, scaled, inverse, gain_vec):
    along = grad_in * gain_vec
    return inverse * (
        along
        - jnp.mean(along, axis=-1, keepdims=True)
        - scaled * jnp.mean(along * scaled, axis=-1, keepdims=True)
    )


def contract_last(left_side, right_side):
    return lax.dot_general(
        left_side, right_side, (((1,), (1,)), ((), ())), preferred_element_type=F32
    )


def contract_first(left_side, right_side):
    return lax.dot_general(
        left_side, right_side, (((0,), (0,)), ((), ())), preferred_element_type=F32
    )


def rotate(values, cosine_table, sine_table):
    half_width = values.shape[-1] // 2
    first_half = values[..., :half_width]
    second_half = values[..., half_width:]
    cosine = cosine_table[:, None, :]
    sine_part = sine_table[:, None, :]
    return jnp.concatenate(
        [
            first_half * cosine - second_half * sine_part,
            second_half * cosine + first_half * sine_part,
        ],
        axis=-1,
    )


def unrotate(values, cosine_table, sine_table):
    half_width = values.shape[-1] // 2
    first_half = values[..., :half_width]
    second_half = values[..., half_width:]
    cosine = cosine_table[:, None, :]
    sine_part = sine_table[:, None, :]
    return jnp.concatenate(
        [
            first_half * cosine + second_half * sine_part,
            second_half * cosine - first_half * sine_part,
        ],
        axis=-1,
    )


def narrow_gather(own, count):
    slots = jnp.broadcast_to(own[None], (count,) + own.shape)
    got = lax.all_to_all(slots, "narrow", 0, 0, tiled=False)
    return got.reshape(count * own.shape[0], own.shape[1])


def narrow_scatter(partial, count):
    blocks = partial.reshape(count, partial.shape[0] // count, partial.shape[1])
    got = lax.all_to_all(blocks, "narrow", 0, 0, tiled=False)
    return jnp.sum(got.astype(F32), axis=0)


def narrow_gather_async(own, count):
    index = lax.axis_index("narrow")
    rows = own.shape[0]
    whole = jnp.zeros((count * rows, own.shape[1]), own.dtype)
    whole = lax.dynamic_update_slice_in_dim(whole, own, index * rows, 0)
    for k in range(1, count):
        got = lax.ppermute(own, "narrow", [((i + k) % count, i) for i in range(count)])
        whole = lax.dynamic_update_slice_in_dim(whole, got, ((index + k) % count) * rows, 0)
    return whole


def split_hi_lo(values):
    high = values.astype(BF16)
    return high, (values - high.astype(F32)).astype(BF16)


def narrow_maps(count):
    plane = count // 2

    def build(mapping):
        return [(z * plane + y, mapping(z, y)) for z in range(2) for y in range(plane)]

    up = build(lambda z, y: z * plane + (y + 1) % plane)
    down = build(lambda z, y: z * plane + (y - 1) % plane)
    across = build(lambda z, y: (1 - z) * plane + y)
    return up, down, across


def tree_gather(own, count):
    up, down, across = narrow_maps(count)
    from_below = lax.ppermute(own, "narrow", up)
    from_above = lax.ppermute(own, "narrow", down)
    from_across = lax.ppermute(own, "narrow", across)
    two_above = lax.ppermute(from_below, "narrow", up)
    across_above = lax.ppermute(from_across, "narrow", down)
    across_below = lax.ppermute(from_below, "narrow", across)
    across_two = lax.ppermute(two_above, "narrow", across)
    return [own, from_below, from_above, from_across, two_above, across_above, across_below, across_two]


def tree_scatter(blocks, count):
    up, down, across = narrow_maps(count)

    def send(value, pairs):
        return lax.ppermute(value.astype(BF16), "narrow", pairs).astype(F32)

    part = [blocks[s].astype(F32) for s in range(count)]
    first = send(part[7], across)
    below = send(part[4] + first, down)
    side = send(part[6], across)
    over = send(part[5], up)
    total = part[0] + send(part[1] + below + side, down)
    total = total + send(part[3] + over, across)
    return total + send(part[2], up)


def slot_sources(count):
    plane = count // 2
    index = lax.axis_index("narrow")
    z, y = index // plane, index % plane
    dz = jnp.array([0, 0, 0, 1, 0, 1, 1, 1], jnp.int32)
    dy = jnp.array([0, -1, 1, 0, 2, 1, -1, 2], jnp.int32)
    return ((z + dz) % 2) * plane + (y + dy) % plane


def source_slots(count):
    plane = count // 2
    index = lax.axis_index("narrow")
    z, y = index // plane, index % plane
    block = jnp.arange(count)
    dz = (block // plane - z) % 2
    dy = (block % plane - y) % plane
    same = jnp.array([0, 2, 4, 1], jnp.int32)
    other = jnp.array([3, 5, 7, 6], jnp.int32)
    return jnp.where(dz == 0, same[dy], other[dy])


def wide_layout(wide):
    chips_x = wide // 4
    w = lax.axis_index("wide")
    return chips_x, w % 2, (w // 2) % chips_x, w // (2 * chips_x)


def wide_map(wide, dcore=0, dx=0, dz=0, flip_core=False, xor_x=0):
    chips_x = wide // 4
    pairs = []
    for v in range(wide):
        c, xx, zz = v % 2, (v // 2) % chips_x, v // (2 * chips_x)
        c2 = (1 - c) if flip_core else c
        x2 = ((xx ^ xor_x) + dx) % chips_x
        z2 = (zz + dz) % 2
        pairs.append((v, z2 * 2 * chips_x + x2 * 2 + c2))
    return pairs


def tie(value, anchor):
    return lax.optimization_barrier((value, anchor))[0]


def core_reduce(grad, wide):
    _, core, _, _ = wide_layout(wide)
    half = grad.shape[0] // 2
    keep = lax.dynamic_slice_in_dim(grad, core * half, half, 0)
    send = lax.dynamic_slice_in_dim(grad, (1 - core) * half, half, 0)
    return keep.astype(F32) + lax.ppermute(send, "wide", wide_map(wide, flip_core=True)).astype(F32)


def x_reduce(summed, wide):
    chips_x, _, xpos, _ = wide_layout(wide)
    quarter = summed.shape[0] // chips_x
    acc = lax.dynamic_slice_in_dim(summed, xpos * quarter, quarter, 0)
    for k in range(1, chips_x):
        piece = lax.dynamic_slice_in_dim(summed, ((xpos + k) % chips_x) * quarter, quarter, 0)
        acc = acc + lax.ppermute(piece.astype(BF16), "wide", wide_map(wide, dx=k)).astype(F32)
    return acc


def z_reduce(acc, wide):
    _, _, _, zhi = wide_layout(wide)
    eighth = acc.shape[0] // 2
    mine = lax.dynamic_slice_in_dim(acc, zhi * eighth, eighth, 0)
    other = lax.dynamic_slice_in_dim(acc, (1 - zhi) * eighth, eighth, 0)
    got = lax.ppermute(other.astype(BF16), "wide", wide_map(wide, dz=1)).astype(F32)
    return (mine + got).astype(BF16)


def z_gather(final, wide):
    return jnp.concatenate([final, lax.ppermute(final, "wide", wide_map(wide, dz=1))], axis=0)


def x_gather(part, wide):
    chips_x = wide // 4
    pieces = [part]
    for k in range(1, chips_x):
        pieces.append(lax.ppermute(part, "wide", wide_map(wide, dx=chips_x - k)))
    return jnp.concatenate(pieces, axis=0)


def core_gather(halfrows, wide):
    partner = lax.ppermute(halfrows, "wide", wide_map(wide, flip_core=True))
    return jnp.concatenate([halfrows, partner], axis=0)


def unrotate_rows(rotated, wide):
    chips_x, core, xpos, zhi = wide_layout(wide)
    count = 4 * chips_x
    block = jnp.arange(count)
    half, quarter, eighth = block // (2 * chips_x), (block // 2) % chips_x, block % 2
    position = ((half - core) % 2) * (2 * chips_x) + ((quarter - xpos) % chips_x) * 2 + (eighth - zhi) % 2
    rows, cols = rotated.shape
    return jnp.take(rotated.reshape(count, rows // count, cols), position, axis=0).reshape(rows, cols)


def wide_allreduce(grad, wide):
    stage = z_gather(z_reduce(x_reduce(core_reduce(grad, wide), wide), wide), wide)
    return unrotate_rows(core_gather(x_gather(stage, wide), wide), wide).astype(F32)


def wide_allreduce_small(values, wide):
    chips_x = wide // 4
    values = values + lax.ppermute(values, "wide", wide_map(wide, flip_core=True))
    values = values + lax.ppermute(values, "wide", wide_map(wide, xor_x=1))
    if chips_x > 2:
        values = values + lax.ppermute(values, "wide", wide_map(wide, xor_x=2))
    return values + lax.ppermute(values, "wide", wide_map(wide, dz=1))


def per_device(
    tokens,
    cotangent,
    segments,
    w_query,
    w_key,
    w_value,
    w_out,
    w_gate,
    w_up,
    w_down,
    gain_one,
    bias_one,
    gain_two,
    bias_two,
):
    count = lax.axis_size("narrow")
    wide = lax.axis_size("wide")
    block, d_model = tokens.shape
    narrow_index = lax.axis_index("narrow")
    own_rows = narrow_index * block

    seg = segments[0]
    length = seg.shape[0]
    column = lax.broadcasted_iota(jnp.int32, (length, length), 1)
    same_orig = seg[:, None] == seg[None, :]
    first_index = jnp.min(jnp.where(same_orig, column, length), axis=-1)
    position = jnp.arange(length, dtype=jnp.int32) - first_index
    order = slot_sources(count)
    seg = jnp.take(seg.reshape(count, block), order, axis=0).reshape(length)
    position = jnp.take(position.reshape(count, block), order, axis=0).reshape(length)
    same_segment = seg[:, None] == seg[None, :]
    inverse = 10000.0 ** (-(2.0 * jnp.arange(HD // 2).astype(F32) / HD))
    angles = position.astype(F32)[:, None] * inverse
    cosine_table, sine_table = jnp.cos(angles), jnp.sin(angles)

    head_rows = w_out.shape[0]
    first = tree_gather(jnp.concatenate([tokens, cotangent, w_out], axis=0), count)
    tok_full = jnp.concatenate([piece[:block] for piece in first], axis=0)
    cot_full = jnp.concatenate([piece[block : 2 * block] for piece in first], axis=0)
    w_out_slots = jnp.stack([piece[2 * block :] for piece in first])

    inputs = tok_full.astype(F32)
    normed_float, scaled_one, inverse_one = normalize(inputs, gain_one, bias_one)
    normed_one = normed_float.astype(BF16)
    own_scaled_one = scaled_one[:block]
    own_inverse_one = inverse_one[:block]

    heads = w_query.shape[1] // HD
    head_shape = (length, heads, HD)
    queries = rotate(
        jnp.dot(normed_one, w_query, preferred_element_type=F32).reshape(head_shape),
        cosine_table,
        sine_table,
    ).astype(BF16)
    key_rows = rotate(
        jnp.dot(normed_one, w_key, preferred_element_type=F32).reshape(head_shape),
        cosine_table,
        sine_table,
    ).astype(BF16)
    value_rows = (
        jnp.dot(normed_one, w_value, preferred_element_type=F32).astype(BF16).reshape(head_shape)
    )
    score_scale = 1.0 / math.sqrt(HD)
    scores = (
        jnp.einsum("qhd,khd->hqk", queries, key_rows, preferred_element_type=F32) * score_scale
    )
    scores = jnp.where(same_segment[None], scores, MASKED)
    row_peak = jnp.max(scores, axis=-1, keepdims=True)
    exponent = jnp.exp(scores - row_peak)
    row_total = jnp.sum(exponent, axis=-1, keepdims=True)
    probs = exponent / row_total
    probs_low = probs.astype(BF16)
    attended = (
        jnp.einsum("hqk,khd->qhd", probs_low, value_rows, preferred_element_type=F32)
        .astype(BF16)
        .reshape(length, -1)
    )

    heads_cols = attended.shape[1]
    attended_orig = jnp.take(
        attended.reshape(count, block, heads_cols), source_slots(count), axis=0
    ).reshape(length, heads_cols)
    attended_all = jnp.stack(
        [
            jnp.take(piece.reshape(count, block, heads_cols), order, axis=0).reshape(length, heads_cols)
            for piece in tree_gather(attended_orig, count)
        ]
    )
    branch = jnp.einsum(
        "jtc,jcd->td", attended_all, w_out_slots, preferred_element_type=F32
    )
    middle = inputs + branch
    normed_two_float, scaled_two, inverse_two = normalize(middle, gain_two, bias_two)
    normed_two = normed_two_float.astype(BF16)

    gate_pre = jnp.dot(normed_two, w_gate, preferred_element_type=F32)
    up_pre = jnp.dot(normed_two, w_up, preferred_element_type=F32)
    sigmoid_gate = jax.nn.sigmoid(gate_pre)
    active = gate_pre * sigmoid_gate
    hidden = (active * up_pre).astype(BF16)
    ffn_partial = jnp.dot(hidden, w_down, preferred_element_type=F32).astype(BF16)

    hidden_grad = contract_last(cot_full, w_down)
    gate_grad = (
        hidden_grad * up_pre * sigmoid_gate * (1.0 + gate_pre * (1.0 - sigmoid_gate))
    ).astype(BF16)
    up_grad = (hidden_grad * active).astype(BF16)
    ffn_grads = jnp.concatenate(
        [
            contract_first(normed_two, jnp.concatenate([gate_grad, up_grad], axis=1)),
            contract_first(hidden, cot_full),
        ],
        axis=0,
    ).astype(BF16)
    ffn_core = core_reduce(ffn_grads, wide)
    two_partial = (contract_last(gate_grad, w_gate) + contract_last(up_grad, w_up)).astype(BF16)
    both = tree_scatter(
        jnp.concatenate([ffn_partial, two_partial], axis=1).reshape(count, block, 2 * d_model), count
    )
    layer_out = middle[:block] + both[:, :d_model]
    own_two_grad = both[:, d_model:]
    own_scaled_two = scaled_two[:block]
    own_inverse_two = inverse_two[:block]

    middle_grad = cotangent.astype(F32) + normalize_back(
        own_two_grad, own_scaled_two, own_inverse_two, gain_two
    )
    ffn_x = x_reduce(ffn_core, wide)
    branch_grad = jnp.concatenate(tree_gather(middle_grad.astype(BF16), count), axis=0)
    ffn_rows = x_gather(z_gather(z_reduce(ffn_x, wide), wide), wide)

    attended_grad = contract_last(branch_grad, w_out).astype(BF16).reshape(head_shape)
    prob_grad = jnp.einsum(
        "qhd,khd->hqk", attended_grad, value_rows, preferred_element_type=F32
    )
    score_grad = (
        probs * (prob_grad - jnp.sum(probs * prob_grad, axis=-1, keepdims=True))
    ).astype(BF16)
    query_grad = score_scale * jnp.einsum(
        "hqk,khd->qhd", score_grad, key_rows, preferred_element_type=F32
    )
    key_grad = score_scale * jnp.einsum(
        "hqk,qhd->khd", score_grad, queries, preferred_element_type=F32
    )
    value_grad = jnp.einsum(
        "hqk,qhd->khd", probs_low, attended_grad, preferred_element_type=F32
    ).astype(BF16).reshape(length, -1)
    query_grad = unrotate(query_grad, cosine_table, sine_table).astype(BF16).reshape(length, -1)
    key_grad = unrotate(key_grad, cosine_table, sine_table).astype(BF16).reshape(length, -1)
    projection_grads = jnp.concatenate([query_grad, key_grad, value_grad], axis=1)
    projections = w_query.shape[1]
    qkv_grads = contract_first(normed_one, projection_grads).astype(BF16)
    attn_grads = jnp.concatenate(
        [qkv_grads, contract_first(branch_grad, attended).astype(BF16)], axis=1
    )
    attn_total = wide_allreduce(attn_grads, wide)
    one_float = contract_last(
        projection_grads, jnp.concatenate([w_query, w_key, w_value], axis=1)
    )
    norm_one = jnp.stack(
        [jnp.sum(one_float * scaled_one, axis=0), jnp.sum(one_float, axis=0)]
    )
    norm_two = jnp.stack(
        [jnp.sum(own_two_grad * own_scaled_two, axis=0), jnp.sum(own_two_grad, axis=0)]
    )
    norm_parts = jnp.concatenate([norm_one, norm_two], axis=0)
    high, low = split_hi_lo(norm_parts)
    extra = jnp.concatenate([high, low, jnp.zeros((8, d_model), BF16)], axis=0)
    one_blocks = one_float.astype(BF16).reshape(count, block, d_model)
    payload = jnp.concatenate(
        [one_blocks, jnp.broadcast_to(extra[None], (count,) + extra.shape)], axis=1
    )
    summed = tree_scatter(payload, count)
    ffn_total = unrotate_rows(core_gather(ffn_rows, wide), wide).astype(F32)
    own_one_grad = summed[:block]
    norm_narrow = summed[block : block + 4] + summed[block + 4 : block + 8]
    norm_total = wide_allreduce_small(norm_narrow, wide)
    input_grad = middle_grad + normalize_back(
        own_one_grad, own_scaled_one, own_inverse_one, gain_one
    )
    ff_cols = w_gate.shape[1]
    return (
        layer_out,
        input_grad,
        attn_total[:, :projections],
        attn_total[:, projections : 2 * projections],
        attn_total[:, 2 * projections : 3 * projections],
        attn_total[:, 3 * projections :].T,
        ffn_total[:d_model, :ff_cols],
        ffn_total[:d_model, ff_cols:],
        ffn_total[d_model:],
        norm_total[0],
        norm_total[1],
        norm_total[2],
        norm_total[3],
    )


def solution(mesh):
    placed = (
        P(("wide", "narrow"), None),
        P(("wide", "narrow"), None),
        P("wide", None),
        P(None, "narrow"),
        P(None, "narrow"),
        P(None, "narrow"),
        P("narrow", None),
        P(None, "narrow"),
        P(None, "narrow"),
        P("narrow", None),
        P(),
        P(),
        P(),
        P(),
    )
    return jax.shard_map(
        per_device,
        mesh=mesh,
        in_specs=placed,
        out_specs=(
            P(("wide", "narrow"), None),
            P(("wide", "narrow"), None),
            P(None, "narrow"),
            P(None, "narrow"),
            P(None, "narrow"),
            P("narrow", None),
            P(None, "narrow"),
            P(None, "narrow"),
            P("narrow", None),
            P(),
            P(),
            P(),
            P(),
        ),
        check_vma=False,
    )
```

```python
import math

import jax
import jax.numpy as jnp
from jax import lax
from jax.sharding import PartitionSpec as P

HD = 64
EPS = 1e-05
MASKED = -1e30
F32 = jnp.float32
BF16 = jnp.bfloat16


def normalize(values, gain_vec, bias_vec):
    centred = values - jnp.mean(values, axis=-1, keepdims=True)
    inverse = lax.rsqrt(jnp.mean(centred * centred, axis=-1, keepdims=True) + EPS)
    scaled = centred * inverse
    return (scaled * gain_vec + bias_vec, scaled, inverse)


def normalize_back(grad_in, scaled, inverse, gain_vec):
    along = grad_in * gain_vec
    return inverse * (
        along
        - jnp.mean(along, axis=-1, keepdims=True)
        - scaled * jnp.mean(along * scaled, axis=-1, keepdims=True)
    )


def contract_last(left_side, right_side):
    return lax.dot_general(
        left_side, right_side, (((1,), (1,)), ((), ())), preferred_element_type=F32
    )


def contract_first(left_side, right_side):
    return lax.dot_general(
        left_side, right_side, (((0,), (0,)), ((), ())), preferred_element_type=F32
    )


def rotate(values, cosine_table, sine_table):
    half_width = values.shape[-1] // 2
    first_half = values[..., :half_width]
    second_half = values[..., half_width:]
    cosine = cosine_table[:, None, :]
    sine_part = sine_table[:, None, :]
    return jnp.concatenate(
        [
            first_half * cosine - second_half * sine_part,
            second_half * cosine + first_half * sine_part,
        ],
        axis=-1,
    )


def unrotate(values, cosine_table, sine_table):
    half_width = values.shape[-1] // 2
    first_half = values[..., :half_width]
    second_half = values[..., half_width:]
    cosine = cosine_table[:, None, :]
    sine_part = sine_table[:, None, :]
    return jnp.concatenate(
        [
            first_half * cosine + second_half * sine_part,
            second_half * cosine - first_half * sine_part,
        ],
        axis=-1,
    )


def narrow_gather(own, count):
    slots = jnp.broadcast_to(own[None], (count,) + own.shape)
    got = lax.all_to_all(slots, "narrow", 0, 0, tiled=False)
    return got.reshape(count * own.shape[0], own.shape[1])


def narrow_scatter(partial, count):
    blocks = partial.reshape(count, partial.shape[0] // count, partial.shape[1])
    got = lax.all_to_all(blocks, "narrow", 0, 0, tiled=False)
    return jnp.sum(got.astype(F32), axis=0)


def narrow_gather_async(own, count):
    index = lax.axis_index("narrow")
    rows = own.shape[0]
    whole = jnp.zeros((count * rows, own.shape[1]), own.dtype)
    whole = lax.dynamic_update_slice_in_dim(whole, own, index * rows, 0)
    for k in range(1, count):
        got = lax.ppermute(own, "narrow", [((i + k) % count, i) for i in range(count)])
        whole = lax.dynamic_update_slice_in_dim(whole, got, ((index + k) % count) * rows, 0)
    return whole


def split_hi_lo(values):
    high = values.astype(BF16)
    return high, (values - high.astype(F32)).astype(BF16)


def narrow_maps(count):
    plane = count // 2

    def build(mapping):
        return [(z * plane + y, mapping(z, y)) for z in range(2) for y in range(plane)]

    up = build(lambda z, y: z * plane + (y + 1) % plane)
    down = build(lambda z, y: z * plane + (y - 1) % plane)
    across = build(lambda z, y: (1 - z) * plane + y)
    return up, down, across


def tree_gather(own, count):
    up, down, across = narrow_maps(count)
    from_below = lax.ppermute(own, "narrow", up)
    from_above = lax.ppermute(own, "narrow", down)
    from_across = lax.ppermute(own, "narrow", across)
    two_above = lax.ppermute(from_below, "narrow", up)
    across_above = lax.ppermute(from_across, "narrow", down)
    across_below = lax.ppermute(from_below, "narrow", across)
    across_two = lax.ppermute(two_above, "narrow", across)
    return [own, from_below, from_above, from_across, two_above, across_above, across_below, across_two]


def tree_scatter(blocks, count):
    up, down, across = narrow_maps(count)

    def send(value, pairs):
        return lax.ppermute(value.astype(BF16), "narrow", pairs).astype(F32)

    part = [blocks[s].astype(F32) for s in range(count)]
    first = send(part[7], across)
    below = send(part[4] + first, down)
    side = send(part[6], across)
    over = send(part[5], up)
    total = part[0] + send(part[1] + below + side, down)
    total = total + send(part[3] + over, across)
    return total + send(part[2], up)


def slot_sources(count):
    plane = count // 2
    index = lax.axis_index("narrow")
    z, y = index // plane, index % plane
    dz = jnp.array([0, 0, 0, 1, 0, 1, 1, 1], jnp.int32)
    dy = jnp.array([0, -1, 1, 0, 2, 1, -1, 2], jnp.int32)
    return ((z + dz) % 2) * plane + (y + dy) % plane


def source_slots(count):
    plane = count // 2
    index = lax.axis_index("narrow")
    z, y = index // plane, index % plane
    block = jnp.arange(count)
    dz = (block // plane - z) % 2
    dy = (block % plane - y) % plane
    same = jnp.array([0, 2, 4, 1], jnp.int32)
    other = jnp.array([3, 5, 7, 6], jnp.int32)
    return jnp.where(dz == 0, same[dy], other[dy])


def wide_layout(wide):
    chips_x = wide // 4
    w = lax.axis_index("wide")
    return chips_x, w % 2, (w // 2) % chips_x, w // (2 * chips_x)


def wide_map(wide, dcore=0, dx=0, dz=0, flip_core=False, xor_x=0):
    chips_x = wide // 4
    pairs = []
    for v in range(wide):
        c, xx, zz = v % 2, (v // 2) % chips_x, v // (2 * chips_x)
        c2 = (1 - c) if flip_core else c
        x2 = ((xx ^ xor_x) + dx) % chips_x
        z2 = (zz + dz) % 2
        pairs.append((v, z2 * 2 * chips_x + x2 * 2 + c2))
    return pairs


def tie(value, anchor):
    return lax.optimization_barrier((value, anchor))[0]


def core_reduce(grad, wide):
    _, core, _, _ = wide_layout(wide)
    half = grad.shape[0] // 2
    keep = lax.dynamic_slice_in_dim(grad, core * half, half, 0)
    send = lax.dynamic_slice_in_dim(grad, (1 - core) * half, half, 0)
    return keep.astype(F32) + lax.ppermute(send, "wide", wide_map(wide, flip_core=True)).astype(F32)


def x_reduce(summed, wide):
    chips_x, _, xpos, _ = wide_layout(wide)
    quarter = summed.shape[0] // chips_x
    acc = lax.dynamic_slice_in_dim(summed, xpos * quarter, quarter, 0)
    for k in range(1, chips_x):
        piece = lax.dynamic_slice_in_dim(summed, ((xpos + k) % chips_x) * quarter, quarter, 0)
        acc = acc + lax.ppermute(piece.astype(BF16), "wide", wide_map(wide, dx=k)).astype(F32)
    return acc


def z_reduce(acc, wide):
    _, _, _, zhi = wide_layout(wide)
    eighth = acc.shape[0] // 2
    mine = lax.dynamic_slice_in_dim(acc, zhi * eighth, eighth, 0)
    other = lax.dynamic_slice_in_dim(acc, (1 - zhi) * eighth, eighth, 0)
    got = lax.ppermute(other.astype(BF16), "wide", wide_map(wide, dz=1)).astype(F32)
    return (mine + got).astype(BF16)


def z_gather(final, wide):
    return jnp.concatenate([final, lax.ppermute(final, "wide", wide_map(wide, dz=1))], axis=0)


def x_gather(part, wide):
    chips_x = wide // 4
    pieces = [part]
    for k in range(1, chips_x):
        pieces.append(lax.ppermute(part, "wide", wide_map(wide, dx=chips_x - k)))
    return jnp.concatenate(pieces, axis=0)


def core_gather(halfrows, wide):
    partner = lax.ppermute(halfrows, "wide", wide_map(wide, flip_core=True))
    return jnp.concatenate([halfrows, partner], axis=0)


def unrotate_rows(rotated, wide):
    chips_x, core, xpos, zhi = wide_layout(wide)
    count = 4 * chips_x
    block = jnp.arange(count)
    half, quarter, eighth = block // (2 * chips_x), (block // 2) % chips_x, block % 2
    position = ((half - core) % 2) * (2 * chips_x) + ((quarter - xpos) % chips_x) * 2 + (eighth - zhi) % 2
    rows, cols = rotated.shape
    return jnp.take(rotated.reshape(count, rows // count, cols), position, axis=0).reshape(rows, cols)


def wide_allreduce(grad, wide):
    stage = z_gather(z_reduce(x_reduce(core_reduce(grad, wide), wide), wide), wide)
    return unrotate_rows(core_gather(x_gather(stage, wide), wide), wide).astype(F32)


def wide_allreduce_small(values, wide):
    chips_x = wide // 4
    values = values + lax.ppermute(values, "wide", wide_map(wide, flip_core=True))
    values = values + lax.ppermute(values, "wide", wide_map(wide, xor_x=1))
    if chips_x > 2:
        values = values + lax.ppermute(values, "wide", wide_map(wide, xor_x=2))
    return values + lax.ppermute(values, "wide", wide_map(wide, dz=1))


def per_device(
    tokens,
    cotangent,
    segments,
    w_query,
    w_key,
    w_value,
    w_out,
    w_gate,
    w_up,
    w_down,
    gain_one,
    bias_one,
    gain_two,
    bias_two,
):
    count = lax.axis_size("narrow")
    wide = lax.axis_size("wide")
    block, d_model = tokens.shape
    narrow_index = lax.axis_index("narrow")
    own_rows = narrow_index * block

    seg = segments[0]
    length = seg.shape[0]
    column = lax.broadcasted_iota(jnp.int32, (length, length), 1)
    same_orig = seg[:, None] == seg[None, :]
    first_index = jnp.min(jnp.where(same_orig, column, length), axis=-1)
    position = jnp.arange(length, dtype=jnp.int32) - first_index
    order = slot_sources(count)
    seg = jnp.take(seg.reshape(count, block), order, axis=0).reshape(length)
    position = jnp.take(position.reshape(count, block), order, axis=0).reshape(length)
    same_segment = seg[:, None] == seg[None, :]
    inverse = 10000.0 ** (-(2.0 * jnp.arange(HD // 2).astype(F32) / HD))
    angles = position.astype(F32)[:, None] * inverse
    cosine_table, sine_table = jnp.cos(angles), jnp.sin(angles)

    head_rows = w_out.shape[0]
    first = tree_gather(jnp.concatenate([tokens, cotangent, w_out], axis=0), count)
    tok_full = jnp.concatenate([piece[:block] for piece in first], axis=0)
    cot_full = jnp.concatenate([piece[block : 2 * block] for piece in first], axis=0)
    w_out_slots = jnp.stack([piece[2 * block :] for piece in first])

    inputs = tok_full.astype(F32)
    normed_float, scaled_one, inverse_one = normalize(inputs, gain_one, bias_one)
    normed_one = normed_float.astype(BF16)
    own_scaled_one = scaled_one[:block]
    own_inverse_one = inverse_one[:block]

    heads = w_query.shape[1] // HD
    head_shape = (length, heads, HD)
    queries = rotate(
        jnp.dot(normed_one, w_query, preferred_element_type=F32).reshape(head_shape),
        cosine_table,
        sine_table,
    ).astype(BF16)
    key_rows = rotate(
        jnp.dot(normed_one, w_key, preferred_element_type=F32).reshape(head_shape),
        cosine_table,
        sine_table,
    ).astype(BF16)
    value_rows = (
        jnp.dot(normed_one, w_value, preferred_element_type=F32).astype(BF16).reshape(head_shape)
    )
    score_scale = 1.0 / math.sqrt(HD)
    scores = (
        jnp.einsum("qhd,khd->hqk", queries, key_rows, preferred_element_type=F32) * score_scale
    )
    scores = jnp.where(same_segment[None], scores, MASKED)
    row_peak = jnp.max(scores, axis=-1, keepdims=True)
    exponent = jnp.exp(scores - row_peak)
    row_total = jnp.sum(exponent, axis=-1, keepdims=True)
    probs = exponent / row_total
    probs_low = probs.astype(BF16)
    attended = (
        jnp.einsum("hqk,khd->qhd", probs_low, value_rows, preferred_element_type=F32)
        .astype(BF16)
        .reshape(length, -1)
    )

    heads_cols = attended.shape[1]
    attended_orig = jnp.take(
        attended.reshape(count, block, heads_cols), source_slots(count), axis=0
    ).reshape(length, heads_cols)
    attended_all = jnp.take(
        jnp.stack(tree_gather(attended_orig, count)).reshape(count, count, block, heads_cols),
        order,
        axis=1,
    ).reshape(count, length, heads_cols)
    branch = jnp.einsum(
        "jtc,jcd->td", attended_all, w_out_slots, preferred_element_type=F32
    )
    middle = inputs + branch
    normed_two_float, scaled_two, inverse_two = normalize(middle, gain_two, bias_two)
    normed_two = normed_two_float.astype(BF16)

    gate_pre = jnp.dot(normed_two, w_gate, preferred_element_type=F32)
    up_pre = jnp.dot(normed_two, w_up, preferred_element_type=F32)
    sigmoid_gate = jax.nn.sigmoid(gate_pre)
    active = gate_pre * sigmoid_gate
    hidden = (active * up_pre).astype(BF16)
    ffn_partial = jnp.dot(hidden, w_down, preferred_element_type=F32).astype(BF16)

    hidden_grad = contract_last(cot_full, w_down)
    gate_grad = (
        hidden_grad * up_pre * sigmoid_gate * (1.0 + gate_pre * (1.0 - sigmoid_gate))
    ).astype(BF16)
    up_grad = (hidden_grad * active).astype(BF16)
    ffn_grads = jnp.concatenate(
        [
            contract_first(normed_two, jnp.concatenate([gate_grad, up_grad], axis=1)),
            contract_first(hidden, cot_full),
        ],
        axis=0,
    ).astype(BF16)
    ffn_core = core_reduce(ffn_grads, wide)
    two_partial = (contract_last(gate_grad, w_gate) + contract_last(up_grad, w_up)).astype(BF16)
    both = tree_scatter(
        jnp.concatenate([ffn_partial, two_partial], axis=1).reshape(count, block, 2 * d_model), count
    )
    layer_out = middle[:block] + both[:, :d_model]
    own_two_grad = both[:, d_model:]
    own_scaled_two = scaled_two[:block]
    own_inverse_two = inverse_two[:block]

    middle_grad = cotangent.astype(F32) + normalize_back(
        own_two_grad, own_scaled_two, own_inverse_two, gain_two
    )
    ffn_x = x_reduce(ffn_core, wide)
    branch_grad = jnp.concatenate(tree_gather(middle_grad.astype(BF16), count), axis=0)
    ffn_rows = x_gather(z_gather(z_reduce(ffn_x, wide), wide), wide)

    attended_grad = contract_last(branch_grad, w_out).astype(BF16).reshape(head_shape)
    prob_grad = jnp.einsum(
        "qhd,khd->hqk", attended_grad, value_rows, preferred_element_type=F32
    )
    score_grad = (
        probs * (prob_grad - jnp.sum(probs * prob_grad, axis=-1, keepdims=True))
    ).astype(BF16)
    query_grad = score_scale * jnp.einsum(
        "hqk,khd->qhd", score_grad, key_rows, preferred_element_type=F32
    )
    key_grad = score_scale * jnp.einsum(
        "hqk,qhd->khd", score_grad, queries, preferred_element_type=F32
    )
    value_grad = jnp.einsum(
        "hqk,qhd->khd", probs_low, attended_grad, preferred_element_type=F32
    ).astype(BF16).reshape(length, -1)
    query_grad = unrotate(query_grad, cosine_table, sine_table).astype(BF16).reshape(length, -1)
    key_grad = unrotate(key_grad, cosine_table, sine_table).astype(BF16).reshape(length, -1)
    projection_grads = jnp.concatenate([query_grad, key_grad, value_grad], axis=1)
    projections = w_query.shape[1]
    qkv_grads = contract_first(normed_one, projection_grads).astype(BF16)
    attn_grads = jnp.concatenate(
        [qkv_grads, contract_first(branch_grad, attended).astype(BF16)], axis=1
    )
    attn_total = wide_allreduce(attn_grads, wide)
    one_float = contract_last(
        projection_grads, jnp.concatenate([w_query, w_key, w_value], axis=1)
    )
    norm_one = jnp.stack(
        [jnp.sum(one_float * scaled_one, axis=0), jnp.sum(one_float, axis=0)]
    )
    norm_two = jnp.stack(
        [jnp.sum(own_two_grad * own_scaled_two, axis=0), jnp.sum(own_two_grad, axis=0)]
    )
    norm_parts = jnp.concatenate([norm_one, norm_two], axis=0)
    high, low = split_hi_lo(norm_parts)
    extra = jnp.concatenate([high, low, jnp.zeros((8, d_model), BF16)], axis=0)
    one_blocks = one_float.astype(BF16).reshape(count, block, d_model)
    payload = jnp.concatenate(
        [one_blocks, jnp.broadcast_to(extra[None], (count,) + extra.shape)], axis=1
    )
    by_device = jnp.take(payload, source_slots(count), axis=0)
    summed = jnp.sum(lax.all_to_all(by_device, "narrow", 0, 0, tiled=False).astype(F32), axis=0)
    ffn_total = unrotate_rows(core_gather(ffn_rows, wide), wide).astype(F32)
    own_one_grad = summed[:block]
    norm_narrow = summed[block : block + 4] + summed[block + 4 : block + 8]
    norm_total = wide_allreduce_small(norm_narrow, wide)
    input_grad = middle_grad + normalize_back(
        own_one_grad, own_scaled_one, own_inverse_one, gain_one
    )
    ff_cols = w_gate.shape[1]
    return (
        layer_out,
        input_grad,
        attn_total[:, :projections],
        attn_total[:, projections : 2 * projections],
        attn_total[:, 2 * projections : 3 * projections],
        attn_total[:, 3 * projections :].T,
        ffn_total[:d_model, :ff_cols],
        ffn_total[:d_model, ff_cols:],
        ffn_total[d_model:],
        norm_total[0],
        norm_total[1],
        norm_total[2],
        norm_total[3],
    )


def solution(mesh):
    placed = (
        P(("wide", "narrow"), None),
        P(("wide", "narrow"), None),
        P("wide", None),
        P(None, "narrow"),
        P(None, "narrow"),
        P(None, "narrow"),
        P("narrow", None),
        P(None, "narrow"),
        P(None, "narrow"),
        P("narrow", None),
        P(),
        P(),
        P(),
        P(),
    )
    return jax.shard_map(
        per_device,
        mesh=mesh,
        in_specs=placed,
        out_specs=(
            P(("wide", "narrow"), None),
            P(("wide", "narrow"), None),
            P(None, "narrow"),
            P(None, "narrow"),
            P(None, "narrow"),
            P("narrow", None),
            P(None, "narrow"),
            P(None, "narrow"),
            P("narrow", None),
            P(),
            P(),
            P(),
            P(),
        ),
        check_vma=False,
    )
```

```python
import math

import jax
import jax.numpy as jnp
from jax import lax
from jax.sharding import PartitionSpec as P

HD = 64
EPS = 1e-05
MASKED = -1e30
F32 = jnp.float32
BF16 = jnp.bfloat16


def normalize(values, gain_vec, bias_vec):
    centred = values - jnp.mean(values, axis=-1, keepdims=True)
    inverse = lax.rsqrt(jnp.mean(centred * centred, axis=-1, keepdims=True) + EPS)
    scaled = centred * inverse
    return (scaled * gain_vec + bias_vec, scaled, inverse)


def normalize_back(grad_in, scaled, inverse, gain_vec):
    along = grad_in * gain_vec
    return inverse * (
        along
        - jnp.mean(along, axis=-1, keepdims=True)
        - scaled * jnp.mean(along * scaled, axis=-1, keepdims=True)
    )


def contract_last(left_side, right_side):
    return lax.dot_general(
        left_side, right_side, (((1,), (1,)), ((), ())), preferred_element_type=F32
    )


def contract_first(left_side, right_side):
    return lax.dot_general(
        left_side, right_side, (((0,), (0,)), ((), ())), preferred_element_type=F32
    )


def rotate(values, cosine_table, sine_table):
    half_width = values.shape[-1] // 2
    first_half = values[..., :half_width]
    second_half = values[..., half_width:]
    cosine = cosine_table[:, None, :]
    sine_part = sine_table[:, None, :]
    return jnp.concatenate(
        [
            first_half * cosine - second_half * sine_part,
            second_half * cosine + first_half * sine_part,
        ],
        axis=-1,
    )


def unrotate(values, cosine_table, sine_table):
    half_width = values.shape[-1] // 2
    first_half = values[..., :half_width]
    second_half = values[..., half_width:]
    cosine = cosine_table[:, None, :]
    sine_part = sine_table[:, None, :]
    return jnp.concatenate(
        [
            first_half * cosine + second_half * sine_part,
            second_half * cosine - first_half * sine_part,
        ],
        axis=-1,
    )


def narrow_gather(own, count):
    slots = jnp.broadcast_to(own[None], (count,) + own.shape)
    got = lax.all_to_all(slots, "narrow", 0, 0, tiled=False)
    return got.reshape(count * own.shape[0], own.shape[1])


def narrow_scatter(partial, count):
    blocks = partial.reshape(count, partial.shape[0] // count, partial.shape[1])
    got = lax.all_to_all(blocks, "narrow", 0, 0, tiled=False)
    return jnp.sum(got.astype(F32), axis=0)


def narrow_gather_async(own, count):
    index = lax.axis_index("narrow")
    rows = own.shape[0]
    whole = jnp.zeros((count * rows, own.shape[1]), own.dtype)
    whole = lax.dynamic_update_slice_in_dim(whole, own, index * rows, 0)
    for k in range(1, count):
        got = lax.ppermute(own, "narrow", [((i + k) % count, i) for i in range(count)])
        whole = lax.dynamic_update_slice_in_dim(whole, got, ((index + k) % count) * rows, 0)
    return whole


def split_hi_lo(values):
    high = values.astype(BF16)
    return high, (values - high.astype(F32)).astype(BF16)


def narrow_maps(count):
    plane = count // 2

    def build(mapping):
        return [(z * plane + y, mapping(z, y)) for z in range(2) for y in range(plane)]

    up = build(lambda z, y: z * plane + (y + 1) % plane)
    down = build(lambda z, y: z * plane + (y - 1) % plane)
    across = build(lambda z, y: (1 - z) * plane + y)
    return up, down, across


def tree_gather(own, count):
    up, down, across = narrow_maps(count)
    from_below = lax.ppermute(own, "narrow", up)
    from_above = lax.ppermute(own, "narrow", down)
    from_across = lax.ppermute(own, "narrow", across)
    two_above = lax.ppermute(from_below, "narrow", up)
    across_above = lax.ppermute(from_across, "narrow", down)
    across_below = lax.ppermute(from_below, "narrow", across)
    across_two = lax.ppermute(two_above, "narrow", across)
    return [own, from_below, from_above, from_across, two_above, across_above, across_below, across_two]


def tree_scatter(blocks, count):
    up, down, across = narrow_maps(count)

    def send(value, pairs):
        return lax.ppermute(value.astype(BF16), "narrow", pairs).astype(F32)

    part = [blocks[s].astype(F32) for s in range(count)]
    first = send(part[7], across)
    below = send(part[4] + first, down)
    side = send(part[6], across)
    over = send(part[5], up)
    total = part[0] + send(part[1] + below + side, down)
    total = total + send(part[3] + over, across)
    return total + send(part[2], up)


def slot_sources(count):
    plane = count // 2
    index = lax.axis_index("narrow")
    z, y = index // plane, index % plane
    dz = jnp.array([0, 0, 0, 1, 0, 1, 1, 1], jnp.int32)
    dy = jnp.array([0, -1, 1, 0, 2, 1, -1, 2], jnp.int32)
    return ((z + dz) % 2) * plane + (y + dy) % plane


def source_slots(count):
    plane = count // 2
    index = lax.axis_index("narrow")
    z, y = index // plane, index % plane
    block = jnp.arange(count)
    dz = (block // plane - z) % 2
    dy = (block % plane - y) % plane
    same = jnp.array([0, 2, 4, 1], jnp.int32)
    other = jnp.array([3, 5, 7, 6], jnp.int32)
    return jnp.where(dz == 0, same[dy], other[dy])


def wide_layout(wide):
    chips_x = wide // 4
    w = lax.axis_index("wide")
    return chips_x, w % 2, (w // 2) % chips_x, w // (2 * chips_x)


def wide_map(wide, dcore=0, dx=0, dz=0, flip_core=False, xor_x=0):
    chips_x = wide // 4
    pairs = []
    for v in range(wide):
        c, xx, zz = v % 2, (v // 2) % chips_x, v // (2 * chips_x)
        c2 = (1 - c) if flip_core else c
        x2 = ((xx ^ xor_x) + dx) % chips_x
        z2 = (zz + dz) % 2
        pairs.append((v, z2 * 2 * chips_x + x2 * 2 + c2))
    return pairs


def tie(value, anchor):
    return lax.optimization_barrier((value, anchor))[0]


def core_reduce(grad, wide):
    _, core, _, _ = wide_layout(wide)
    half = grad.shape[0] // 2
    keep = lax.dynamic_slice_in_dim(grad, core * half, half, 0)
    send = lax.dynamic_slice_in_dim(grad, (1 - core) * half, half, 0)
    return keep.astype(F32) + lax.ppermute(send, "wide", wide_map(wide, flip_core=True)).astype(F32)


def x_reduce(summed, wide):
    chips_x, _, xpos, _ = wide_layout(wide)
    quarter = summed.shape[0] // chips_x
    acc = lax.dynamic_slice_in_dim(summed, xpos * quarter, quarter, 0)
    for k in range(1, chips_x):
        piece = lax.dynamic_slice_in_dim(summed, ((xpos + k) % chips_x) * quarter, quarter, 0)
        acc = acc + lax.ppermute(piece.astype(BF16), "wide", wide_map(wide, dx=k)).astype(F32)
    return acc


def z_reduce(acc, wide):
    _, _, _, zhi = wide_layout(wide)
    eighth = acc.shape[0] // 2
    mine = lax.dynamic_slice_in_dim(acc, zhi * eighth, eighth, 0)
    other = lax.dynamic_slice_in_dim(acc, (1 - zhi) * eighth, eighth, 0)
    got = lax.ppermute(other.astype(BF16), "wide", wide_map(wide, dz=1)).astype(F32)
    return (mine + got).astype(BF16)


def z_gather(final, wide):
    return jnp.concatenate([final, lax.ppermute(final, "wide", wide_map(wide, dz=1))], axis=0)


def x_gather(part, wide):
    chips_x = wide // 4
    pieces = [part]
    for k in range(1, chips_x):
        pieces.append(lax.ppermute(part, "wide", wide_map(wide, dx=chips_x - k)))
    return jnp.concatenate(pieces, axis=0)


def core_gather(halfrows, wide):
    partner = lax.ppermute(halfrows, "wide", wide_map(wide, flip_core=True))
    return jnp.concatenate([halfrows, partner], axis=0)


def unrotate_rows(rotated, wide):
    chips_x, core, xpos, zhi = wide_layout(wide)
    count = 4 * chips_x
    block = jnp.arange(count)
    half, quarter, eighth = block // (2 * chips_x), (block // 2) % chips_x, block % 2
    position = ((half - core) % 2) * (2 * chips_x) + ((quarter - xpos) % chips_x) * 2 + (eighth - zhi) % 2
    rows, cols = rotated.shape
    return jnp.take(rotated.reshape(count, rows // count, cols), position, axis=0).reshape(rows, cols)


def wide_allreduce(grad, wide):
    stage = z_gather(z_reduce(x_reduce(core_reduce(grad, wide), wide), wide), wide)
    return unrotate_rows(core_gather(x_gather(stage, wide), wide), wide).astype(F32)


def wide_allreduce_small(values, wide):
    chips_x = wide // 4
    values = values + lax.ppermute(values, "wide", wide_map(wide, flip_core=True))
    values = values + lax.ppermute(values, "wide", wide_map(wide, xor_x=1))
    if chips_x > 2:
        values = values + lax.ppermute(values, "wide", wide_map(wide, xor_x=2))
    return values + lax.ppermute(values, "wide", wide_map(wide, dz=1))


def per_device(
    tokens,
    cotangent,
    segments,
    w_query,
    w_key,
    w_value,
    w_out,
    w_gate,
    w_up,
    w_down,
    gain_one,
    bias_one,
    gain_two,
    bias_two,
):
    count = lax.axis_size("narrow")
    wide = lax.axis_size("wide")
    block, d_model = tokens.shape
    narrow_index = lax.axis_index("narrow")
    own_rows = narrow_index * block

    seg = segments[0]
    length = seg.shape[0]
    column = lax.broadcasted_iota(jnp.int32, (length, length), 1)
    same_orig = seg[:, None] == seg[None, :]
    first_index = jnp.min(jnp.where(same_orig, column, length), axis=-1)
    position = jnp.arange(length, dtype=jnp.int32) - first_index
    order = slot_sources(count)
    seg = jnp.take(seg.reshape(count, block), order, axis=0).reshape(length)
    position = jnp.take(position.reshape(count, block), order, axis=0).reshape(length)
    same_segment = seg[:, None] == seg[None, :]
    inverse = 10000.0 ** (-(2.0 * jnp.arange(HD // 2).astype(F32) / HD))
    angles = position.astype(F32)[:, None] * inverse
    cosine_table, sine_table = jnp.cos(angles), jnp.sin(angles)

    head_rows = w_out.shape[0]
    first = tree_gather(jnp.concatenate([tokens, cotangent, w_out], axis=0), count)
    tok_full = jnp.concatenate([piece[:block] for piece in first], axis=0)
    cot_full = jnp.concatenate([piece[block : 2 * block] for piece in first], axis=0)
    w_out_slots = jnp.stack([piece[2 * block :] for piece in first])

    inputs = tok_full.astype(F32)
    normed_float, scaled_one, inverse_one = normalize(inputs, gain_one, bias_one)
    normed_one = normed_float.astype(BF16)
    own_scaled_one = scaled_one[:block]
    own_inverse_one = inverse_one[:block]

    heads = w_query.shape[1] // HD
    head_shape = (length, heads, HD)
    queries = rotate(
        jnp.dot(normed_one, w_query, preferred_element_type=F32).reshape(head_shape),
        cosine_table,
        sine_table,
    ).astype(BF16)
    key_rows = rotate(
        jnp.dot(normed_one, w_key, preferred_element_type=F32).reshape(head_shape),
        cosine_table,
        sine_table,
    ).astype(BF16)
    value_rows = (
        jnp.dot(normed_one, w_value, preferred_element_type=F32).astype(BF16).reshape(head_shape)
    )
    score_scale = 1.0 / math.sqrt(HD)
    scores = (
        jnp.einsum("qhd,khd->hqk", queries, key_rows, preferred_element_type=F32) * score_scale
    )
    scores = jnp.where(same_segment[None], scores, MASKED)
    row_peak = jnp.max(scores, axis=-1, keepdims=True)
    exponent = jnp.exp(scores - row_peak)
    row_total = jnp.sum(exponent, axis=-1, keepdims=True)
    probs = exponent * (1.0 / row_total)
    probs_low = probs.astype(BF16)
    attended = (
        jnp.einsum("hqk,khd->qhd", probs_low, value_rows, preferred_element_type=F32)
        .astype(BF16)
        .reshape(length, -1)
    )

    heads_cols = attended.shape[1]
    attended_orig = jnp.take(
        attended.reshape(count, block, heads_cols), source_slots(count), axis=0
    ).reshape(length, heads_cols)
    attended_all = jnp.take(
        jnp.stack(tree_gather(attended_orig, count)).reshape(count, count, block, heads_cols),
        order,
        axis=1,
    ).reshape(count, length, heads_cols)
    branch = jnp.einsum(
        "jtc,jcd->td", attended_all, w_out_slots, preferred_element_type=F32
    )
    middle = inputs + branch
    normed_two_float, scaled_two, inverse_two = normalize(middle, gain_two, bias_two)
    normed_two = normed_two_float.astype(BF16)

    gate_pre = jnp.dot(normed_two, w_gate, preferred_element_type=F32)
    up_pre = jnp.dot(normed_two, w_up, preferred_element_type=F32)
    sigmoid_gate = jax.nn.sigmoid(gate_pre)
    active = gate_pre * sigmoid_gate
    hidden = (active * up_pre).astype(BF16)
    ffn_partial = jnp.dot(hidden, w_down, preferred_element_type=F32).astype(BF16)

    hidden_grad = contract_last(cot_full, w_down)
    gate_grad = (
        hidden_grad * up_pre * sigmoid_gate * (1.0 + gate_pre * (1.0 - sigmoid_gate))
    ).astype(BF16)
    up_grad = (hidden_grad * active).astype(BF16)
    ffn_grads = jnp.concatenate(
        [
            contract_first(normed_two, jnp.concatenate([gate_grad, up_grad], axis=1)),
            contract_first(hidden, cot_full),
        ],
        axis=0,
    ).astype(BF16)
    ffn_core = core_reduce(ffn_grads, wide)
    two_partial = (contract_last(gate_grad, w_gate) + contract_last(up_grad, w_up)).astype(BF16)
    both = tree_scatter(
        jnp.concatenate([ffn_partial, two_partial], axis=1).reshape(count, block, 2 * d_model), count
    )
    layer_out = middle[:block] + both[:, :d_model]
    own_two_grad = both[:, d_model:]
    own_scaled_two = scaled_two[:block]
    own_inverse_two = inverse_two[:block]

    middle_grad = cotangent.astype(F32) + normalize_back(
        own_two_grad, own_scaled_two, own_inverse_two, gain_two
    )
    ffn_x = x_reduce(ffn_core, wide)
    branch_grad = jnp.concatenate(tree_gather(middle_grad.astype(BF16), count), axis=0)
    ffn_rows = x_gather(z_gather(z_reduce(ffn_x, wide), wide), wide)

    attended_grad = contract_last(branch_grad, w_out).astype(BF16).reshape(head_shape)
    prob_grad = jnp.einsum(
        "qhd,khd->hqk", attended_grad, value_rows, preferred_element_type=F32
    )
    score_grad = (
        probs * (prob_grad - jnp.sum(probs * prob_grad, axis=-1, keepdims=True))
    ).astype(BF16)
    query_grad = score_scale * jnp.einsum(
        "hqk,khd->qhd", score_grad, key_rows, preferred_element_type=F32
    )
    key_grad = score_scale * jnp.einsum(
        "hqk,qhd->khd", score_grad, queries, preferred_element_type=F32
    )
    value_grad = jnp.einsum(
        "hqk,qhd->khd", probs_low, attended_grad, preferred_element_type=F32
    ).astype(BF16).reshape(length, -1)
    query_grad = unrotate(query_grad, cosine_table, sine_table).astype(BF16).reshape(length, -1)
    key_grad = unrotate(key_grad, cosine_table, sine_table).astype(BF16).reshape(length, -1)
    projection_grads = jnp.concatenate([query_grad, key_grad, value_grad], axis=1)
    projections = w_query.shape[1]
    qkv_grads = contract_first(normed_one, projection_grads).astype(BF16)
    attn_grads = jnp.concatenate(
        [qkv_grads, contract_first(branch_grad, attended).astype(BF16)], axis=1
    )
    attn_total = wide_allreduce(attn_grads, wide)
    one_float = contract_last(
        projection_grads, jnp.concatenate([w_query, w_key, w_value], axis=1)
    )
    norm_one = jnp.stack(
        [jnp.sum(one_float * scaled_one, axis=0), jnp.sum(one_float, axis=0)]
    )
    norm_two = jnp.stack(
        [jnp.sum(own_two_grad * own_scaled_two, axis=0), jnp.sum(own_two_grad, axis=0)]
    )
    norm_parts = jnp.concatenate([norm_one, norm_two], axis=0)
    high, low = split_hi_lo(norm_parts)
    extra = jnp.concatenate([high, low, jnp.zeros((8, d_model), BF16)], axis=0)
    one_blocks = one_float.astype(BF16).reshape(count, block, d_model)
    payload = jnp.concatenate(
        [one_blocks, jnp.broadcast_to(extra[None], (count,) + extra.shape)], axis=1
    )
    summed = tree_scatter(payload, count)
    ffn_total = unrotate_rows(core_gather(ffn_rows, wide), wide).astype(F32)
    own_one_grad = summed[:block]
    norm_narrow = summed[block : block + 4] + summed[block + 4 : block + 8]
    norm_total = wide_allreduce_small(norm_narrow, wide)
    input_grad = middle_grad + normalize_back(
        own_one_grad, own_scaled_one, own_inverse_one, gain_one
    )
    ff_cols = w_gate.shape[1]
    return (
        layer_out,
        input_grad,
        attn_total[:, :projections],
        attn_total[:, projections : 2 * projections],
        attn_total[:, 2 * projections : 3 * projections],
        attn_total[:, 3 * projections :].T,
        ffn_total[:d_model, :ff_cols],
        ffn_total[:d_model, ff_cols:],
        ffn_total[d_model:],
        norm_total[0],
        norm_total[1],
        norm_total[2],
        norm_total[3],
    )


def solution(mesh):
    placed = (
        P(("wide", "narrow"), None),
        P(("wide", "narrow"), None),
        P("wide", None),
        P(None, "narrow"),
        P(None, "narrow"),
        P(None, "narrow"),
        P("narrow", None),
        P(None, "narrow"),
        P(None, "narrow"),
        P("narrow", None),
        P(),
        P(),
        P(),
        P(),
    )
    return jax.shard_map(
        per_device,
        mesh=mesh,
        in_specs=placed,
        out_specs=(
            P(("wide", "narrow"), None),
            P(("wide", "narrow"), None),
            P(None, "narrow"),
            P(None, "narrow"),
            P(None, "narrow"),
            P("narrow", None),
            P(None, "narrow"),
            P(None, "narrow"),
            P("narrow", None),
            P(),
            P(),
            P(),
            P(),
        ),
        check_vma=False,
    )
```

```python
import math

import jax
import jax.numpy as jnp
from jax import lax
from jax.sharding import PartitionSpec as P

HD = 64
EPS = 1e-05
MASKED = -1e30
F32 = jnp.float32
BF16 = jnp.bfloat16


def normalize(values, gain_vec, bias_vec):
    centred = values - jnp.mean(values, axis=-1, keepdims=True)
    inverse = lax.rsqrt(jnp.mean(centred * centred, axis=-1, keepdims=True) + EPS)
    scaled = centred * inverse
    return (scaled * gain_vec + bias_vec, scaled, inverse)


def normalize_back(grad_in, scaled, inverse, gain_vec):
    along = grad_in * gain_vec
    return inverse * (
        along
        - jnp.mean(along, axis=-1, keepdims=True)
        - scaled * jnp.mean(along * scaled, axis=-1, keepdims=True)
    )


def contract_last(left_side, right_side):
    return lax.dot_general(
        left_side, right_side, (((1,), (1,)), ((), ())), preferred_element_type=F32
    )


def contract_first(left_side, right_side):
    return lax.dot_general(
        left_side, right_side, (((0,), (0,)), ((), ())), preferred_element_type=F32
    )


def rotate(values, cosine_table, sine_table):
    half_width = values.shape[-1] // 2
    first_half = values[..., :half_width]
    second_half = values[..., half_width:]
    cosine = cosine_table[:, None, :]
    sine_part = sine_table[:, None, :]
    return jnp.concatenate(
        [
            first_half * cosine - second_half * sine_part,
            second_half * cosine + first_half * sine_part,
        ],
        axis=-1,
    )


def unrotate(values, cosine_table, sine_table):
    half_width = values.shape[-1] // 2
    first_half = values[..., :half_width]
    second_half = values[..., half_width:]
    cosine = cosine_table[:, None, :]
    sine_part = sine_table[:, None, :]
    return jnp.concatenate(
        [
            first_half * cosine + second_half * sine_part,
            second_half * cosine - first_half * sine_part,
        ],
        axis=-1,
    )


def narrow_gather(own, count):
    slots = jnp.broadcast_to(own[None], (count,) + own.shape)
    got = lax.all_to_all(slots, "narrow", 0, 0, tiled=False)
    return got.reshape(count * own.shape[0], own.shape[1])


def narrow_scatter(partial, count):
    blocks = partial.reshape(count, partial.shape[0] // count, partial.shape[1])
    got = lax.all_to_all(blocks, "narrow", 0, 0, tiled=False)
    return jnp.sum(got.astype(F32), axis=0)


def narrow_gather_async(own, count):
    index = lax.axis_index("narrow")
    rows = own.shape[0]
    whole = jnp.zeros((count * rows, own.shape[1]), own.dtype)
    whole = lax.dynamic_update_slice_in_dim(whole, own, index * rows, 0)
    for k in range(1, count):
        got = lax.ppermute(own, "narrow", [((i + k) % count, i) for i in range(count)])
        whole = lax.dynamic_update_slice_in_dim(whole, got, ((index + k) % count) * rows, 0)
    return whole


def split_hi_lo(values):
    high = values.astype(BF16)
    return high, (values - high.astype(F32)).astype(BF16)


def narrow_maps(count):
    plane = count // 2

    def build(mapping):
        return [(z * plane + y, mapping(z, y)) for z in range(2) for y in range(plane)]

    up = build(lambda z, y: z * plane + (y + 1) % plane)
    down = build(lambda z, y: z * plane + (y - 1) % plane)
    across = build(lambda z, y: (1 - z) * plane + y)
    return up, down, across


def tree_gather(own, count):
    up, down, across = narrow_maps(count)
    from_below = lax.ppermute(own, "narrow", up)
    from_above = lax.ppermute(own, "narrow", down)
    from_across = lax.ppermute(own, "narrow", across)
    two_above = lax.ppermute(from_below, "narrow", up)
    across_above = lax.ppermute(from_across, "narrow", down)
    across_below = lax.ppermute(from_below, "narrow", across)
    across_two = lax.ppermute(two_above, "narrow", across)
    return [own, from_below, from_above, from_across, two_above, across_above, across_below, across_two]


def tree_scatter(blocks, count):
    up, down, across = narrow_maps(count)

    def send(value, pairs):
        return lax.ppermute(value.astype(BF16), "narrow", pairs).astype(F32)

    part = [blocks[s].astype(F32) for s in range(count)]
    first = send(part[7], across)
    below = send(part[4] + first, down)
    side = send(part[6], across)
    over = send(part[5], up)
    total = part[0] + send(part[1] + below + side, down)
    total = total + send(part[3] + over, across)
    return total + send(part[2], up)


def slot_sources(count):
    plane = count // 2
    index = lax.axis_index("narrow")
    z, y = index // plane, index % plane
    dz = jnp.array([0, 0, 0, 1, 0, 1, 1, 1], jnp.int32)
    dy = jnp.array([0, -1, 1, 0, 2, 1, -1, 2], jnp.int32)
    return ((z + dz) % 2) * plane + (y + dy) % plane


def source_slots(count):
    plane = count // 2
    index = lax.axis_index("narrow")
    z, y = index // plane, index % plane
    block = jnp.arange(count)
    dz = (block // plane - z) % 2
    dy = (block % plane - y) % plane
    same = jnp.array([0, 2, 4, 1], jnp.int32)
    other = jnp.array([3, 5, 7, 6], jnp.int32)
    return jnp.where(dz == 0, same[dy], other[dy])


def wide_layout(wide):
    chips_x = wide // 4
    w = lax.axis_index("wide")
    return chips_x, w % 2, (w // 2) % chips_x, w // (2 * chips_x)


def wide_map(wide, dcore=0, dx=0, dz=0, flip_core=False, xor_x=0):
    chips_x = wide // 4
    pairs = []
    for v in range(wide):
        c, xx, zz = v % 2, (v // 2) % chips_x, v // (2 * chips_x)
        c2 = (1 - c) if flip_core else c
        x2 = ((xx ^ xor_x) + dx) % chips_x
        z2 = (zz + dz) % 2
        pairs.append((v, z2 * 2 * chips_x + x2 * 2 + c2))
    return pairs


def tie(value, anchor):
    return lax.optimization_barrier((value, anchor))[0]


def core_reduce(grad, wide):
    _, core, _, _ = wide_layout(wide)
    half = grad.shape[0] // 2
    keep = lax.dynamic_slice_in_dim(grad, core * half, half, 0)
    send = lax.dynamic_slice_in_dim(grad, (1 - core) * half, half, 0)
    return keep.astype(F32) + lax.ppermute(send, "wide", wide_map(wide, flip_core=True)).astype(F32)


def x_reduce(summed, wide):
    chips_x, _, xpos, _ = wide_layout(wide)
    quarter = summed.shape[0] // chips_x
    acc = lax.dynamic_slice_in_dim(summed, xpos * quarter, quarter, 0)
    for k in range(1, chips_x):
        piece = lax.dynamic_slice_in_dim(summed, ((xpos + k) % chips_x) * quarter, quarter, 0)
        acc = acc + lax.ppermute(piece.astype(BF16), "wide", wide_map(wide, dx=k)).astype(F32)
    return acc


def z_reduce(acc, wide):
    _, _, _, zhi = wide_layout(wide)
    eighth = acc.shape[0] // 2
    mine = lax.dynamic_slice_in_dim(acc, zhi * eighth, eighth, 0)
    other = lax.dynamic_slice_in_dim(acc, (1 - zhi) * eighth, eighth, 0)
    got = lax.ppermute(other.astype(BF16), "wide", wide_map(wide, dz=1)).astype(F32)
    return (mine + got).astype(BF16)


def z_gather(final, wide):
    return jnp.concatenate([final, lax.ppermute(final, "wide", wide_map(wide, dz=1))], axis=0)


def x_gather(part, wide):
    chips_x = wide // 4
    pieces = [part]
    for k in range(1, chips_x):
        pieces.append(lax.ppermute(part, "wide", wide_map(wide, dx=chips_x - k)))
    return jnp.concatenate(pieces, axis=0)


def core_gather(halfrows, wide):
    partner = lax.ppermute(halfrows, "wide", wide_map(wide, flip_core=True))
    return jnp.concatenate([halfrows, partner], axis=0)


def unrotate_rows(rotated, wide):
    chips_x, core, xpos, zhi = wide_layout(wide)
    count = 4 * chips_x
    block = jnp.arange(count)
    half, quarter, eighth = block // (2 * chips_x), (block // 2) % chips_x, block % 2
    position = ((half - core) % 2) * (2 * chips_x) + ((quarter - xpos) % chips_x) * 2 + (eighth - zhi) % 2
    rows, cols = rotated.shape
    return jnp.take(rotated.reshape(count, rows // count, cols), position, axis=0).reshape(rows, cols)


def wide_allreduce(grad, wide):
    stage = z_gather(z_reduce(x_reduce(core_reduce(grad, wide), wide), wide), wide)
    return unrotate_rows(core_gather(x_gather(stage, wide), wide), wide).astype(F32)


def wide_allreduce_small(values, wide):
    chips_x = wide // 4
    values = values + lax.ppermute(values, "wide", wide_map(wide, flip_core=True))
    values = values + lax.ppermute(values, "wide", wide_map(wide, xor_x=1))
    if chips_x > 2:
        values = values + lax.ppermute(values, "wide", wide_map(wide, xor_x=2))
    return values + lax.ppermute(values, "wide", wide_map(wide, dz=1))


def per_device(
    tokens,
    cotangent,
    segments,
    w_query,
    w_key,
    w_value,
    w_out,
    w_gate,
    w_up,
    w_down,
    gain_one,
    bias_one,
    gain_two,
    bias_two,
):
    count = lax.axis_size("narrow")
    wide = lax.axis_size("wide")
    block, d_model = tokens.shape
    narrow_index = lax.axis_index("narrow")
    own_rows = narrow_index * block

    seg = segments[0]
    length = seg.shape[0]
    column = lax.broadcasted_iota(jnp.int32, (length, length), 1)
    same_orig = seg[:, None] == seg[None, :]
    first_index = jnp.min(jnp.where(same_orig, column, length), axis=-1)
    position = jnp.arange(length, dtype=jnp.int32) - first_index
    order = slot_sources(count)
    seg = jnp.take(seg.reshape(count, block), order, axis=0).reshape(length)
    position = jnp.take(position.reshape(count, block), order, axis=0).reshape(length)
    same_segment = seg[:, None] == seg[None, :]
    inverse = 10000.0 ** (-(2.0 * jnp.arange(HD // 2).astype(F32) / HD))
    angles = position.astype(F32)[:, None] * inverse
    cosine_table, sine_table = jnp.cos(angles), jnp.sin(angles)

    head_rows = w_out.shape[0]
    first = tree_gather(jnp.concatenate([tokens, cotangent, w_out], axis=0), count)
    tok_full = jnp.concatenate([piece[:block] for piece in first], axis=0)
    cot_full = jnp.concatenate([piece[block : 2 * block] for piece in first], axis=0)
    w_out_slots = jnp.stack([piece[2 * block :] for piece in first])

    inputs = tok_full.astype(F32)
    normed_float, scaled_one, inverse_one = normalize(inputs, gain_one, bias_one)
    normed_one = normed_float.astype(BF16)
    own_scaled_one = scaled_one[:block]
    own_inverse_one = inverse_one[:block]

    heads = w_query.shape[1] // HD
    head_shape = (length, heads, HD)
    queries = rotate(
        jnp.dot(normed_one, w_query, preferred_element_type=F32).reshape(head_shape),
        cosine_table,
        sine_table,
    ).astype(BF16)
    key_rows = rotate(
        jnp.dot(normed_one, w_key, preferred_element_type=F32).reshape(head_shape),
        cosine_table,
        sine_table,
    ).astype(BF16)
    value_rows = (
        jnp.dot(normed_one, w_value, preferred_element_type=F32).astype(BF16).reshape(head_shape)
    )
    score_scale = 1.0 / math.sqrt(HD)
    scores = (
        jnp.einsum("qhd,khd->hqk", queries, key_rows, preferred_element_type=F32) * score_scale
    )
    scores = jnp.where(same_segment[None], scores, MASKED)
    row_peak = jnp.max(scores, axis=-1, keepdims=True)
    exponent = jnp.exp(scores - row_peak)
    row_total = jnp.sum(exponent, axis=-1, keepdims=True)
    probs = exponent * (1.0 / row_total)
    probs_low = probs.astype(BF16)
    attended = (
        jnp.einsum("hqk,khd->qhd", probs_low, value_rows, preferred_element_type=F32)
        .astype(BF16)
        .reshape(length, -1)
    )

    heads_cols = attended.shape[1]
    attended_orig = jnp.take(
        attended.reshape(count, block, heads_cols), source_slots(count), axis=0
    ).reshape(length, heads_cols)
    attended_all = jnp.take(
        jnp.stack(tree_gather(attended_orig, count)).reshape(count, count, block, heads_cols),
        order,
        axis=1,
    ).reshape(count, length, heads_cols)
    branch = jnp.einsum(
        "jtc,jcd->td", attended_all, w_out_slots, preferred_element_type=F32
    )
    middle = inputs + branch
    normed_two_float, scaled_two, inverse_two = normalize(middle, gain_two, bias_two)
    normed_two = normed_two_float.astype(BF16)

    ff_cols = w_gate.shape[1]
    w_gate_up = jnp.concatenate([w_gate, w_up], axis=1)
    gate_up = jnp.dot(normed_two, w_gate_up, preferred_element_type=F32)
    gate_pre, up_pre = gate_up[:, :ff_cols], gate_up[:, ff_cols:]
    sigmoid_gate = jax.nn.sigmoid(gate_pre)
    active = gate_pre * sigmoid_gate
    hidden = (active * up_pre).astype(BF16)
    ffn_partial = jnp.dot(hidden, w_down, preferred_element_type=F32).astype(BF16)

    hidden_grad = contract_last(cot_full, w_down)
    gate_grad = (
        hidden_grad * up_pre * sigmoid_gate * (1.0 + gate_pre * (1.0 - sigmoid_gate))
    ).astype(BF16)
    up_grad = (hidden_grad * active).astype(BF16)
    gate_up_grad = jnp.concatenate([gate_grad, up_grad], axis=1)
    ffn_grads = jnp.concatenate(
        [
            contract_first(normed_two, gate_up_grad),
            contract_first(hidden, cot_full),
        ],
        axis=0,
    ).astype(BF16)
    ffn_core = core_reduce(ffn_grads, wide)
    two_partial = contract_last(gate_up_grad, w_gate_up).astype(BF16)
    both = tree_scatter(
        jnp.concatenate([ffn_partial, two_partial], axis=1).reshape(count, block, 2 * d_model), count
    )
    layer_out = middle[:block] + both[:, :d_model]
    own_two_grad = both[:, d_model:]
    own_scaled_two = scaled_two[:block]
    own_inverse_two = inverse_two[:block]

    middle_grad = cotangent.astype(F32) + normalize_back(
        own_two_grad, own_scaled_two, own_inverse_two, gain_two
    )
    ffn_x = x_reduce(ffn_core, wide)
    branch_grad = jnp.concatenate(tree_gather(middle_grad.astype(BF16), count), axis=0)
    ffn_rows = x_gather(z_gather(z_reduce(ffn_x, wide), wide), wide)

    attended_grad = contract_last(branch_grad, w_out).astype(BF16).reshape(head_shape)
    prob_grad = jnp.einsum(
        "qhd,khd->hqk", attended_grad, value_rows, preferred_element_type=F32
    )
    score_grad = (
        probs * (prob_grad - jnp.sum(probs * prob_grad, axis=-1, keepdims=True))
    ).astype(BF16)
    query_grad = score_scale * jnp.einsum(
        "hqk,khd->qhd", score_grad, key_rows, preferred_element_type=F32
    )
    key_grad = score_scale * jnp.einsum(
        "hqk,qhd->khd", score_grad, queries, preferred_element_type=F32
    )
    value_grad = jnp.einsum(
        "hqk,qhd->khd", probs_low, attended_grad, preferred_element_type=F32
    ).astype(BF16).reshape(length, -1)
    query_grad = unrotate(query_grad, cosine_table, sine_table).astype(BF16).reshape(length, -1)
    key_grad = unrotate(key_grad, cosine_table, sine_table).astype(BF16).reshape(length, -1)
    projection_grads = jnp.concatenate([query_grad, key_grad, value_grad], axis=1)
    projections = w_query.shape[1]
    qkv_grads = contract_first(normed_one, projection_grads).astype(BF16)
    attn_grads = jnp.concatenate(
        [qkv_grads, contract_first(branch_grad, attended).astype(BF16)], axis=1
    )
    attn_total = wide_allreduce(attn_grads, wide)
    one_float = contract_last(
        projection_grads, jnp.concatenate([w_query, w_key, w_value], axis=1)
    )
    norm_one = jnp.stack(
        [jnp.sum(one_float * scaled_one, axis=0), jnp.sum(one_float, axis=0)]
    )
    norm_two = jnp.stack(
        [jnp.sum(own_two_grad * own_scaled_two, axis=0), jnp.sum(own_two_grad, axis=0)]
    )
    norm_parts = jnp.concatenate([norm_one, norm_two], axis=0)
    high, low = split_hi_lo(norm_parts)
    extra = jnp.concatenate([high, low, jnp.zeros((8, d_model), BF16)], axis=0)
    one_blocks = one_float.astype(BF16).reshape(count, block, d_model)
    payload = jnp.concatenate(
        [one_blocks, jnp.broadcast_to(extra[None], (count,) + extra.shape)], axis=1
    )
    summed = tree_scatter(payload, count)
    ffn_total = unrotate_rows(core_gather(ffn_rows, wide), wide).astype(F32)
    own_one_grad = summed[:block]
    norm_narrow = summed[block : block + 4] + summed[block + 4 : block + 8]
    norm_total = wide_allreduce_small(norm_narrow, wide)
    input_grad = middle_grad + normalize_back(
        own_one_grad, own_scaled_one, own_inverse_one, gain_one
    )
    return (
        layer_out,
        input_grad,
        attn_total[:, :projections],
        attn_total[:, projections : 2 * projections],
        attn_total[:, 2 * projections : 3 * projections],
        attn_total[:, 3 * projections :].T,
        ffn_total[:d_model, :ff_cols],
        ffn_total[:d_model, ff_cols:],
        ffn_total[d_model:],
        norm_total[0],
        norm_total[1],
        norm_total[2],
        norm_total[3],
    )


def solution(mesh):
    placed = (
        P(("wide", "narrow"), None),
        P(("wide", "narrow"), None),
        P("wide", None),
        P(None, "narrow"),
        P(None, "narrow"),
        P(None, "narrow"),
        P("narrow", None),
        P(None, "narrow"),
        P(None, "narrow"),
        P("narrow", None),
        P(),
        P(),
        P(),
        P(),
    )
    return jax.shard_map(
        per_device,
        mesh=mesh,
        in_specs=placed,
        out_specs=(
            P(("wide", "narrow"), None),
            P(("wide", "narrow"), None),
            P(None, "narrow"),
            P(None, "narrow"),
            P(None, "narrow"),
            P("narrow", None),
            P(None, "narrow"),
            P(None, "narrow"),
            P("narrow", None),
            P(),
            P(),
            P(),
            P(),
        ),
        check_vma=False,
    )
```

```python
import math

import jax
import jax.numpy as jnp
from jax import lax
from jax.sharding import PartitionSpec as P

HD = 64
EPS = 1e-05
MASKED = -1e30
F32 = jnp.float32
BF16 = jnp.bfloat16


def normalize(values, gain_vec, bias_vec):
    centred = values - jnp.mean(values, axis=-1, keepdims=True)
    inverse = lax.rsqrt(jnp.mean(centred * centred, axis=-1, keepdims=True) + EPS)
    scaled = centred * inverse
    return (scaled * gain_vec + bias_vec, scaled, inverse)


def normalize_back(grad_in, scaled, inverse, gain_vec):
    along = grad_in * gain_vec
    return inverse * (
        along
        - jnp.mean(along, axis=-1, keepdims=True)
        - scaled * jnp.mean(along * scaled, axis=-1, keepdims=True)
    )


def contract_last(left_side, right_side):
    return lax.dot_general(
        left_side, right_side, (((1,), (1,)), ((), ())), preferred_element_type=F32
    )


def contract_first(left_side, right_side):
    return lax.dot_general(
        left_side, right_side, (((0,), (0,)), ((), ())), preferred_element_type=F32
    )


def rotate(values, cosine_table, sine_table):
    half_width = values.shape[-1] // 2
    first_half = values[..., :half_width]
    second_half = values[..., half_width:]
    cosine = cosine_table[:, None, :]
    sine_part = sine_table[:, None, :]
    return jnp.concatenate(
        [
            first_half * cosine - second_half * sine_part,
            second_half * cosine + first_half * sine_part,
        ],
        axis=-1,
    )


def unrotate(values, cosine_table, sine_table):
    half_width = values.shape[-1] // 2
    first_half = values[..., :half_width]
    second_half = values[..., half_width:]
    cosine = cosine_table[:, None, :]
    sine_part = sine_table[:, None, :]
    return jnp.concatenate(
        [
            first_half * cosine + second_half * sine_part,
            second_half * cosine - first_half * sine_part,
        ],
        axis=-1,
    )


def narrow_gather(own, count):
    slots = jnp.broadcast_to(own[None], (count,) + own.shape)
    got = lax.all_to_all(slots, "narrow", 0, 0, tiled=False)
    return got.reshape(count * own.shape[0], own.shape[1])


def narrow_scatter(partial, count):
    blocks = partial.reshape(count, partial.shape[0] // count, partial.shape[1])
    got = lax.all_to_all(blocks, "narrow", 0, 0, tiled=False)
    return jnp.sum(got.astype(F32), axis=0)


def narrow_gather_async(own, count):
    index = lax.axis_index("narrow")
    rows = own.shape[0]
    whole = jnp.zeros((count * rows, own.shape[1]), own.dtype)
    whole = lax.dynamic_update_slice_in_dim(whole, own, index * rows, 0)
    for k in range(1, count):
        got = lax.ppermute(own, "narrow", [((i + k) % count, i) for i in range(count)])
        whole = lax.dynamic_update_slice_in_dim(whole, got, ((index + k) % count) * rows, 0)
    return whole


def split_hi_lo(values):
    high = values.astype(BF16)
    return high, (values - high.astype(F32)).astype(BF16)


def narrow_maps(count):
    plane = count // 2

    def build(mapping):
        return [(z * plane + y, mapping(z, y)) for z in range(2) for y in range(plane)]

    up = build(lambda z, y: z * plane + (y + 1) % plane)
    down = build(lambda z, y: z * plane + (y - 1) % plane)
    across = build(lambda z, y: (1 - z) * plane + y)
    return up, down, across


def tree_gather(own, count):
    up, down, across = narrow_maps(count)
    from_below = lax.ppermute(own, "narrow", up)
    from_above = lax.ppermute(own, "narrow", down)
    from_across = lax.ppermute(own, "narrow", across)
    two_above = lax.ppermute(from_below, "narrow", up)
    across_above = lax.ppermute(from_across, "narrow", down)
    across_below = lax.ppermute(from_below, "narrow", across)
    across_two = lax.ppermute(two_above, "narrow", across)
    return [own, from_below, from_above, from_across, two_above, across_above, across_below, across_two]


def tree_scatter(blocks, count):
    up, down, across = narrow_maps(count)

    def send(value, pairs):
        return lax.ppermute(value.astype(BF16), "narrow", pairs).astype(F32)

    part = [blocks[s].astype(F32) for s in range(count)]
    first = send(part[7], across)
    below = send(part[4] + first, down)
    side = send(part[6], across)
    over = send(part[5], up)
    total = part[0] + send(part[1] + below + side, down)
    total = total + send(part[3] + over, across)
    return total + send(part[2], up)


def slot_sources(count):
    plane = count // 2
    index = lax.axis_index("narrow")
    z, y = index // plane, index % plane
    dz = jnp.array([0, 0, 0, 1, 0, 1, 1, 1], jnp.int32)
    dy = jnp.array([0, -1, 1, 0, 2, 1, -1, 2], jnp.int32)
    return ((z + dz) % 2) * plane + (y + dy) % plane


def source_slots(count):
    plane = count // 2
    index = lax.axis_index("narrow")
    z, y = index // plane, index % plane
    block = jnp.arange(count)
    dz = (block // plane - z) % 2
    dy = (block % plane - y) % plane
    same = jnp.array([0, 2, 4, 1], jnp.int32)
    other = jnp.array([3, 5, 7, 6], jnp.int32)
    return jnp.where(dz == 0, same[dy], other[dy])


def wide_layout(wide):
    chips_x = wide // 4
    w = lax.axis_index("wide")
    return chips_x, w % 2, (w // 2) % chips_x, w // (2 * chips_x)


def wide_map(wide, dcore=0, dx=0, dz=0, flip_core=False, xor_x=0):
    chips_x = wide // 4
    pairs = []
    for v in range(wide):
        c, xx, zz = v % 2, (v // 2) % chips_x, v // (2 * chips_x)
        c2 = (1 - c) if flip_core else c
        x2 = ((xx ^ xor_x) + dx) % chips_x
        z2 = (zz + dz) % 2
        pairs.append((v, z2 * 2 * chips_x + x2 * 2 + c2))
    return pairs


def tie(value, anchor):
    return lax.optimization_barrier((value, anchor))[0]


def core_reduce(grad, wide):
    _, core, _, _ = wide_layout(wide)
    half = grad.shape[0] // 2
    keep = lax.dynamic_slice_in_dim(grad, core * half, half, 0)
    send = lax.dynamic_slice_in_dim(grad, (1 - core) * half, half, 0)
    return keep.astype(F32) + lax.ppermute(send, "wide", wide_map(wide, flip_core=True)).astype(F32)


def x_reduce(summed, wide):
    chips_x, _, xpos, _ = wide_layout(wide)
    quarter = summed.shape[0] // chips_x
    acc = lax.dynamic_slice_in_dim(summed, xpos * quarter, quarter, 0)
    for k in range(1, chips_x):
        piece = lax.dynamic_slice_in_dim(summed, ((xpos + k) % chips_x) * quarter, quarter, 0)
        acc = acc + lax.ppermute(piece.astype(BF16), "wide", wide_map(wide, dx=k)).astype(F32)
    return acc


def z_reduce(acc, wide):
    _, _, _, zhi = wide_layout(wide)
    eighth = acc.shape[0] // 2
    mine = lax.dynamic_slice_in_dim(acc, zhi * eighth, eighth, 0)
    other = lax.dynamic_slice_in_dim(acc, (1 - zhi) * eighth, eighth, 0)
    got = lax.ppermute(other.astype(BF16), "wide", wide_map(wide, dz=1)).astype(F32)
    return (mine + got).astype(BF16)


def z_gather(final, wide):
    return jnp.concatenate([final, lax.ppermute(final, "wide", wide_map(wide, dz=1))], axis=0)


def x_gather(part, wide):
    chips_x = wide // 4
    pieces = [part]
    for k in range(1, chips_x):
        pieces.append(lax.ppermute(part, "wide", wide_map(wide, dx=chips_x - k)))
    return jnp.concatenate(pieces, axis=0)


def core_gather(halfrows, wide):
    partner = lax.ppermute(halfrows, "wide", wide_map(wide, flip_core=True))
    return jnp.concatenate([halfrows, partner], axis=0)


def unrotate_rows(rotated, wide):
    chips_x, core, xpos, zhi = wide_layout(wide)
    count = 4 * chips_x
    block = jnp.arange(count)
    half, quarter, eighth = block // (2 * chips_x), (block // 2) % chips_x, block % 2
    position = ((half - core) % 2) * (2 * chips_x) + ((quarter - xpos) % chips_x) * 2 + (eighth - zhi) % 2
    rows, cols = rotated.shape
    return jnp.take(rotated.reshape(count, rows // count, cols), position, axis=0).reshape(rows, cols)


def wide_allreduce(grad, wide):
    stage = z_gather(z_reduce(x_reduce(core_reduce(grad, wide), wide), wide), wide)
    return unrotate_rows(core_gather(x_gather(stage, wide), wide), wide).astype(F32)


def wide_allreduce_small(values, wide):
    chips_x = wide // 4
    values = values + lax.ppermute(values, "wide", wide_map(wide, flip_core=True))
    values = values + lax.ppermute(values, "wide", wide_map(wide, xor_x=1))
    if chips_x > 2:
        values = values + lax.ppermute(values, "wide", wide_map(wide, xor_x=2))
    return values + lax.ppermute(values, "wide", wide_map(wide, dz=1))


def per_device(
    tokens,
    cotangent,
    segments,
    w_query,
    w_key,
    w_value,
    w_out,
    w_gate,
    w_up,
    w_down,
    gain_one,
    bias_one,
    gain_two,
    bias_two,
):
    count = lax.axis_size("narrow")
    wide = lax.axis_size("wide")
    block, d_model = tokens.shape
    narrow_index = lax.axis_index("narrow")
    own_rows = narrow_index * block

    seg = segments[0]
    length = seg.shape[0]
    column = lax.broadcasted_iota(jnp.int32, (length, length), 1)
    same_orig = seg[:, None] == seg[None, :]
    first_index = jnp.min(jnp.where(same_orig, column, length), axis=-1)
    position = jnp.arange(length, dtype=jnp.int32) - first_index
    order = slot_sources(count)
    seg = jnp.take(seg.reshape(count, block), order, axis=0).reshape(length)
    position = jnp.take(position.reshape(count, block), order, axis=0).reshape(length)
    same_segment = seg[:, None] == seg[None, :]
    inverse = 10000.0 ** (-(2.0 * jnp.arange(HD // 2).astype(F32) / HD))
    angles = position.astype(F32)[:, None] * inverse
    cosine_table, sine_table = jnp.cos(angles), jnp.sin(angles)

    head_rows = w_out.shape[0]
    first = tree_gather(jnp.concatenate([tokens, cotangent, w_out], axis=0), count)
    tok_full = jnp.concatenate([piece[:block] for piece in first], axis=0)
    cot_full = jnp.concatenate([piece[block : 2 * block] for piece in first], axis=0)
    w_out_slots = jnp.stack([piece[2 * block :] for piece in first])

    inputs = tok_full.astype(F32)
    normed_float, scaled_one, inverse_one = normalize(inputs, gain_one, bias_one)
    normed_one = normed_float.astype(BF16)
    own_scaled_one = scaled_one[:block]
    own_inverse_one = inverse_one[:block]

    heads = w_query.shape[1] // HD
    head_shape = (length, heads, HD)
    queries = rotate(
        jnp.dot(normed_one, w_query, preferred_element_type=F32).reshape(head_shape),
        cosine_table,
        sine_table,
    ).astype(BF16)
    key_rows = rotate(
        jnp.dot(normed_one, w_key, preferred_element_type=F32).reshape(head_shape),
        cosine_table,
        sine_table,
    ).astype(BF16)
    value_rows = (
        jnp.dot(normed_one, w_value, preferred_element_type=F32).astype(BF16).reshape(head_shape)
    )
    score_scale = 1.0 / math.sqrt(HD)
    scores = (
        jnp.einsum("qhd,khd->hqk", queries, key_rows, preferred_element_type=F32) * score_scale
    )
    scores = jnp.where(same_segment[None], scores, MASKED)
    row_peak = jnp.max(scores, axis=-1, keepdims=True)
    exponent = jnp.exp(scores - row_peak)
    row_total = jnp.sum(exponent, axis=-1, keepdims=True)
    probs = exponent * (1.0 / row_total)
    probs_low = probs.astype(BF16)
    attended = (
        jnp.einsum("hqk,khd->qhd", probs_low, value_rows, preferred_element_type=F32)
        .astype(BF16)
        .reshape(length, -1)
    )

    heads_cols = attended.shape[1]
    attended_orig = jnp.take(
        attended.reshape(count, block, heads_cols), source_slots(count), axis=0
    ).reshape(length, heads_cols)
    attended_all = jnp.take(
        jnp.stack(tree_gather(attended_orig, count)).reshape(count, count, block, heads_cols),
        order,
        axis=1,
    ).reshape(count, length, heads_cols)
    branch = jnp.einsum(
        "jtc,jcd->td", attended_all, w_out_slots, preferred_element_type=F32
    )
    middle = inputs + branch
    normed_two_float, scaled_two, inverse_two = normalize(middle, gain_two, bias_two)
    normed_two = normed_two_float.astype(BF16)

    gate_pre = jnp.dot(normed_two, w_gate, preferred_element_type=F32)
    up_pre = jnp.dot(normed_two, w_up, preferred_element_type=F32)
    sigmoid_gate = 0.5 + 0.5 * jnp.tanh(0.5 * gate_pre)
    active = gate_pre * sigmoid_gate
    hidden = (active * up_pre).astype(BF16)
    ffn_partial = jnp.dot(hidden, w_down, preferred_element_type=F32).astype(BF16)

    hidden_grad = contract_last(cot_full, w_down)
    gate_grad = (
        hidden_grad * up_pre * sigmoid_gate * (1.0 + gate_pre * (1.0 - sigmoid_gate))
    ).astype(BF16)
    up_grad = (hidden_grad * active).astype(BF16)
    ffn_grads = jnp.concatenate(
        [
            contract_first(normed_two, jnp.concatenate([gate_grad, up_grad], axis=1)),
            contract_first(hidden, cot_full),
        ],
        axis=0,
    ).astype(BF16)
    ffn_core = core_reduce(ffn_grads, wide)
    two_partial = (contract_last(gate_grad, w_gate) + contract_last(up_grad, w_up)).astype(BF16)
    both = tree_scatter(
        jnp.concatenate([ffn_partial, two_partial], axis=1).reshape(count, block, 2 * d_model), count
    )
    layer_out = middle[:block] + both[:, :d_model]
    own_two_grad = both[:, d_model:]
    own_scaled_two = scaled_two[:block]
    own_inverse_two = inverse_two[:block]

    middle_grad = cotangent.astype(F32) + normalize_back(
        own_two_grad, own_scaled_two, own_inverse_two, gain_two
    )
    ffn_x = x_reduce(ffn_core, wide)
    branch_grad = jnp.concatenate(tree_gather(middle_grad.astype(BF16), count), axis=0)
    ffn_rows = x_gather(z_gather(z_reduce(ffn_x, wide), wide), wide)

    attended_grad = contract_last(branch_grad, w_out).astype(BF16).reshape(head_shape)
    prob_grad = jnp.einsum(
        "qhd,khd->hqk", attended_grad, value_rows, preferred_element_type=F32
    )
    score_grad = (
        probs * (prob_grad - jnp.sum(probs * prob_grad, axis=-1, keepdims=True))
    ).astype(BF16)
    query_grad = score_scale * jnp.einsum(
        "hqk,khd->qhd", score_grad, key_rows, preferred_element_type=F32
    )
    key_grad = score_scale * jnp.einsum(
        "hqk,qhd->khd", score_grad, queries, preferred_element_type=F32
    )
    value_grad = jnp.einsum(
        "hqk,qhd->khd", probs_low, attended_grad, preferred_element_type=F32
    ).astype(BF16).reshape(length, -1)
    query_grad = unrotate(query_grad, cosine_table, sine_table).astype(BF16).reshape(length, -1)
    key_grad = unrotate(key_grad, cosine_table, sine_table).astype(BF16).reshape(length, -1)
    projection_grads = jnp.concatenate([query_grad, key_grad, value_grad], axis=1)
    projections = w_query.shape[1]
    qkv_grads = contract_first(normed_one, projection_grads).astype(BF16)
    attn_grads = jnp.concatenate(
        [qkv_grads, contract_first(branch_grad, attended).astype(BF16)], axis=1
    )
    attn_total = wide_allreduce(attn_grads, wide)
    one_float = contract_last(
        projection_grads, jnp.concatenate([w_query, w_key, w_value], axis=1)
    )
    norm_one = jnp.stack(
        [jnp.sum(one_float * scaled_one, axis=0), jnp.sum(one_float, axis=0)]
    )
    norm_two = jnp.stack(
        [jnp.sum(own_two_grad * own_scaled_two, axis=0), jnp.sum(own_two_grad, axis=0)]
    )
    norm_parts = jnp.concatenate([norm_one, norm_two], axis=0)
    high, low = split_hi_lo(norm_parts)
    extra = jnp.concatenate([high, low, jnp.zeros((8, d_model), BF16)], axis=0)
    one_blocks = one_float.astype(BF16).reshape(count, block, d_model)
    payload = jnp.concatenate(
        [one_blocks, jnp.broadcast_to(extra[None], (count,) + extra.shape)], axis=1
    )
    summed = tree_scatter(payload, count)
    ffn_total = unrotate_rows(core_gather(ffn_rows, wide), wide).astype(F32)
    own_one_grad = summed[:block]
    norm_narrow = summed[block : block + 4] + summed[block + 4 : block + 8]
    norm_total = wide_allreduce_small(norm_narrow, wide)
    input_grad = middle_grad + normalize_back(
        own_one_grad, own_scaled_one, own_inverse_one, gain_one
    )
    ff_cols = w_gate.shape[1]
    return (
        layer_out,
        input_grad,
        attn_total[:, :projections],
        attn_total[:, projections : 2 * projections],
        attn_total[:, 2 * projections : 3 * projections],
        attn_total[:, 3 * projections :].T,
        ffn_total[:d_model, :ff_cols],
        ffn_total[:d_model, ff_cols:],
        ffn_total[d_model:],
        norm_total[0],
        norm_total[1],
        norm_total[2],
        norm_total[3],
    )


def solution(mesh):
    placed = (
        P(("wide", "narrow"), None),
        P(("wide", "narrow"), None),
        P("wide", None),
        P(None, "narrow"),
        P(None, "narrow"),
        P(None, "narrow"),
        P("narrow", None),
        P(None, "narrow"),
        P(None, "narrow"),
        P("narrow", None),
        P(),
        P(),
        P(),
        P(),
    )
    return jax.shard_map(
        per_device,
        mesh=mesh,
        in_specs=placed,
        out_specs=(
            P(("wide", "narrow"), None),
            P(("wide", "narrow"), None),
            P(None, "narrow"),
            P(None, "narrow"),
            P(None, "narrow"),
            P("narrow", None),
            P(None, "narrow"),
            P(None, "narrow"),
            P("narrow", None),
            P(),
            P(),
            P(),
            P(),
        ),
        check_vma=False,
    )
```

```python
import math

import jax
import jax.numpy as jnp
from jax import lax
from jax.sharding import PartitionSpec as P

HD = 64
EPS = 1e-05
MASKED = -1e30
F32 = jnp.float32
BF16 = jnp.bfloat16


def normalize(values, gain_vec, bias_vec):
    centred = values - jnp.mean(values, axis=-1, keepdims=True)
    inverse = lax.rsqrt(jnp.mean(centred * centred, axis=-1, keepdims=True) + EPS)
    scaled = centred * inverse
    return (scaled * gain_vec + bias_vec, scaled, inverse)


def normalize_back(grad_in, scaled, inverse, gain_vec):
    along = grad_in * gain_vec
    return inverse * (
        along
        - jnp.mean(along, axis=-1, keepdims=True)
        - scaled * jnp.mean(along * scaled, axis=-1, keepdims=True)
    )


def contract_last(left_side, right_side):
    return lax.dot_general(
        left_side, right_side, (((1,), (1,)), ((), ())), preferred_element_type=F32
    )


def contract_first(left_side, right_side):
    return lax.dot_general(
        left_side, right_side, (((0,), (0,)), ((), ())), preferred_element_type=F32
    )


def rotate(values, cosine_table, sine_table):
    half_width = values.shape[-1] // 2
    first_half = values[..., :half_width]
    second_half = values[..., half_width:]
    cosine = cosine_table[:, None, :]
    sine_part = sine_table[:, None, :]
    return jnp.concatenate(
        [
            first_half * cosine - second_half * sine_part,
            second_half * cosine + first_half * sine_part,
        ],
        axis=-1,
    )


def unrotate(values, cosine_table, sine_table):
    half_width = values.shape[-1] // 2
    first_half = values[..., :half_width]
    second_half = values[..., half_width:]
    cosine = cosine_table[:, None, :]
    sine_part = sine_table[:, None, :]
    return jnp.concatenate(
        [
            first_half * cosine + second_half * sine_part,
            second_half * cosine - first_half * sine_part,
        ],
        axis=-1,
    )


def narrow_gather(own, count):
    slots = jnp.broadcast_to(own[None], (count,) + own.shape)
    got = lax.all_to_all(slots, "narrow", 0, 0, tiled=False)
    return got.reshape(count * own.shape[0], own.shape[1])


def narrow_scatter(partial, count):
    blocks = partial.reshape(count, partial.shape[0] // count, partial.shape[1])
    got = lax.all_to_all(blocks, "narrow", 0, 0, tiled=False)
    return jnp.sum(got.astype(F32), axis=0)


def narrow_gather_async(own, count):
    index = lax.axis_index("narrow")
    rows = own.shape[0]
    whole = jnp.zeros((count * rows, own.shape[1]), own.dtype)
    whole = lax.dynamic_update_slice_in_dim(whole, own, index * rows, 0)
    for k in range(1, count):
        got = lax.ppermute(own, "narrow", [((i + k) % count, i) for i in range(count)])
        whole = lax.dynamic_update_slice_in_dim(whole, got, ((index + k) % count) * rows, 0)
    return whole


def split_hi_lo(values):
    high = values.astype(BF16)
    return high, (values - high.astype(F32)).astype(BF16)


def narrow_maps(count):
    plane = count // 2

    def build(mapping):
        return [(z * plane + y, mapping(z, y)) for z in range(2) for y in range(plane)]

    up = build(lambda z, y: z * plane + (y + 1) % plane)
    down = build(lambda z, y: z * plane + (y - 1) % plane)
    across = build(lambda z, y: (1 - z) * plane + y)
    return up, down, across


def tree_gather(own, count):
    up, down, across = narrow_maps(count)
    from_below = lax.ppermute(own, "narrow", up)
    from_above = lax.ppermute(own, "narrow", down)
    from_across = lax.ppermute(own, "narrow", across)
    two_above = lax.ppermute(from_below, "narrow", up)
    across_above = lax.ppermute(from_across, "narrow", down)
    across_below = lax.ppermute(from_below, "narrow", across)
    across_two = lax.ppermute(two_above, "narrow", across)
    return [own, from_below, from_above, from_across, two_above, across_above, across_below, across_two]


def tree_scatter(blocks, count):
    up, down, across = narrow_maps(count)

    def send(value, pairs):
        return lax.ppermute(value.astype(BF16), "narrow", pairs).astype(F32)

    part = [blocks[s].astype(F32) for s in range(count)]
    first = send(part[7], across)
    below = send(part[4] + first, down)
    side = send(part[6], across)
    over = send(part[5], up)
    total = part[0] + send(part[1] + below + side, down)
    total = total + send(part[3] + over, across)
    return total + send(part[2], up)


def slot_sources(count):
    plane = count // 2
    index = lax.axis_index("narrow")
    z, y = index // plane, index % plane
    dz = jnp.array([0, 0, 0, 1, 0, 1, 1, 1], jnp.int32)
    dy = jnp.array([0, -1, 1, 0, 2, 1, -1, 2], jnp.int32)
    return ((z + dz) % 2) * plane + (y + dy) % plane


def source_slots(count):
    plane = count // 2
    index = lax.axis_index("narrow")
    z, y = index // plane, index % plane
    block = jnp.arange(count)
    dz = (block // plane - z) % 2
    dy = (block % plane - y) % plane
    same = jnp.array([0, 2, 4, 1], jnp.int32)
    other = jnp.array([3, 5, 7, 6], jnp.int32)
    return jnp.where(dz == 0, same[dy], other[dy])


def wide_layout(wide):
    chips_x = wide // 4
    w = lax.axis_index("wide")
    return chips_x, w % 2, (w // 2) % chips_x, w // (2 * chips_x)


def wide_map(wide, dcore=0, dx=0, dz=0, flip_core=False, xor_x=0):
    chips_x = wide // 4
    pairs = []
    for v in range(wide):
        c, xx, zz = v % 2, (v // 2) % chips_x, v // (2 * chips_x)
        c2 = (1 - c) if flip_core else c
        x2 = ((xx ^ xor_x) + dx) % chips_x
        z2 = (zz + dz) % 2
        pairs.append((v, z2 * 2 * chips_x + x2 * 2 + c2))
    return pairs


def tie(value, anchor):
    return lax.optimization_barrier((value, anchor))[0]


def core_reduce(grad, wide):
    _, core, _, _ = wide_layout(wide)
    half = grad.shape[0] // 2
    keep = lax.dynamic_slice_in_dim(grad, core * half, half, 0)
    send = lax.dynamic_slice_in_dim(grad, (1 - core) * half, half, 0)
    return keep.astype(F32) + lax.ppermute(send, "wide", wide_map(wide, flip_core=True)).astype(F32)


def x_reduce(summed, wide):
    chips_x, _, xpos, _ = wide_layout(wide)
    quarter = summed.shape[0] // chips_x
    acc = lax.dynamic_slice_in_dim(summed, xpos * quarter, quarter, 0)
    for k in range(1, chips_x):
        piece = lax.dynamic_slice_in_dim(summed, ((xpos + k) % chips_x) * quarter, quarter, 0)
        acc = acc + lax.ppermute(piece.astype(BF16), "wide", wide_map(wide, dx=k)).astype(F32)
    return acc


def z_reduce(acc, wide):
    _, _, _, zhi = wide_layout(wide)
    eighth = acc.shape[0] // 2
    mine = lax.dynamic_slice_in_dim(acc, zhi * eighth, eighth, 0)
    other = lax.dynamic_slice_in_dim(acc, (1 - zhi) * eighth, eighth, 0)
    got = lax.ppermute(other.astype(BF16), "wide", wide_map(wide, dz=1)).astype(F32)
    return (mine + got).astype(BF16)


def z_gather(final, wide):
    return jnp.concatenate([final, lax.ppermute(final, "wide", wide_map(wide, dz=1))], axis=0)


def x_gather(part, wide):
    chips_x = wide // 4
    pieces = [part]
    for k in range(1, chips_x):
        pieces.append(lax.ppermute(part, "wide", wide_map(wide, dx=chips_x - k)))
    return jnp.concatenate(pieces, axis=0)


def core_gather(halfrows, wide):
    partner = lax.ppermute(halfrows, "wide", wide_map(wide, flip_core=True))
    return jnp.concatenate([halfrows, partner], axis=0)


def unrotate_rows(rotated, wide):
    chips_x, core, xpos, zhi = wide_layout(wide)
    count = 4 * chips_x
    block = jnp.arange(count)
    half, quarter, eighth = block // (2 * chips_x), (block // 2) % chips_x, block % 2
    position = ((half - core) % 2) * (2 * chips_x) + ((quarter - xpos) % chips_x) * 2 + (eighth - zhi) % 2
    rows, cols = rotated.shape
    return jnp.take(rotated.reshape(count, rows // count, cols), position, axis=0).reshape(rows, cols)


def wide_allreduce(grad, wide):
    stage = z_gather(z_reduce(x_reduce(core_reduce(grad, wide), wide), wide), wide)
    return unrotate_rows(core_gather(x_gather(stage, wide), wide), wide).astype(F32)


def wide_allreduce_small(values, wide):
    chips_x = wide // 4
    values = values + lax.ppermute(values, "wide", wide_map(wide, flip_core=True))
    values = values + lax.ppermute(values, "wide", wide_map(wide, xor_x=1))
    if chips_x > 2:
        values = values + lax.ppermute(values, "wide", wide_map(wide, xor_x=2))
    return values + lax.ppermute(values, "wide", wide_map(wide, dz=1))


def per_device(
    tokens,
    cotangent,
    segments,
    w_query,
    w_key,
    w_value,
    w_out,
    w_gate,
    w_up,
    w_down,
    gain_one,
    bias_one,
    gain_two,
    bias_two,
):
    count = lax.axis_size("narrow")
    wide = lax.axis_size("wide")
    block, d_model = tokens.shape
    narrow_index = lax.axis_index("narrow")
    own_rows = narrow_index * block

    seg = segments[0]
    length = seg.shape[0]
    column = lax.broadcasted_iota(jnp.int32, (length, length), 1)
    same_orig = seg[:, None] == seg[None, :]
    first_index = jnp.min(jnp.where(same_orig, column, length), axis=-1)
    position = jnp.arange(length, dtype=jnp.int32) - first_index
    order = slot_sources(count)
    seg = jnp.take(seg.reshape(count, block), order, axis=0).reshape(length)
    position = jnp.take(position.reshape(count, block), order, axis=0).reshape(length)
    same_segment = seg[:, None] == seg[None, :]
    inverse = 10000.0 ** (-(2.0 * jnp.arange(HD // 2).astype(F32) / HD))
    angles = position.astype(F32)[:, None] * inverse
    cosine_table, sine_table = jnp.cos(angles), jnp.sin(angles)

    head_rows = w_out.shape[0]
    first = tree_gather(jnp.concatenate([tokens, cotangent, w_out], axis=0), count)
    tok_full = jnp.concatenate([piece[:block] for piece in first], axis=0)
    cot_full = jnp.concatenate([piece[block : 2 * block] for piece in first], axis=0)
    w_out_slots = jnp.stack([piece[2 * block :] for piece in first])

    inputs = tok_full.astype(F32)
    normed_float, scaled_one, inverse_one = normalize(inputs, gain_one, bias_one)
    normed_one = normed_float.astype(BF16)
    own_scaled_one = scaled_one[:block]
    own_inverse_one = inverse_one[:block]

    heads = w_query.shape[1] // HD
    head_shape = (length, heads, HD)
    queries = rotate(
        jnp.dot(normed_one, w_query, preferred_element_type=F32).reshape(head_shape),
        cosine_table,
        sine_table,
    ).astype(BF16)
    key_rows = rotate(
        jnp.dot(normed_one, w_key, preferred_element_type=F32).reshape(head_shape),
        cosine_table,
        sine_table,
    ).astype(BF16)
    value_rows = (
        jnp.dot(normed_one, w_value, preferred_element_type=F32).astype(BF16).reshape(head_shape)
    )
    score_scale = 1.0 / math.sqrt(HD)
    scaled_queries = queries * jnp.asarray(score_scale, BF16)
    scores = jnp.einsum("qhd,khd->hqk", scaled_queries, key_rows, preferred_element_type=F32)
    scores = jnp.where(same_segment[None], scores, MASKED)
    row_peak = jnp.max(scores, axis=-1, keepdims=True)
    exponent = jnp.exp(scores - row_peak)
    row_total = jnp.sum(exponent, axis=-1, keepdims=True)
    probs = exponent * (1.0 / row_total)
    probs_low = probs.astype(BF16)
    attended = (
        jnp.einsum("hqk,khd->qhd", probs_low, value_rows, preferred_element_type=F32)
        .astype(BF16)
        .reshape(length, -1)
    )

    heads_cols = attended.shape[1]
    attended_orig = jnp.take(
        attended.reshape(count, block, heads_cols), source_slots(count), axis=0
    ).reshape(length, heads_cols)
    attended_all = jnp.take(
        jnp.stack(tree_gather(attended_orig, count)).reshape(count, count, block, heads_cols),
        order,
        axis=1,
    ).reshape(count, length, heads_cols)
    branch = jnp.einsum(
        "jtc,jcd->td", attended_all, w_out_slots, preferred_element_type=F32
    )
    middle = inputs + branch
    normed_two_float, scaled_two, inverse_two = normalize(middle, gain_two, bias_two)
    normed_two = normed_two_float.astype(BF16)

    gate_pre = jnp.dot(normed_two, w_gate, preferred_element_type=F32)
    up_pre = jnp.dot(normed_two, w_up, preferred_element_type=F32)
    sigmoid_gate = jax.nn.sigmoid(gate_pre)
    active = gate_pre * sigmoid_gate
    hidden = (active * up_pre).astype(BF16)
    ffn_partial = jnp.dot(hidden, w_down, preferred_element_type=F32).astype(BF16)

    hidden_grad = contract_last(cot_full, w_down)
    gate_grad = (
        hidden_grad * up_pre * sigmoid_gate * (1.0 + gate_pre * (1.0 - sigmoid_gate))
    ).astype(BF16)
    up_grad = (hidden_grad * active).astype(BF16)
    ffn_grads = jnp.concatenate(
        [
            contract_first(normed_two, jnp.concatenate([gate_grad, up_grad], axis=1)),
            contract_first(hidden, cot_full),
        ],
        axis=0,
    ).astype(BF16)
    ffn_core = core_reduce(ffn_grads, wide)
    two_partial = (contract_last(gate_grad, w_gate) + contract_last(up_grad, w_up)).astype(BF16)
    both = tree_scatter(
        jnp.concatenate([ffn_partial, two_partial], axis=1).reshape(count, block, 2 * d_model), count
    )
    layer_out = middle[:block] + both[:, :d_model]
    own_two_grad = both[:, d_model:]
    own_scaled_two = scaled_two[:block]
    own_inverse_two = inverse_two[:block]

    middle_grad = cotangent.astype(F32) + normalize_back(
        own_two_grad, own_scaled_two, own_inverse_two, gain_two
    )
    ffn_x = x_reduce(ffn_core, wide)
    branch_grad = jnp.concatenate(tree_gather(middle_grad.astype(BF16), count), axis=0)
    ffn_rows = x_gather(z_gather(z_reduce(ffn_x, wide), wide), wide)

    attended_grad = contract_last(branch_grad, w_out).astype(BF16).reshape(head_shape)
    prob_grad = jnp.einsum(
        "qhd,khd->hqk", attended_grad, value_rows, preferred_element_type=F32
    )
    score_grad = (
        probs * (prob_grad - jnp.sum(probs * prob_grad, axis=-1, keepdims=True))
    ).astype(BF16)
    query_grad = score_scale * jnp.einsum(
        "hqk,khd->qhd", score_grad, key_rows, preferred_element_type=F32
    )
    key_grad = jnp.einsum("hqk,qhd->khd", score_grad, scaled_queries, preferred_element_type=F32)
    value_grad = jnp.einsum(
        "hqk,qhd->khd", probs_low, attended_grad, preferred_element_type=F32
    ).astype(BF16).reshape(length, -1)
    query_grad = unrotate(query_grad, cosine_table, sine_table).astype(BF16).reshape(length, -1)
    key_grad = unrotate(key_grad, cosine_table, sine_table).astype(BF16).reshape(length, -1)
    projection_grads = jnp.concatenate([query_grad, key_grad, value_grad], axis=1)
    projections = w_query.shape[1]
    qkv_grads = contract_first(normed_one, projection_grads).astype(BF16)
    attn_grads = jnp.concatenate(
        [qkv_grads, contract_first(branch_grad, attended).astype(BF16)], axis=1
    )
    attn_total = wide_allreduce(attn_grads, wide)
    one_float = contract_last(
        projection_grads, jnp.concatenate([w_query, w_key, w_value], axis=1)
    )
    norm_one = jnp.stack(
        [jnp.sum(one_float * scaled_one, axis=0), jnp.sum(one_float, axis=0)]
    )
    norm_two = jnp.stack(
        [jnp.sum(own_two_grad * own_scaled_two, axis=0), jnp.sum(own_two_grad, axis=0)]
    )
    norm_parts = jnp.concatenate([norm_one, norm_two], axis=0)
    high, low = split_hi_lo(norm_parts)
    extra = jnp.concatenate([high, low, jnp.zeros((8, d_model), BF16)], axis=0)
    one_blocks = one_float.astype(BF16).reshape(count, block, d_model)
    payload = jnp.concatenate(
        [one_blocks, jnp.broadcast_to(extra[None], (count,) + extra.shape)], axis=1
    )
    summed = tree_scatter(payload, count)
    ffn_total = unrotate_rows(core_gather(ffn_rows, wide), wide).astype(F32)
    own_one_grad = summed[:block]
    norm_narrow = summed[block : block + 4] + summed[block + 4 : block + 8]
    norm_total = wide_allreduce_small(norm_narrow, wide)
    input_grad = middle_grad + normalize_back(
        own_one_grad, own_scaled_one, own_inverse_one, gain_one
    )
    ff_cols = w_gate.shape[1]
    return (
        layer_out,
        input_grad,
        attn_total[:, :projections],
        attn_total[:, projections : 2 * projections],
        attn_total[:, 2 * projections : 3 * projections],
        attn_total[:, 3 * projections :].T,
        ffn_total[:d_model, :ff_cols],
        ffn_total[:d_model, ff_cols:],
        ffn_total[d_model:],
        norm_total[0],
        norm_total[1],
        norm_total[2],
        norm_total[3],
    )


def solution(mesh):
    placed = (
        P(("wide", "narrow"), None),
        P(("wide", "narrow"), None),
        P("wide", None),
        P(None, "narrow"),
        P(None, "narrow"),
        P(None, "narrow"),
        P("narrow", None),
        P(None, "narrow"),
        P(None, "narrow"),
        P("narrow", None),
        P(),
        P(),
        P(),
        P(),
    )
    return jax.shard_map(
        per_device,
        mesh=mesh,
        in_specs=placed,
        out_specs=(
            P(("wide", "narrow"), None),
            P(("wide", "narrow"), None),
            P(None, "narrow"),
            P(None, "narrow"),
            P(None, "narrow"),
            P("narrow", None),
            P(None, "narrow"),
            P(None, "narrow"),
            P("narrow", None),
            P(),
            P(),
            P(),
            P(),
        ),
        check_vma=False,
    )
```

```python
import math

import jax
import jax.numpy as jnp
from jax import lax
from jax.sharding import PartitionSpec as P

HD = 64
EPS = 1e-05
MASKED = -1e30
F32 = jnp.float32
BF16 = jnp.bfloat16


def normalize(values, gain_vec, bias_vec):
    centred = values - jnp.mean(values, axis=-1, keepdims=True)
    inverse = lax.rsqrt(jnp.mean(centred * centred, axis=-1, keepdims=True) + EPS)
    scaled = centred * inverse
    return (scaled * gain_vec + bias_vec, scaled, inverse)


def normalize_back(grad_in, scaled, inverse, gain_vec):
    along = grad_in * gain_vec
    return inverse * (
        along
        - jnp.mean(along, axis=-1, keepdims=True)
        - scaled * jnp.mean(along * scaled, axis=-1, keepdims=True)
    )


def contract_last(left_side, right_side):
    return lax.dot_general(
        left_side, right_side, (((1,), (1,)), ((), ())), preferred_element_type=F32
    )


def contract_first(left_side, right_side):
    return lax.dot_general(
        left_side, right_side, (((0,), (0,)), ((), ())), preferred_element_type=F32
    )


def rotate(values, cosine_table, sine_table):
    half_width = values.shape[-1] // 2
    first_half = values[..., :half_width]
    second_half = values[..., half_width:]
    cosine = cosine_table[:, None, :]
    sine_part = sine_table[:, None, :]
    return jnp.concatenate(
        [
            first_half * cosine - second_half * sine_part,
            second_half * cosine + first_half * sine_part,
        ],
        axis=-1,
    )


def unrotate(values, cosine_table, sine_table):
    half_width = values.shape[-1] // 2
    first_half = values[..., :half_width]
    second_half = values[..., half_width:]
    cosine = cosine_table[:, None, :]
    sine_part = sine_table[:, None, :]
    return jnp.concatenate(
        [
            first_half * cosine + second_half * sine_part,
            second_half * cosine - first_half * sine_part,
        ],
        axis=-1,
    )


def narrow_gather(own, count):
    slots = jnp.broadcast_to(own[None], (count,) + own.shape)
    got = lax.all_to_all(slots, "narrow", 0, 0, tiled=False)
    return got.reshape(count * own.shape[0], own.shape[1])


def narrow_scatter(partial, count):
    blocks = partial.reshape(count, partial.shape[0] // count, partial.shape[1])
    got = lax.all_to_all(blocks, "narrow", 0, 0, tiled=False)
    return jnp.sum(got.astype(F32), axis=0)


def narrow_gather_async(own, count):
    index = lax.axis_index("narrow")
    rows = own.shape[0]
    whole = jnp.zeros((count * rows, own.shape[1]), own.dtype)
    whole = lax.dynamic_update_slice_in_dim(whole, own, index * rows, 0)
    for k in range(1, count):
        got = lax.ppermute(own, "narrow", [((i + k) % count, i) for i in range(count)])
        whole = lax.dynamic_update_slice_in_dim(whole, got, ((index + k) % count) * rows, 0)
    return whole


def split_hi_lo(values):
    high = values.astype(BF16)
    return high, (values - high.astype(F32)).astype(BF16)


def narrow_maps(count):
    plane = count // 2

    def build(mapping):
        return [(z * plane + y, mapping(z, y)) for z in range(2) for y in range(plane)]

    up = build(lambda z, y: z * plane + (y + 1) % plane)
    down = build(lambda z, y: z * plane + (y - 1) % plane)
    across = build(lambda z, y: (1 - z) * plane + y)
    return up, down, across


def tree_gather(own, count):
    up, down, across = narrow_maps(count)
    from_below = lax.ppermute(own, "narrow", up)
    from_above = lax.ppermute(own, "narrow", down)
    from_across = lax.ppermute(own, "narrow", across)
    two_above = lax.ppermute(from_below, "narrow", up)
    across_above = lax.ppermute(from_across, "narrow", down)
    across_below = lax.ppermute(from_below, "narrow", across)
    across_two = lax.ppermute(two_above, "narrow", across)
    return [own, from_below, from_above, from_across, two_above, across_above, across_below, across_two]


def tree_scatter(blocks, count):
    up, down, across = narrow_maps(count)

    def send(value, pairs):
        return lax.ppermute(value.astype(BF16), "narrow", pairs).astype(F32)

    part = [blocks[s].astype(F32) for s in range(count)]
    first = send(part[7], across)
    below = send(part[4] + first, down)
    side = send(part[6], across)
    over = send(part[5], up)
    total = part[0] + send(part[1] + below + side, down)
    total = total + send(part[3] + over, across)
    return total + send(part[2], up)


def slot_sources(count):
    plane = count // 2
    index = lax.axis_index("narrow")
    z, y = index // plane, index % plane
    dz = jnp.array([0, 0, 0, 1, 0, 1, 1, 1], jnp.int32)
    dy = jnp.array([0, -1, 1, 0, 2, 1, -1, 2], jnp.int32)
    return ((z + dz) % 2) * plane + (y + dy) % plane


def source_slots(count):
    plane = count // 2
    index = lax.axis_index("narrow")
    z, y = index // plane, index % plane
    block = jnp.arange(count)
    dz = (block // plane - z) % 2
    dy = (block % plane - y) % plane
    same = jnp.array([0, 2, 4, 1], jnp.int32)
    other = jnp.array([3, 5, 7, 6], jnp.int32)
    return jnp.where(dz == 0, same[dy], other[dy])


def wide_layout(wide):
    chips_x = wide // 4
    w = lax.axis_index("wide")
    return chips_x, w % 2, (w // 2) % chips_x, w // (2 * chips_x)


def wide_map(wide, dcore=0, dx=0, dz=0, flip_core=False, xor_x=0):
    chips_x = wide // 4
    pairs = []
    for v in range(wide):
        c, xx, zz = v % 2, (v // 2) % chips_x, v // (2 * chips_x)
        c2 = (1 - c) if flip_core else c
        x2 = ((xx ^ xor_x) + dx) % chips_x
        z2 = (zz + dz) % 2
        pairs.append((v, z2 * 2 * chips_x + x2 * 2 + c2))
    return pairs


def tie(value, anchor):
    return lax.optimization_barrier((value, anchor))[0]


def core_reduce(grad, wide):
    _, core, _, _ = wide_layout(wide)
    half = grad.shape[0] // 2
    keep = lax.dynamic_slice_in_dim(grad, core * half, half, 0)
    send = lax.dynamic_slice_in_dim(grad, (1 - core) * half, half, 0)
    return keep.astype(F32) + lax.ppermute(send, "wide", wide_map(wide, flip_core=True)).astype(F32)


def x_reduce(summed, wide):
    chips_x, _, xpos, _ = wide_layout(wide)
    quarter = summed.shape[0] // chips_x
    acc = lax.dynamic_slice_in_dim(summed, xpos * quarter, quarter, 0)
    for k in range(1, chips_x):
        piece = lax.dynamic_slice_in_dim(summed, ((xpos + k) % chips_x) * quarter, quarter, 0)
        acc = acc + lax.ppermute(piece.astype(BF16), "wide", wide_map(wide, dx=k)).astype(F32)
    return acc


def z_reduce(acc, wide):
    _, _, _, zhi = wide_layout(wide)
    eighth = acc.shape[0] // 2
    mine = lax.dynamic_slice_in_dim(acc, zhi * eighth, eighth, 0)
    other = lax.dynamic_slice_in_dim(acc, (1 - zhi) * eighth, eighth, 0)
    got = lax.ppermute(other.astype(BF16), "wide", wide_map(wide, dz=1)).astype(F32)
    return (mine + got).astype(BF16)


def z_gather(final, wide):
    return jnp.concatenate([final, lax.ppermute(final, "wide", wide_map(wide, dz=1))], axis=0)


def x_gather(part, wide):
    chips_x = wide // 4
    pieces = [part]
    for k in range(1, chips_x):
        pieces.append(lax.ppermute(part, "wide", wide_map(wide, dx=chips_x - k)))
    return jnp.concatenate(pieces, axis=0)


def core_gather(halfrows, wide):
    partner = lax.ppermute(halfrows, "wide", wide_map(wide, flip_core=True))
    return jnp.concatenate([halfrows, partner], axis=0)


def z_allreduce(acc, wide):
    mine = acc.astype(BF16)
    other = lax.ppermute(mine, "wide", wide_map(wide, dz=1))
    return (mine.astype(F32) + other.astype(F32)).astype(BF16)


def unrotate_rows(rotated, wide):
    chips_x, core, xpos, _ = wide_layout(wide)
    count = 2 * chips_x
    block = jnp.arange(count)
    half, quarter = block // chips_x, block % chips_x
    position = ((half - core) % 2) * chips_x + (quarter - xpos) % chips_x
    rows, cols = rotated.shape
    return jnp.take(rotated.reshape(count, rows // count, cols), position, axis=0).reshape(rows, cols)


def wide_allreduce(grad, wide):
    stage = z_allreduce(x_reduce(core_reduce(grad, wide), wide), wide)
    return unrotate_rows(core_gather(x_gather(stage, wide), wide), wide).astype(F32)


def wide_allreduce_small(values, wide):
    chips_x = wide // 4
    values = values + lax.ppermute(values, "wide", wide_map(wide, flip_core=True))
    values = values + lax.ppermute(values, "wide", wide_map(wide, xor_x=1))
    if chips_x > 2:
        values = values + lax.ppermute(values, "wide", wide_map(wide, xor_x=2))
    return values + lax.ppermute(values, "wide", wide_map(wide, dz=1))


def per_device(
    tokens,
    cotangent,
    segments,
    w_query,
    w_key,
    w_value,
    w_out,
    w_gate,
    w_up,
    w_down,
    gain_one,
    bias_one,
    gain_two,
    bias_two,
):
    count = lax.axis_size("narrow")
    wide = lax.axis_size("wide")
    block, d_model = tokens.shape
    narrow_index = lax.axis_index("narrow")
    own_rows = narrow_index * block

    seg = segments[0]
    length = seg.shape[0]
    column = lax.broadcasted_iota(jnp.int32, (length, length), 1)
    same_orig = seg[:, None] == seg[None, :]
    first_index = jnp.min(jnp.where(same_orig, column, length), axis=-1)
    position = jnp.arange(length, dtype=jnp.int32) - first_index
    order = slot_sources(count)
    seg = jnp.take(seg.reshape(count, block), order, axis=0).reshape(length)
    position = jnp.take(position.reshape(count, block), order, axis=0).reshape(length)
    same_segment = seg[:, None] == seg[None, :]
    inverse = 10000.0 ** (-(2.0 * jnp.arange(HD // 2).astype(F32) / HD))
    angles = position.astype(F32)[:, None] * inverse
    cosine_table, sine_table = jnp.cos(angles), jnp.sin(angles)

    head_rows = w_out.shape[0]
    first = tree_gather(jnp.concatenate([tokens, cotangent, w_out], axis=0), count)
    tok_full = jnp.concatenate([piece[:block] for piece in first], axis=0)
    cot_full = jnp.concatenate([piece[block : 2 * block] for piece in first], axis=0)
    w_out_slots = jnp.stack([piece[2 * block :] for piece in first])

    inputs = tok_full.astype(F32)
    normed_float, scaled_one, inverse_one = normalize(inputs, gain_one, bias_one)
    normed_one = normed_float.astype(BF16)
    own_scaled_one = scaled_one[:block]
    own_inverse_one = inverse_one[:block]

    heads = w_query.shape[1] // HD
    head_shape = (length, heads, HD)
    queries = rotate(
        jnp.dot(normed_one, w_query, preferred_element_type=F32).reshape(head_shape),
        cosine_table,
        sine_table,
    ).astype(BF16)
    key_rows = rotate(
        jnp.dot(normed_one, w_key, preferred_element_type=F32).reshape(head_shape),
        cosine_table,
        sine_table,
    ).astype(BF16)
    value_rows = (
        jnp.dot(normed_one, w_value, preferred_element_type=F32).astype(BF16).reshape(head_shape)
    )
    score_scale = 1.0 / math.sqrt(HD)
    scores = (
        jnp.einsum("qhd,khd->hqk", queries, key_rows, preferred_element_type=F32) * score_scale
    )
    scores = jnp.where(same_segment[None], scores, MASKED)
    row_peak = jnp.max(scores, axis=-1, keepdims=True)
    exponent = jnp.exp(scores - row_peak)
    row_total = jnp.sum(exponent, axis=-1, keepdims=True)
    probs = exponent * (1.0 / row_total)
    probs_low = probs.astype(BF16)
    attended = (
        jnp.einsum("hqk,khd->qhd", probs_low, value_rows, preferred_element_type=F32)
        .astype(BF16)
        .reshape(length, -1)
    )

    heads_cols = attended.shape[1]
    attended_orig = jnp.take(
        attended.reshape(count, block, heads_cols), source_slots(count), axis=0
    ).reshape(length, heads_cols)
    attended_all = jnp.take(
        jnp.stack(tree_gather(attended_orig, count)).reshape(count, count, block, heads_cols),
        order,
        axis=1,
    ).reshape(count, length, heads_cols)
    branch = jnp.einsum(
        "jtc,jcd->td", attended_all, w_out_slots, preferred_element_type=F32
    )
    middle = inputs + branch
    normed_two_float, scaled_two, inverse_two = normalize(middle, gain_two, bias_two)
    normed_two = normed_two_float.astype(BF16)

    gate_pre = jnp.dot(normed_two, w_gate, preferred_element_type=F32)
    up_pre = jnp.dot(normed_two, w_up, preferred_element_type=F32)
    sigmoid_gate = jax.nn.sigmoid(gate_pre)
    active = gate_pre * sigmoid_gate
    hidden = (active * up_pre).astype(BF16)
    ffn_partial = jnp.dot(hidden, w_down, preferred_element_type=F32).astype(BF16)

    hidden_grad = contract_last(cot_full, w_down)
    gate_grad = (
        hidden_grad * up_pre * sigmoid_gate * (1.0 + gate_pre * (1.0 - sigmoid_gate))
    ).astype(BF16)
    up_grad = (hidden_grad * active).astype(BF16)
    ffn_grads = jnp.concatenate(
        [
            contract_first(normed_two, jnp.concatenate([gate_grad, up_grad], axis=1)),
            contract_first(hidden, cot_full),
        ],
        axis=0,
    ).astype(BF16)
    ffn_core = core_reduce(ffn_grads, wide)
    two_partial = (contract_last(gate_grad, w_gate) + contract_last(up_grad, w_up)).astype(BF16)
    both = tree_scatter(
        jnp.concatenate([ffn_partial, two_partial], axis=1).reshape(count, block, 2 * d_model), count
    )
    layer_out = middle[:block] + both[:, :d_model]
    own_two_grad = both[:, d_model:]
    own_scaled_two = scaled_two[:block]
    own_inverse_two = inverse_two[:block]

    middle_grad = cotangent.astype(F32) + normalize_back(
        own_two_grad, own_scaled_two, own_inverse_two, gain_two
    )
    ffn_x = x_reduce(ffn_core, wide)
    branch_grad = jnp.concatenate(tree_gather(middle_grad.astype(BF16), count), axis=0)
    ffn_rows = x_gather(z_allreduce(ffn_x, wide), wide)

    attended_grad = contract_last(branch_grad, w_out).astype(BF16).reshape(head_shape)
    prob_grad = jnp.einsum(
        "qhd,khd->hqk", attended_grad, value_rows, preferred_element_type=F32
    )
    score_grad = (
        probs * (prob_grad - jnp.sum(probs * prob_grad, axis=-1, keepdims=True))
    ).astype(BF16)
    query_grad = score_scale * jnp.einsum(
        "hqk,khd->qhd", score_grad, key_rows, preferred_element_type=F32
    )
    key_grad = score_scale * jnp.einsum(
        "hqk,qhd->khd", score_grad, queries, preferred_element_type=F32
    )
    value_grad = jnp.einsum(
        "hqk,qhd->khd", probs_low, attended_grad, preferred_element_type=F32
    ).astype(BF16).reshape(length, -1)
    query_grad = unrotate(query_grad, cosine_table, sine_table).astype(BF16).reshape(length, -1)
    key_grad = unrotate(key_grad, cosine_table, sine_table).astype(BF16).reshape(length, -1)
    projection_grads = jnp.concatenate([query_grad, key_grad, value_grad], axis=1)
    projections = w_query.shape[1]
    qkv_grads = contract_first(normed_one, projection_grads).astype(BF16)
    attn_grads = jnp.concatenate(
        [qkv_grads, contract_first(branch_grad, attended).astype(BF16)], axis=1
    )
    attn_total = wide_allreduce(attn_grads, wide)
    one_float = contract_last(
        projection_grads, jnp.concatenate([w_query, w_key, w_value], axis=1)
    )
    norm_one = jnp.stack(
        [jnp.sum(one_float * scaled_one, axis=0), jnp.sum(one_float, axis=0)]
    )
    norm_two = jnp.stack(
        [jnp.sum(own_two_grad * own_scaled_two, axis=0), jnp.sum(own_two_grad, axis=0)]
    )
    norm_parts = jnp.concatenate([norm_one, norm_two], axis=0)
    high, low = split_hi_lo(norm_parts)
    extra = jnp.concatenate([high, low, jnp.zeros((8, d_model), BF16)], axis=0)
    one_blocks = one_float.astype(BF16).reshape(count, block, d_model)
    payload = jnp.concatenate(
        [one_blocks, jnp.broadcast_to(extra[None], (count,) + extra.shape)], axis=1
    )
    summed = tree_scatter(payload, count)
    ffn_total = unrotate_rows(core_gather(ffn_rows, wide), wide).astype(F32)
    own_one_grad = summed[:block]
    norm_narrow = summed[block : block + 4] + summed[block + 4 : block + 8]
    norm_total = wide_allreduce_small(norm_narrow, wide)
    input_grad = middle_grad + normalize_back(
        own_one_grad, own_scaled_one, own_inverse_one, gain_one
    )
    ff_cols = w_gate.shape[1]
    return (
        layer_out,
        input_grad,
        attn_total[:, :projections],
        attn_total[:, projections : 2 * projections],
        attn_total[:, 2 * projections : 3 * projections],
        attn_total[:, 3 * projections :].T,
        ffn_total[:d_model, :ff_cols],
        ffn_total[:d_model, ff_cols:],
        ffn_total[d_model:],
        norm_total[0],
        norm_total[1],
        norm_total[2],
        norm_total[3],
    )


def solution(mesh):
    placed = (
        P(("wide", "narrow"), None),
        P(("wide", "narrow"), None),
        P("wide", None),
        P(None, "narrow"),
        P(None, "narrow"),
        P(None, "narrow"),
        P("narrow", None),
        P(None, "narrow"),
        P(None, "narrow"),
        P("narrow", None),
        P(),
        P(),
        P(),
        P(),
    )
    return jax.shard_map(
        per_device,
        mesh=mesh,
        in_specs=placed,
        out_specs=(
            P(("wide", "narrow"), None),
            P(("wide", "narrow"), None),
            P(None, "narrow"),
            P(None, "narrow"),
            P(None, "narrow"),
            P("narrow", None),
            P(None, "narrow"),
            P(None, "narrow"),
            P("narrow", None),
            P(),
            P(),
            P(),
            P(),
        ),
        check_vma=False,
    )
```

```python
import math

import jax
import jax.numpy as jnp
from jax import lax
from jax.experimental import pallas as pl
from jax.sharding import PartitionSpec as P

HD = 64
EPS = 1e-05
MASKED = -1e30
F32 = jnp.float32
BF16 = jnp.bfloat16


def normalize(values, gain_vec, bias_vec):
    centred = values - jnp.mean(values, axis=-1, keepdims=True)
    inverse = lax.rsqrt(jnp.mean(centred * centred, axis=-1, keepdims=True) + EPS)
    scaled = centred * inverse
    return (scaled * gain_vec + bias_vec, scaled, inverse)


def normalize_back(grad_in, scaled, inverse, gain_vec):
    along = grad_in * gain_vec
    return inverse * (
        along
        - jnp.mean(along, axis=-1, keepdims=True)
        - scaled * jnp.mean(along * scaled, axis=-1, keepdims=True)
    )


def contract_last(left_side, right_side):
    return lax.dot_general(
        left_side, right_side, (((1,), (1,)), ((), ())), preferred_element_type=F32
    )


def contract_first(left_side, right_side):
    return lax.dot_general(
        left_side, right_side, (((0,), (0,)), ((), ())), preferred_element_type=F32
    )


def rotate(values, cosine_table, sine_table):
    half_width = values.shape[-1] // 2
    first_half = values[..., :half_width]
    second_half = values[..., half_width:]
    cosine = cosine_table[:, None, :]
    sine_part = sine_table[:, None, :]
    return jnp.concatenate(
        [
            first_half * cosine - second_half * sine_part,
            second_half * cosine + first_half * sine_part,
        ],
        axis=-1,
    )


def unrotate(values, cosine_table, sine_table):
    half_width = values.shape[-1] // 2
    first_half = values[..., :half_width]
    second_half = values[..., half_width:]
    cosine = cosine_table[:, None, :]
    sine_part = sine_table[:, None, :]
    return jnp.concatenate(
        [
            first_half * cosine + second_half * sine_part,
            second_half * cosine - first_half * sine_part,
        ],
        axis=-1,
    )


def join_rows(parts, splits=None):
    cols, dtype = parts[0].shape[1], parts[0].dtype
    if splits is None:
        pieces = [[(0, part.shape[0])] for part in parts]
        sizes = [sum(part.shape[0] for part in parts)]
        layout = [[(i, 0, part.shape[0]) for i, part in enumerate(parts)]]
    else:
        layout = []
        start = 0
        for size in splits:
            layout.append([(i, start, size) for i in range(len(parts))])
            start += size
        sizes = [len(parts) * size for size in splits]
    count = len(parts)

    def kernel(*refs):
        ins, outs = refs[:count], refs[count:]
        for out, plan in zip(outs, layout):
            row = 0
            for i, start, size in plan:
                out[row : row + size, :] = ins[i][start : start + size, :]
                row += size

    total = sum(part.shape[0] for part in parts)
    return pl.pallas_call(
        kernel,
        out_shape=[jax.ShapeDtypeStruct((size, cols), dtype) for size in sizes],
        cost_estimate=pl.CostEstimate(flops=0, transcendentals=0, bytes_accessed=4 * total * cols),
    )(*parts)


def narrow_gather(own, count):
    slots = jnp.broadcast_to(own[None], (count,) + own.shape)
    got = lax.all_to_all(slots, "narrow", 0, 0, tiled=False)
    return got.reshape(count * own.shape[0], own.shape[1])


def narrow_scatter(partial, count):
    blocks = partial.reshape(count, partial.shape[0] // count, partial.shape[1])
    got = lax.all_to_all(blocks, "narrow", 0, 0, tiled=False)
    return jnp.sum(got.astype(F32), axis=0)


def narrow_gather_async(own, count):
    index = lax.axis_index("narrow")
    rows = own.shape[0]
    whole = jnp.zeros((count * rows, own.shape[1]), own.dtype)
    whole = lax.dynamic_update_slice_in_dim(whole, own, index * rows, 0)
    for k in range(1, count):
        got = lax.ppermute(own, "narrow", [((i + k) % count, i) for i in range(count)])
        whole = lax.dynamic_update_slice_in_dim(whole, got, ((index + k) % count) * rows, 0)
    return whole


def split_hi_lo(values):
    high = values.astype(BF16)
    return high, (values - high.astype(F32)).astype(BF16)


def narrow_maps(count):
    plane = count // 2

    def build(mapping):
        return [(z * plane + y, mapping(z, y)) for z in range(2) for y in range(plane)]

    up = build(lambda z, y: z * plane + (y + 1) % plane)
    down = build(lambda z, y: z * plane + (y - 1) % plane)
    across = build(lambda z, y: (1 - z) * plane + y)
    return up, down, across


def tree_gather(own, count):
    up, down, across = narrow_maps(count)
    from_below = lax.ppermute(own, "narrow", up)
    from_above = lax.ppermute(own, "narrow", down)
    from_across = lax.ppermute(own, "narrow", across)
    two_above = lax.ppermute(from_below, "narrow", up)
    across_above = lax.ppermute(from_across, "narrow", down)
    across_below = lax.ppermute(from_below, "narrow", across)
    across_two = lax.ppermute(two_above, "narrow", across)
    return [own, from_below, from_above, from_across, two_above, across_above, across_below, across_two]


def tree_scatter(blocks, count):
    up, down, across = narrow_maps(count)

    def send(value, pairs):
        return lax.ppermute(value.astype(BF16), "narrow", pairs).astype(F32)

    part = [blocks[s].astype(F32) for s in range(count)]
    first = send(part[7], across)
    below = send(part[4] + first, down)
    side = send(part[6], across)
    over = send(part[5], up)
    total = part[0] + send(part[1] + below + side, down)
    total = total + send(part[3] + over, across)
    return total + send(part[2], up)


def slot_sources(count):
    plane = count // 2
    index = lax.axis_index("narrow")
    z, y = index // plane, index % plane
    dz = jnp.array([0, 0, 0, 1, 0, 1, 1, 1], jnp.int32)
    dy = jnp.array([0, -1, 1, 0, 2, 1, -1, 2], jnp.int32)
    return ((z + dz) % 2) * plane + (y + dy) % plane


def source_slots(count):
    plane = count // 2
    index = lax.axis_index("narrow")
    z, y = index // plane, index % plane
    block = jnp.arange(count)
    dz = (block // plane - z) % 2
    dy = (block % plane - y) % plane
    same = jnp.array([0, 2, 4, 1], jnp.int32)
    other = jnp.array([3, 5, 7, 6], jnp.int32)
    return jnp.where(dz == 0, same[dy], other[dy])


def wide_layout(wide):
    chips_x = wide // 4
    w = lax.axis_index("wide")
    return chips_x, w % 2, (w // 2) % chips_x, w // (2 * chips_x)


def wide_map(wide, dcore=0, dx=0, dz=0, flip_core=False, xor_x=0):
    chips_x = wide // 4
    pairs = []
    for v in range(wide):
        c, xx, zz = v % 2, (v // 2) % chips_x, v // (2 * chips_x)
        c2 = (1 - c) if flip_core else c
        x2 = ((xx ^ xor_x) + dx) % chips_x
        z2 = (zz + dz) % 2
        pairs.append((v, z2 * 2 * chips_x + x2 * 2 + c2))
    return pairs


def tie(value, anchor):
    return lax.optimization_barrier((value, anchor))[0]


def core_reduce(grad, wide):
    _, core, _, _ = wide_layout(wide)
    half = grad.shape[0] // 2
    keep = lax.dynamic_slice_in_dim(grad, core * half, half, 0)
    send = lax.dynamic_slice_in_dim(grad, (1 - core) * half, half, 0)
    return keep.astype(F32) + lax.ppermute(send, "wide", wide_map(wide, flip_core=True)).astype(F32)


def x_reduce(summed, wide):
    chips_x, _, xpos, _ = wide_layout(wide)
    quarter = summed.shape[0] // chips_x
    acc = lax.dynamic_slice_in_dim(summed, xpos * quarter, quarter, 0)
    for k in range(1, chips_x):
        piece = lax.dynamic_slice_in_dim(summed, ((xpos + k) % chips_x) * quarter, quarter, 0)
        acc = acc + lax.ppermute(piece.astype(BF16), "wide", wide_map(wide, dx=k)).astype(F32)
    return acc


def z_reduce(acc, wide):
    _, _, _, zhi = wide_layout(wide)
    eighth = acc.shape[0] // 2
    mine = lax.dynamic_slice_in_dim(acc, zhi * eighth, eighth, 0)
    other = lax.dynamic_slice_in_dim(acc, (1 - zhi) * eighth, eighth, 0)
    got = lax.ppermute(other.astype(BF16), "wide", wide_map(wide, dz=1)).astype(F32)
    return (mine + got).astype(BF16)


def z_gather(final, wide):
    return jnp.concatenate([final, lax.ppermute(final, "wide", wide_map(wide, dz=1))], axis=0)


def x_gather(part, wide):
    chips_x = wide // 4
    pieces = [part]
    for k in range(1, chips_x):
        pieces.append(lax.ppermute(part, "wide", wide_map(wide, dx=chips_x - k)))
    return jnp.concatenate(pieces, axis=0)


def core_gather(halfrows, wide):
    partner = lax.ppermute(halfrows, "wide", wide_map(wide, flip_core=True))
    return jnp.concatenate([halfrows, partner], axis=0)


def unrotate_rows(rotated, wide):
    chips_x, core, xpos, zhi = wide_layout(wide)
    count = 4 * chips_x
    block = jnp.arange(count)
    half, quarter, eighth = block // (2 * chips_x), (block // 2) % chips_x, block % 2
    position = ((half - core) % 2) * (2 * chips_x) + ((quarter - xpos) % chips_x) * 2 + (eighth - zhi) % 2
    rows, cols = rotated.shape
    return jnp.take(rotated.reshape(count, rows // count, cols), position, axis=0).reshape(rows, cols)


def wide_allreduce(grad, wide):
    stage = z_gather(z_reduce(x_reduce(core_reduce(grad, wide), wide), wide), wide)
    return unrotate_rows(core_gather(x_gather(stage, wide), wide), wide).astype(F32)


def wide_allreduce_small(values, wide):
    chips_x = wide // 4
    values = values + lax.ppermute(values, "wide", wide_map(wide, flip_core=True))
    values = values + lax.ppermute(values, "wide", wide_map(wide, xor_x=1))
    if chips_x > 2:
        values = values + lax.ppermute(values, "wide", wide_map(wide, xor_x=2))
    return values + lax.ppermute(values, "wide", wide_map(wide, dz=1))


def per_device(
    tokens,
    cotangent,
    segments,
    w_query,
    w_key,
    w_value,
    w_out,
    w_gate,
    w_up,
    w_down,
    gain_one,
    bias_one,
    gain_two,
    bias_two,
):
    count = lax.axis_size("narrow")
    wide = lax.axis_size("wide")
    block, d_model = tokens.shape
    narrow_index = lax.axis_index("narrow")
    own_rows = narrow_index * block

    seg = segments[0]
    length = seg.shape[0]
    column = lax.broadcasted_iota(jnp.int32, (length, length), 1)
    same_orig = seg[:, None] == seg[None, :]
    first_index = jnp.min(jnp.where(same_orig, column, length), axis=-1)
    position = jnp.arange(length, dtype=jnp.int32) - first_index
    order = slot_sources(count)
    seg = jnp.take(seg.reshape(count, block), order, axis=0).reshape(length)
    position = jnp.take(position.reshape(count, block), order, axis=0).reshape(length)
    same_segment = seg[:, None] == seg[None, :]
    inverse = 10000.0 ** (-(2.0 * jnp.arange(HD // 2).astype(F32) / HD))
    angles = position.astype(F32)[:, None] * inverse
    cosine_table, sine_table = jnp.cos(angles), jnp.sin(angles)

    head_rows = w_out.shape[0]
    first = tree_gather(join_rows([tokens, cotangent, w_out])[0], count)
    tok_full = jnp.concatenate([piece[:block] for piece in first], axis=0)
    cot_full = jnp.concatenate([piece[block : 2 * block] for piece in first], axis=0)
    w_out_slots = jnp.stack([piece[2 * block :] for piece in first])

    inputs = tok_full.astype(F32)
    normed_float, scaled_one, inverse_one = normalize(inputs, gain_one, bias_one)
    normed_one = normed_float.astype(BF16)
    own_scaled_one = scaled_one[:block]
    own_inverse_one = inverse_one[:block]

    heads = w_query.shape[1] // HD
    head_shape = (length, heads, HD)
    queries = rotate(
        jnp.dot(normed_one, w_query, preferred_element_type=F32).reshape(head_shape),
        cosine_table,
        sine_table,
    ).astype(BF16)
    key_rows = rotate(
        jnp.dot(normed_one, w_key, preferred_element_type=F32).reshape(head_shape),
        cosine_table,
        sine_table,
    ).astype(BF16)
    value_rows = (
        jnp.dot(normed_one, w_value, preferred_element_type=F32).astype(BF16).reshape(head_shape)
    )
    score_scale = 1.0 / math.sqrt(HD)
    scores = (
        jnp.einsum("qhd,khd->hqk", queries, key_rows, preferred_element_type=F32) * score_scale
    )
    scores = jnp.where(same_segment[None], scores, MASKED)
    row_peak = jnp.max(scores, axis=-1, keepdims=True)
    exponent = jnp.exp(scores - row_peak)
    row_total = jnp.sum(exponent, axis=-1, keepdims=True)
    probs = exponent * (1.0 / row_total)
    probs_low = probs.astype(BF16)
    attended = (
        jnp.einsum("hqk,khd->qhd", probs_low, value_rows, preferred_element_type=F32)
        .astype(BF16)
        .reshape(length, -1)
    )

    heads_cols = attended.shape[1]
    attended_orig = jnp.take(
        attended.reshape(count, block, heads_cols), source_slots(count), axis=0
    ).reshape(length, heads_cols)
    attended_all = jnp.take(
        jnp.stack(tree_gather(attended_orig, count)).reshape(count, count, block, heads_cols),
        order,
        axis=1,
    ).reshape(count, length, heads_cols)
    branch = jnp.einsum(
        "jtc,jcd->td", attended_all, w_out_slots, preferred_element_type=F32
    )
    middle = inputs + branch
    normed_two_float, scaled_two, inverse_two = normalize(middle, gain_two, bias_two)
    normed_two = normed_two_float.astype(BF16)

    gate_pre = jnp.dot(normed_two, w_gate, preferred_element_type=F32)
    up_pre = jnp.dot(normed_two, w_up, preferred_element_type=F32)
    sigmoid_gate = jax.nn.sigmoid(gate_pre)
    active = gate_pre * sigmoid_gate
    hidden = (active * up_pre).astype(BF16)
    ffn_partial = jnp.dot(hidden, w_down, preferred_element_type=F32).astype(BF16)

    hidden_grad = contract_last(cot_full, w_down)
    gate_grad = (
        hidden_grad * up_pre * sigmoid_gate * (1.0 + gate_pre * (1.0 - sigmoid_gate))
    ).astype(BF16)
    up_grad = (hidden_grad * active).astype(BF16)
    ffn_grads = jnp.concatenate(
        [
            contract_first(normed_two, jnp.concatenate([gate_grad, up_grad], axis=1)),
            contract_first(hidden, cot_full),
        ],
        axis=0,
    ).astype(BF16)
    ffn_core = core_reduce(ffn_grads, wide)
    two_partial = (contract_last(gate_grad, w_gate) + contract_last(up_grad, w_up)).astype(BF16)
    both = tree_scatter(
        jnp.concatenate([ffn_partial, two_partial], axis=1).reshape(count, block, 2 * d_model), count
    )
    layer_out = middle[:block] + both[:, :d_model]
    own_two_grad = both[:, d_model:]
    own_scaled_two = scaled_two[:block]
    own_inverse_two = inverse_two[:block]

    middle_grad = cotangent.astype(F32) + normalize_back(
        own_two_grad, own_scaled_two, own_inverse_two, gain_two
    )
    ffn_x = x_reduce(ffn_core, wide)
    branch_grad = jnp.concatenate(tree_gather(middle_grad.astype(BF16), count), axis=0)
    ffn_rows = x_gather(z_gather(z_reduce(ffn_x, wide), wide), wide)

    attended_grad = contract_last(branch_grad, w_out).astype(BF16).reshape(head_shape)
    prob_grad = jnp.einsum(
        "qhd,khd->hqk", attended_grad, value_rows, preferred_element_type=F32
    )
    score_grad = (
        probs * (prob_grad - jnp.sum(probs * prob_grad, axis=-1, keepdims=True))
    ).astype(BF16)
    query_grad = score_scale * jnp.einsum(
        "hqk,khd->qhd", score_grad, key_rows, preferred_element_type=F32
    )
    key_grad = score_scale * jnp.einsum(
        "hqk,qhd->khd", score_grad, queries, preferred_element_type=F32
    )
    value_grad = jnp.einsum(
        "hqk,qhd->khd", probs_low, attended_grad, preferred_element_type=F32
    ).astype(BF16).reshape(length, -1)
    query_grad = unrotate(query_grad, cosine_table, sine_table).astype(BF16).reshape(length, -1)
    key_grad = unrotate(key_grad, cosine_table, sine_table).astype(BF16).reshape(length, -1)
    projection_grads = jnp.concatenate([query_grad, key_grad, value_grad], axis=1)
    projections = w_query.shape[1]
    qkv_grads = contract_first(normed_one, projection_grads).astype(BF16)
    attn_grads = jnp.concatenate(
        [qkv_grads, contract_first(branch_grad, attended).astype(BF16)], axis=1
    )
    attn_total = wide_allreduce(attn_grads, wide)
    one_float = contract_last(
        projection_grads, jnp.concatenate([w_query, w_key, w_value], axis=1)
    )
    norm_one = jnp.stack(
        [jnp.sum(one_float * scaled_one, axis=0), jnp.sum(one_float, axis=0)]
    )
    norm_two = jnp.stack(
        [jnp.sum(own_two_grad * own_scaled_two, axis=0), jnp.sum(own_two_grad, axis=0)]
    )
    norm_parts = jnp.concatenate([norm_one, norm_two], axis=0)
    high, low = split_hi_lo(norm_parts)
    extra = jnp.concatenate([high, low, jnp.zeros((8, d_model), BF16)], axis=0)
    one_blocks = one_float.astype(BF16).reshape(count, block, d_model)
    payload = jnp.concatenate(
        [one_blocks, jnp.broadcast_to(extra[None], (count,) + extra.shape)], axis=1
    )
    summed = tree_scatter(payload, count)
    ffn_total = unrotate_rows(core_gather(ffn_rows, wide), wide).astype(F32)
    own_one_grad = summed[:block]
    norm_narrow = summed[block : block + 4] + summed[block + 4 : block + 8]
    norm_total = wide_allreduce_small(norm_narrow, wide)
    input_grad = middle_grad + normalize_back(
        own_one_grad, own_scaled_one, own_inverse_one, gain_one
    )
    ff_cols = w_gate.shape[1]
    return (
        layer_out,
        input_grad,
        attn_total[:, :projections],
        attn_total[:, projections : 2 * projections],
        attn_total[:, 2 * projections : 3 * projections],
        attn_total[:, 3 * projections :].T,
        ffn_total[:d_model, :ff_cols],
        ffn_total[:d_model, ff_cols:],
        ffn_total[d_model:],
        norm_total[0],
        norm_total[1],
        norm_total[2],
        norm_total[3],
    )


def solution(mesh):
    placed = (
        P(("wide", "narrow"), None),
        P(("wide", "narrow"), None),
        P("wide", None),
        P(None, "narrow"),
        P(None, "narrow"),
        P(None, "narrow"),
        P("narrow", None),
        P(None, "narrow"),
        P(None, "narrow"),
        P("narrow", None),
        P(),
        P(),
        P(),
        P(),
    )
    return jax.shard_map(
        per_device,
        mesh=mesh,
        in_specs=placed,
        out_specs=(
            P(("wide", "narrow"), None),
            P(("wide", "narrow"), None),
            P(None, "narrow"),
            P(None, "narrow"),
            P(None, "narrow"),
            P("narrow", None),
            P(None, "narrow"),
            P(None, "narrow"),
            P("narrow", None),
            P(),
            P(),
            P(),
            P(),
        ),
        check_vma=False,
    )
```
